32 devices in a mesh: wide: 8 (over z, y), narrow: 4 (over x, core).
Axes of the slice: x: 2, y: 2, z: 4, core: 2. Of those that a mesh axis runs over, the one named last changes fastest.
Arguments:
- latents: bfloat16 [32, 256, 768], P('wide', None, 'narrow'), may hold values from -6 to 6
- cotangent: bfloat16 [32, 256, 768], P('wide', None, 'narrow'), may hold values from -6 to 6
- timesteps: int32 [32], replicated, may hold values from 0 to 999, as said below
- time_in: float32 [256, 768], replicated, may hold values from -0.375 to 0.375
- time_out: float32 [768, 768], replicated, may hold values from -0.21875 to 0.21875
- ada_weight: float32 [768, 4608], replicated, may hold values from -0.21875 to 0.21875
- ada_bias: float32 [4608], replicated, may hold values from -3 to 3
- attn_kernel: float32 [9, 768], replicated, may hold values from -2 to 2
- qkv_weight: bfloat16 [3, 768, 768], P(None, None, 'narrow'), may hold values from -0.21875 to 0.21875
- out_weight: bfloat16 [768, 768], P('narrow'), may hold values from -0.875 to 0.875
- up_weight: bfloat16 [768, 3072], P(None, 'narrow'), may hold values from -0.21875 to 0.21875
- ffn_kernel: float32 [9, 3072], P(None, 'narrow'), may hold values from -2 to 2
- down_weight: bfloat16 [3072, 768], P('narrow'), may hold values from -0.21875 to 0.21875
Outputs:
- outputs: bfloat16 [32, 256, 768], P('wide', None, 'narrow')
- input_grad: bfloat16 [32, 256, 768], P('wide', None, 'narrow')
- time_in_grad: float32 [256, 768], replicated
- time_out_grad: float32 [768, 768], replicated
- ada_weight_grad: float32 [768, 4608], replicated
- ada_bias_grad: float32 [4608], replicated
- attn_kernel_grad: float32 [9, 768], replicated
- qkv_weight_grad: float32 [3, 768, 768], P(None, None, 'narrow')
- out_weight_grad: float32 [768, 768], P('narrow')
- up_weight_grad: float32 [768, 3072], P(None, 'narrow')
- ffn_kernel_grad: float32 [9, 3072], P(None, 'narrow')
- down_weight_grad: float32 [3072, 768], P('narrow')
The draws below stay inside these ranges and needn't reach their ends.
Inputs may be any that keep to these rules, and one draw needn't show every extreme that they name: `timesteps`: no two latents of one wide index fall into the same bucket; each bucket holds at most 2 * 4 latents, and some bucket holds exactly 2 * 4.
All inputs are finite; a program needn't handle non-finite values.
Results may differ from the reference program's by a relative error of at most 0.022.
Values may be sent and summed in bfloat16 or wider, within the bound.
No kernel may reach another device: no remote copies, remote signals or barrier semaphores. Data moves between devices by JAX's collectives and lax.ppermute only.
A program may use at most 256 MiB of HBM per device.

```python
import math
import jax
import jax.numpy as jnp
from jax import lax

HEADS = 12
HEAD_DIM = 64
FF = 3072
FREQ = 256
SIDE = 16
LAT_DEV = 4
D = 768
P_SIZE = 256
LATENTS = 32
N_WIDE = 8
N_NARROW = 4


def draw_timesteps(key, part):
    groups = N_WIDE
    per_dev = LAT_DEV
    latent_total = LATENTS
    streams = jax.random.split(jax.random.fold_in(key, 11), 5)
    offsets = jax.random.randint(streams[0], (groups // 2,), 0, per_dev + 1)
    offsets = offsets.at[0].set(per_dev)
    burden = jnp.stack([per_dev + offsets, per_dev - offsets], 1).reshape(groups)
    burden = burden[jax.random.permutation(streams[1], groups)]
    bounds = jnp.cumsum(burden)
    places = jnp.arange(latent_total, dtype=jnp.int32)
    target = jnp.sum((bounds[None, :] <= places[:, None]).astype(jnp.int32), 1)
    senders = jax.random.permutation(streams[2], groups)[places % groups]
    rotate = jax.random.randint(streams[3], (groups,), 0, per_dev)
    within = (places // groups + rotate[senders]) % per_dev
    latent_ids = senders * per_dev + within
    bucket = jnp.zeros((latent_total,), jnp.int32).at[latent_ids].set(target)
    lowest = (bucket * 1000 + groups - 1) // groups
    highest = ((bucket + 1) * 1000 + groups - 1) // groups
    jitter = jax.random.randint(streams[4], (latent_total,), 0, 1 << 20)
    return lowest + jitter % (highest - lowest)


def block_scale(own_key, dims, cuts, least, top_value):
    level = 1.0
    for axis_at, blocks in cuts:
        draws = jax.random.uniform(jax.random.fold_in(jax.random.fold_in(own_key, 6), axis_at), (blocks,), jnp.float32, least / len(cuts), top_value / len(cuts))
        level = level * jnp.repeat(jnp.exp(draws), dims[axis_at] // blocks).reshape((-1,) + (1,) * (len(dims) - 1 - axis_at))
    return level


def normal_values(stream_key, dims, scale, limit, cuts=(), held_as=jnp.bfloat16):
    loudness = block_scale(stream_key, dims, cuts, -0.22, 0.18) if cuts else 1.0
    values = jax.random.normal(stream_key, dims, jnp.float32) * scale * loudness
    return jnp.minimum(jnp.maximum(values, -limit), limit).astype(held_as)


def setup_inputs(seed: int = 0) -> dict:
    splits = jax.random.split(jax.random.key(seed), 14)
    latents = normal_values(splits[0], (LATENTS, P_SIZE, D), 1.0, 6.0, ((0, 8), (2, 4)))
    cotangent = normal_values(splits[1], (LATENTS, P_SIZE, D), 1.0, 6.0, ((0, 8), (2, 4)))
    timesteps = draw_timesteps(jax.random.fold_in(splits[13], 71), 0)
    time_in = normal_values(splits[3], (FREQ, D), FREQ ** -0.5, 0.375, (), jnp.float32)
    time_out = normal_values(splits[4], (D, D), D ** -0.5, 0.21875, (), jnp.float32)
    ada_weight = normal_values(splits[5], (D, 6 * D), D ** -0.5, 0.21875, (), jnp.float32)
    ada_bias = normal_values(splits[6], (6 * D,), 0.5, 3.0, (), jnp.float32)
    attn_kernel = normal_values(splits[7], (9, D), 9 ** -0.5, 2.0, (), jnp.float32)
    qkv_weight = normal_values(splits[8], (3, D, D), D ** -0.5, 0.21875, ((2, 4),))
    out_weight = normal_values(splits[9], (D, D), (D // 16) ** -0.5, 0.875, ((0, 4),))
    up_weight = normal_values(splits[10], (D, FF), D ** -0.5, 0.21875, ((1, 4),))
    ffn_kernel = normal_values(splits[11], (9, FF), 9 ** -0.5, 2.0, ((1, 4),), jnp.float32)
    down_weight = normal_values(splits[12], (FF, D), (FF // 4) ** -0.5, 0.21875, ((0, 4),))
    return dict(latents=latents, cotangent=cotangent, timesteps=timesteps, time_in=time_in, time_out=time_out, ada_weight=ada_weight, ada_bias=ada_bias, attn_kernel=attn_kernel, qkv_weight=qkv_weight, out_weight=out_weight, up_weight=up_weight, ffn_kernel=ffn_kernel, down_weight=down_weight)


@jax.custom_vjp
def low(v):
    return lax.optimization_barrier(v.astype(jnp.bfloat16)).astype(jnp.float32)

@jax.custom_vjp
def low_back(v):
    return v

def low_keep(v):
    return (low(v), None)

def low_pass(kept, grad):
    return (grad,)

def back_keep(v):
    return (v, None)

def back_low(kept, grad):
    return (low(grad),)
low.defvjp(low_keep, low_pass)
low_back.defvjp(back_keep, back_low)
HIGHEST = lax.Precision.HIGHEST

def layer_norm(values):
    center = values - lax.optimization_barrier(jnp.mean(values, -1, keepdims=True))
    spread = lax.optimization_barrier(jnp.mean(center * center, -1, keepdims=True))
    return center * lax.rsqrt(spread + 1e-06)

def conv_taps(values, kernel):
    extent = values.shape[1]
    padded = jnp.pad(values, ((0, 0), (1, 1), (1, 1), (0, 0)))
    result = jnp.zeros(values.shape, jnp.float32)
    for r in range(3):
        for c in range(3):
            result = result + padded[:, r:r + extent, c:c + extent, :] * kernel[3 * r + c]
    return result

def unshuffle(values):
    leading, extent, _, channels = values.shape
    halved = extent // 2
    moved = values.reshape(leading, halved, 2, halved, 2, channels).transpose(0, 2, 4, 1, 3, 5)
    return moved.reshape(leading, 4, halved * halved, channels)

def shuffle(values, extent):
    leading, _, _, channels = values.shape
    halved = extent // 2
    moved = values.reshape(leading, 2, 2, halved, halved, channels).transpose(0, 3, 1, 4, 2, 5)
    return moved.reshape(leading, extent * extent, channels)

def embed_times(stamps):
    halved = FREQ // 2
    freqs = jnp.exp(-math.log(10000.0) * jnp.arange(halved, dtype=jnp.float32) / halved)
    angles = stamps[:, None] * freqs[None, :]
    return jnp.concatenate([jnp.cos(angles), jnp.sin(angles)], 1)

def condition(stamps, time_in, time_out, ada_weight, ada_bias):
    embedded = embed_times(stamps)
    inner = jax.nn.silu(jnp.dot(embedded, time_in, precision=HIGHEST))
    outer = jax.nn.silu(jnp.dot(inner, time_out, precision=HIGHEST))
    return jnp.dot(outer, ada_weight, precision=HIGHEST) + ada_bias

def block(inputs, stamps, time_in, time_out, ada_weight, ada_bias, attn_kernel, qkv_weight, out_weight, up_weight, ffn_kernel, down_weight):
    leading = inputs.shape[0]
    width = inputs.shape[2]
    quarter = SIDE // 2 * (SIDE // 2)
    modulation = condition(stamps, time_in, time_out, ada_weight, ada_bias)
    pieces = [modulation[:, None, k * width:(k + 1) * width] for k in range(6)]
    first = layer_norm(inputs) * (1.0 + pieces[1]) + pieces[0]
    grouped = low(unshuffle(conv_taps(first.reshape(leading, SIDE, SIDE, width), attn_kernel)))
    share = width // N_NARROW
    units = up_weight.shape[1] // N_NARROW
    head_count = HEADS // N_NARROW
    factor = 1.0 / math.sqrt(HEAD_DIM)
    attended = jnp.zeros(grouped.shape, jnp.float32)
    for g in range(N_NARROW):
        branch = low_back(grouped)
        project = []
        for k in range(3):
            column = jnp.einsum('bgnd,de->bgne', branch, qkv_weight[k][:, g * share:(g + 1) * share], precision=HIGHEST)
            project.append(low_back(low(column)).reshape(leading, 4, quarter, head_count, HEAD_DIM))
        scores = low_back(jnp.einsum('bgqhe,bgkhe->bghqk', project[0], project[1], precision=HIGHEST) * factor)
        attention = low_back(low(jax.nn.softmax(scores, axis=-1)))
        context = jnp.einsum('bghqk,bgkhe->bgqhe', attention, project[2], precision=HIGHEST)
        context = low_back(low(context.reshape(leading, 4, quarter, share)))
        attended = attended + low(jnp.einsum('bgne,ed->bgnd', context, out_weight[g * share:(g + 1) * share], precision=HIGHEST))
    attended = low_back(attended)
    middle = inputs + pieces[2] * shuffle(attended, SIDE)
    second = low(layer_norm(middle) * (1.0 + pieces[4]) + pieces[3])
    fed = jnp.zeros(inputs.shape, jnp.float32)
    for g in range(N_NARROW):
        branch = low_back(second)
        hidden = low_back(jnp.einsum('bpd,df->bpf', branch, up_weight[:, g * units:(g + 1) * units], precision=HIGHEST))
        mixed = conv_taps(hidden.reshape(leading, SIDE, SIDE, units), ffn_kernel[:, g * units:(g + 1) * units])
        active = low_back(low(jax.nn.gelu(mixed.reshape(leading, SIDE * SIDE, units))))
        fed = fed + low(jnp.einsum('bpf,fd->bpd', active, down_weight[g * units:(g + 1) * units], precision=HIGHEST))
    fed = low_back(fed)
    return middle + pieces[5] * fed

def reference(latents, cotangent, timesteps, time_in, time_out, ada_weight, ada_bias, attn_kernel, qkv_weight, out_weight, up_weight, ffn_kernel, down_weight):
    latent_total = latents.shape[0]
    width = latents.shape[2]
    params = (time_in, time_out, ada_weight, ada_bias, attn_kernel, qkv_weight.astype(jnp.float32), out_weight.astype(jnp.float32), up_weight.astype(jnp.float32), ffn_kernel, down_weight.astype(jnp.float32))
    sections = latent_total // LAT_DEV
    shaped = latents.astype(jnp.float32).reshape(sections, LAT_DEV, SIDE * SIDE, width)
    upward = cotangent.astype(jnp.float32).reshape(sections, LAT_DEV, SIDE * SIDE, width)
    stamps = timesteps.astype(jnp.float32).reshape(sections, LAT_DEV)

    def advance(totals, segment):
        inputs, upstream, moments = segment

        def forward(values, *weights):
            return block(values, moments, *weights)
        result, backward = jax.vjp(forward, inputs, *params)
        gradients = backward(upstream)
        totals = tuple((a + b for a, b in zip(totals, gradients[1:])))
        return (totals, (result.astype(jnp.bfloat16), gradients[0].astype(jnp.bfloat16)))
    start = tuple((jnp.zeros(w.shape, jnp.float32) for w in params))
    totals, (produced, returned) = lax.scan(advance, start, (shaped, upward, stamps))
    factor = 1.0 / latent_total
    return (produced.reshape(latent_total, SIDE * SIDE, width), returned.reshape(latent_total, SIDE * SIDE, width), totals[0] * factor, totals[1] * factor, totals[2] * factor, totals[3] * factor, totals[4] * factor, totals[5] * factor, totals[6] * factor, totals[7] * factor, totals[8] * factor, totals[9] * factor)
```

```python
import functools
import math

import jax
import jax.numpy as jnp
from jax import lax
from jax.experimental import pallas as pl
from jax.experimental.pallas import tpu as pltpu
from jax.sharding import PartitionSpec as P

HEAD_DIM = 64
FREQ = 256
SIDE = 16
PAIR = 2

BF = jnp.bfloat16
F32 = jnp.float32
HIGHEST = lax.Precision.HIGHEST
LANES = 128
ROWS = 32
BAND = 64
GELU_A = math.sqrt(2.0 / math.pi)
GELU_B = 0.044715
EPS = 1e-06
VMEM_LIMIT = 56 * 1024 * 1024


def dot(a, b):
    return lax.dot_general(a, b, (((1,), (0,)), ((), ())), preferred_element_type=F32)


def dot_nt(a, b):
    return lax.dot_general(a, b, (((1,), (1,)), ((), ())), preferred_element_type=F32)


def dot_tn(a, b):
    return lax.dot_general(a, b, (((0,), (0,)), ((), ())), preferred_element_type=F32)


def column_of(rows):
    return lax.broadcasted_iota(jnp.int32, (rows, LANES), 0) % SIDE


def from_left(v):
    moved = pltpu.roll(v, 1, 0)
    return jnp.where(column_of(v.shape[0]) == 0, 0.0, moved)


def from_right(v):
    moved = pltpu.roll(v, v.shape[0] - 1, 0)
    return jnp.where(column_of(v.shape[0]) == SIDE - 1, 0.0, moved)


def conv_band(padded, at, lanes, kern):
    rows = [padded[at + SIDE * r : at + SIDE * r + BAND, lanes] for r in range(3)]
    mixed = [
        rows[0] * kern[c] + rows[1] * kern[3 + c] + rows[2] * kern[6 + c] for c in range(3)
    ]
    return from_left(mixed[0]) + mixed[1] + from_right(mixed[2])


def conv_back_band(padded_grad, at, lanes, kern):
    wide = padded_grad[at : at + BAND + 2 * SIDE, lanes]
    shifted = [from_right(wide), wide, from_left(wide)]
    total = None
    for r in range(3):
        for c in range(3):
            low = SIDE * (2 - r)
            term = shifted[c][low : low + BAND] * kern[3 * r + c]
            total = term if total is None else total + term
    return total, [s[SIDE : SIDE + BAND] for s in shifted]


def fold_rows(v):
    total = v[0:8]
    for at in range(8, v.shape[0], 8):
        total = total + v[at : at + 8]
    return total


def taps_of(kern_ref, lanes):
    block = kern_ref[:, lanes]
    return [block[t : t + 1] for t in range(9)]


def zero_edges(ref):
    edge = jnp.zeros((SIDE, ref.shape[1]), F32)
    ref[0:SIDE, :] = edge
    ref[ref.shape[0] - SIDE :, :] = edge


def gather_features(n, parts, held, width):
    for step, part in enumerate(parts):
        held[jnp.bitwise_xor(n, step)] = part[0]
    return jnp.concatenate([held[k] for k in range(len(parts))], axis=1)


def own_slice(n, values, share):
    out = values[:, 0:share]
    for k in range(1, values.shape[1] // share):
        out = jnp.where(n == k, values[:, k * share : (k + 1) * share], out)
    return out


def norm_stats(v):
    width = v.shape[1]
    mean = jnp.sum(v, -1, keepdims=True) * (1.0 / width)
    center = v - mean
    spread = jnp.sum(center * center, -1, keepdims=True) * (1.0 / width)
    scale = lax.rsqrt(spread + EPS)
    return center * scale, scale


def head_masks(share):
    lane = lax.broadcasted_iota(jnp.int32, (1, share), 1) // HEAD_DIM
    return [(lane == h).astype(F32).astype(BF) for h in range(share // HEAD_DIM)]


def half_rows(v, parity):
    tokens, width = v.shape
    split = v.reshape(tokens // (2 * SIDE), 2, SIDE, width)
    return split[:, parity].reshape(tokens // 2, width)


def join_rows(even, odd):
    half, width = even.shape
    both = jnp.stack([even.reshape(half // SIDE, SIDE, width), odd.reshape(half // SIDE, SIDE, width)], 1)
    return both.reshape(2 * half, width)


def softmax_rows(queries, keys):
    scores = dot_nt(queries, keys) * (1.0 / math.sqrt(HEAD_DIM))
    rows = lax.broadcasted_iota(jnp.int32, scores.shape, 0)
    cols = lax.broadcasted_iota(jnp.int32, scores.shape, 1)
    same = (rows + cols) % 2 == 0
    scores = jnp.where(same, scores, -1e30)
    top = jnp.max(scores, -1, keepdims=True)
    grown = jnp.where(same, jnp.exp(scores - top), 0.0)
    return grown / jnp.sum(grown, -1, keepdims=True)


def beside(stacked, heads):
    rows = stacked.shape[0] // heads
    return jnp.concatenate([stacked[h * rows : (h + 1) * rows] for h in range(heads)], axis=1)


def lane_loop(width, body):
    def step(j, carry):
        body(pl.ds(pl.multiple_of(j * LANES, LANES), LANES))
        return carry

    lax.fori_loop(0, width // LANES, step, 0)


def row_loop(tokens, body):
    def step(j, carry):
        body(pl.multiple_of(j * ROWS, ROWS))
        return carry

    lax.fori_loop(0, tokens // ROWS, step, 0)


def attn_kernel_body(
    s_ref, xo, xc, xx, xd, mod, kern, wqkv, wout,
    full_out, grouped_out, q_out, k_out, v_out, ctx_out, keep_out, send_out,
    held, padded,
):
    rel = pl.program_id(0)
    n = s_ref[0]
    tokens, share = xo.shape[1], xo.shape[2]
    width = full_out.shape[2]
    full_out[0] = gather_features(n, (xo, xc, xx, xd), held, width)
    zero_edges(padded)
    shift, scale = mod[0, 0:1, :], 1.0 + mod[0, 1:2, :]

    def rows(at):
        normed, _ = norm_stats(full_out[0, pl.ds(at, ROWS), :].astype(F32))
        padded[pl.ds(at + SIDE, ROWS), :] = normed * scale + shift

    row_loop(tokens, rows)

    def lanes(at):
        taps = taps_of(kern, at)
        for band in range(0, tokens, BAND):
            grouped_out[0, band : band + BAND, at] = conv_band(padded, band, at, taps).astype(BF)

    lane_loop(width, lanes)
    grouped = grouped_out[0]
    query = dot(grouped, wqkv[0]).astype(BF)
    key = dot(grouped, wqkv[1]).astype(BF)
    value = dot(grouped, wqkv[2]).astype(BF)
    q_out[0], k_out[0], v_out[0] = query, key, value
    masks = head_masks(share)
    heads = len(masks)
    parts = []
    for parity in range(2):
        q = half_rows(query, parity)
        k = half_rows(key, parity)
        v = half_rows(value, parity)
        probs = softmax_rows(jnp.concatenate([q * m for m in masks], axis=0), k)
        low = beside(probs.astype(BF), heads)
        parts.append(dot(low, jnp.concatenate([v * m for m in masks], axis=0)).astype(BF))
    context = join_rows(*parts)
    ctx_out[0] = context
    partial = dot(context, wout[...]).astype(BF)

    @pl.when(rel == 0)
    def _():
        keep_out[...] = partial

    @pl.when(rel == 1)
    def _():
        send_out[...] = partial


def ffn_kernel_body(
    s_ref, full, att_own, att_peer, go, gc, gx, gd, mod, up, down, kern,
    g_out, second_out, active_out, gfed_out, ghid_out, mid_out, fkeep_out, fsend_out, keep_out, send_out, kgrad_out,
    held, padded, slope, gpad, att,
):
    rel = pl.program_id(0)
    n = s_ref[0]
    core = jnp.bitwise_and(n, 1)
    tokens, width = full.shape[1], full.shape[2]
    share = go.shape[2]
    units = up.shape[1]
    g_out[0] = gather_features(n, (go, gc, gx, gd), held, width)
    zero_edges(padded)
    zero_edges(gpad)

    @pl.when(rel == 0)
    def _():
        att[...] = att_own[...]
        kgrad_out[...] = jnp.zeros(kgrad_out.shape, F32)

    @pl.when(rel == 1)
    def _():
        att[...] = att_peer[...]

    gate1, gate2 = mod[0, 2:3, :], mod[0, 5:6, :]
    shift, scale = mod[0, 3:4, :], 1.0 + mod[0, 4:5, :]

    def rows(at):
        here = pl.ds(at, ROWS)
        middle = full[0, here, :].astype(F32) + gate1 * att[here, :].astype(F32)
        mid_out[0, here, :] = own_slice(n, middle, share)
        normed, _ = norm_stats(middle)
        second_out[0, here, :] = (normed * scale + shift).astype(BF)
        gfed_out[0, here, :] = (gate2 * g_out[0, here, :].astype(F32)).astype(BF)

    row_loop(tokens, rows)
    padded[SIDE : SIDE + tokens, :] = dot(second_out[0], up[...])

    def lanes(at):
        taps = taps_of(kern, at)
        for band in range(0, tokens, BAND):
            mixed = conv_band(padded, band, at, taps)
            square = mixed * mixed
            curve = jnp.tanh(GELU_A * mixed * (1.0 + GELU_B * square))
            half = 0.5 * (1.0 + curve)
            active_out[0, band : band + BAND, at] = (mixed * half).astype(BF)
            slope[band : band + BAND, at] = half + (0.5 * GELU_A) * mixed * (1.0 - curve * curve) * (
                1.0 + (3.0 * GELU_B) * square
            )

    lane_loop(units, lanes)
    fed = dot(active_out[0], down[...]).astype(BF)
    pieces = [fed[:, k * share : (k + 1) * share] for k in range(4)]
    for x in range(2):
        even, odd = pieces[2 * x], pieces[2 * x + 1]
        fkeep_out[x, 0] = jnp.where(core == 0, even, odd)
        fsend_out[x, 0] = jnp.where(core == 0, odd, even)
    gact = dot_nt(gfed_out[0], down[...]).astype(BF).astype(F32)
    gpad[SIDE : SIDE + tokens, :] = gact * slope[...]

    def lanes_back(at):
        taps = taps_of(kern, at)
        sums = [None] * 9
        for band in range(0, tokens, BAND):
            total, shifted = conv_back_band(gpad, band, at, taps)
            ghid_out[0, band : band + BAND, at] = total.astype(BF)
            for r in range(3):
                values = padded[band + SIDE * r : band + SIDE * r + BAND, at]
                for c in range(3):
                    part = fold_rows(values * shifted[c])
                    sums[3 * r + c] = part if sums[3 * r + c] is None else sums[3 * r + c] + part
        for t in range(9):
            kgrad_out[t : t + 1, at] += jnp.sum(sums[t], 0, keepdims=True)

    lane_loop(units, lanes_back)
    partial = dot_nt(ghid_out[0], up[...]).astype(BF)

    @pl.when(rel == 0)
    def _():
        keep_out[...] = partial

    @pl.when(rel == 1)
    def _():
        send_out[...] = partial


def attn_back_body(
    s_ref, full, att_own, att_peer, gs_own, gs_peer, gfull, mod, q_in, k_in, v_in, kern, wqkv, wout,
    gatt_out, gq_out, gk_out, gv_out, gmid_out, keep_out, send_out, mods_out, kgrad_out,
    att, gsec, normed1, scale1, first, gpad, gback,
):
    rel = pl.program_id(0)
    n = s_ref[0]
    core = jnp.bitwise_and(n, 1)
    tokens, width = full.shape[1], full.shape[2]
    share = q_in.shape[2]
    zero_edges(first)
    zero_edges(gpad)

    @pl.when(rel == 0)
    def _():
        att[...] = att_own[...]
        gsec[...] = gs_own[...]
        kgrad_out[...] = jnp.zeros(kgrad_out.shape, F32)

    @pl.when(rel == 1)
    def _():
        att[...] = att_peer[...]
        gsec[...] = gs_peer[...]

    mods_out[...] = jnp.zeros(mods_out.shape, F32)
    gate1 = mod[0, 2:3, :]
    low_scale, low_shift = 1.0 + mod[0, 1:2, :], mod[0, 0:1, :]
    scale2 = 1.0 + mod[0, 4:5, :]

    def rows(at):
        here = pl.ds(at, ROWS)
        x = full[0, here, :].astype(F32)
        attended = att[here, :].astype(F32)
        normed, inv = norm_stats(x + gate1 * attended)
        grad = gsec[here, :].astype(F32)
        inner = grad * scale2
        mean_a = jnp.sum(inner, -1, keepdims=True) * (1.0 / width)
        mean_b = jnp.sum(inner * normed, -1, keepdims=True) * (1.0 / width)
        gmid = gfull[0, here, :].astype(F32) + inv * (inner - mean_a - normed * mean_b)
        gmid_out[0, here, :] = own_slice(n, gmid, share)
        gatt_out[0, here, :] = (gate1 * gmid).astype(BF)
        mods_out[0, 2:3, :] += jnp.sum(fold_rows(attended * gmid), 0, keepdims=True)
        mods_out[0, 3:4, :] += jnp.sum(fold_rows(grad), 0, keepdims=True)
        mods_out[0, 4:5, :] += jnp.sum(fold_rows(grad * normed), 0, keepdims=True)
        low, inv1 = norm_stats(x)
        normed1[here, :] = low
        scale1[here, :] = jnp.broadcast_to(inv1, (ROWS, LANES))
        first[pl.ds(at + SIDE, ROWS), :] = low * low_scale + low_shift

    row_loop(tokens, rows)
    gctx = dot_nt(gatt_out[0], wout[...]).astype(BF)
    masks = head_masks(share)
    heads = len(masks)
    factor = 1.0 / math.sqrt(HEAD_DIM)
    parts_q, parts_k, parts_v = [], [], []
    for parity in range(2):
        q = half_rows(q_in[0], parity)
        k = half_rows(k_in[0], parity)
        v = half_rows(v_in[0], parity)
        gc = half_rows(gctx, parity)
        q_all = jnp.concatenate([q * m for m in masks], axis=0)
        k_all = jnp.concatenate([k * m for m in masks], axis=0)
        gc_all = jnp.concatenate([gc * m for m in masks], axis=0)
        probs = softmax_rows(q_all, k)
        parts_v.append(dot_tn(probs.astype(BF), gc_all).astype(BF))
        gprobs = dot_nt(gc_all, v).astype(BF).astype(F32)
        gscores = (probs * (gprobs - jnp.sum(probs * gprobs, -1, keepdims=True))).astype(BF)
        parts_q.append((dot(beside(gscores, heads), k_all) * factor).astype(BF))
        parts_k.append((dot_tn(gscores, q_all) * factor).astype(BF))
    gq, gk, gv = join_rows(*parts_q), join_rows(*parts_k), join_rows(*parts_v)
    gq_out[0], gk_out[0], gv_out[0] = gq, gk, gv
    gpad[SIDE : SIDE + tokens, :] = dot_nt(gq, wqkv[0]) + dot_nt(gk, wqkv[1]) + dot_nt(gv, wqkv[2])

    def lanes(at):
        taps = taps_of(kern, at)
        sums = [None] * 9
        shift_sum, scale_sum = None, None
        for band in range(0, tokens, BAND):
            total, shifted = conv_back_band(gpad, band, at, taps)
            gback[band : band + BAND, at] = total
            part_a, part_b = fold_rows(total), fold_rows(total * normed1[band : band + BAND, at])
            shift_sum = part_a if shift_sum is None else shift_sum + part_a
            scale_sum = part_b if scale_sum is None else scale_sum + part_b
            for r in range(3):
                values = first[band + SIDE * r : band + SIDE * r + BAND, at]
                for c in range(3):
                    part = fold_rows(values * shifted[c])
                    sums[3 * r + c] = part if sums[3 * r + c] is None else sums[3 * r + c] + part
        for t in range(9):
            kgrad_out[t : t + 1, at] += jnp.sum(sums[t], 0, keepdims=True)
        mods_out[0, 0:1, at] = jnp.sum(shift_sum, 0, keepdims=True)
        mods_out[0, 1:2, at] = jnp.sum(scale_sum, 0, keepdims=True)

    lane_loop(width, lanes)

    def rows_back(at):
        here = pl.ds(at, ROWS)
        inner = gback[here, :] * low_scale
        normed = normed1[here, :]
        mean_a = jnp.sum(inner, -1, keepdims=True) * (1.0 / width)
        mean_b = jnp.sum(inner * normed, -1, keepdims=True) * (1.0 / width)
        grad = scale1[here, 0:1] * (inner - mean_a - normed * mean_b)
        low = grad.astype(BF)
        pieces = [low[:, k * share : (k + 1) * share] for k in range(4)]
        for x in range(2):
            even, odd = pieces[2 * x], pieces[2 * x + 1]
            keep_out[x, 0, here, :] = jnp.where(core == 0, even, odd)
            send_out[x, 0, here, :] = jnp.where(core == 0, odd, even)

    row_loop(tokens, rows_back)


def call(body, name, grid, scalars, ins, outs, scratch, flops):
    in_specs = [s for _, s in ins]
    bytes_moved = sum(math.prod(o.shape) * o.dtype.itemsize for o, _ in outs)
    return pl.pallas_call(
        body,
        name=name,
        out_shape=[o for o, _ in outs],
        grid_spec=pltpu.PrefetchScalarGridSpec(
            num_scalar_prefetch=1,
            grid=grid,
            in_specs=in_specs,
            out_specs=[s for _, s in outs],
            scratch_shapes=scratch,
        ),
        compiler_params=pltpu.CompilerParams(vmem_limit_bytes=VMEM_LIMIT),
        cost_estimate=pl.CostEstimate(flops=flops, bytes_accessed=bytes_moved, transcendentals=0),
    )(scalars, *[a for a, _ in ins])


def shape_of(dims, dtype):
    return jax.ShapeDtypeStruct(dims, dtype)


def whole(array):
    dims = array.shape
    return (array, pl.BlockSpec(dims, lambda i, s: (0,) * len(dims)))


def whole_out(dims, dtype):
    return (shape_of(dims, dtype), pl.BlockSpec(dims, lambda i, s: (0,) * len(dims)))


def by_latent(array, base):
    dims = (1,) + array.shape[1:]
    rest = (0,) * (len(dims) - 1)
    return (array, pl.BlockSpec(dims, lambda i, s: (base + jnp.bitwise_xor(i, jnp.bitwise_and(s[0], 1)),) + rest))


def by_step(array):
    dims = (1,) + array.shape[1:]
    rest = (0,) * (len(dims) - 1)
    return (array, pl.BlockSpec(dims, lambda i, s: (i,) + rest))


def step_out(dims, dtype):
    rest = (0,) * (len(dims) - 1)
    return (shape_of(dims, dtype), pl.BlockSpec((1,) + dims[1:], lambda i, s: (i,) + rest))


def latent_out(dims, dtype):
    rest = (0,) * (len(dims) - 1)
    return (
        shape_of(dims, dtype),
        pl.BlockSpec((1,) + dims[1:], lambda i, s: (jnp.bitwise_xor(i, jnp.bitwise_and(s[0], 1)),) + rest),
    )


def halves_out(tokens, share):
    return (
        shape_of((2, PAIR, tokens, share), BF),
        pl.BlockSpec(
            (2, 1, tokens, share), lambda i, s: (0, jnp.bitwise_xor(i, jnp.bitwise_and(s[0], 1)), 0, 0)
        ),
    )


def core_swap(v):
    return lax.ppermute(v, "narrow", [(0, 1), (1, 0), (2, 3), (3, 2)])


def x_swap(v):
    return lax.ppermute(v, "narrow", [(0, 2), (2, 0), (1, 3), (3, 1)])


def sum_pair(a, b):
    return (a.astype(F32) + b.astype(F32)).astype(BF)


def reduce_pair(keep, send):
    here = sum_pair(keep, core_swap(send))
    own = sum_pair(here, x_swap(here))
    return own, core_swap(own)


def reduce_slices(n, keep, send):
    x = n // 2
    both = sum_pair(keep, core_swap(send))
    mine = lax.dynamic_index_in_dim(both, x, 0, keepdims=False)
    other = lax.dynamic_index_in_dim(both, 1 - x, 0, keepdims=False)
    return mine.astype(F32) + x_swap(other).astype(F32)


def wide_swap(v, bit, count):
    return lax.ppermute(v, "wide", [(i, i ^ bit) for i in range(count)])


def wide_gather(v, count):
    held = v[None]
    bit = 1
    while bit < count:
        held = jnp.concatenate([held, wide_swap(held, bit, count)], 0)
        bit *= 2
    return held


def wide_sum(v, count):
    rows, width = v.shape
    groups = count // 2
    at = lax.axis_index("wide")
    half, place = at % 2, at // 2
    split = v.reshape(2, groups, rows // count, width)
    mine = lax.dynamic_index_in_dim(split, half, 0, keepdims=False)
    other = lax.dynamic_index_in_dim(split, 1 - half, 0, keepdims=False)
    both = sum_pair(mine, wide_swap(other, 1, count))
    total = lax.dynamic_index_in_dim(both, place, 0, keepdims=False).astype(F32)

    def shift(v, d):
        return lax.ppermute(v, "wide", [(i, (i + 2 * d) % count) for i in range(count)])

    arrived = [
        shift(lax.dynamic_index_in_dim(both, (place + d) % groups, 0, keepdims=False), d)
        for d in range(1, groups)
    ]
    for part in arrived:
        total = total + part.astype(F32)
    total = total.astype(BF)
    gathered = jnp.zeros((groups, rows // count, width), BF)
    gathered = lax.dynamic_update_index_in_dim(gathered, total, place, 0)
    for d in range(1, groups):
        gathered = lax.dynamic_update_index_in_dim(gathered, shift(total, d), (place - d) % groups, 0)
    peer = wide_swap(gathered, 1, count)
    low = jnp.where(half == 0, gathered, peer)
    high = jnp.where(half == 0, peer, gathered)
    return jnp.concatenate([low, high], 0).reshape(rows, width)


def embed_times(stamps):
    halved = FREQ // 2
    freqs = jnp.exp(-math.log(10000.0) * jnp.arange(halved, dtype=F32) / halved)
    angles = stamps[:, None] * freqs[None, :]
    return jnp.concatenate([jnp.cos(angles), jnp.sin(angles)], 1)


def silu_slope(v):
    gate = jax.nn.sigmoid(v)
    return gate * (1.0 + v * (1.0 - gate))


def body(
    latents, cotangent, timesteps, time_in, time_out, ada_weight, ada_bias,
    attn_kernel, qkv_weight, out_weight, up_weight, ffn_kernel, down_weight,
):
    wide_count = lax.axis_size("wide")
    wide_at = lax.axis_index("wide")
    n = lax.axis_index("narrow")
    per_dev, tokens, share = latents.shape
    width = out_weight.shape[1]
    units = up_weight.shape[1]
    latent_total = timesteps.shape[0]
    scalars = jnp.stack([n, n]).astype(jnp.int32)

    order = jnp.bitwise_xor(jnp.arange(wide_count, dtype=jnp.int32), wide_at)
    stamps = timesteps.reshape(wide_count, per_dev)[order].reshape(latent_total).astype(F32)
    embedded = embed_times(stamps)
    inner_pre = jnp.dot(embedded, time_in, precision=HIGHEST)
    inner = jax.nn.silu(inner_pre)
    outer_pre = jnp.dot(inner, time_out, precision=HIGHEST)
    outer = jax.nn.silu(outer_pre)
    modulation = jnp.dot(outer[:per_dev], ada_weight, precision=HIGHEST) + ada_bias
    mod = modulation.reshape(per_dev, 6, width)

    x_across = x_swap(latents)
    x_core = core_swap(latents)
    x_diag = core_swap(x_across)
    g_across = x_swap(cotangent)
    g_core = core_swap(cotangent)
    g_diag = core_swap(g_across)

    pairs = range(0, per_dev, PAIR)
    tile = (PAIR, tokens, width)
    thin = (PAIR, tokens, share)
    flat = (tokens, width)

    forward = []
    for base in pairs:
        res = call(
            attn_kernel_body, "attn_fwd", (PAIR,), scalars,
            [by_latent(latents, base), by_latent(x_core, base), by_latent(x_across, base), by_latent(x_diag, base),
             by_latent(mod, base), whole(attn_kernel), whole(qkv_weight), whole(out_weight)],
            [step_out(tile, BF), step_out(tile, BF), step_out(thin, BF), step_out(thin, BF), step_out(thin, BF),
             step_out(thin, BF), whole_out(flat, BF), whole_out(flat, BF)],
            [pltpu.VMEM((4, tokens, share), BF), pltpu.VMEM((tokens + 2 * SIDE, width), F32)],
            2_000_000_000,
        )
        forward.append(res)
    attended = [reduce_pair(res[6], res[7]) for res in forward]

    middle = []
    for base, res, att in zip(pairs, forward, attended):
        out = call(
            ffn_kernel_body, "ffn", (PAIR,), scalars,
            [by_step(res[0]), whole(att[0]), whole(att[1]),
             by_latent(cotangent, base), by_latent(g_core, base), by_latent(g_across, base), by_latent(g_diag, base),
             by_latent(mod, base), whole(up_weight), whole(down_weight), whole(ffn_kernel)],
            [step_out(tile, BF), step_out(tile, BF), step_out((PAIR, tokens, units), BF), step_out(tile, BF),
             step_out((PAIR, tokens, units), BF), latent_out(thin, F32), halves_out(tokens, share),
             halves_out(tokens, share), whole_out(flat, BF), whole_out(flat, BF), whole_out((9, units), F32)],
            [pltpu.VMEM((4, tokens, share), BF), pltpu.VMEM((tokens + 2 * SIDE, units), F32),
             pltpu.VMEM((tokens, units), F32), pltpu.VMEM((tokens + 2 * SIDE, units), F32),
             pltpu.VMEM(flat, BF)],
            4_000_000_000,
        )
        middle.append(out)
    grad_second = [reduce_pair(out[8], out[9]) for out in middle]
    fed = [reduce_slices(n, out[6], out[7]) for out in middle]

    back = []
    for base, res, att, out, gsec in zip(pairs, forward, attended, middle, grad_second):
        got = call(
            attn_back_body, "attn_bwd", (PAIR,), scalars,
            [by_step(res[0]), whole(att[0]), whole(att[1]), whole(gsec[0]), whole(gsec[1]), by_step(out[0]),
             by_latent(mod, base), by_step(res[2]), by_step(res[3]), by_step(res[4]),
             whole(attn_kernel), whole(qkv_weight), whole(out_weight)],
            [step_out(tile, BF), step_out(thin, BF), step_out(thin, BF), step_out(thin, BF), latent_out(thin, F32),
             halves_out(tokens, share), halves_out(tokens, share), latent_out((PAIR, 8, width), F32),
             whole_out((9, width), F32)],
            [pltpu.VMEM(flat, BF), pltpu.VMEM(flat, BF), pltpu.VMEM(flat, F32), pltpu.VMEM((tokens, LANES), F32),
             pltpu.VMEM((tokens + 2 * SIDE, width), F32), pltpu.VMEM((tokens + 2 * SIDE, width), F32),
             pltpu.VMEM(flat, F32)],
            3_000_000_000,
        )
        back.append(got)
    grad_in = [reduce_slices(n, got[5], got[6]) for got in back]

    own = lambda v: lax.dynamic_slice_in_dim(v, n * share, share, v.ndim - 1)
    gate2 = own(mod[:, 5, :])[:, None, :]
    fed_all = jnp.concatenate(fed, 0)
    mid_all = jnp.concatenate([out[5] for out in middle], 0)
    final_out = (mid_all + gate2 * fed_all).astype(BF)
    gate2_grad = jnp.sum(fed_all * cotangent.astype(F32), 1)
    gmid_all = jnp.concatenate([got[4] for got in back], 0)
    final_grad = (gmid_all + jnp.concatenate(grad_in, 0)).astype(BF)

    factor = 1.0 / latent_total

    def token_product(lefts, rights):
        total = None
        for a, b in zip(lefts, rights):
            part = lax.dot_general(
                a.reshape(-1, a.shape[-1]), b.reshape(-1, b.shape[-1]),
                (((0,), (0,)), ((), ())), preferred_element_type=F32,
            )
            total = part if total is None else total + part
        return (total * factor).astype(BF)

    down_grad = token_product([o[2] for o in middle], [o[3] for o in middle])
    up_grad = token_product([o[1] for o in middle], [o[4] for o in middle])
    out_grad = token_product([r[5] for r in forward], [g[0] for g in back])
    qkv_grads = [token_product([g[k] for g in back], [r[1] for r in forward]) for k in (1, 2, 3)]
    down_grad = wide_sum(down_grad, wide_count).astype(F32)
    up_grad = wide_sum(up_grad, wide_count).astype(F32)
    attn_grads = wide_sum(jnp.concatenate([out_grad] + qkv_grads, 0), wide_count).astype(F32)
    out_grad = attn_grads[:share]
    qkv_grad = jnp.swapaxes(attn_grads[share:].reshape(3, share, width), 1, 2)

    mods = jnp.concatenate([got[7] for got in back], 0)
    gate2_row = lax.dynamic_update_slice_in_dim(jnp.zeros((per_dev, width), F32), gate2_grad, n * share, 1)
    pieces = jnp.stack(
        [mods[:, 0], mods[:, 1], 0.25 * mods[:, 2], 0.25 * mods[:, 3], 0.25 * mods[:, 4], gate2_row], 1
    ).reshape(per_dev, 6 * width)
    attn_taps = sum(got[8] for got in back)
    ffn_taps = sum(out[10] for out in middle)

    def narrow_sum(v):
        v = v + core_swap(v)
        return v + x_swap(v)

    packed = narrow_sum(jnp.concatenate([pieces.reshape(-1), attn_taps.reshape(-1)]).reshape(-1, LANES))
    packed = jnp.concatenate([packed, ffn_taps.reshape(-1, LANES)], 0)
    gathered = wide_gather(packed, wide_count)
    count_a = per_dev * 6 * width // LANES
    count_b = count_a + 9 * width // LANES
    gmod = gathered[:, :count_a].reshape(latent_total, 6 * width)
    attn_taps = jnp.sum(gathered[:, count_a:count_b], 0).reshape(9, width) * factor
    ffn_taps = jnp.sum(gathered[:, count_b:], 0).reshape(9, units) * factor

    scaled = gmod * factor
    ada_bias_grad = jnp.sum(scaled, 0)
    ada_weight_grad = jnp.dot(outer.T, scaled, precision=HIGHEST)
    outer_grad = jnp.dot(scaled, ada_weight.T, precision=HIGHEST) * silu_slope(outer_pre)
    time_out_grad = jnp.dot(inner.T, outer_grad, precision=HIGHEST)
    inner_grad = jnp.dot(outer_grad, time_out.T, precision=HIGHEST) * silu_slope(inner_pre)
    time_in_grad = jnp.dot(embedded.T, inner_grad, precision=HIGHEST)
    return (
        final_out, final_grad, time_in_grad, time_out_grad, ada_weight_grad, ada_bias_grad,
        attn_taps, qkv_grad, out_grad, up_grad, ffn_taps, down_grad,
    )


def solution(mesh):
    tokens = P("wide", None, "narrow")
    weights = (P(None, None, "narrow"), P("narrow", None), P(None, "narrow"), P(None, "narrow"), P("narrow", None))
    return jax.shard_map(
        body,
        mesh=mesh,
        in_specs=(tokens, tokens, P(), P(), P(), P(), P(), P()) + weights,
        out_specs=(tokens, tokens, P(), P(), P(), P(), P()) + weights,
        check_vma=False,
    )
```

```python
import functools
import math

import jax
import jax.numpy as jnp
from jax import lax
from jax.experimental import pallas as pl
from jax.experimental.pallas import tpu as pltpu
from jax.sharding import PartitionSpec as P

HEAD_DIM = 64
FREQ = 256
SIDE = 16
PAIR = 2

BF = jnp.bfloat16
F32 = jnp.float32
HIGHEST = lax.Precision.HIGHEST
LANES = 128
ROWS = 128
BAND = 64
GELU_A = math.sqrt(2.0 / math.pi)
GELU_B = 0.044715
EPS = 1e-06
VMEM_LIMIT = 60 * 1024 * 1024


def dot(a, b):
    return lax.dot_general(a, b, (((1,), (0,)), ((), ())), preferred_element_type=F32)


def dot_nt(a, b):
    return lax.dot_general(a, b, (((1,), (1,)), ((), ())), preferred_element_type=F32)


def dot_tn(a, b):
    return lax.dot_general(a, b, (((0,), (0,)), ((), ())), preferred_element_type=F32)


def column_of(rows):
    return lax.broadcasted_iota(jnp.int32, (rows, LANES), 0) % SIDE


def from_left(v):
    moved = pltpu.roll(v, 1, 0)
    return jnp.where(column_of(v.shape[0]) == 0, 0.0, moved)


def from_right(v):
    moved = pltpu.roll(v, v.shape[0] - 1, 0)
    return jnp.where(column_of(v.shape[0]) == SIDE - 1, 0.0, moved)


def conv_band(padded, at, lanes, kern):
    rows = [padded[pl.ds(at + SIDE * r, BAND), lanes] for r in range(3)]
    mixed = [
        rows[0] * kern[c] + rows[1] * kern[3 + c] + rows[2] * kern[6 + c] for c in range(3)
    ]
    return from_left(mixed[0]) + mixed[1] + from_right(mixed[2])


def conv_back_band(padded_grad, at, lanes, kern):
    wide = padded_grad[pl.ds(at, BAND + 2 * SIDE), lanes]
    shifted = [from_right(wide), wide, from_left(wide)]
    total = None
    for r in range(3):
        for c in range(3):
            low = SIDE * (2 - r)
            term = shifted[c][low : low + BAND] * kern[3 * r + c]
            total = term if total is None else total + term
    return total, [s[SIDE : SIDE + BAND] for s in shifted]


def fold_rows(v):
    total = v[0:8]
    for at in range(8, v.shape[0], 8):
        total = total + v[at : at + 8]
    return total


def taps_of(kern_ref, lanes):
    block = kern_ref[:, lanes]
    return [block[t : t + 1] for t in range(9)]


def zero_edges(ref):
    edge = jnp.zeros((SIDE, ref.shape[1]), F32)
    tall = ref.shape[0] // PAIR
    for rel in range(PAIR):
        ref[rel * tall : rel * tall + SIDE, :] = edge
        ref[(rel + 1) * tall - SIDE : (rel + 1) * tall, :] = edge


def inside(ref, rel):
    tall = ref.shape[0] // PAIR
    return slice(rel * tall + SIDE, (rel + 1) * tall - SIDE)


def gather_features(n, lats, parts, held, out):
    _, share, tokens = parts[0].shape
    for rel, lat in enumerate(lats):
        for step, part in enumerate(parts):
            held[jnp.bitwise_xor(n, step)] = part[lat]
        out[rel * tokens : (rel + 1) * tokens, :] = held[...].reshape(len(parts) * share, tokens).T


def by_core(core, lats, low, share, keep_out, send_out):
    tokens = low.shape[0] // PAIR
    for rel, lat in enumerate(lats):
        turned = low[rel * tokens : (rel + 1) * tokens, :].T
        for parity in range(2):

            @pl.when(core == parity)
            def _():
                for x in range(2):
                    here, there = 2 * x + parity, 2 * x + 1 - parity
                    keep_out[x, lat] = turned[here * share : (here + 1) * share]
                    send_out[x, lat] = turned[there * share : (there + 1) * share]


def norm_stats(v):
    width = v.shape[1]
    mean = jnp.sum(v, -1, keepdims=True) * (1.0 / width)
    center = v - mean
    spread = jnp.sum(center * center, -1, keepdims=True) * (1.0 / width)
    scale = lax.rsqrt(spread + EPS)
    return center * scale, scale


def head_masks(share):
    lane = lax.broadcasted_iota(jnp.int32, (1, share), 1) // HEAD_DIM
    return [(lane == h).astype(F32).astype(BF) for h in range(share // HEAD_DIM)]


def half_rows(v, parity):
    tokens, width = v.shape
    split = v.reshape(tokens // (2 * SIDE), 2, SIDE, width)
    return split[:, parity].reshape(tokens // 2, width)


def join_rows(even, odd):
    half, width = even.shape
    both = jnp.stack([even.reshape(half // SIDE, SIDE, width), odd.reshape(half // SIDE, SIDE, width)], 1)
    return both.reshape(2 * half, width)


def softmax_rows(queries, keys):
    scores = dot_nt(queries, keys) * (1.0 / math.sqrt(HEAD_DIM))
    rows = lax.broadcasted_iota(jnp.int32, scores.shape, 0)
    cols = lax.broadcasted_iota(jnp.int32, scores.shape, 1)
    same = (rows + cols) % 2 == 0
    scores = jnp.where(same, scores, -1e30)
    top = jnp.max(scores, -1, keepdims=True)
    grown = jnp.where(same, jnp.exp(scores - top), 0.0)
    return grown / jnp.sum(grown, -1, keepdims=True)


def beside(stacked, heads):
    rows = stacked.shape[0] // heads
    return jnp.concatenate([stacked[h * rows : (h + 1) * rows] for h in range(heads)], axis=1)


def lane_loop(width, body):
    count = width // LANES

    def step(j, carry):
        body(j // count, pl.ds(pl.multiple_of((j % count) * LANES, LANES), LANES))
        return carry

    lax.fori_loop(0, PAIR * count, step, 0)


def row_loop(tokens, body):
    def step(j, carry):
        body(pl.multiple_of(j * ROWS, ROWS))
        return carry

    lax.fori_loop(0, tokens // ROWS, step, 0)


def pair_loop(body):
    def step(j, carry):
        body(j)
        return carry

    lax.fori_loop(0, PAIR, step, 0)


def attn_kernel_body(
    s_ref, xo, xc, xx, xd, mod, kern, wqkv, wout,
    full_out, grouped_out, q_out, k_out, v_out, ctx_out, keep_out, send_out,
    held, padded,
):
    n = s_ref[0]
    core = jnp.bitwise_and(n, 1)
    share, tokens = xo.shape[1], xo.shape[2]
    width = full_out.shape[1]
    tall = tokens + 2 * SIDE
    lats = [core, 1 - core]
    gather_features(n, lats, (xo, xc, xx, xd), held, full_out)
    zero_edges(padded)
    for rel, lat in enumerate(lats):
        shift, scale = mod[lat, 0:1, :], 1.0 + mod[lat, 1:2, :]

        def rows(at):
            normed, _ = norm_stats(full_out[pl.ds(at + rel * tokens, ROWS), :].astype(F32))
            padded[pl.ds(at + rel * tall + SIDE, ROWS), :] = normed * scale + shift

        row_loop(tokens, rows)

    def lanes(rel, at):
        taps = taps_of(kern, at)
        for band in range(0, tokens, BAND):
            here = pl.ds(pl.multiple_of(rel * tokens + band, BAND), BAND)
            grouped_out[here, at] = conv_band(padded, pl.multiple_of(rel * tall + band, SIDE), at, taps).astype(BF)

    lane_loop(width, lanes)
    grouped = grouped_out[...]
    q_out[...] = dot_nt(grouped, wqkv[0]).astype(BF)
    k_out[...] = dot_nt(grouped, wqkv[1]).astype(BF)
    v_out[...] = dot_nt(grouped, wqkv[2]).astype(BF)
    masks = head_masks(share)
    heads = len(masks)

    def attend(rel):
        here = pl.ds(pl.multiple_of(rel * tokens, tokens), tokens)
        query, key, value = q_out[here, :], k_out[here, :], v_out[here, :]
        parts = []
        for parity in range(2):
            q = half_rows(query, parity)
            k = half_rows(key, parity)
            v = half_rows(value, parity)
            probs = softmax_rows(jnp.concatenate([q * m for m in masks], axis=0), k)
            low = beside(probs.astype(BF), heads)
            parts.append(dot(low, jnp.concatenate([v * m for m in masks], axis=0)).astype(BF))
        ctx_out[here, :] = join_rows(*parts)

    pair_loop(attend)
    keep_out[...] = dot(ctx_out[0:tokens, :], wout[...]).astype(BF)
    send_out[...] = dot(ctx_out[tokens : 2 * tokens, :], wout[...]).astype(BF)


def ffn_kernel_body(
    s_ref, full, att_own, att_peer, go, gc, gx, gd, mod, up, down, kern,
    g_out, second_out, active_out, gfed_out, ghid_out, keep_out, send_out, mods_out, kgrad_out, fkeep_out, fsend_out,
    held, padded, slope, gpad, mid, fed, low, sums,
):
    n = s_ref[0]
    core = jnp.bitwise_and(n, 1)
    share, tokens = go.shape[1], go.shape[2]
    units = up.shape[1]
    tall = tokens + 2 * SIDE
    lats = [core, 1 - core]
    gather_features(n, lats, (go, gc, gx, gd), held, g_out)
    zero_edges(padded)
    zero_edges(gpad)
    kgrad_out[...] = jnp.zeros(kgrad_out.shape, F32)
    for rel, (lat, att) in enumerate(zip(lats, (att_own, att_peer))):
        gate1, gate2 = mod[lat, 0:1, :], mod[lat, 3:4, :]
        shift, scale = mod[lat, 1:2, :], 1.0 + mod[lat, 2:3, :]

        def rows(at):
            here = pl.ds(at + rel * tokens, ROWS)
            middle = full[here, :].astype(F32) + gate1 * att[pl.ds(at, ROWS), :].astype(F32)
            mid[here, :] = middle
            normed, _ = norm_stats(middle)
            second_out[here, :] = (normed * scale + shift).astype(BF)
            gfed_out[here, :] = (gate2 * g_out[here, :].astype(F32)).astype(BF)

        row_loop(tokens, rows)

    hidden = dot(second_out[...], up[...])
    for rel in range(PAIR):
        padded[inside(padded, rel), :] = hidden[rel * tokens : (rel + 1) * tokens]

    def lanes(rel, at):
        taps = taps_of(kern, at)
        for band in range(0, tokens, BAND):
            here = pl.ds(pl.multiple_of(rel * tokens + band, BAND), BAND)
            mixed = conv_band(padded, pl.multiple_of(rel * tall + band, SIDE), at, taps)
            square = mixed * mixed
            curve = jnp.tanh(GELU_A * mixed * (1.0 + GELU_B * square))
            half = 0.5 * (1.0 + curve)
            active_out[here, at] = (mixed * half).astype(BF)
            slope[here, at] = half + (0.5 * GELU_A) * mixed * (1.0 - curve * curve) * (
                1.0 + (3.0 * GELU_B) * square
            )

    lane_loop(units, lanes)
    fed[...] = dot(active_out[...], down[...])
    sums[...] = jnp.zeros(sums.shape, F32)
    for rel, lat in enumerate(lats):
        gate2 = mod[lat, 3:4, :]

        def rows_fed(at):
            here = pl.ds(at + rel * tokens, ROWS)
            term = fed[here, :]
            sums[rel] += fold_rows(term * g_out[here, :].astype(F32))
            low[here, :] = (gate2 * term + 0.25 * mid[here, :]).astype(BF)

        row_loop(tokens, rows_fed)
        mods_out[lat] = jnp.sum(sums[rel], 0, keepdims=True)
    by_core(core, lats, low, share, fkeep_out, fsend_out)
    gact = dot_nt(gfed_out[...], down[...]).astype(BF).astype(F32)
    for rel in range(PAIR):
        here = slice(rel * tokens, (rel + 1) * tokens)
        gpad[inside(gpad, rel), :] = gact[here] * slope[here, :]

    def lanes_back(rel, at):
        taps = taps_of(kern, at)
        sums = [None] * 9
        for band in range(0, tokens, BAND):
            here = pl.ds(pl.multiple_of(rel * tokens + band, BAND), BAND)
            base = pl.multiple_of(rel * tall + band, SIDE)
            total, shifted = conv_back_band(gpad, base, at, taps)
            ghid_out[here, at] = total.astype(BF)
            for r in range(3):
                values = padded[pl.ds(base + SIDE * r, BAND), at]
                for c in range(3):
                    part = fold_rows(values * shifted[c])
                    sums[3 * r + c] = part if sums[3 * r + c] is None else sums[3 * r + c] + part
        for t in range(9):
            kgrad_out[t : t + 1, at] += jnp.sum(sums[t], 0, keepdims=True)

    lane_loop(units, lanes_back)
    keep_out[...] = dot_nt(ghid_out[0:tokens, :], up[...]).astype(BF)
    send_out[...] = dot_nt(ghid_out[tokens : 2 * tokens, :], up[...]).astype(BF)


def attn_back_body(
    s_ref, full, att_own, att_peer, gs_own, gs_peer, gfull, mod, mod_b, q_in, k_in, v_in, kern, wqkv, wout,
    gatt_out, gq_out, gk_out, gv_out, mods_out, kgrad_out, keep_out, send_out,
    sums2, gmid, normed1, scale1, first, gpad, gback, low,
):
    n = s_ref[0]
    core = jnp.bitwise_and(n, 1)
    tokens = att_own.shape[0]
    width = full.shape[1]
    share = q_in.shape[1]
    tall = tokens + 2 * SIDE
    lats = [core, 1 - core]
    zero_edges(first)
    zero_edges(gpad)
    kgrad_out[...] = jnp.zeros(kgrad_out.shape, F32)
    mods_out[...] = jnp.zeros(mods_out.shape, F32)
    sums2[...] = jnp.zeros(sums2.shape, F32)
    for rel, (lat, att, gs) in enumerate(zip(lats, (att_own, att_peer), (gs_own, gs_peer))):
        gate1 = mod_b[lat, 0:1, :]
        low_scale, low_shift = 1.0 + mod[lat, 1:2, :], mod[lat, 0:1, :]
        scale2 = 1.0 + mod_b[lat, 2:3, :]

        def rows(at):
            here = pl.ds(at + rel * tokens, ROWS)
            x = full[here, :].astype(F32)
            attended = att[pl.ds(at, ROWS), :].astype(F32)
            normed, inv = norm_stats(x + gate1 * attended)
            grad = gs[pl.ds(at, ROWS), :].astype(F32)
            inner = grad * scale2
            mean_a = jnp.sum(inner, -1, keepdims=True) * (1.0 / width)
            mean_b = jnp.sum(inner * normed, -1, keepdims=True) * (1.0 / width)
            whole_grad = gfull[here, :].astype(F32) + inv * (inner - mean_a - normed * mean_b)
            gmid[here, :] = whole_grad
            gatt_out[here, :] = (gate1 * whole_grad).astype(BF)
            sums2[3 * rel] += fold_rows(attended * whole_grad)
            sums2[3 * rel + 1] += fold_rows(grad)
            sums2[3 * rel + 2] += fold_rows(grad * normed)

        row_loop(tokens, rows)

        def rows_first(at):
            here = pl.ds(at + rel * tokens, ROWS)
            normed, inv = norm_stats(full[here, :].astype(F32))
            normed1[here, :] = normed
            scale1[here, :] = jnp.broadcast_to(inv, (ROWS, LANES))
            first[pl.ds(at + rel * tall + SIDE, ROWS), :] = normed * low_scale + low_shift

        row_loop(tokens, rows_first)
        for k in range(3):
            mods_out[lat, 2 + k : 3 + k, :] = 0.25 * jnp.sum(sums2[3 * rel + k], 0, keepdims=True)
    gctx = dot_nt(gatt_out[...], wout[...]).astype(BF)
    gv_out[...] = gctx
    masks = head_masks(share)
    heads = len(masks)
    factor = 1.0 / math.sqrt(HEAD_DIM)

    def attend(rel):
        here = pl.ds(pl.multiple_of(rel * tokens, tokens), tokens)
        query, key, value, grads = q_in[here, :], k_in[here, :], v_in[here, :], gv_out[here, :]
        parts_q, parts_k, parts_v = [], [], []
        for parity in range(2):
            q = half_rows(query, parity)
            k = half_rows(key, parity)
            v = half_rows(value, parity)
            gc = half_rows(grads, parity)
            q_all = jnp.concatenate([q * m for m in masks], axis=0)
            k_all = jnp.concatenate([k * m for m in masks], axis=0)
            gc_all = jnp.concatenate([gc * m for m in masks], axis=0)
            probs = softmax_rows(q_all, k)
            parts_v.append(dot_tn(probs.astype(BF), gc_all).astype(BF))
            gprobs = dot_nt(gc_all, v).astype(BF).astype(F32)
            gscores = (probs * (gprobs - jnp.sum(probs * gprobs, -1, keepdims=True))).astype(BF)
            parts_q.append((dot(beside(gscores, heads), k_all) * factor).astype(BF))
            parts_k.append((dot_tn(gscores, q_all) * factor).astype(BF))
        gq_out[here, :], gk_out[here, :], gv_out[here, :] = join_rows(*parts_q), join_rows(*parts_k), join_rows(*parts_v)

    pair_loop(attend)
    for rel in range(PAIR):
        here = slice(rel * tokens, (rel + 1) * tokens)
        gpad[inside(gpad, rel), :] = (
            dot(gq_out[here, :], wqkv[0]) + dot(gk_out[here, :], wqkv[1]) + dot(gv_out[here, :], wqkv[2])
        )

    def lanes(rel, at):
        taps = taps_of(kern, at)
        sums = [None] * 9
        shift_sum, scale_sum = None, None
        for band in range(0, tokens, BAND):
            here = pl.ds(pl.multiple_of(rel * tokens + band, BAND), BAND)
            base = pl.multiple_of(rel * tall + band, SIDE)
            total, shifted = conv_back_band(gpad, base, at, taps)
            gback[here, at] = total
            part_a, part_b = fold_rows(total), fold_rows(total * normed1[here, at])
            shift_sum = part_a if shift_sum is None else shift_sum + part_a
            scale_sum = part_b if scale_sum is None else scale_sum + part_b
            for r in range(3):
                values = first[pl.ds(base + SIDE * r, BAND), at]
                for c in range(3):
                    part = fold_rows(values * shifted[c])
                    sums[3 * r + c] = part if sums[3 * r + c] is None else sums[3 * r + c] + part
        for t in range(9):
            kgrad_out[t : t + 1, at] += jnp.sum(sums[t], 0, keepdims=True)
        lat = jnp.bitwise_xor(rel, core)
        mods_out[lat, 0:1, at] = jnp.sum(shift_sum, 0, keepdims=True)
        mods_out[lat, 1:2, at] = jnp.sum(scale_sum, 0, keepdims=True)

    lane_loop(width, lanes)
    for rel, lat in enumerate(lats):
        low_scale = 1.0 + mod[lat, 1:2, :]

        def rows_back(at):
            here = pl.ds(at + rel * tokens, ROWS)
            inner = gback[here, :] * low_scale
            normed = normed1[here, :]
            mean_a = jnp.sum(inner, -1, keepdims=True) * (1.0 / width)
            mean_b = jnp.sum(inner * normed, -1, keepdims=True) * (1.0 / width)
            grad = scale1[here, 0:1] * (inner - mean_a - normed * mean_b)
            low[here, :] = (grad + 0.25 * gmid[here, :]).astype(BF)

        row_loop(tokens, rows_back)
    by_core(core, lats, low, share, keep_out, send_out)


def call(body, name, scalars, ins, outs, scratch, flops, held=()):
    bytes_moved = sum(math.prod(o.shape) * o.dtype.itemsize for o, _ in outs)
    count = len(ins)

    def run(*refs):
        body(*refs[: 1 + count], *refs[1 + count + len(held) :])

    return pl.pallas_call(
        run,
        name=name,
        out_shape=[o for o, _ in outs],
        grid_spec=pltpu.PrefetchScalarGridSpec(
            num_scalar_prefetch=1,
            grid=(1,),
            in_specs=[s for _, s in ins] + [pl.BlockSpec(memory_space=pl.ANY)] * len(held),
            out_specs=[s for _, s in outs],
            scratch_shapes=scratch,
        ),
        input_output_aliases={1 + count + k: len(outs) - len(held) + k for k in range(len(held))},
        compiler_params=pltpu.CompilerParams(vmem_limit_bytes=VMEM_LIMIT),
        cost_estimate=pl.CostEstimate(flops=flops, bytes_accessed=bytes_moved, transcendentals=0),
    )(scalars, *[a for a, _ in ins], *held)


def slices_out(slots, slot, share, tokens):
    return (
        jax.ShapeDtypeStruct((2, slots, share, tokens), BF),
        pl.BlockSpec((2, PAIR, share, tokens), lambda i, s: (0, slot, 0, 0)),
    )


def whole(array):
    dims = array.shape
    return (array, pl.BlockSpec(dims, lambda i, s: (0,) * len(dims)))


def whole_out(dims, dtype):
    return (jax.ShapeDtypeStruct(dims, dtype), pl.BlockSpec(dims, lambda i, s: (0,) * len(dims)))


def pair_of(array, pair):
    dims = (PAIR,) + array.shape[1:]
    return (array, pl.BlockSpec(dims, lambda i, s: (pair,) + (0,) * (len(dims) - 1)))


def split_low(v):
    high = v.astype(BF)
    return high, (v - high.astype(F32)).astype(BF)


def rows_product(a, b):
    (ah, al), (bh, bl) = split_low(a), split_low(b)
    return dot_tn(jnp.concatenate([ah, al, ah], 0), jnp.concatenate([bh, bh, bl], 0))


def back_product(a, weight):
    (ah, al), (wh, wl) = split_low(a), split_low(weight)
    return dot_nt(ah, wh) + dot_nt(al, wh) + dot_nt(ah, wl)


def ada_step(factor, gmod, outer, ada, grad_out, bias_out, total):
    grads = gmod[0]
    high, low = split_low(outer[...])
    grad_out[...] = dot_tn(jnp.concatenate([high, low], 0), jnp.concatenate([grads, grads], 0)) * factor
    bias_out[...] = jnp.sum(grads.astype(F32), 0, keepdims=True) * factor
    high, low = split_low(ada[...])
    total[...] += (dot_nt(grads, high) + dot_nt(grads, low)) * factor


def ada_body(factor, gmod, outer, ada, grad_out, bias_out, total_out):
    @pl.when(pl.program_id(0) == 0)
    def _():
        total_out[...] = jnp.zeros(total_out.shape, F32)

    ada_step(factor, gmod, outer, ada, grad_out, bias_out, total_out)


def time_body(
    factor, gmod, outer, ada, held_grad, held_bias, so_far, embedded, inner, inner_pre, outer_pre, time_out,
    grad_out, bias_out, time_out_grad, time_in_grad, total,
):
    del held_grad, held_bias

    @pl.when(pl.program_id(0) == 0)
    def _():
        total[...] = so_far[...]

    ada_step(factor, gmod, outer, ada, grad_out, bias_out, total)

    @pl.when(pl.program_id(0) == pl.num_programs(0) - 1)
    def _():
        outer_grad = total[...] * silu_slope(outer_pre[...])
        time_out_grad[...] = rows_product(inner[...], outer_grad)
        inner_grad = back_product(outer_grad, time_out[...]) * silu_slope(inner_pre[...])
        time_in_grad[...] = rows_product(embedded[...], inner_grad)


def fixed(dims):
    return pl.BlockSpec(dims, lambda i: (0,) * len(dims))


def ada_specs(gmod, outer, ada_weight, first):
    depth, width = outer.shape[1], gmod.shape[2]
    columns = lambda rows: pl.BlockSpec((rows, width), lambda i: (0, i + first))
    ins = [pl.BlockSpec((1,) + gmod.shape[1:], lambda i: (i, 0, 0)), fixed(outer.shape), columns(depth)]
    shapes = [jax.ShapeDtypeStruct((rows, ada_weight.shape[1]), F32) for rows in (depth, 1)]
    return ins, [columns(depth), columns(1)], shapes


def ada_backward(gmod, outer, ada_weight, factor):
    ins, outs, shapes = ada_specs(gmod, outer, ada_weight, 2)
    return pl.pallas_call(
        functools.partial(ada_body, factor),
        name="ada_bwd",
        grid=(gmod.shape[0],),
        in_specs=ins,
        out_specs=outs + [fixed(outer.shape)],
        out_shape=shapes + [jax.ShapeDtypeStruct(outer.shape, F32)],
        compiler_params=pltpu.CompilerParams(vmem_limit_bytes=VMEM_LIMIT),
        cost_estimate=pl.CostEstimate(flops=10**9, bytes_accessed=24 * 10**6, transcendentals=0),
    )(gmod, outer, ada_weight)


def time_backward(gmod, outer, ada_weight, factor, held, so_far, *rest):
    embedded, time_out = rest[0], rest[-1]
    ins, outs, shapes = ada_specs(gmod, outer, ada_weight, 0)
    ins = ins + [pl.BlockSpec(memory_space=pl.ANY)] * 2 + [fixed(so_far.shape)] + [fixed(v.shape) for v in rest]
    more = [time_out.shape, (embedded.shape[1], time_out.shape[0])]
    return pl.pallas_call(
        functools.partial(time_body, factor),
        name="time_bwd",
        grid=(gmod.shape[0],),
        in_specs=ins,
        out_specs=outs + [fixed(dims) for dims in more],
        out_shape=shapes + [jax.ShapeDtypeStruct(dims, F32) for dims in more],
        scratch_shapes=[pltpu.VMEM(outer.shape, F32)],
        input_output_aliases={3: 0, 4: 1},
        compiler_params=pltpu.CompilerParams(vmem_limit_bytes=VMEM_LIMIT),
        cost_estimate=pl.CostEstimate(flops=10**9, bytes_accessed=16 * 10**6, transcendentals=0),
    )(gmod, outer, ada_weight, *held, so_far, *rest)


def attn_forward(scalars, pair, x_parts, mod, attn_kernel, qkv_weight, out_weight):
    _, share, tokens = x_parts[0].shape
    width = out_weight.shape[1]
    rows = PAIR * tokens
    thin = whole_out((rows, share), BF)
    half = whole_out((tokens, width), BF)
    return call(
        attn_kernel_body, "attn_fwd", scalars,
        [pair_of(v, pair) for v in x_parts] + [pair_of(mod, pair), whole(attn_kernel), whole(qkv_weight), whole(out_weight)],
        [whole_out((rows, width), BF), whole_out((rows, width), BF), thin, thin, thin, thin, half, half],
        [pltpu.VMEM((4, share, tokens), BF), pltpu.VMEM((PAIR * (tokens + 2 * SIDE), width), F32)],
        6_000_000_000,
    )


def feed_forward(scalars, pair, full, att, g_parts, mod, up_weight, down_weight, ffn_kernel, slots, held):
    _, share, tokens = g_parts[0].shape
    width, units = up_weight.shape
    rows = PAIR * tokens
    tall = PAIR * (tokens + 2 * SIDE)
    broad = whole_out((rows, width), BF)
    hidden = whole_out((rows, units), BF)
    half = whole_out((tokens, width), BF)
    slices = slices_out(slots, pair, share, tokens)
    return call(
        ffn_kernel_body, "ffn", scalars,
        [whole(full), whole(att[0]), whole(att[1])] + [pair_of(v, pair) for v in g_parts]
        + [pair_of(mod, pair), whole(up_weight), whole(down_weight), whole(ffn_kernel)],
        [broad, broad, hidden, broad, hidden, half, half, whole_out((PAIR, 1, width), F32), whole_out((9, units), F32),
         slices, slices],
        [pltpu.VMEM((4, share, tokens), BF), pltpu.VMEM((tall, units), F32), pltpu.VMEM((rows, units), F32),
         pltpu.VMEM((tall, units), F32), pltpu.VMEM((rows, width), F32), pltpu.VMEM((rows, width), F32),
         pltpu.VMEM((rows, width), BF), pltpu.VMEM((PAIR, 8, width), F32)],
        10_000_000_000, held,
    )


def attn_backward(
    scalars, pair, full, att, gsec, gfull, mod, mod_b, qkv, attn_kernel, qkv_weight, out_weight, slots, held
):
    tokens, width = att[0].shape
    share = out_weight.shape[0]
    rows = PAIR * tokens
    tall = PAIR * (tokens + 2 * SIDE)
    thin = whole_out((rows, share), BF)
    slices = slices_out(slots, slots // PAIR // 2 + pair, share, tokens)
    return call(
        attn_back_body, "attn_bwd", scalars,
        [whole(full), whole(att[0]), whole(att[1]), whole(gsec[0]), whole(gsec[1]), whole(gfull), pair_of(mod, pair),
         pair_of(mod_b, pair)]
        + [whole(v) for v in qkv] + [whole(attn_kernel), whole(qkv_weight), whole(out_weight)],
        [whole_out((rows, width), BF), thin, thin, thin, whole_out((PAIR, 8, width), F32), whole_out((9, width), F32),
         slices, slices],
        [pltpu.VMEM((3 * PAIR, 8, width), F32), pltpu.VMEM((rows, width), F32), pltpu.VMEM((rows, width), F32),
         pltpu.VMEM((rows, LANES), F32), pltpu.VMEM((tall, width), F32), pltpu.VMEM((tall, width), F32),
         pltpu.VMEM((rows, width), F32), pltpu.VMEM((rows, width), BF)],
        10_000_000_000, held,
    )


def core_swap(v):
    return lax.ppermute(v, "narrow", [(0, 1), (1, 0), (2, 3), (3, 2)])


def x_swap(v):
    return lax.ppermute(v, "narrow", [(0, 2), (2, 0), (1, 3), (3, 1)])


def sum_pair(a, b):
    return (a.astype(F32) + b.astype(F32)).astype(BF)


def slice_halves(x, keep, arrived):
    both = sum_pair(keep, arrived)
    return (
        lax.dynamic_index_in_dim(both, x, 0, keepdims=False),
        lax.dynamic_index_in_dim(both, 1 - x, 0, keepdims=False),
    )


def wide_swap(v, bit, count):
    return lax.ppermute(v, "wide", [(i, i ^ bit) for i in range(count)])


def pick(v, parts, at):
    rows = v.shape[0] // parts
    return lax.dynamic_slice_in_dim(v, at * rows, rows, 0)


def in_place(bit, own, came):
    return jnp.concatenate([jnp.where(bit == 0, own, came), jnp.where(bit == 0, came, own)], 0)


class WideSum:
    def __init__(self, order, product, at, count):
        self.order, self.count = order, count
        self.levels = count.bit_length() - 1
        self.bits = [at // (1 << k) % 2 for k in range(self.levels)]
        self.level, self.down = 0, True
        self.held = product
        self.swap(order(lambda v, bit: pick(v, 2, 1 - bit), product, self.bits[0]))

    def swap(self, sent):
        self.came = wide_swap(sent, 1 << self.level, self.count)

    def halve(self, held, came):
        if self.level == 0:
            held = pick(held, 2, self.bits[0])
        if self.level == self.levels - 1:
            return (sum_pair(held, came),)
        bit = self.bits[self.level + 1]
        return tuple(sum_pair(pick(held, 2, at), pick(came, 2, at)) for at in (1 - bit, bit))

    def step(self):
        if self.down:
            out = self.order(self.halve, self.held, self.came)
            self.held = out[-1]
            if len(out) == 1:
                self.down = False
            else:
                self.level += 1
            self.swap(out[0])
        else:
            self.held = self.order(functools.partial(in_place, self.bits[self.level]), self.held, self.came)
            self.level -= 1
            self.swap(self.held)

    def ready(self):
        return not self.down and self.level == 0

    def finish(self):
        return self.order(
            lambda a, b: in_place(self.bits[0], a.astype(F32), b.astype(F32)), self.held, self.came
        )


def after(value, *others):
    return lax.optimization_barrier((value, others))[0]


class Order:
    def __init__(self):
        self.last = ()

    def __call__(self, step, *inputs):
        inputs, _ = lax.optimization_barrier((inputs, self.last))
        out = step(*inputs)
        self.last = tuple(jax.tree.leaves(out)[:1])
        return out


def embed_times(stamps):
    halved = FREQ // 2
    freqs = jnp.exp(-math.log(10000.0) * jnp.arange(halved, dtype=F32) / halved)
    angles = stamps[:, None] * freqs[None, :]
    return jnp.concatenate([jnp.cos(angles), jnp.sin(angles)], 1)


def silu_slope(v):
    gate = jax.nn.sigmoid(v)
    return gate * (1.0 + v * (1.0 - gate))


def body(
    latents, cotangent, timesteps, time_in, time_out, ada_weight, ada_bias,
    attn_kernel, qkv_weight, out_weight, up_weight, ffn_kernel, down_weight,
):
    wide_count = lax.axis_size("wide")
    wide_at = lax.axis_index("wide")
    n = lax.axis_index("narrow")
    per_dev, tokens, share = latents.shape
    width = out_weight.shape[1]
    units = up_weight.shape[1]
    latent_total = timesteps.shape[0]
    scalars = jnp.stack([n, n]).astype(jnp.int32)

    met = jnp.bitwise_xor(jnp.arange(wide_count, dtype=jnp.int32), wide_at)
    stamps = timesteps.reshape(wide_count, per_dev)[met].reshape(latent_total).astype(F32)
    embedded = embed_times(stamps)
    high = lax.Precision.HIGH
    inner_pre = jnp.dot(embedded, time_in, precision=high)
    inner = jax.nn.silu(inner_pre)
    outer_pre = jnp.dot(inner, time_out, precision=high)
    outer = jax.nn.silu(outer_pre)
    x = n // 2
    factor = 1.0 / latent_total

    def pieces_of(first, count, rows):
        cols = slice(first * width, (first + count) * width)
        out = jnp.dot(rows, ada_weight[:, cols], precision=high) + ada_bias[cols]
        return out.reshape(per_dev, count, width)

    own_outer = outer[:per_dev]

    def token_product(lefts, rights):
        total = None
        for a, b in zip(lefts, rights):
            part = dot_tn(a, b)
            total = part if total is None else total + part
        return (total * factor).astype(BF)

    x_own = jnp.swapaxes(latents, 1, 2)
    g_own = jnp.swapaxes(cotangent, 1, 2)
    qkv_rows = jnp.swapaxes(qkv_weight, 1, 2)
    order = Order()
    x_across = x_swap(x_own)
    mod_a = order(lambda rows: pieces_of(0, 2, rows), own_outer)
    x_across = after(x_across, mod_a)
    g_across = x_swap(after(g_own, x_across))
    x_parts = (x_own, core_swap(x_own), x_across, core_swap(x_across))
    g_parts = (g_own, core_swap(g_own), g_across, core_swap(g_across))

    def attend(pair):
        return lambda parts: attn_forward(scalars, pair, parts, mod_a, attn_kernel, qkv_rows, out_weight)

    fwd_a = order(attend(0), x_parts)
    here_a = order(sum_pair, fwd_a[6], core_swap(fwd_a[7]))
    fwd_b = order(attend(1), after(x_parts, g_across))
    att_a = order(sum_pair, here_a, x_swap(here_a))
    here_b = order(sum_pair, fwd_b[6], core_swap(fwd_b[7]))
    mod_b = order(lambda rows: pieces_of(2, 4, rows), own_outer)
    att_a = (att_a, core_swap(att_a))

    slots = 2 * per_dev

    def feed(pair, full, held=()):
        return lambda att, parts: feed_forward(
            scalars, pair, full, att, parts, mod_b, up_weight, down_weight, ffn_kernel, slots, held
        )

    ffn_a = order(feed(0, fwd_a[0]), att_a, g_parts)
    att_b = order(sum_pair, here_b, x_swap(here_b))
    att_b = (att_b, core_swap(att_b))
    here_a = order(sum_pair, ffn_a[5], core_swap(ffn_a[6]))
    ffn_b = order(feed(1, fwd_b[0], ffn_a[9:11]), att_b, g_parts)
    sec_a = order(sum_pair, here_a, x_swap(here_a))
    sec_a = (sec_a, core_swap(sec_a))
    down_product = order(token_product, [ffn_a[2], ffn_b[2]], [ffn_a[3], ffn_b[3]])
    down_sum = WideSum(order, down_product, wide_at, wide_count)
    here_b = order(sum_pair, ffn_b[5], core_swap(ffn_b[6]))
    up_product = order(token_product, [ffn_a[1], ffn_b[1]], [ffn_a[4], ffn_b[4]])
    up_sum = WideSum(order, up_product, wide_at, wide_count)

    def attend_back(pair, full, gfull, qkv, held):
        return lambda att, sec: attn_backward(
            scalars, pair, full, att, sec, gfull, mod_a, mod_b, qkv, attn_kernel, qkv_rows, out_weight, slots, held
        )

    back_a = order(attend_back(0, fwd_a[0], ffn_a[0], fwd_a[2:5], ffn_b[9:11]), att_a, sec_a)
    sec_b = order(sum_pair, here_b, x_swap(here_b))
    sec_b = (sec_b, core_swap(sec_b))
    down_sum.step()
    back_b = order(attend_back(1, fwd_b[0], ffn_b[0], fwd_b[2:5], back_a[6:8]), att_b, sec_b)
    forward, back = (fwd_a, fwd_b), (back_a, back_b)

    lefts = [[r[5] for r in forward]] + [[g[k] for g in back] for k in (1, 2, 3)]
    rights = [[g[0] for g in back]] + [[r[1] for r in forward]] * 3
    attn_product = order(
        lambda *v: jnp.concatenate([token_product(v[2 * i], v[2 * i + 1]) for i in range(len(v) // 2)], 0),
        *[v for i in range(4) for v in (lefts[i], rights[i])],
    )
    attn_sum = WideSum(order, attn_product, wide_at, wide_count)
    down_sum.step()
    up_sum.step()

    rows_a, rows_b = 4 * per_dev, 2 * per_dev

    def pack_rows(back_mods, gates, taps, units_taps):
        mods = jnp.concatenate(back_mods, 0)
        late = jnp.concatenate([mods[:, 0], mods[:, 1], taps[0] + taps[1]], 0)
        early = jnp.concatenate([mods[:, 2], mods[:, 3], mods[:, 4], jnp.concatenate(gates, 0)[:, 0]], 0)
        ffn = (units_taps[0] + units_taps[1]).reshape(9 * units // width, width)
        return jnp.concatenate([early, late], 0).astype(BF), ffn.astype(BF)

    packed, ffn_taps = order(
        pack_rows, [g[4] for g in back], [ffn_a[7], ffn_b[7]], [g[5] for g in back], [ffn_a[8], ffn_b[8]]
    )
    packed = order(sum_pair, packed, core_swap(packed))
    down_sum.step()
    attn_sum.step()
    packed = order(lambda a, b, c: jnp.concatenate([sum_pair(a, b), c], 0), packed, x_swap(packed), ffn_taps)
    held, bit = packed[None], 1
    made = order(functools.partial(slice_halves, x), back_b[6], core_swap(back_b[7]))
    sums = (up_sum, down_sum, attn_sum)
    while bit < wide_count:
        for each in sums:
            if not each.ready():
                each.step()
        held = order(lambda a, b: jnp.concatenate([a, b], 0), held, wide_swap(held, bit, wide_count))
        bit *= 2
    def by_piece(v, rows):
        split = v[:, :rows].reshape(wide_count, rows // per_dev, per_dev, width)
        return jnp.swapaxes(split, 0, 1).reshape(rows // per_dev, latent_total, width)

    def unpack(held):
        both = by_piece(held, rows_a + rows_b)
        taps = jnp.sum(held[:, rows_a + rows_b :].astype(F32), 0) * factor
        return both[:4], both[4:], taps[:9], taps[9:].reshape(9, units)

    gmod_a, gmod_b, attn_taps, ffn_taps = order(unpack, held)
    for each in sums:
        if not each.ready():
            each.step()
    *ada_grads, outer_grad = order(lambda g: ada_backward(g, outer, ada_weight, factor), gmod_a)
    for each in sums:
        if not each.ready():
            each.step()
    finals = order(sum_pair, made[0], x_swap(made[1]))
    ada_weight_grad, ada_bias_grad, time_out_grad, time_in_grad = order(
        lambda g, held_grads, so_far: time_backward(
            g, outer, ada_weight, factor, held_grads, so_far, embedded, inner, inner_pre, outer_pre, time_out
        ),
        gmod_b, ada_grads, outer_grad,
    )
    ada_bias_grad = ada_bias_grad.reshape(6 * width)
    while not all(each.ready() for each in sums):
        for each in sums:
            if not each.ready():
                each.step()
    down_grad = down_sum.finish()
    up_grad = up_sum.finish()
    attn_grads = attn_sum.finish()
    out_grad, qkv_rows_grad = attn_grads[:share], attn_grads[share:]
    qkv_grad = jnp.swapaxes(qkv_rows_grad.reshape(3, share, width), 1, 2)
    final_out = jnp.swapaxes(finals[:per_dev], 1, 2)
    final_grad = jnp.swapaxes(finals[per_dev:], 1, 2)
    return (
        final_out, final_grad, time_in_grad, time_out_grad, ada_weight_grad, ada_bias_grad,
        attn_taps, qkv_grad, out_grad, up_grad, ffn_taps, down_grad,
    )


def solution(mesh):
    tokens = P("wide", None, "narrow")
    weights = (P(None, None, "narrow"), P("narrow", None), P(None, "narrow"), P(None, "narrow"), P("narrow", None))
    return jax.shard_map(
        body,
        mesh=mesh,
        in_specs=(tokens, tokens, P(), P(), P(), P(), P(), P()) + weights,
        out_specs=(tokens, tokens, P(), P(), P(), P(), P()) + weights,
        check_vma=False,
    )
```

```python
import functools
import math

import jax
import jax.numpy as jnp
from jax import lax
from jax.experimental import pallas as pl
from jax.experimental.pallas import tpu as pltpu
from jax.sharding import PartitionSpec as P

HEAD_DIM = 64
FREQ = 256
SIDE = 16
PAIR = 2

BF = jnp.bfloat16
F32 = jnp.float32
HIGHEST = lax.Precision.HIGHEST
LANES = 128
ROWS = 256
BAND = 64
GELU_A = math.sqrt(2.0 / math.pi)
GELU_B = 0.044715
EPS = 1e-06
VMEM_LIMIT = 60 * 1024 * 1024
WEIGHT_ROWS = 256
PACKED = 40


def dot(a, b):
    return lax.dot_general(a, b, (((1,), (0,)), ((), ())), preferred_element_type=F32)


def dot_nt(a, b):
    return lax.dot_general(a, b, (((1,), (1,)), ((), ())), preferred_element_type=F32)


def dot_tn(a, b):
    return lax.dot_general(a, b, (((0,), (0,)), ((), ())), preferred_element_type=F32)


def column_of(rows):
    return lax.broadcasted_iota(jnp.int32, (rows, LANES), 0) % SIDE


def from_left(v):
    moved = pltpu.roll(v, 1, 0)
    return jnp.where(column_of(v.shape[0]) == 0, 0.0, moved)


def from_right(v):
    moved = pltpu.roll(v, v.shape[0] - 1, 0)
    return jnp.where(column_of(v.shape[0]) == SIDE - 1, 0.0, moved)


def conv_band(padded, at, lanes, kern):
    rows = [padded[pl.ds(at + SIDE * r, BAND), lanes] for r in range(3)]
    mixed = [
        rows[0] * kern[c] + rows[1] * kern[3 + c] + rows[2] * kern[6 + c] for c in range(3)
    ]
    return from_left(mixed[0]) + mixed[1] + from_right(mixed[2])


def conv_back_band(padded_grad, at, lanes, kern):
    wide = padded_grad[pl.ds(at, BAND + 2 * SIDE), lanes]
    shifted = [from_right(wide), wide, from_left(wide)]
    total = None
    for r in range(3):
        for c in range(3):
            low = SIDE * (2 - r)
            term = shifted[c][low : low + BAND] * kern[3 * r + c]
            total = term if total is None else total + term
    return total, [s[SIDE : SIDE + BAND] for s in shifted]


def fold_rows(v):
    total = v[0:8]
    for at in range(8, v.shape[0], 8):
        total = total + v[at : at + 8]
    return total


def taps_of(kern_ref, lanes):
    block = kern_ref[:, lanes]
    return [block[t : t + 1] for t in range(9)]


def zero_edges(ref):
    edge = jnp.zeros((SIDE, ref.shape[1]), F32)
    tall = ref.shape[0] // PAIR
    for rel in range(PAIR):
        ref[rel * tall : rel * tall + SIDE, :] = edge
        ref[(rel + 1) * tall - SIDE : (rel + 1) * tall, :] = edge


def inside(ref, rel):
    tall = ref.shape[0] // PAIR
    return slice(rel * tall + SIDE, (rel + 1) * tall - SIDE)


def gather_features(n, lats, parts, held, out):
    _, share, tokens = parts[0].shape
    for rel, lat in enumerate(lats):
        for step, part in enumerate(parts):
            held[jnp.bitwise_xor(n, step)] = part[lat]
        out[rel * tokens : (rel + 1) * tokens, :] = held[...].reshape(len(parts) * share, tokens).T


def by_core(core, lats, low, share, keep_out, send_out):
    tokens = low.shape[0] // PAIR
    for rel, lat in enumerate(lats):
        turned = low[rel * tokens : (rel + 1) * tokens, :].T
        for parity in range(2):

            @pl.when(core == parity)
            def _():
                for x in range(2):
                    here, there = 2 * x + parity, 2 * x + 1 - parity
                    keep_out[x, lat] = turned[here * share : (here + 1) * share]
                    send_out[x, lat] = turned[there * share : (there + 1) * share]


def norm_stats(v):
    width = v.shape[1]
    mean = jnp.sum(v, -1, keepdims=True) * (1.0 / width)
    center = v - mean
    spread = jnp.sum(center * center, -1, keepdims=True) * (1.0 / width)
    scale = lax.rsqrt(spread + EPS)
    return center * scale, scale


def head_masks(share):
    lane = lax.broadcasted_iota(jnp.int32, (1, share), 1) // HEAD_DIM
    return [(lane == h).astype(F32).astype(BF) for h in range(share // HEAD_DIM)]


def half_rows(v, parity):
    tokens, width = v.shape
    split = v.reshape(tokens // (2 * SIDE), 2, SIDE, width)
    return split[:, parity].reshape(tokens // 2, width)


def join_rows(even, odd):
    half, width = even.shape
    both = jnp.stack([even.reshape(half // SIDE, SIDE, width), odd.reshape(half // SIDE, SIDE, width)], 1)
    return both.reshape(2 * half, width)


def softmax_rows(queries, keys):
    scores = dot_nt(queries, keys) * (1.0 / math.sqrt(HEAD_DIM))
    rows = lax.broadcasted_iota(jnp.int32, scores.shape, 0)
    cols = lax.broadcasted_iota(jnp.int32, scores.shape, 1)
    same = (rows + cols) % 2 == 0
    scores = jnp.where(same, scores, -1e30)
    top = jnp.max(scores, -1, keepdims=True)
    grown = jnp.where(same, jnp.exp(scores - top), 0.0)
    return grown / jnp.sum(grown, -1, keepdims=True)


def beside(stacked, heads):
    rows = stacked.shape[0] // heads
    return jnp.concatenate([stacked[h * rows : (h + 1) * rows] for h in range(heads)], axis=1)


def lane_loop(width, body):
    count = width // LANES

    def step(j, carry):
        body(j // count, pl.ds(pl.multiple_of((j % count) * LANES, LANES), LANES))
        return carry

    lax.fori_loop(0, PAIR * count, step, 0)


def row_loop(tokens, body):
    def step(j, carry):
        body(pl.multiple_of(j * ROWS, ROWS))
        return carry

    lax.fori_loop(0, tokens // ROWS, step, 0)


def pair_loop(body):
    def step(j, carry):
        body(j)
        return carry

    lax.fori_loop(0, PAIR, step, 0)


def attn_kernel_body(
    flow, s_ref, xo, xc, xx, xd, mod, kern, wqkv, wout,
    full_out, grouped_out, q_out, k_out, v_out, ctx_out, keep_out, send_out,
    held, padded,
):
    n = s_ref[0]
    core = jnp.bitwise_and(n, 1)
    share, tokens = xo.shape[1], xo.shape[2]
    width = full_out.shape[1]
    tall = tokens + 2 * SIDE
    lats = [core, 1 - core]
    zero_edges(padded)
    flow.need(xo, xc, xx, xd, mod, kern)
    gather_features(n, lats, (xo, xc, xx, xd), held, full_out)
    flow.sent(full_out)
    for rel, lat in enumerate(lats):
        shift, scale = mod[lat, 0:1, :], 1.0 + mod[lat, 1:2, :]

        def rows(at):
            normed, _ = norm_stats(full_out[pl.ds(at + rel * tokens, ROWS), :].astype(F32))
            padded[pl.ds(at + rel * tall + SIDE, ROWS), :] = normed * scale + shift

        row_loop(tokens, rows)

    def lanes(rel, at):
        taps = taps_of(kern, at)
        for band in range(0, tokens, BAND):
            here = pl.ds(pl.multiple_of(rel * tokens + band, BAND), BAND)
            grouped_out[here, at] = conv_band(padded, pl.multiple_of(rel * tall + band, SIDE), at, taps).astype(BF)

    lane_loop(width, lanes)
    flow.sent(grouped_out)
    flow.need(wqkv, wout)
    grouped = grouped_out[...]
    q_out[...] = dot_nt(grouped, wqkv[0]).astype(BF)
    k_out[...] = dot_nt(grouped, wqkv[1]).astype(BF)
    v_out[...] = dot_nt(grouped, wqkv[2]).astype(BF)
    flow.sent(q_out, k_out, v_out)
    masks = head_masks(share)
    heads = len(masks)

    def attend(rel):
        here = pl.ds(pl.multiple_of(rel * tokens, tokens), tokens)
        query, key, value = q_out[here, :], k_out[here, :], v_out[here, :]
        parts = []
        for parity in range(2):
            q = half_rows(query, parity)
            k = half_rows(key, parity)
            v = half_rows(value, parity)
            probs = softmax_rows(jnp.concatenate([q * m for m in masks], axis=0), k)
            low = beside(probs.astype(BF), heads)
            parts.append(dot(low, jnp.concatenate([v * m for m in masks], axis=0)).astype(BF))
        ctx_out[here, :] = join_rows(*parts)

    pair_loop(attend)
    flow.sent(ctx_out)
    send_out[...] = dot(ctx_out[tokens : 2 * tokens, :], wout[...]).astype(BF)
    flow.sent(send_out)
    keep_out[...] = dot(ctx_out[0:tokens, :], wout[...]).astype(BF)
    flow.sent(keep_out)


def ffn_kernel_body(
    first, flow, s_ref, go, gc, gx, gd, full, att_own, att_peer, mod, up, down, kern, kgrad_in,
    g_out, second_out, active_out, gfed_out, ghid_out, keep_out, send_out, mods_out, kgrad_out, fkeep_out, fsend_out,
    held, padded, slope, gpad, mid, fed, low, sums,
):
    n = s_ref[0]
    core = jnp.bitwise_and(n, 1)
    share, tokens = go.shape[1], go.shape[2]
    units = up.shape[1]
    tall = tokens + 2 * SIDE
    lats = [core, 1 - core]
    zero_edges(padded)
    zero_edges(gpad)
    flow.need(go, gc, gx, gd)
    gather_features(n, lats, (go, gc, gx, gd), held, g_out)
    flow.sent(g_out)
    flow.need(full, att_own, att_peer, mod)
    flow.need(kgrad_in)
    kgrad_out[...] = jnp.zeros(kgrad_out.shape, F32) if first else kgrad_in[...]
    for rel, (lat, att) in enumerate(zip(lats, (att_own, att_peer))):
        gate1, gate2 = mod[lat, 2:3, :], mod[lat, 5:6, :]
        shift, scale = mod[lat, 3:4, :], 1.0 + mod[lat, 4:5, :]

        def rows(at):
            here = pl.ds(at + rel * tokens, ROWS)
            middle = full[here, :].astype(F32) + gate1 * att[pl.ds(at, ROWS), :].astype(F32)
            mid[here, :] = middle
            normed, _ = norm_stats(middle)
            second_out[here, :] = (normed * scale + shift).astype(BF)
            gfed_out[here, :] = (gate2 * g_out[here, :].astype(F32)).astype(BF)

        row_loop(tokens, rows)

    flow.sent(second_out, gfed_out)
    flow.need(up, kern)
    hidden = dot(second_out[...], up[...])
    for rel in range(PAIR):
        padded[inside(padded, rel), :] = hidden[rel * tokens : (rel + 1) * tokens]

    def lanes(rel, at):
        taps = taps_of(kern, at)
        for band in range(0, tokens, BAND):
            here = pl.ds(pl.multiple_of(rel * tokens + band, BAND), BAND)
            mixed = conv_band(padded, pl.multiple_of(rel * tall + band, SIDE), at, taps)
            square = mixed * mixed
            curve = jnp.tanh(GELU_A * mixed * (1.0 + GELU_B * square))
            half = 0.5 * (1.0 + curve)
            active_out[here, at] = (mixed * half).astype(BF)
            slope[here, at] = half + (0.5 * GELU_A) * mixed * (1.0 - curve * curve) * (
                1.0 + (3.0 * GELU_B) * square
            )

    lane_loop(units, lanes)
    flow.sent(active_out)
    flow.need(down)
    fed[...] = dot(active_out[...], down[...])
    sums[...] = jnp.zeros(sums.shape, F32)
    for rel, lat in enumerate(lats):
        gate2 = mod[lat, 5:6, :]

        def rows_fed(at):
            here = pl.ds(at + rel * tokens, ROWS)
            term = fed[here, :]
            sums[rel] += fold_rows(term * g_out[here, :].astype(F32))
            low[here, :] = (gate2 * term + 0.25 * mid[here, :]).astype(BF)

        row_loop(tokens, rows_fed)
        mods_out[lat] = jnp.sum(sums[rel], 0, keepdims=True)
    by_core(core, lats, low, share, fkeep_out, fsend_out)
    flow.sent(fkeep_out, fsend_out, mods_out)
    gact = dot_nt(gfed_out[...], down[...]).astype(BF).astype(F32)
    for rel in range(PAIR):
        here = slice(rel * tokens, (rel + 1) * tokens)
        gpad[inside(gpad, rel), :] = gact[here] * slope[here, :]

    def lanes_back(rel, at):
        taps = taps_of(kern, at)
        sums = [None] * 9
        for band in range(0, tokens, BAND):
            here = pl.ds(pl.multiple_of(rel * tokens + band, BAND), BAND)
            base = pl.multiple_of(rel * tall + band, SIDE)
            total, shifted = conv_back_band(gpad, base, at, taps)
            ghid_out[here, at] = total.astype(BF)
            for r in range(3):
                values = padded[pl.ds(base + SIDE * r, BAND), at]
                for c in range(3):
                    part = fold_rows(values * shifted[c])
                    sums[3 * r + c] = part if sums[3 * r + c] is None else sums[3 * r + c] + part
        for t in range(9):
            kgrad_out[t : t + 1, at] += jnp.sum(sums[t], 0, keepdims=True)

    lane_loop(units, lanes_back)
    flow.sent(ghid_out, kgrad_out)
    send_out[...] = dot_nt(ghid_out[tokens : 2 * tokens, :], up[...]).astype(BF)
    flow.sent(send_out)
    keep_out[...] = dot_nt(ghid_out[0:tokens, :], up[...]).astype(BF)
    flow.sent(keep_out)


def attn_back_body(
    flow, s_ref, full, att_own, att_peer, gs_own, gs_peer, gfull, mod, q_in, k_in, v_in, wout, gates,
    gatt_out, gqkv_out, gmid_out, mods_out,
    sums, gctx,
):
    core = jnp.bitwise_and(s_ref[0], 1)
    tokens = att_own.shape[0]
    width = full.shape[1]
    share = q_in.shape[1]
    lats = [core, 1 - core]
    mods_out[...] = jnp.zeros(mods_out.shape, F32)
    sums[...] = jnp.zeros(sums.shape, F32)
    flow.need(full, att_own, att_peer, gs_own, gs_peer, gfull, mod)
    for rel, (lat, att, gs) in enumerate(zip(lats, (att_own, att_peer), (gs_own, gs_peer))):
        gate1 = mod[lat, 2:3, :]
        scale2 = 1.0 + mod[lat, 4:5, :]

        def rows(at):
            here = pl.ds(at + rel * tokens, ROWS)
            attended = att[pl.ds(at, ROWS), :].astype(F32)
            normed, inv = norm_stats(full[here, :].astype(F32) + gate1 * attended)
            grad = gs[pl.ds(at, ROWS), :].astype(F32)
            inner = grad * scale2
            mean_a = jnp.sum(inner, -1, keepdims=True) * (1.0 / width)
            mean_b = jnp.sum(inner * normed, -1, keepdims=True) * (1.0 / width)
            whole_grad = gfull[here, :].astype(F32) + inv * (inner - mean_a - normed * mean_b)
            gmid_out[here, :] = whole_grad.astype(BF)
            gatt_out[here, :] = (gate1 * whole_grad).astype(BF)
            sums[3 * rel] += fold_rows(attended * whole_grad)
            sums[3 * rel + 1] += fold_rows(grad)
            sums[3 * rel + 2] += fold_rows(grad * normed)

        row_loop(tokens, rows)
        for k in range(3):
            mods_out[lat, 2 + k : 3 + k, :] = 0.25 * jnp.sum(sums[3 * rel + k], 0, keepdims=True)
    flow.need(wout, q_in, k_in, v_in, gates)
    for lat in range(PAIR):
        mods_out[lat, 5:6, :] = gates[lat]
    flow.sent(gatt_out, gmid_out, mods_out)
    gctx[...] = dot_nt(gatt_out[...], wout[...]).astype(BF)
    masks = head_masks(share)
    heads = len(masks)
    factor = 1.0 / math.sqrt(HEAD_DIM)

    def attend(rel):
        here = pl.ds(pl.multiple_of(rel * tokens, tokens), tokens)
        query, key, value, grads = q_in[here, :], k_in[here, :], v_in[here, :], gctx[here, :]
        parts_q, parts_k, parts_v = [], [], []
        for parity in range(2):
            q = half_rows(query, parity)
            k = half_rows(key, parity)
            v = half_rows(value, parity)
            gc = half_rows(grads, parity)
            q_all = jnp.concatenate([q * m for m in masks], axis=0)
            k_all = jnp.concatenate([k * m for m in masks], axis=0)
            gc_all = jnp.concatenate([gc * m for m in masks], axis=0)
            probs = softmax_rows(q_all, k)
            parts_v.append(dot_tn(probs.astype(BF), gc_all).astype(BF))
            gprobs = dot_nt(gc_all, v).astype(BF).astype(F32)
            gscores = (probs * (gprobs - jnp.sum(probs * gprobs, -1, keepdims=True))).astype(BF)
            parts_q.append((dot(beside(gscores, heads), k_all) * factor).astype(BF))
            parts_k.append((dot_tn(gscores, q_all) * factor).astype(BF))
        for k, parts in enumerate((parts_q, parts_k, parts_v)):
            gqkv_out[here, k * share : (k + 1) * share] = join_rows(*parts)

    pair_loop(attend)
    flow.sent(gqkv_out)


def input_back_body(
    closing, flow, s_ref, full, mod, gqkv, wqkv, kern, kgrad_in, gmid, mods_in, before,
    kgrad_out, mods_out, keep_out, send_out,
    normed1, scale1, first, gpad, gback, low, mods, rows_out,
):
    core = jnp.bitwise_and(s_ref[0], 1)
    tokens = full.shape[0] // PAIR
    width = full.shape[1]
    share = gqkv.shape[1] // 3
    tall = tokens + 2 * SIDE
    lats = [core, 1 - core]
    zero_edges(first)
    zero_edges(gpad)
    flow.need(full, mod)
    for rel, lat in enumerate(lats):
        low_scale, low_shift = 1.0 + mod[lat, 1:2, :], mod[lat, 0:1, :]

        def rows_first(at):
            here = pl.ds(at + rel * tokens, ROWS)
            normed, inv = norm_stats(full[here, :].astype(F32))
            normed1[here, :] = normed
            scale1[here, :] = jnp.broadcast_to(inv, (ROWS, LANES))
            first[pl.ds(at + rel * tall + SIDE, ROWS), :] = normed * low_scale + low_shift

        row_loop(tokens, rows_first)
    flow.need(gqkv, wqkv, kern, kgrad_in, gmid, mods_in, before)
    kgrad_out[...] = kgrad_in[...] if closing else jnp.zeros(kgrad_out.shape, F32)
    mods[...] = mods_in[...]
    for rel in range(PAIR):
        here = slice(rel * tokens, (rel + 1) * tokens)
        gpad[inside(gpad, rel), :] = dot(gqkv[here, :], wqkv[...])

    def lanes(rel, at):
        taps = taps_of(kern, at)
        sums = [None] * 9
        shift_sum, scale_sum = None, None
        for band in range(0, tokens, BAND):
            here = pl.ds(pl.multiple_of(rel * tokens + band, BAND), BAND)
            base = pl.multiple_of(rel * tall + band, SIDE)
            total, shifted = conv_back_band(gpad, base, at, taps)
            gback[here, at] = total
            part_a, part_b = fold_rows(total), fold_rows(total * normed1[here, at])
            shift_sum = part_a if shift_sum is None else shift_sum + part_a
            scale_sum = part_b if scale_sum is None else scale_sum + part_b
            for r in range(3):
                values = first[pl.ds(base + SIDE * r, BAND), at]
                for c in range(3):
                    part = fold_rows(values * shifted[c])
                    sums[3 * r + c] = part if sums[3 * r + c] is None else sums[3 * r + c] + part
        for t in range(9):
            kgrad_out[t : t + 1, at] += jnp.sum(sums[t], 0, keepdims=True)
        lat = jnp.bitwise_xor(rel, core)
        mods[lat, 0:1, at] = jnp.sum(shift_sum, 0, keepdims=True)
        mods[lat, 1:2, at] = jnp.sum(scale_sum, 0, keepdims=True)

    lane_loop(width, lanes)
    if closing:
        rows_out[...] = jnp.zeros(rows_out.shape, F32)
        for lat in range(PAIR):
            rows_out[6 * lat : 6 * lat + 6, :] = before[lat, 0:6, :]
            rows_out[6 * (PAIR + lat) : 6 * (PAIR + lat) + 6, :] = mods[lat, 0:6, :]
        rows_out[12 * PAIR : 12 * PAIR + 9, :] = kgrad_out[0:9, :]
        mods_out[...] = rows_out[...].astype(BF)
    else:
        mods_out[...] = mods[...]
    flow.sent(mods_out, kgrad_out)
    for rel, lat in enumerate(lats):
        low_scale = 1.0 + mod[lat, 1:2, :]

        def rows_back(at):
            here = pl.ds(at + rel * tokens, ROWS)
            inner = gback[here, :] * low_scale
            normed = normed1[here, :]
            mean_a = jnp.sum(inner, -1, keepdims=True) * (1.0 / width)
            mean_b = jnp.sum(inner * normed, -1, keepdims=True) * (1.0 / width)
            grad = scale1[here, 0:1] * (inner - mean_a - normed * mean_b)
            low[here, :] = (grad + 0.25 * gmid[here, :].astype(F32)).astype(BF)

        row_loop(tokens, rows_back)
    by_core(core, lats, low, share, keep_out, send_out)
    flow.sent(keep_out, send_out)


class Flow:
    def __init__(self, arrivals, departures):
        self.arrivals, self.departures = arrivals, departures
        self.leaving = []
        for _, copy in arrivals:
            copy.start()

    def need(self, *refs):
        for ref in refs:
            for at, (held, copy) in enumerate(self.arrivals):
                if held is ref:
                    copy.wait()
                    del self.arrivals[at]
                    break

    def sent(self, *refs):
        for ref in refs:
            for held, copy in self.departures:
                if held is ref:
                    copy.start()
                    self.leaving.append(copy)

    def end(self):
        for copy in self.leaving:
            copy.wait()


def call(body, name, scalars, ins, outs, scratch, flops, held=()):
    n_in, n_out = len(ins), len(outs)

    def run(s_ref, *refs):
        sources = refs[:n_in]
        targets = refs[n_in + len(held) : n_in + len(held) + n_out]
        buffers = refs[n_in + len(held) + n_out : -1]
        sems = refs[-1]
        buffers_in, buffers_out, rest = buffers[:n_in], buffers[n_in : n_in + n_out], buffers[n_in + n_out :]
        arrivals, departures = [], []
        for k, (source, buffer, (_, window)) in enumerate(zip(sources, buffers_in, ins)):
            view = source if window is None else source.at[window]
            arrivals.append((buffer, pltpu.make_async_copy(view, buffer, sems.at[k])))
        for k, (target, buffer, out) in enumerate(zip(targets, buffers_out, outs)):
            view = target if out[2] is None else target.at[out[2]]
            departures.append((buffer, pltpu.make_async_copy(buffer, view, sems.at[n_in + k])))
        flow = Flow(arrivals, departures)
        body(flow, s_ref, *buffers_in, *buffers_out, *rest)
        flow.end()

    anywhere = pl.BlockSpec(memory_space=pl.ANY)
    size = lambda array, window: array.shape if window is None else (PAIR,) + array.shape[1:]
    return pl.pallas_call(
        run,
        name=name,
        out_shape=[jax.ShapeDtypeStruct(o[0], o[1]) for o in outs],
        grid_spec=pltpu.PrefetchScalarGridSpec(
            num_scalar_prefetch=1,
            grid=(1,),
            in_specs=[anywhere] * (n_in + len(held)),
            out_specs=[anywhere] * n_out,
            scratch_shapes=[pltpu.VMEM(size(a, w), a.dtype) for a, w in ins]
            + [pltpu.VMEM(o[3], o[1]) for o in outs]
            + scratch
            + [pltpu.SemaphoreType.DMA((n_in + n_out,))],
        ),
        input_output_aliases={1 + n_in + k: n_out - len(held) + k for k in range(len(held))},
        compiler_params=pltpu.CompilerParams(vmem_limit_bytes=VMEM_LIMIT),
        cost_estimate=pl.CostEstimate(flops=flops, bytes_accessed=10**6, transcendentals=0),
    )(scalars, *[a for a, _ in ins], *held)


def slices_out(slots, slot, share, tokens):
    return ((2, slots, share, tokens), BF, (slice(None), pl.ds(PAIR * slot, PAIR)), (2, PAIR, share, tokens))


def whole(array):
    return (array, None)


def whole_out(dims, dtype):
    return (dims, dtype, None, dims)


def pair_of(array, pair):
    return (array, (pl.ds(PAIR * pair, PAIR),))


def split_low(v):
    high = v.astype(BF)
    return high, (v - high.astype(F32)).astype(BF)


def rows_product(a, b):
    (ah, al), (bh, bl) = split_low(a), split_low(b)
    return dot_tn(jnp.concatenate([ah, al, ah], 0), jnp.concatenate([bh, bh, bl], 0))


def back_product(a, weight):
    (ah, al), (wh, wl) = split_low(a), split_low(weight)
    return dot_nt(ah, wh) + dot_nt(al, wh) + dot_nt(ah, wl)


def product(a, weight):
    (ah, al), (wh, wl) = split_low(a), split_low(weight)
    return dot(ah, wh) + dot(al, wh) + dot(ah, wl)


def silu(v):
    return v / (1.0 + jnp.exp(-v))


def silu_slope(v):
    gate = 1.0 / (1.0 + jnp.exp(-v))
    return gate * (1.0 + v * (1.0 - gate))


def row_blocks(source, target, sems, rows):
    return [
        pltpu.make_async_copy(source.at[pl.ds(at, rows)], target.at[pl.ds(at, rows)], sems.at[at // rows])
        for at in range(0, source.shape[0], rows)
    ]


def condition_body(
    embedded, bias, time_in, time_out, ada, mod_out, inner_pre, inner, outer_pre, outer, held_in, held_out, held, sems,
):
    depth = ada.shape[0]
    per_dev, count, width = mod_out.shape
    first = pltpu.make_async_copy(time_in, held_in, sems.at[0])
    second = pltpu.make_async_copy(time_out, held_out, sems.at[1])
    blocks = row_blocks(ada, held, sems.at[pl.ds(2, depth // WEIGHT_ROWS)], WEIGHT_ROWS)
    for copy in [first, second] + blocks:
        copy.start()
    first.wait()
    inner_pre[...] = product(embedded[...], held_in[...])
    inner[...] = silu(inner_pre[...])
    second.wait()
    outer_pre[...] = product(inner[...], held_out[...])
    outer[...] = silu(outer_pre[...])
    wide_bias = [jnp.concatenate([bias[k + j : k + j + 1, :] for j in range(width // LANES)], 1)
                 for k in range(0, bias.shape[0], width // LANES)]
    total = jnp.concatenate(wide_bias, 1)
    for k, copy in enumerate(blocks):
        copy.wait()
        rows = slice(k * WEIGHT_ROWS, (k + 1) * WEIGHT_ROWS)
        total = total + product(outer[0:8, rows], held[rows, :])
    for lat in range(per_dev):
        for k in range(count):
            mod_out[lat, k : k + 1, :] = total[lat : lat + 1, k * width : (k + 1) * width]


def condition(embedded, time_in, time_out, ada_weight, ada_bias, per_dev, width):
    latent_total = embedded.shape[0]
    depth, columns = ada_weight.shape
    vmem = pl.BlockSpec(memory_space=pltpu.VMEM)
    anywhere = pl.BlockSpec(memory_space=pl.ANY)
    rows = jax.ShapeDtypeStruct((latent_total, depth), F32)
    return pl.pallas_call(
        condition_body,
        name="condition",
        in_specs=[vmem, vmem, anywhere, anywhere, anywhere],
        out_specs=[vmem] * 5,
        out_shape=[jax.ShapeDtypeStruct((per_dev, columns // width, width), F32), rows, rows, rows, rows],
        scratch_shapes=[
            pltpu.VMEM(time_in.shape, F32),
            pltpu.VMEM(time_out.shape, F32),
            pltpu.VMEM(ada_weight.shape, F32),
            pltpu.SemaphoreType.DMA((2 + depth // WEIGHT_ROWS,)),
        ],
        compiler_params=pltpu.CompilerParams(vmem_limit_bytes=VMEM_LIMIT),
        cost_estimate=pl.CostEstimate(flops=8 * 10**9, bytes_accessed=10**6, transcendentals=0),
    )(embedded, ada_bias.reshape(columns // LANES, LANES), time_in, time_out, ada_weight)


def condition_back_body(
    factor, gmod, embedded, inner_pre, inner, outer_pre, outer, time_out, ada,
    time_in_grad, time_out_grad, ada_grad, held_out, held, outer_grad, sems,
):
    depth = ada.shape[0]
    count = depth // WEIGHT_ROWS
    first = pltpu.make_async_copy(time_out, held_out, sems.at[0])
    blocks = row_blocks(ada, held, sems.at[pl.ds(1, count)], WEIGHT_ROWS)
    leaving = row_blocks(held, ada_grad, sems.at[pl.ds(1 + count, count)], WEIGHT_ROWS)
    for copy in blocks + [first]:
        copy.start()
    grads = gmod[...]
    twice = jnp.concatenate([grads, grads], 0)
    for k, (copy, leave) in enumerate(zip(blocks, leaving)):
        rows = slice(k * WEIGHT_ROWS, (k + 1) * WEIGHT_ROWS)
        copy.wait()
        high, low = split_low(held[rows, :])
        outer_grad[rows, :] = dot_nt(high, grads) + dot_nt(low, grads)
        high, low = split_low(outer[:, rows])
        held[rows, :] = dot_tn(jnp.concatenate([high, low], 0), twice) * factor
        leave.start()
    first.wait()
    back = outer_grad[...].T * factor * silu_slope(outer_pre[...])
    time_out_grad[...] = rows_product(inner[...], back)
    back = back_product(back, held_out[...]) * silu_slope(inner_pre[...])
    time_in_grad[...] = rows_product(embedded[...], back)
    for leave in leaving:
        leave.wait()


def condition_back(gmod, embedded, stages, time_out, ada_weight, factor):
    depth = ada_weight.shape[0]
    latent_total = gmod.shape[0]
    vmem = pl.BlockSpec(memory_space=pltpu.VMEM)
    anywhere = pl.BlockSpec(memory_space=pl.ANY)
    time_in_dims = (embedded.shape[1], time_out.shape[0])
    return pl.pallas_call(
        functools.partial(condition_back_body, factor),
        name="condition_back",
        in_specs=[vmem] * 6 + [anywhere] * 2,
        out_specs=[vmem, vmem, anywhere],
        out_shape=[
            jax.ShapeDtypeStruct(time_in_dims, F32),
            jax.ShapeDtypeStruct(time_out.shape, F32),
            jax.ShapeDtypeStruct(ada_weight.shape, F32),
        ],
        scratch_shapes=[
            pltpu.VMEM(time_out.shape, F32),
            pltpu.VMEM(ada_weight.shape, F32),
            pltpu.VMEM((depth, latent_total), F32),
            pltpu.SemaphoreType.DMA((1 + 2 * (depth // WEIGHT_ROWS),)),
        ],
        compiler_params=pltpu.CompilerParams(vmem_limit_bytes=VMEM_LIMIT),
        cost_estimate=pl.CostEstimate(flops=1, bytes_accessed=1, transcendentals=0),
    )(gmod, embedded, *stages, time_out, ada_weight)


def attn_forward(scalars, pair, x_parts, mod, attn_kernel, qkv_weight, out_weight):
    _, share, tokens = x_parts[0].shape
    width = out_weight.shape[1]
    rows = PAIR * tokens
    thin = whole_out((rows, share), BF)
    half = whole_out((tokens, width), BF)
    return call(
        attn_kernel_body, "attn_fwd", scalars,
        [pair_of(v, pair) for v in x_parts] + [pair_of(mod, pair), whole(attn_kernel), whole(qkv_weight), whole(out_weight)],
        [whole_out((rows, width), BF), whole_out((rows, width), BF), thin, thin, thin, thin, half, half],
        [pltpu.VMEM((4, share, tokens), BF), pltpu.VMEM((PAIR * (tokens + 2 * SIDE), width), F32)],
        6_000_000_000,
    )


def feed_forward(scalars, pair, full, att, g_parts, mod, up_weight, down_weight, ffn_kernel, slots, taps, held):
    _, share, tokens = g_parts[0].shape
    width, units = up_weight.shape
    rows = PAIR * tokens
    tall = PAIR * (tokens + 2 * SIDE)
    broad = whole_out((rows, width), BF)
    hidden = whole_out((rows, units), BF)
    half = whole_out((tokens, width), BF)
    slices = slices_out(slots, pair, share, tokens)
    return call(
        functools.partial(ffn_kernel_body, pair == 0), "ffn", scalars,
        [pair_of(v, pair) for v in g_parts] + [whole(full), whole(att[0]), whole(att[1])]
        + [pair_of(mod, pair), whole(up_weight), whole(down_weight), whole(ffn_kernel), whole(taps)],
        [broad, broad, hidden, broad, hidden, half, half, whole_out((PAIR, 1, width), F32), whole_out((16, units), F32),
         slices, slices],
        [pltpu.VMEM((4, share, tokens), BF), pltpu.VMEM((tall, units), F32), pltpu.VMEM((rows, units), F32),
         pltpu.VMEM((tall, units), F32), pltpu.VMEM((rows, width), F32), pltpu.VMEM((rows, width), F32),
         pltpu.VMEM((rows, width), BF), pltpu.VMEM((PAIR, 8, width), F32)],
        10_000_000_000, held,
    )


def attn_backward(scalars, pair, full, att, gsec, gfull, mod, qkv, out_weight, gates):
    tokens, width = att[0].shape
    share = out_weight.shape[0]
    rows = PAIR * tokens
    broad = whole_out((rows, width), BF)
    return call(
        attn_back_body, "attn_bwd", scalars,
        [whole(full), whole(att[0]), whole(att[1]), whole(gsec[0]), whole(gsec[1]), whole(gfull), pair_of(mod, pair)]
        + [whole(v) for v in qkv] + [whole(out_weight), whole(gates)],
        [broad, whole_out((rows, 3 * share), BF), broad, whole_out((PAIR, 8, width), F32)],
        [pltpu.VMEM((3 * PAIR, 8, width), F32), pltpu.VMEM((rows, share), BF)],
        6_000_000_000,
    )


def input_backward(scalars, pair, full, mod, gqkv, qkv_weight, attn_kernel, taps, gmid, mods_in, before, slots, held):
    rows, width = full.shape
    tokens = rows // PAIR
    share = gqkv.shape[1] // 3
    tall = PAIR * (tokens + 2 * SIDE)
    slices = slices_out(slots, slots // PAIR // 2 + pair, share, tokens)
    closing = pair > 0
    mods = whole_out((PACKED, width), BF) if closing else whole_out((PAIR, 8, width), F32)
    return call(
        functools.partial(input_back_body, closing), "input_bwd", scalars,
        [whole(full), pair_of(mod, pair), whole(gqkv), whole(qkv_weight), whole(attn_kernel), whole(taps), whole(gmid),
         whole(mods_in), whole(before)],
        [whole_out((16, width), F32), mods, slices, slices],
        [pltpu.VMEM((rows, width), F32), pltpu.VMEM((rows, LANES), F32), pltpu.VMEM((tall, width), F32),
         pltpu.VMEM((tall, width), F32), pltpu.VMEM((rows, width), F32), pltpu.VMEM((rows, width), BF),
         pltpu.VMEM((PAIR, 8, width), F32), pltpu.VMEM((PACKED, width), F32)],
        6_000_000_000, held,
    )


def core_swap(v):
    return lax.ppermute(v, "narrow", [(0, 1), (1, 0), (2, 3), (3, 2)])


def x_swap(v):
    return lax.ppermute(v, "narrow", [(0, 2), (2, 0), (1, 3), (3, 1)])


def sum_pair(a, b):
    return (a.astype(F32) + b.astype(F32)).astype(BF)


def slice_halves(x, keep, arrived):
    both = sum_pair(keep, arrived)
    return (
        lax.dynamic_index_in_dim(both, x, 0, keepdims=False),
        lax.dynamic_index_in_dim(both, 1 - x, 0, keepdims=False),
    )


def wide_swap(v, bit, count):
    return lax.ppermute(v, "wide", [(i, i ^ bit) for i in range(count)])


def pick(v, parts, at):
    rows = v.shape[0] // parts
    return lax.dynamic_slice_in_dim(v, at * rows, rows, 0)


def in_place(bit, own, came, axis):
    dims = own.shape[:axis] + (2,) + own.shape[axis + 1 :]
    return jnp.where(lax.broadcasted_iota(jnp.int32, dims, axis) == bit, own, came)


class WideSum:
    def __init__(self, product, at, count, back=None):
        self.count, self.dims = count, product.shape
        self.levels = count.bit_length() - 1
        self.bits = [at // (1 << k) % 2 for k in range(self.levels)]
        self.ahead = list(range(self.levels))
        self.back = list(reversed(self.ahead)) if back is None else back
        self.opened = False
        self.held = product

    def swap(self, sent, level):
        self.came = wide_swap(sent, 1 << level, self.count)

    def halve(self, held, came):
        level = self.ahead[0]
        if level == 0:
            held = pick(held, 2, self.bits[0])
        if len(self.ahead) == 1:
            return (sum_pair(held, came),)
        bit = self.bits[level + 1]
        return tuple(sum_pair(pick(held, 2, at), pick(came, 2, at)) for at in (1 - bit, bit))

    def pending(self):
        if not self.opened:
            return lambda v: pick(v, 2, 1 - self.bits[0]), (self.held,)
        if self.ahead:
            return self.halve, (self.held, self.came)
        level = self.back[0]
        return lambda a, b: in_place(self.bits[level], a, b, level), (self.held, self.came)

    def accept(self, out):
        if not self.opened:
            self.opened = True
            self.swap(out, 0)
        elif self.ahead:
            self.ahead.pop(0)
            self.held = out[-1]
            if self.ahead:
                self.swap(out[0], self.ahead[0])
            else:
                self.held = self.held.reshape((1,) * self.levels + self.held.shape)
                self.swap(self.held, self.back[0])
        else:
            self.back.pop(0)
            self.held = out
            self.swap(out, self.back[0])

    def done(self):
        return self.opened and not self.ahead and len(self.back) == 1

    def finish(self, order, shape=lambda v: v):
        level = self.back[0]
        return order(
            lambda a, b: shape(in_place(self.bits[level], a, b, level).reshape(self.dims)), self.held, self.came
        )


class Steps:
    def __init__(self, came, steps):
        self.came, self.steps = came, list(steps)

    def pending(self):
        return self.steps[0][0], self.came

    def accept(self, out):
        _, move = self.steps.pop(0)
        self.came = move(out)

    def done(self):
        return not self.steps


class Order:
    def __init__(self):
        self.last = ()

    def __call__(self, step, *inputs):
        inputs, _ = lax.optimization_barrier((inputs, self.last))
        out = step(*inputs)
        self.last = tuple(jax.tree.leaves(out)[:1])
        return out

    def advance(self, *chains):
        chains = [c for c in chains if not c.done()]
        if chains:
            work = [c.pending() for c in chains]
            outs = self(lambda *v: [w[0](*a) for w, a in zip(work, v)], *[w[1] for w in work])
            self.last = tuple(jax.tree.leaves(out)[0] for out in outs)
            for chain, out in zip(chains, outs):
                chain.accept(out)


def after(value, *others):
    return lax.optimization_barrier((value, others))[0]


def embed_times(stamps):
    halved = FREQ // 2
    freqs = jnp.exp(-math.log(10000.0) * jnp.arange(halved, dtype=F32) / halved)
    angles = stamps[:, None] * freqs[None, :]
    return jnp.concatenate([jnp.cos(angles), jnp.sin(angles)], 1)


def body(
    latents, cotangent, timesteps, time_in, time_out, ada_weight, ada_bias,
    attn_kernel, qkv_weight, out_weight, up_weight, ffn_kernel, down_weight,
):
    wide_count = lax.axis_size("wide")
    wide_at = lax.axis_index("wide")
    n = lax.axis_index("narrow")
    per_dev, tokens, share = latents.shape
    width = out_weight.shape[1]
    units = up_weight.shape[1]
    latent_total = timesteps.shape[0]
    scalars = n.astype(jnp.int32).reshape(1)

    steps, bit = [0], wide_count // 2
    while bit:
        steps, bit = steps + [k ^ bit for k in steps], bit // 2
    met = jnp.bitwise_xor(jnp.array(steps, jnp.int32), wide_at)
    stamps = timesteps.reshape(wide_count, per_dev)[met].reshape(latent_total).astype(F32)
    embedded = embed_times(stamps)
    mod, *stages = condition(embedded, time_in, time_out, ada_weight, ada_bias, per_dev, width)
    x = n // 2
    factor = 1.0 / latent_total

    def token_product(lefts, rights):
        total = None
        for a, b in zip(lefts, rights):
            part = dot_tn(a, b)
            total = part if total is None else total + part
        return (total * factor).astype(BF)

    x_own = jnp.swapaxes(latents, 1, 2)
    g_own = jnp.swapaxes(cotangent, 1, 2)
    qkv_rows = jnp.swapaxes(qkv_weight, 1, 2)
    qkv_all = qkv_rows.reshape(3 * share, width)
    order = Order()
    x_across = x_swap(x_own)
    x_across = after(x_across, mod)
    g_across = x_swap(after(g_own, x_across))
    x_parts = (x_own, core_swap(x_own), x_across, core_swap(x_across))
    g_parts = (g_own, core_swap(g_own), g_across, core_swap(g_across))

    def attend(pair):
        return lambda parts: attn_forward(scalars, pair, parts, mod, attn_kernel, qkv_rows, out_weight)

    fwd_a = order(attend(0), x_parts)
    here_a = order(sum_pair, fwd_a[6], core_swap(fwd_a[7]))
    fwd_b = order(attend(1), after(x_parts, g_across))
    att_a = order(sum_pair, here_a, x_swap(here_a))
    here_b = order(sum_pair, fwd_b[6], core_swap(fwd_b[7]))
    att_a = (att_a, core_swap(att_a))

    slots = 2 * per_dev

    def feed(pair, full, taps, held=()):
        return lambda att, parts: feed_forward(
            scalars, pair, full, att, parts, mod, up_weight, down_weight, ffn_kernel, slots, taps, held
        )

    ffn_a = order(feed(0, fwd_a[0], ffn_kernel), att_a, g_parts)
    att_b = order(sum_pair, here_b, x_swap(here_b))
    att_b = (att_b, core_swap(att_b))
    here_a = order(sum_pair, ffn_a[5], core_swap(ffn_a[6]))
    ffn_b = order(feed(1, fwd_b[0], ffn_a[8], ffn_a[9:11]), att_b, g_parts)
    sec_a = order(sum_pair, here_a, x_swap(here_a))
    sec_a = (sec_a, core_swap(sec_a))
    down_product = order(token_product, [ffn_a[2], ffn_b[2]], [ffn_a[3], ffn_b[3]])
    down_sum = WideSum(down_product, wide_at, wide_count)
    order.advance(down_sum)
    here_b = order(sum_pair, ffn_b[5], core_swap(ffn_b[6]))
    up_product = order(token_product, [ffn_a[1], ffn_b[1]], [ffn_a[4], ffn_b[4]])
    up_sum = WideSum(up_product, wide_at, wide_count)
    order.advance(up_sum)

    def attend_back(pair, fwd, ffn):
        return lambda att, sec: attn_backward(
            scalars, pair, fwd[0], att, sec, ffn[0], mod, fwd[2:5], out_weight, ffn[7]
        )

    def input_back(pair, fwd, taps, before, held):
        return lambda gqkv, gmid, mods: input_backward(
            scalars, pair, fwd[0], mod, gqkv, qkv_all, attn_kernel, taps, gmid, mods, before, slots, held
        )

    back_a = order(attend_back(0, fwd_a, ffn_a), att_a, sec_a)
    sec_b = order(sum_pair, here_b, x_swap(here_b))
    sec_b = (sec_b, core_swap(sec_b))
    order.advance(down_sum)
    back_b = order(attend_back(1, fwd_b, ffn_b), att_b, sec_b)
    order.advance(down_sum)
    attn_product = order(
        lambda grads, grouped, contexts, attended: jnp.concatenate(
            [token_product(grads, grouped), token_product(contexts, attended)], 0
        ),
        [back_a[1], back_b[1]], [fwd_a[1], fwd_b[1]], [fwd_a[5], fwd_b[5]], [back_a[0], back_b[0]],
    )
    levels = wide_count.bit_length() - 1
    attn_sum = WideSum(attn_product, wide_at, wide_count, [0] + list(range(levels - 1, 0, -1)))
    order.advance(attn_sum)
    order.advance(up_sum)
    order.advance(down_sum)
    in_a = order(input_back(0, fwd_a, attn_kernel, attn_kernel, ffn_b[9:11]), *back_a[1:4])
    order.advance(down_sum, up_sum)
    order.advance(attn_sum)
    in_b = order(input_back(1, fwd_b, in_a[0], in_a[1], in_a[2:4]), *back_b[1:4])
    order.advance(down_sum)

    rows = 6 * per_dev
    bits = [1 << k for k in reversed(range(levels))]
    moves = [lambda v, bit=bit: (v, wide_swap(v, bit, wide_count)) for bit in bits]
    join = lambda a, b: jnp.concatenate([a, b], 0)
    whole_rows = lambda a, b, c: join(sum_pair(a, b)[: rows + 9], c[:9].astype(BF))[None]
    mods = Steps(
        (in_b[1], core_swap(in_b[1])),
        [(sum_pair, lambda v: (v, x_swap(v), ffn_b[8]))]
        + [(work, move) for work, move in zip([whole_rows] + [join] * len(bits), moves)],
    )
    order.advance(up_sum)
    order.advance(mods)
    order.advance(attn_sum)
    order.advance(mods)
    order.advance(up_sum)
    while not down_sum.done():
        order.advance(down_sum)
    down_grad = down_sum.finish(order, lambda v: v.astype(F32))
    order.advance(attn_sum, mods)
    order.advance(mods)
    order.advance(up_sum)
    order.advance(attn_sum)
    made = order(functools.partial(slice_halves, x), in_b[2], core_swap(in_b[3]))
    while not all(c.done() for c in (mods, up_sum)):
        order.advance(mods)
        order.advance(up_sum)

    def unpack(held):
        gmod = held[:, :rows].reshape(latent_total, 6 * width)
        taps = jnp.sum(held[:, rows:].astype(F32), 0) * factor
        return gmod, jnp.sum(gmod.astype(F32), 0) * factor, taps[:9], taps[9:]

    gmod, ada_bias_grad, attn_taps, ffn_taps = order(lambda a, b: unpack(join(a, b)), *mods.came)
    while not attn_sum.done():
        order.advance(attn_sum)
    time_in_grad, time_out_grad, ada_weight_grad = order(
        lambda g: condition_back(g, embedded, stages, time_out, ada_weight, factor), gmod
    )
    up_grad = up_sum.finish(order, lambda v: v.astype(F32))
    finals = order(sum_pair, made[0], x_swap(made[1]))
    qkv_rows_grad, out_grad = attn_sum.finish(order, lambda v: (v[: 3 * share].astype(F32), v[3 * share :].astype(F32)))
    qkv_grad = jnp.swapaxes(qkv_rows_grad.reshape(3, share, width), 1, 2)
    final_out = jnp.swapaxes(finals[:per_dev], 1, 2)
    final_grad = jnp.swapaxes(finals[per_dev:], 1, 2)
    return (
        final_out, final_grad, time_in_grad, time_out_grad, ada_weight_grad, ada_bias_grad,
        attn_taps, qkv_grad, out_grad, up_grad, ffn_taps, down_grad,
    )


def solution(mesh):
    tokens = P("wide", None, "narrow")
    weights = (P(None, None, "narrow"), P("narrow", None), P(None, "narrow"), P(None, "narrow"), P("narrow", None))
    return jax.shard_map(
        body,
        mesh=mesh,
        in_specs=(tokens, tokens, P(), P(), P(), P(), P(), P()) + weights,
        out_specs=(tokens, tokens, P(), P(), P(), P(), P()) + weights,
        check_vma=False,
    )
```

```python
import functools
import math

import jax
import jax.numpy as jnp
from jax import lax
from jax.experimental import pallas as pl
from jax.experimental.pallas import tpu as pltpu
from jax.sharding import PartitionSpec as P

HEAD_DIM = 64
FREQ = 256
SIDE = 16
PAIR = 2

BF = jnp.bfloat16
F32 = jnp.float32
HIGHEST = lax.Precision.HIGHEST
LANES = 128
ROWS = 256
BAND = 64
GELU_A = math.sqrt(2.0 / math.pi)
GELU_B = 0.044715
EPS = 1e-06
VMEM_LIMIT = 60 * 1024 * 1024
WEIGHT_ROWS = 256
BACK_ROWS = 128
PACKED = 40


def dot(a, b):
    return lax.dot_general(a, b, (((1,), (0,)), ((), ())), preferred_element_type=F32)


def dot_nt(a, b):
    return lax.dot_general(a, b, (((1,), (1,)), ((), ())), preferred_element_type=F32)


def dot_tn(a, b):
    return lax.dot_general(a, b, (((0,), (0,)), ((), ())), preferred_element_type=F32)


def column_of(rows):
    return lax.broadcasted_iota(jnp.int32, (rows, LANES), 0) % SIDE


def from_left(v):
    moved = pltpu.roll(v, 1, 0)
    return jnp.where(column_of(v.shape[0]) == 0, 0.0, moved)


def from_right(v):
    moved = pltpu.roll(v, v.shape[0] - 1, 0)
    return jnp.where(column_of(v.shape[0]) == SIDE - 1, 0.0, moved)


def conv_band(padded, at, lanes, kern):
    rows = [padded[pl.ds(at + SIDE * r, BAND), lanes] for r in range(3)]
    mixed = [
        rows[0] * kern[c] + rows[1] * kern[3 + c] + rows[2] * kern[6 + c] for c in range(3)
    ]
    return from_left(mixed[0]) + mixed[1] + from_right(mixed[2])


def conv_back_band(padded_grad, at, lanes, kern):
    wide = padded_grad[pl.ds(at, BAND + 2 * SIDE), lanes]
    shifted = [from_right(wide), wide, from_left(wide)]
    total = None
    for r in range(3):
        for c in range(3):
            low = SIDE * (2 - r)
            term = shifted[c][low : low + BAND] * kern[3 * r + c]
            total = term if total is None else total + term
    return total, [s[SIDE : SIDE + BAND] for s in shifted]


def fold_rows(v):
    total = v[0:8]
    for at in range(8, v.shape[0], 8):
        total = total + v[at : at + 8]
    return total


def taps_of(kern_ref, lanes):
    block = kern_ref[:, lanes]
    return [block[t : t + 1] for t in range(9)]


def zero_edges(ref):
    edge = jnp.zeros((SIDE, ref.shape[1]), F32)
    tall = ref.shape[0] // PAIR
    for rel in range(PAIR):
        ref[rel * tall : rel * tall + SIDE, :] = edge
        ref[(rel + 1) * tall - SIDE : (rel + 1) * tall, :] = edge


def inside(ref, rel):
    tall = ref.shape[0] // PAIR
    return slice(rel * tall + SIDE, (rel + 1) * tall - SIDE)


def gather_features(n, parts, held, out):
    _, share, tokens = parts[0].shape
    core = jnp.bitwise_and(n, 1)

    def one(rel):
        for step, part in enumerate(parts):
            held[jnp.bitwise_xor(n, step)] = part[jnp.bitwise_xor(rel, core)]
        out[pl.ds(pl.multiple_of(rel * tokens, tokens), tokens), :] = held[...].reshape(len(parts) * share, tokens).T

    pair_loop(one)


def by_core(core, low, share, keep_out, send_out, turned):
    tokens = low.shape[0] // PAIR

    def one(rel):
        lat = jnp.bitwise_xor(rel, core)
        turned[...] = low[pl.ds(pl.multiple_of(rel * tokens, tokens), tokens), :].T
        for x in range(2):
            here = pl.ds(pl.multiple_of((2 * x + core) * share, 16), share)
            there = pl.ds(pl.multiple_of((2 * x + 1 - core) * share, 16), share)
            keep_out[x, lat] = turned[here, :]
            send_out[x, lat] = turned[there, :]

    pair_loop(one)


def norm_stats(v):
    width = v.shape[1]
    mean = jnp.sum(v, -1, keepdims=True) * (1.0 / width)
    center = v - mean
    spread = jnp.sum(center * center, -1, keepdims=True) * (1.0 / width)
    scale = lax.rsqrt(spread + EPS)
    return center * scale, scale


def head_masks(share):
    lane = lax.broadcasted_iota(jnp.int32, (1, share), 1) // HEAD_DIM
    return [(lane == h).astype(F32).astype(BF) for h in range(share // HEAD_DIM)]


def half_rows(v, parity):
    tokens, width = v.shape
    split = v.reshape(tokens // (2 * SIDE), 2, SIDE, width)
    return split[:, parity].reshape(tokens // 2, width)


def join_rows(even, odd):
    half, width = even.shape
    both = jnp.stack([even.reshape(half // SIDE, SIDE, width), odd.reshape(half // SIDE, SIDE, width)], 1)
    return both.reshape(2 * half, width)


def softmax_rows(queries, keys):
    scores = dot_nt(queries, keys) * (1.0 / math.sqrt(HEAD_DIM))
    rows = lax.broadcasted_iota(jnp.int32, scores.shape, 0)
    cols = lax.broadcasted_iota(jnp.int32, scores.shape, 1)
    same = (rows + cols) % 2 == 0
    scores = jnp.where(same, scores, -1e30)
    top = jnp.max(scores, -1, keepdims=True)
    grown = jnp.where(same, jnp.exp(scores - top), 0.0)
    return grown / jnp.sum(grown, -1, keepdims=True)


def beside(stacked, heads):
    rows = stacked.shape[0] // heads
    return jnp.concatenate([stacked[h * rows : (h + 1) * rows] for h in range(heads)], axis=1)


def lane_loop(width, body):
    count = width // LANES

    def step(j, carry):
        body(j // count, pl.ds(pl.multiple_of((j % count) * LANES, LANES), LANES))
        return carry

    lax.fori_loop(0, PAIR * count, step, 0)


def row_loop_each(tokens, body):
    for rel in range(PAIR):

        def step(j, carry):
            body(rel, pl.multiple_of(rel * tokens + j * ROWS, ROWS))
            return carry

        lax.fori_loop(0, tokens // ROWS, step, 0)


def row_loop(tokens, body):
    count = tokens // ROWS

    def step(j, carry):
        body(j // count, pl.multiple_of(j * ROWS, ROWS))
        return carry

    lax.fori_loop(0, PAIR * count, step, 0)


def pair_loop(body):
    def step(j, carry):
        body(j)
        return carry

    lax.fori_loop(0, PAIR, step, 0)


def attn_kernel_body(
    flow, s_ref, xo, xc, xx, xd, mod, kern, wqkv, wout,
    full_out, grouped_out, q_out, k_out, v_out, ctx_out, keep_out, send_out,
    held, padded,
):
    n = s_ref[0]
    core = jnp.bitwise_and(n, 1)
    share, tokens = xo.shape[1], xo.shape[2]
    width = full_out.shape[1]
    tall = tokens + 2 * SIDE
    zero_edges(padded)
    flow.need(xo, xc, xx, xd, mod, kern)
    gather_features(n, (xo, xc, xx, xd), held, full_out)
    flow.sent(full_out)

    def rows(rel, at):
        lat = jnp.bitwise_xor(rel, core)
        normed, _ = norm_stats(full_out[pl.ds(at, ROWS), :].astype(F32))
        here = pl.ds(pl.multiple_of(at + (2 * rel + 1) * SIDE, SIDE), ROWS)
        padded[here, :] = normed * (1.0 + mod[lat, 1:2, :]) + mod[lat, 0:1, :]

    row_loop(tokens, rows)

    def lanes(rel, at):
        taps = taps_of(kern, at)
        for band in range(0, tokens, BAND):
            here = pl.ds(pl.multiple_of(rel * tokens + band, BAND), BAND)
            grouped_out[here, at] = conv_band(padded, pl.multiple_of(rel * tall + band, SIDE), at, taps).astype(BF)

    lane_loop(width, lanes)
    flow.sent(grouped_out)
    flow.need(wqkv, wout)
    grouped = grouped_out[...]
    q_out[...] = dot_nt(grouped, wqkv[0]).astype(BF)
    k_out[...] = dot_nt(grouped, wqkv[1]).astype(BF)
    v_out[...] = dot_nt(grouped, wqkv[2]).astype(BF)
    flow.sent(q_out, k_out, v_out)
    masks = head_masks(share)
    heads = len(masks)

    def attend(rel):
        here = pl.ds(pl.multiple_of(rel * tokens, tokens), tokens)
        query, key, value = q_out[here, :], k_out[here, :], v_out[here, :]
        parts = []
        for parity in range(2):
            q = half_rows(query, parity)
            k = half_rows(key, parity)
            v = half_rows(value, parity)
            probs = softmax_rows(jnp.concatenate([q * m for m in masks], axis=0), k)
            low = beside(probs.astype(BF), heads)
            parts.append(dot(low, jnp.concatenate([v * m for m in masks], axis=0)).astype(BF))
        ctx_out[here, :] = join_rows(*parts)

    pair_loop(attend)
    flow.sent(ctx_out)
    send_out[...] = dot(ctx_out[tokens : 2 * tokens, :], wout[...]).astype(BF)
    flow.sent(send_out)
    keep_out[...] = dot(ctx_out[0:tokens, :], wout[...]).astype(BF)
    flow.sent(keep_out)


def ffn_kernel_body(
    first, flow, s_ref, go, gc, gx, gd, full, att, mod, up, down, kern, kgrad_in,
    g_out, second_out, active_out, gfed_out, ghid_out, keep_out, send_out, mods_out, kgrad_out, fkeep_out, fsend_out,
    held, padded, slope, gpad, mid, fed, low, sums, turned,
):
    n = s_ref[0]
    core = jnp.bitwise_and(n, 1)
    share, tokens = go.shape[1], go.shape[2]
    units = up.shape[1]
    tall = tokens + 2 * SIDE
    zero_edges(padded)
    zero_edges(gpad)
    flow.need(go, gc, gx, gd)
    gather_features(n, (go, gc, gx, gd), held, g_out)
    flow.sent(g_out)
    flow.need(full, att, mod, kgrad_in)
    kgrad_out[...] = jnp.zeros(kgrad_out.shape, F32) if first else kgrad_in[...]

    def rows(rel, at):
        lat = jnp.bitwise_xor(rel, core)
        here = pl.ds(at, ROWS)
        middle = full[here, :].astype(F32) + mod[lat, 2:3, :] * att[here, :].astype(F32)
        mid[here, :] = middle
        normed, _ = norm_stats(middle)
        second_out[here, :] = (normed * (1.0 + mod[lat, 4:5, :]) + mod[lat, 3:4, :]).astype(BF)
        gfed_out[here, :] = (mod[lat, 5:6, :] * g_out[here, :].astype(F32)).astype(BF)

    row_loop_each(tokens, rows)
    flow.sent(second_out, gfed_out)
    flow.need(up, kern)
    hidden = dot(second_out[...], up[...])
    for rel in range(PAIR):
        padded[inside(padded, rel), :] = hidden[rel * tokens : (rel + 1) * tokens]

    def lanes(rel, at):
        taps = taps_of(kern, at)
        for band in range(0, tokens, BAND):
            here = pl.ds(pl.multiple_of(rel * tokens + band, BAND), BAND)
            mixed = conv_band(padded, pl.multiple_of(rel * tall + band, SIDE), at, taps)
            square = mixed * mixed
            curve = jnp.tanh(GELU_A * mixed * (1.0 + GELU_B * square))
            half = 0.5 * (1.0 + curve)
            active_out[here, at] = (mixed * half).astype(BF)
            slope[here, at] = half + (0.5 * GELU_A) * mixed * (1.0 - curve * curve) * (
                1.0 + (3.0 * GELU_B) * square
            )

    lane_loop(units, lanes)
    flow.sent(active_out)
    flow.need(down)
    fed[...] = dot(active_out[...], down[...])
    sums[...] = jnp.zeros(sums.shape, F32)

    def rows_fed(rel, at):
        lat = jnp.bitwise_xor(rel, core)
        here = pl.ds(at, ROWS)
        term = fed[here, :]
        sums[lat] += fold_rows(term * g_out[here, :].astype(F32))
        low[here, :] = (mod[lat, 5:6, :] * term + 0.25 * mid[here, :]).astype(BF)

    row_loop_each(tokens, rows_fed)
    for lat in range(PAIR):
        mods_out[lat] = jnp.sum(sums[lat], 0, keepdims=True)
    by_core(core, low, share, fkeep_out, fsend_out, turned)
    flow.sent(fkeep_out, fsend_out, mods_out)
    gact = dot_nt(gfed_out[...], down[...]).astype(BF).astype(F32)
    for rel in range(PAIR):
        here = slice(rel * tokens, (rel + 1) * tokens)
        gpad[inside(gpad, rel), :] = gact[here] * slope[here, :]

    def lanes_back(rel, at):
        taps = taps_of(kern, at)
        sums = [None] * 9
        for band in range(0, tokens, BAND):
            here = pl.ds(pl.multiple_of(rel * tokens + band, BAND), BAND)
            base = pl.multiple_of(rel * tall + band, SIDE)
            total, shifted = conv_back_band(gpad, base, at, taps)
            ghid_out[here, at] = total.astype(BF)
            for r in range(3):
                values = padded[pl.ds(base + SIDE * r, BAND), at]
                for c in range(3):
                    part = fold_rows(values * shifted[c])
                    sums[3 * r + c] = part if sums[3 * r + c] is None else sums[3 * r + c] + part
        for t in range(9):
            kgrad_out[t : t + 1, at] += jnp.sum(sums[t], 0, keepdims=True)

    lane_loop(units, lanes_back)
    flow.sent(ghid_out, kgrad_out)
    send_out[...] = dot_nt(ghid_out[tokens : 2 * tokens, :], up[...]).astype(BF)
    flow.sent(send_out)
    keep_out[...] = dot_nt(ghid_out[0:tokens, :], up[...]).astype(BF)
    flow.sent(keep_out)


def attn_back_body(
    flow, s_ref, full, att, gs, gfull, mod, q_in, k_in, v_in, wout, gates,
    gatt_out, gqkv_out, gmid_out, mods_out,
    sums, gctx,
):
    core = jnp.bitwise_and(s_ref[0], 1)
    tokens = full.shape[0] // PAIR
    width = full.shape[1]
    share = q_in.shape[1]
    mods_out[...] = jnp.zeros(mods_out.shape, F32)
    sums[...] = jnp.zeros(sums.shape, F32)
    flow.need(full, att, gs, gfull, mod)

    def rows(rel, at):
        lat = jnp.bitwise_xor(rel, core)
        here = pl.ds(at, ROWS)
        gate1 = mod[lat, 2:3, :]
        attended = att[here, :].astype(F32)
        normed, inv = norm_stats(full[here, :].astype(F32) + gate1 * attended)
        grad = gs[here, :].astype(F32)
        inner = grad * (1.0 + mod[lat, 4:5, :])
        mean_a = jnp.sum(inner, -1, keepdims=True) * (1.0 / width)
        mean_b = jnp.sum(inner * normed, -1, keepdims=True) * (1.0 / width)
        whole_grad = gfull[here, :].astype(F32) + inv * (inner - mean_a - normed * mean_b)
        gmid_out[here, :] = whole_grad.astype(BF)
        gatt_out[here, :] = (gate1 * whole_grad).astype(BF)
        sums[3 * lat] += fold_rows(attended * whole_grad)
        sums[3 * lat + 1] += fold_rows(grad)
        sums[3 * lat + 2] += fold_rows(grad * normed)

    row_loop(tokens, rows)
    for lat in range(PAIR):
        for k in range(3):
            mods_out[lat, 2 + k : 3 + k, :] = 0.25 * jnp.sum(sums[3 * lat + k], 0, keepdims=True)
    flow.need(wout, q_in, k_in, v_in, gates)
    for lat in range(PAIR):
        mods_out[lat, 5:6, :] = gates[lat]
    flow.sent(gatt_out, gmid_out, mods_out)
    gctx[...] = dot_nt(gatt_out[...], wout[...]).astype(BF)
    masks = head_masks(share)
    heads = len(masks)
    factor = 1.0 / math.sqrt(HEAD_DIM)

    def attend(rel):
        here = pl.ds(pl.multiple_of(rel * tokens, tokens), tokens)
        query, key, value, grads = q_in[here, :], k_in[here, :], v_in[here, :], gctx[here, :]
        parts_q, parts_k, parts_v = [], [], []
        for parity in range(2):
            q = half_rows(query, parity)
            k = half_rows(key, parity)
            v = half_rows(value, parity)
            gc = half_rows(grads, parity)
            q_all = jnp.concatenate([q * m for m in masks], axis=0)
            k_all = jnp.concatenate([k * m for m in masks], axis=0)
            gc_all = jnp.concatenate([gc * m for m in masks], axis=0)
            probs = softmax_rows(q_all, k)
            parts_v.append(dot_tn(probs.astype(BF), gc_all).astype(BF))
            gprobs = dot_nt(gc_all, v).astype(BF).astype(F32)
            gscores = (probs * (gprobs - jnp.sum(probs * gprobs, -1, keepdims=True))).astype(BF)
            parts_q.append((dot(beside(gscores, heads), k_all) * factor).astype(BF))
            parts_k.append((dot_tn(gscores, q_all) * factor).astype(BF))
        for k, parts in enumerate((parts_q, parts_k, parts_v)):
            gqkv_out[here, k * share : (k + 1) * share] = join_rows(*parts)

    pair_loop(attend)
    flow.sent(gqkv_out)


def input_back_body(
    closing, flow, s_ref, full, mod, gqkv, wqkv, kern, kgrad_in, gmid, mods_in, before,
    kgrad_out, mods_out, keep_out, send_out,
    normed1, scale1, first, gpad, gback, low, mods, rows_out, turned,
):
    core = jnp.bitwise_and(s_ref[0], 1)
    tokens = full.shape[0] // PAIR
    width = full.shape[1]
    share = gqkv.shape[1] // 3
    tall = tokens + 2 * SIDE
    zero_edges(first)
    zero_edges(gpad)
    flow.need(full, mod)

    def rows_first(rel, at):
        lat = jnp.bitwise_xor(rel, core)
        here = pl.ds(at, ROWS)
        normed, inv = norm_stats(full[here, :].astype(F32))
        normed1[here, :] = normed
        scale1[here, :] = jnp.broadcast_to(inv, (ROWS, LANES))
        inside_rows = pl.ds(pl.multiple_of(at + (2 * rel + 1) * SIDE, SIDE), ROWS)
        first[inside_rows, :] = normed * (1.0 + mod[lat, 1:2, :]) + mod[lat, 0:1, :]

    row_loop(tokens, rows_first)
    flow.need(gqkv, wqkv, kern, kgrad_in, gmid, mods_in, before)
    kgrad_out[...] = kgrad_in[...] if closing else jnp.zeros(kgrad_out.shape, F32)
    mods[...] = mods_in[...]
    for rel in range(PAIR):
        here = slice(rel * tokens, (rel + 1) * tokens)
        gpad[inside(gpad, rel), :] = dot(gqkv[here, :], wqkv[...])

    def lanes(rel, at):
        taps = taps_of(kern, at)
        sums = [None] * 9
        shift_sum, scale_sum = None, None
        for band in range(0, tokens, BAND):
            here = pl.ds(pl.multiple_of(rel * tokens + band, BAND), BAND)
            base = pl.multiple_of(rel * tall + band, SIDE)
            total, shifted = conv_back_band(gpad, base, at, taps)
            gback[here, at] = total
            part_a, part_b = fold_rows(total), fold_rows(total * normed1[here, at])
            shift_sum = part_a if shift_sum is None else shift_sum + part_a
            scale_sum = part_b if scale_sum is None else scale_sum + part_b
            for r in range(3):
                values = first[pl.ds(base + SIDE * r, BAND), at]
                for c in range(3):
                    part = fold_rows(values * shifted[c])
                    sums[3 * r + c] = part if sums[3 * r + c] is None else sums[3 * r + c] + part
        for t in range(9):
            kgrad_out[t : t + 1, at] += jnp.sum(sums[t], 0, keepdims=True)
        lat = jnp.bitwise_xor(rel, core)
        mods[lat, 0:1, at] = jnp.sum(shift_sum, 0, keepdims=True)
        mods[lat, 1:2, at] = jnp.sum(scale_sum, 0, keepdims=True)

    lane_loop(width, lanes)
    if closing:
        rows_out[...] = jnp.zeros(rows_out.shape, F32)
        for lat in range(PAIR):
            rows_out[6 * lat : 6 * lat + 6, :] = before[lat, 0:6, :]
            rows_out[6 * (PAIR + lat) : 6 * (PAIR + lat) + 6, :] = mods[lat, 0:6, :]
        rows_out[12 * PAIR : 12 * PAIR + 9, :] = kgrad_out[0:9, :]
        mods_out[...] = rows_out[...].astype(BF)
    else:
        mods_out[...] = mods[...]
    flow.sent(mods_out, kgrad_out)

    def rows_back(rel, at):
        lat = jnp.bitwise_xor(rel, core)
        here = pl.ds(at, ROWS)
        inner = gback[here, :] * (1.0 + mod[lat, 1:2, :])
        normed = normed1[here, :]
        mean_a = jnp.sum(inner, -1, keepdims=True) * (1.0 / width)
        mean_b = jnp.sum(inner * normed, -1, keepdims=True) * (1.0 / width)
        grad = scale1[here, 0:1] * (inner - mean_a - normed * mean_b)
        low[here, :] = (grad + 0.25 * gmid[here, :].astype(F32)).astype(BF)

    row_loop(tokens, rows_back)
    by_core(core, low, share, keep_out, send_out, turned)
    flow.sent(keep_out, send_out)


class Flow:
    def __init__(self, arrivals, departures):
        self.arrivals, self.departures = arrivals, departures
        self.leaving = []
        for _, copy in arrivals:
            copy.start()

    def need(self, *refs):
        for ref in refs:
            for _, copy in [a for a in self.arrivals if a[0] is ref]:
                copy.wait()
            self.arrivals = [a for a in self.arrivals if a[0] is not ref]

    def sent(self, *refs):
        for ref in refs:
            for held, copy in self.departures:
                if held is ref:
                    copy.start()
                    self.leaving.append(copy)

    def end(self):
        for copy in self.leaving:
            copy.wait()


def call(body, name, scalars, ins, outs, scratch, flops, held=()):
    n_in, n_out = len(ins), len(outs)
    places, buffer_shapes = [], []
    for array, window, into in ins:
        dims = array.shape if window is None else (PAIR,) + array.shape[1:]
        if into is None:
            buffer_shapes.append((dims, array.dtype))
        elif into[0].start == 0:
            buffer_shapes.append(((PAIR * dims[0],) + dims[1:], array.dtype))
        places.append(len(buffer_shapes) - 1)

    def run(s_ref, *refs):
        sources = refs[:n_in]
        targets = refs[n_in + len(held) : n_in + len(held) + n_out]
        buffers = refs[n_in + len(held) + n_out : -1]
        sems = refs[-1]
        n_held = len(buffer_shapes)
        buffers_in, buffers_out = buffers[:n_held], buffers[n_held : n_held + n_out]
        rest = buffers[n_held + n_out :]
        arrivals, departures = [], []
        for k, (source, (_, window, into)) in enumerate(zip(sources, ins)):
            view = source if window is None else source.at[window]
            buffer = buffers_in[places[k]]
            target = buffer if into is None else buffer.at[into]
            arrivals.append((buffer, pltpu.make_async_copy(view, target, sems.at[k])))
        for k, (target, buffer, out) in enumerate(zip(targets, buffers_out, outs)):
            view = target if out[2] is None else target.at[out[2]]
            departures.append((buffer, pltpu.make_async_copy(buffer, view, sems.at[n_in + k])))
        flow = Flow(arrivals, departures)
        body(flow, s_ref, *buffers_in, *buffers_out, *rest)
        flow.end()

    anywhere = pl.BlockSpec(memory_space=pl.ANY)
    return pl.pallas_call(
        run,
        name=name,
        out_shape=[jax.ShapeDtypeStruct(o[0], o[1]) for o in outs],
        grid_spec=pltpu.PrefetchScalarGridSpec(
            num_scalar_prefetch=1,
            grid=(1,),
            in_specs=[anywhere] * (n_in + len(held)),
            out_specs=[anywhere] * n_out,
            scratch_shapes=[pltpu.VMEM(dims, dtype) for dims, dtype in buffer_shapes]
            + [pltpu.VMEM(o[3], o[1]) for o in outs]
            + scratch
            + [pltpu.SemaphoreType.DMA((n_in + n_out,))],
        ),
        input_output_aliases={1 + n_in + k: n_out - len(held) + k for k in range(len(held))},
        compiler_params=pltpu.CompilerParams(vmem_limit_bytes=VMEM_LIMIT),
        cost_estimate=pl.CostEstimate(flops=flops, bytes_accessed=10**6, transcendentals=0),
    )(scalars, *[i[0] for i in ins], *held)


def slices_out(slots, slot, share, tokens):
    return ((2, slots, share, tokens), BF, (slice(None), pl.ds(PAIR * slot, PAIR)), (2, PAIR, share, tokens))


def whole(array):
    return (array, None, None)


def stacked(arrays):
    rows = arrays[0].shape[0]
    return [(v, None, (pl.ds(k * rows, rows),)) for k, v in enumerate(arrays)]


def whole_out(dims, dtype):
    return (dims, dtype, None, dims)


def pair_of(array, pair):
    return (array, (pl.ds(PAIR * pair, PAIR),), None)


def split_low(v):
    high = v.astype(BF)
    return high, (v - high.astype(F32)).astype(BF)


def rows_product(a, b):
    (ah, al), (bh, bl) = split_low(a), split_low(b)
    return dot_tn(jnp.concatenate([ah, al, ah], 0), jnp.concatenate([bh, bh, bl], 0))


def back_product(a, weight):
    (ah, al), (wh, wl) = split_low(a), split_low(weight)
    return dot_nt(ah, wh) + dot_nt(al, wh) + dot_nt(ah, wl)


def product(a, weight):
    (ah, al), (wh, wl) = split_low(a), split_low(weight)
    return dot(ah, wh) + dot(al, wh) + dot(ah, wl)


def silu(v):
    return v / (1.0 + jnp.exp(-v))


def silu_slope(v):
    gate = 1.0 / (1.0 + jnp.exp(-v))
    return gate * (1.0 + v * (1.0 - gate))


def row_blocks(source, target, sems, rows):
    return [
        pltpu.make_async_copy(source.at[pl.ds(at, rows)], target.at[pl.ds(at, rows)], sems.at[at // rows])
        for at in range(0, source.shape[0], rows)
    ]


def condition_body(
    embedded, bias, time_in, time_out, ada, mod_out, inner_pre, inner, outer_pre, outer, held_in, held_out, held, sums, parts, sems,
):
    depth = ada.shape[0]
    per_dev, count, width = mod_out.shape
    first = pltpu.make_async_copy(time_in, held_in, sems.at[0])
    second = pltpu.make_async_copy(time_out, held_out, sems.at[1])
    blocks = row_blocks(ada, held, sems.at[pl.ds(2, depth // WEIGHT_ROWS)], WEIGHT_ROWS)
    for copy in [first, second] + blocks:
        copy.start()
    first.wait()
    inner_pre[...] = product(embedded[...], held_in[...])
    inner[...] = silu(inner_pre[...])
    second.wait()
    outer_pre[...] = product(inner[...], held_out[...])
    outer[...] = silu(outer_pre[...])
    wide_bias = [jnp.concatenate([bias[k + j : k + j + 1, :] for j in range(width // LANES)], 1)
                 for k in range(0, bias.shape[0], width // LANES)]
    total = jnp.concatenate(wide_bias, 1)
    sums[...] = jnp.broadcast_to(total, sums.shape)
    for k in range(depth // WEIGHT_ROWS):
        parts[k] = outer[0:8, k * WEIGHT_ROWS : (k + 1) * WEIGHT_ROWS]

    def add(k, carry):
        rows = pl.ds(pl.multiple_of(k * WEIGHT_ROWS, WEIGHT_ROWS), WEIGHT_ROWS)
        pltpu.make_async_copy(ada.at[rows], held.at[rows], sems.at[2 + k]).wait()
        sums[...] += product(parts[k], held[rows, :])
        return carry

    lax.fori_loop(0, depth // WEIGHT_ROWS, add, 0)
    total = sums[...]
    for lat in range(per_dev):
        for k in range(count):
            mod_out[lat, k : k + 1, :] = total[lat : lat + 1, k * width : (k + 1) * width]


def condition(embedded, time_in, time_out, ada_weight, ada_bias, per_dev, width):
    latent_total = embedded.shape[0]
    depth, columns = ada_weight.shape
    vmem = pl.BlockSpec(memory_space=pltpu.VMEM)
    anywhere = pl.BlockSpec(memory_space=pl.ANY)
    rows = jax.ShapeDtypeStruct((latent_total, depth), F32)
    return pl.pallas_call(
        condition_body,
        name="condition",
        in_specs=[vmem, vmem, anywhere, anywhere, anywhere],
        out_specs=[vmem] * 5,
        out_shape=[jax.ShapeDtypeStruct((per_dev, columns // width, width), F32), rows, rows, rows, rows],
        scratch_shapes=[
            pltpu.VMEM(time_in.shape, F32),
            pltpu.VMEM(time_out.shape, F32),
            pltpu.VMEM(ada_weight.shape, F32),
            pltpu.VMEM((8, columns), F32),
            pltpu.VMEM((depth // WEIGHT_ROWS, 8, WEIGHT_ROWS), F32),
            pltpu.SemaphoreType.DMA((2 + depth // WEIGHT_ROWS,)),
        ],
        compiler_params=pltpu.CompilerParams(vmem_limit_bytes=VMEM_LIMIT),
        cost_estimate=pl.CostEstimate(flops=8 * 10**9, bytes_accessed=10**6, transcendentals=0),
    )(embedded, ada_bias.reshape(columns // LANES, LANES), time_in, time_out, ada_weight)


def condition_back_body(
    factor, gmod, embedded, inner_pre, inner, outer_pre, outer, time_out, ada,
    time_in_grad, time_out_grad, ada_grad, held_out, held, outer_grad, columns, sems, arriving, leaving,
):
    count = ada.shape[0] // BACK_ROWS

    def block_copy(source, target, sem, k):
        rows = pl.ds(k * BACK_ROWS, BACK_ROWS)
        return pltpu.make_async_copy(source.at[rows], target.at[rows], sem.at[k])

    first = pltpu.make_async_copy(time_out, held_out, sems.at[0])
    for k in range(count):
        block_copy(ada, held, arriving, k).start()
    first.start()
    high, low = split_low(outer[...])
    both = jnp.concatenate([high, low], 0)
    for k in range(count):
        columns[k] = both[:, k * BACK_ROWS : (k + 1) * BACK_ROWS]

    def block(k, carry):
        rows = pl.ds(pl.multiple_of(k * BACK_ROWS, BACK_ROWS), BACK_ROWS)
        block_copy(ada, held, arriving, k).wait()
        grads = gmod[...]
        high, low = split_low(held[rows, :])
        outer_grad[rows, :] = dot_nt(high, grads) + dot_nt(low, grads)
        held[rows, :] = dot_tn(columns[k], jnp.concatenate([grads, grads], 0)) * factor
        block_copy(held, ada_grad, leaving, k).start()
        return carry

    lax.fori_loop(0, count, block, 0)
    first.wait()
    back = outer_grad[...].T * factor * silu_slope(outer_pre[...])
    time_out_grad[...] = rows_product(inner[...], back)
    back = back_product(back, held_out[...]) * silu_slope(inner_pre[...])
    time_in_grad[...] = rows_product(embedded[...], back)
    for k in range(count):
        block_copy(held, ada_grad, leaving, k).wait()


def condition_back(gmod, embedded, stages, time_out, ada_weight, factor):
    depth = ada_weight.shape[0]
    latent_total = gmod.shape[0]
    vmem = pl.BlockSpec(memory_space=pltpu.VMEM)
    anywhere = pl.BlockSpec(memory_space=pl.ANY)
    time_in_dims = (embedded.shape[1], time_out.shape[0])
    return pl.pallas_call(
        functools.partial(condition_back_body, factor),
        name="condition_back",
        in_specs=[vmem] * 6 + [anywhere] * 2,
        out_specs=[vmem, vmem, anywhere],
        out_shape=[
            jax.ShapeDtypeStruct(time_in_dims, F32),
            jax.ShapeDtypeStruct(time_out.shape, F32),
            jax.ShapeDtypeStruct(ada_weight.shape, F32),
        ],
        scratch_shapes=[
            pltpu.VMEM(time_out.shape, F32),
            pltpu.VMEM(ada_weight.shape, F32),
            pltpu.VMEM((depth, latent_total), F32),
            pltpu.VMEM((depth // BACK_ROWS, 2 * latent_total, BACK_ROWS), BF),
            pltpu.SemaphoreType.DMA((1,)),
            pltpu.SemaphoreType.DMA((depth // BACK_ROWS,)),
            pltpu.SemaphoreType.DMA((depth // BACK_ROWS,)),
        ],
        compiler_params=pltpu.CompilerParams(vmem_limit_bytes=VMEM_LIMIT),
        cost_estimate=pl.CostEstimate(flops=1, bytes_accessed=1, transcendentals=0),
    )(gmod, embedded, *stages, time_out, ada_weight)


def attn_forward(scalars, pair, x_parts, mod, attn_kernel, qkv_weight, out_weight):
    _, share, tokens = x_parts[0].shape
    width = out_weight.shape[1]
    rows = PAIR * tokens
    thin = whole_out((rows, share), BF)
    half = whole_out((tokens, width), BF)
    return call(
        attn_kernel_body, "attn_fwd", scalars,
        [pair_of(v, pair) for v in x_parts] + [pair_of(mod, pair), whole(attn_kernel), whole(qkv_weight), whole(out_weight)],
        [whole_out((rows, width), BF), whole_out((rows, width), BF), thin, thin, thin, thin, half, half],
        [pltpu.VMEM((4, share, tokens), BF), pltpu.VMEM((PAIR * (tokens + 2 * SIDE), width), F32)],
        6_000_000_000,
    )


def feed_forward(scalars, pair, full, att, g_parts, mod, up_weight, down_weight, ffn_kernel, slots, taps, held):
    _, share, tokens = g_parts[0].shape
    width, units = up_weight.shape
    rows = PAIR * tokens
    tall = PAIR * (tokens + 2 * SIDE)
    broad = whole_out((rows, width), BF)
    hidden = whole_out((rows, units), BF)
    half = whole_out((tokens, width), BF)
    slices = slices_out(slots, pair, share, tokens)
    return call(
        functools.partial(ffn_kernel_body, pair == 0), "ffn", scalars,
        [pair_of(v, pair) for v in g_parts] + [whole(full)] + stacked(att)
        + [pair_of(mod, pair), whole(up_weight), whole(down_weight), whole(ffn_kernel), whole(taps)],
        [broad, broad, hidden, broad, hidden, half, half, whole_out((PAIR, 1, width), F32), whole_out((16, units), F32),
         slices, slices],
        [pltpu.VMEM((4, share, tokens), BF), pltpu.VMEM((tall, units), F32), pltpu.VMEM((rows, units), F32),
         pltpu.VMEM((tall, units), F32), pltpu.VMEM((rows, width), F32), pltpu.VMEM((rows, width), F32),
         pltpu.VMEM((rows, width), BF), pltpu.VMEM((PAIR, 8, width), F32), pltpu.VMEM((width, tokens), BF)],
        10_000_000_000, held,
    )


def attn_backward(scalars, pair, full, att, gsec, gfull, mod, qkv, out_weight, gates):
    tokens, width = att[0].shape
    share = out_weight.shape[0]
    rows = PAIR * tokens
    broad = whole_out((rows, width), BF)
    return call(
        attn_back_body, "attn_bwd", scalars,
        [whole(full)] + stacked(att) + stacked(gsec) + [whole(gfull), pair_of(mod, pair)]
        + [whole(v) for v in qkv] + [whole(out_weight), whole(gates)],
        [broad, whole_out((rows, 3 * share), BF), broad, whole_out((PAIR, 8, width), F32)],
        [pltpu.VMEM((3 * PAIR, 8, width), F32), pltpu.VMEM((rows, share), BF)],
        6_000_000_000,
    )


def input_backward(scalars, pair, full, mod, gqkv, qkv_weight, attn_kernel, taps, gmid, mods_in, before, slots, held):
    rows, width = full.shape
    tokens = rows // PAIR
    share = gqkv.shape[1] // 3
    tall = PAIR * (tokens + 2 * SIDE)
    slices = slices_out(slots, slots // PAIR // 2 + pair, share, tokens)
    closing = pair > 0
    mods = whole_out((PACKED, width), BF) if closing else whole_out((PAIR, 8, width), F32)
    return call(
        functools.partial(input_back_body, closing), "input_bwd", scalars,
        [whole(full), pair_of(mod, pair), whole(gqkv), whole(qkv_weight), whole(attn_kernel), whole(taps), whole(gmid),
         whole(mods_in), whole(before)],
        [whole_out((16, width), F32), mods, slices, slices],
        [pltpu.VMEM((rows, width), F32), pltpu.VMEM((rows, LANES), F32), pltpu.VMEM((tall, width), F32),
         pltpu.VMEM((tall, width), F32), pltpu.VMEM((rows, width), F32), pltpu.VMEM((rows, width), BF),
         pltpu.VMEM((PAIR, 8, width), F32), pltpu.VMEM((PACKED, width), F32), pltpu.VMEM((width, tokens), BF)],
        6_000_000_000, held,
    )


def core_swap(v):
    return lax.ppermute(v, "narrow", [(0, 1), (1, 0), (2, 3), (3, 2)])


def x_swap(v):
    return lax.ppermute(v, "narrow", [(0, 2), (2, 0), (1, 3), (3, 1)])


def sum_pair(a, b):
    return (a.astype(F32) + b.astype(F32)).astype(BF)


def slice_halves(x, keep, arrived):
    both = sum_pair(keep, arrived)
    return (
        lax.dynamic_index_in_dim(both, x, 0, keepdims=False),
        lax.dynamic_index_in_dim(both, 1 - x, 0, keepdims=False),
    )


def wide_swap(v, bit, count):
    return lax.ppermute(v, "wide", [(i, i ^ bit) for i in range(count)])


def pick(v, parts, at):
    rows = v.shape[0] // parts
    return lax.dynamic_slice_in_dim(v, at * rows, rows, 0)


def in_place(bit, own, came, axis):
    dims = own.shape[:axis] + (2,) + own.shape[axis + 1 :]
    return jnp.where(lax.broadcasted_iota(jnp.int32, dims, axis) == bit, own, came)


class WideSum:
    def __init__(self, product, at, count, back=None):
        self.count, self.dims = count, product.shape
        self.levels = count.bit_length() - 1
        self.bits = [at // (1 << k) % 2 for k in range(self.levels)]
        self.ahead = list(range(self.levels))
        self.back = list(reversed(self.ahead)) if back is None else back
        self.opened = False
        self.held = product

    def swap(self, sent, level):
        self.came = wide_swap(sent, 1 << level, self.count)

    def halve(self, held, came):
        level = self.ahead[0]
        if level == 0:
            held = pick(held, 2, self.bits[0])
        if len(self.ahead) == 1:
            return (sum_pair(held, came),)
        bit = self.bits[level + 1]
        return tuple(sum_pair(pick(held, 2, at), pick(came, 2, at)) for at in (1 - bit, bit))

    def pending(self):
        if not self.opened:
            return lambda v: pick(v, 2, 1 - self.bits[0]), (self.held,)
        if self.ahead:
            return self.halve, (self.held, self.came)
        level = self.back[0]
        return lambda a, b: in_place(self.bits[level], a, b, level), (self.held, self.came)

    def accept(self, out):
        if not self.opened:
            self.opened = True
            self.swap(out, 0)
        elif self.ahead:
            self.ahead.pop(0)
            self.held = out[-1]
            if self.ahead:
                self.swap(out[0], self.ahead[0])
            else:
                self.held = self.held.reshape((1,) * self.levels + self.held.shape)
                self.swap(self.held, self.back[0])
        else:
            self.back.pop(0)
            self.held = out
            self.swap(out, self.back[0])

    def done(self):
        return self.opened and not self.ahead and len(self.back) == 1

    def finish(self, order, shape=lambda v: v):
        level = self.back[0]
        return order(
            lambda a, b: shape(in_place(self.bits[level], a, b, level).reshape(self.dims)), self.held, self.came
        )


class Steps:
    def __init__(self, came, steps):
        self.came, self.steps = came, list(steps)

    def pending(self):
        return self.steps[0][0], self.came

    def accept(self, out):
        _, move = self.steps.pop(0)
        self.came = move(out)

    def done(self):
        return not self.steps


class Order:
    def __init__(self):
        self.last = ()

    def __call__(self, step, *inputs):
        inputs, _ = lax.optimization_barrier((inputs, self.last))
        out = step(*inputs)
        self.last = tuple(jax.tree.leaves(out)[:1])
        return out

    def advance(self, *chains):
        chains = [c for c in chains if not c.done()]
        if chains:
            work = [c.pending() for c in chains]
            outs = self(lambda *v: [w[0](*a) for w, a in zip(work, v)], *[w[1] for w in work])
            self.last = tuple(jax.tree.leaves(out)[0] for out in outs)
            for chain, out in zip(chains, outs):
                chain.accept(out)


def after(value, *others):
    return lax.optimization_barrier((value, others))[0]


def embed_times(stamps):
    halved = FREQ // 2
    freqs = jnp.exp(-math.log(10000.0) * jnp.arange(halved, dtype=F32) / halved)
    angles = stamps[:, None] * freqs[None, :]
    return jnp.concatenate([jnp.cos(angles), jnp.sin(angles)], 1)


def body(
    latents, cotangent, timesteps, time_in, time_out, ada_weight, ada_bias,
    attn_kernel, qkv_weight, out_weight, up_weight, ffn_kernel, down_weight,
):
    wide_count = lax.axis_size("wide")
    wide_at = lax.axis_index("wide")
    n = lax.axis_index("narrow")
    per_dev, tokens, share = latents.shape
    width = out_weight.shape[1]
    units = up_weight.shape[1]
    latent_total = timesteps.shape[0]
    scalars = n.astype(jnp.int32).reshape(1)

    steps, bit = [0], wide_count // 2
    while bit:
        steps, bit = steps + [k ^ bit for k in steps], bit // 2
    met = jnp.bitwise_xor(jnp.array(steps, jnp.int32), wide_at)
    stamps = timesteps.reshape(wide_count, per_dev)[met].reshape(latent_total).astype(F32)
    embedded = embed_times(stamps)
    mod, *stages = condition(embedded, time_in, time_out, ada_weight, ada_bias, per_dev, width)
    x = n // 2
    factor = 1.0 / latent_total

    def token_product(lefts, rights):
        total = None
        for a, b in zip(lefts, rights):
            part = dot_tn(a, b)
            total = part if total is None else total + part
        return (total * factor).astype(BF)

    x_own = jnp.swapaxes(latents, 1, 2)
    g_own = jnp.swapaxes(cotangent, 1, 2)
    qkv_rows = jnp.swapaxes(qkv_weight, 1, 2)
    qkv_all = qkv_rows.reshape(3 * share, width)
    order = Order()
    x_across = x_swap(x_own)
    x_across = after(x_across, mod)
    g_across = x_swap(after(g_own, x_across))
    x_parts = (x_own, core_swap(x_own), x_across, core_swap(x_across))
    g_parts = (g_own, core_swap(g_own), g_across, core_swap(g_across))

    def attend(pair):
        return lambda parts: attn_forward(scalars, pair, parts, mod, attn_kernel, qkv_rows, out_weight)

    fwd_a = order(attend(0), x_parts)
    here_a = order(sum_pair, fwd_a[6], core_swap(fwd_a[7]))
    fwd_b = order(attend(1), after(x_parts, g_across))
    att_a = order(sum_pair, here_a, x_swap(here_a))
    here_b = order(sum_pair, fwd_b[6], core_swap(fwd_b[7]))
    att_a = (att_a, core_swap(att_a))

    slots = 2 * per_dev

    def feed(pair, full, taps, held=()):
        return lambda att, parts: feed_forward(
            scalars, pair, full, att, parts, mod, up_weight, down_weight, ffn_kernel, slots, taps, held
        )

    ffn_a = order(feed(0, fwd_a[0], ffn_kernel), att_a, g_parts)
    att_b = order(sum_pair, here_b, x_swap(here_b))
    att_b = (att_b, core_swap(att_b))
    here_a = order(sum_pair, ffn_a[5], core_swap(ffn_a[6]))
    ffn_b = order(feed(1, fwd_b[0], ffn_a[8], ffn_a[9:11]), att_b, g_parts)
    sec_a = order(sum_pair, here_a, x_swap(here_a))
    sec_a = (sec_a, core_swap(sec_a))
    down_product = order(token_product, [ffn_a[2], ffn_b[2]], [ffn_a[3], ffn_b[3]])
    down_sum = WideSum(down_product, wide_at, wide_count)
    order.advance(down_sum)
    here_b = order(sum_pair, ffn_b[5], core_swap(ffn_b[6]))
    up_product = order(token_product, [ffn_a[1], ffn_b[1]], [ffn_a[4], ffn_b[4]])
    up_sum = WideSum(up_product, wide_at, wide_count)
    order.advance(up_sum)

    def attend_back(pair, fwd, ffn):
        return lambda att, sec: attn_backward(
            scalars, pair, fwd[0], att, sec, ffn[0], mod, fwd[2:5], out_weight, ffn[7]
        )

    def input_back(pair, fwd, taps, before, held):
        return lambda gqkv, gmid, mods: input_backward(
            scalars, pair, fwd[0], mod, gqkv, qkv_all, attn_kernel, taps, gmid, mods, before, slots, held
        )

    back_a = order(attend_back(0, fwd_a, ffn_a), att_a, sec_a)
    sec_b = order(sum_pair, here_b, x_swap(here_b))
    sec_b = (sec_b, core_swap(sec_b))
    order.advance(down_sum)
    back_b = order(attend_back(1, fwd_b, ffn_b), att_b, sec_b)
    order.advance(down_sum)
    attn_product = order(
        lambda grads, grouped, contexts, attended: jnp.concatenate(
            [token_product(grads, grouped), token_product(contexts, attended)], 0
        ),
        [back_a[1], back_b[1]], [fwd_a[1], fwd_b[1]], [fwd_a[5], fwd_b[5]], [back_a[0], back_b[0]],
    )
    levels = wide_count.bit_length() - 1
    attn_sum = WideSum(attn_product, wide_at, wide_count, [0] + list(range(levels - 1, 0, -1)))
    order.advance(attn_sum)
    order.advance(up_sum)
    order.advance(down_sum)
    in_a = order(input_back(0, fwd_a, attn_kernel, attn_kernel, ffn_b[9:11]), *back_a[1:4])
    order.advance(down_sum, up_sum)
    order.advance(attn_sum)
    in_b = order(input_back(1, fwd_b, in_a[0], in_a[1], in_a[2:4]), *back_b[1:4])
    order.advance(down_sum)

    rows = 6 * per_dev
    bits = [1 << k for k in reversed(range(levels))]
    moves = [lambda v, bit=bit: (v, wide_swap(v, bit, wide_count)) for bit in bits]
    join = lambda a, b: jnp.concatenate([a, b], 0)
    whole_rows = lambda a, b, c: join(sum_pair(a, b)[: rows + 9], c[:9].astype(BF))[None]
    mods = Steps(
        (in_b[1], core_swap(in_b[1])),
        [(sum_pair, lambda v: (v, x_swap(v), ffn_b[8]))]
        + [(work, move) for work, move in zip([whole_rows] + [join] * len(bits), moves)],
    )
    order.advance(up_sum)
    order.advance(mods)
    order.advance(attn_sum)
    order.advance(mods)
    order.advance(up_sum)
    while not down_sum.done():
        order.advance(down_sum)
    down_grad = down_sum.finish(order, lambda v: v.astype(F32))
    order.advance(attn_sum, mods)
    order.advance(mods)
    order.advance(up_sum)
    order.advance(attn_sum)
    made = order(functools.partial(slice_halves, x), in_b[2], core_swap(in_b[3]))
    while not all(c.done() for c in (mods, up_sum)):
        order.advance(mods)
        order.advance(up_sum)

    def unpack(held):
        gmod = held[:, :rows].reshape(latent_total, 6 * width)
        taps = jnp.sum(held[:, rows:].astype(F32), 0) * factor
        return gmod, jnp.sum(gmod.astype(F32), 0) * factor, taps[:9], taps[9:]

    gmod, ada_bias_grad, attn_taps, ffn_taps = order(lambda a, b: unpack(join(a, b)), *mods.came)
    while not attn_sum.done():
        order.advance(attn_sum)
    time_in_grad, time_out_grad, ada_weight_grad = order(
        lambda g: condition_back(g, embedded, stages, time_out, ada_weight, factor), gmod
    )
    up_grad = up_sum.finish(order, lambda v: v.astype(F32))
    finals = order(sum_pair, made[0], x_swap(made[1]))
    qkv_rows_grad, out_grad = attn_sum.finish(order, lambda v: (v[: 3 * share].astype(F32), v[3 * share :].astype(F32)))
    qkv_grad = jnp.swapaxes(qkv_rows_grad.reshape(3, share, width), 1, 2)
    final_out = jnp.swapaxes(finals[:per_dev], 1, 2)
    final_grad = jnp.swapaxes(finals[per_dev:], 1, 2)
    return (
        final_out, final_grad, time_in_grad, time_out_grad, ada_weight_grad, ada_bias_grad,
        attn_taps, qkv_grad, out_grad, up_grad, ffn_taps, down_grad,
    )


def solution(mesh):
    tokens = P("wide", None, "narrow")
    weights = (P(None, None, "narrow"), P("narrow", None), P(None, "narrow"), P(None, "narrow"), P("narrow", None))
    return jax.shard_map(
        body,
        mesh=mesh,
        in_specs=(tokens, tokens, P(), P(), P(), P(), P(), P()) + weights,
        out_specs=(tokens, tokens, P(), P(), P(), P(), P()) + weights,
        check_vma=False,
    )
```

```python
import functools
import math

import jax
import jax.numpy as jnp
from jax import lax
from jax.experimental import pallas as pl
from jax.experimental.pallas import tpu as pltpu
from jax.sharding import PartitionSpec as P

HEAD_DIM = 64
FREQ = 256
SIDE = 16
PAIR = 2

BF = jnp.bfloat16
F32 = jnp.float32
HIGHEST = lax.Precision.HIGHEST
LANES = 128
ROWS = 128
FEW_ROWS = 64
BAND = 64
GELU_A = math.sqrt(2.0 / math.pi)
GELU_B = 0.044715
EPS = 1e-06
VMEM_LIMIT = 60 * 1024 * 1024
WEIGHT_ROWS = 256
BACK_ROWS = 64
PACKED = 40


def dot(a, b):
    return lax.dot_general(a, b, (((1,), (0,)), ((), ())), preferred_element_type=F32)


def dot_nt(a, b):
    return lax.dot_general(a, b, (((1,), (1,)), ((), ())), preferred_element_type=F32)


def dot_tn(a, b):
    return lax.dot_general(a, b, (((0,), (0,)), ((), ())), preferred_element_type=F32)


def column_of(rows):
    return lax.broadcasted_iota(jnp.int32, (rows, LANES), 0) % SIDE


def from_left(v):
    moved = pltpu.roll(v, 1, 0)
    return jnp.where(column_of(v.shape[0]) == 0, 0.0, moved)


def from_right(v):
    moved = pltpu.roll(v, v.shape[0] - 1, 0)
    return jnp.where(column_of(v.shape[0]) == SIDE - 1, 0.0, moved)


def conv_band(padded, at, lanes, kern):
    rows = [padded[pl.ds(at + SIDE * r, BAND), lanes] for r in range(3)]
    mixed = [
        rows[0] * kern[c] + rows[1] * kern[3 + c] + rows[2] * kern[6 + c] for c in range(3)
    ]
    return from_left(mixed[0]) + mixed[1] + from_right(mixed[2])


def conv_back_band(padded_grad, at, lanes, kern):
    wide = padded_grad[pl.ds(at, BAND + 2 * SIDE), lanes]
    shifted = [from_right(wide), wide, from_left(wide)]
    total = None
    for r in range(3):
        for c in range(3):
            low = SIDE * (2 - r)
            term = shifted[c][low : low + BAND] * kern[3 * r + c]
            total = term if total is None else total + term
    return total, [s[SIDE : SIDE + BAND] for s in shifted]


def fold_rows(v):
    total = v[0:8]
    for at in range(8, v.shape[0], 8):
        total = total + v[at : at + 8]
    return total


def taps_of(kern_ref, lanes):
    block = kern_ref[:, lanes]
    return [block[t : t + 1] for t in range(9)]


def zero_edges(ref):
    edge = jnp.zeros((SIDE, ref.shape[1]), F32)
    tall = ref.shape[0] // PAIR
    for rel in range(PAIR):
        ref[rel * tall : rel * tall + SIDE, :] = edge
        ref[(rel + 1) * tall - SIDE : (rel + 1) * tall, :] = edge


def inside(ref, rel):
    tall = ref.shape[0] // PAIR
    return slice(rel * tall + SIDE, (rel + 1) * tall - SIDE)


def gather_features(n, parts, held, out):
    _, share, tokens = parts[0].shape
    core = jnp.bitwise_and(n, 1)

    def one(rel):
        for step, part in enumerate(parts):
            held[jnp.bitwise_xor(n, step)] = part[jnp.bitwise_xor(rel, core)]
        out[pl.ds(pl.multiple_of(rel * tokens, tokens), tokens), :] = held[...].reshape(len(parts) * share, tokens).T

    pair_loop(one)


def by_core(core, low, share, keep_out, send_out, turned):
    tokens = low.shape[0] // PAIR

    def one(rel):
        lat = jnp.bitwise_xor(rel, core)
        turned[...] = low[pl.ds(pl.multiple_of(rel * tokens, tokens), tokens), :].T
        for x in range(2):
            here = pl.ds(pl.multiple_of((2 * x + core) * share, 16), share)
            there = pl.ds(pl.multiple_of((2 * x + 1 - core) * share, 16), share)
            keep_out[x, lat] = turned[here, :]
            send_out[x, lat] = turned[there, :]

    pair_loop(one)


def norm_stats(v):
    width = v.shape[1]
    mean = jnp.sum(v, -1, keepdims=True) * (1.0 / width)
    center = v - mean
    spread = jnp.sum(center * center, -1, keepdims=True) * (1.0 / width)
    scale = lax.rsqrt(spread + EPS)
    return center * scale, scale


def head_masks(share):
    lane = lax.broadcasted_iota(jnp.int32, (1, share), 1) // HEAD_DIM
    return [(lane == h).astype(F32).astype(BF) for h in range(share // HEAD_DIM)]


def half_rows(v, parity):
    tokens, width = v.shape
    split = v.reshape(tokens // (2 * SIDE), 2, SIDE, width)
    return split[:, parity].reshape(tokens // 2, width)


def join_rows(even, odd):
    half, width = even.shape
    both = jnp.stack([even.reshape(half // SIDE, SIDE, width), odd.reshape(half // SIDE, SIDE, width)], 1)
    return both.reshape(2 * half, width)


def softmax_rows(queries, keys):
    scores = dot_nt(queries, keys) * (1.0 / math.sqrt(HEAD_DIM))
    rows = lax.broadcasted_iota(jnp.int32, scores.shape, 0)
    cols = lax.broadcasted_iota(jnp.int32, scores.shape, 1)
    same = (rows + cols) % 2 == 0
    scores = jnp.where(same, scores, -1e30)
    top = jnp.max(scores, -1, keepdims=True)
    grown = jnp.where(same, jnp.exp(scores - top), 0.0)
    return grown / jnp.sum(grown, -1, keepdims=True)


def beside(stacked, heads):
    rows = stacked.shape[0] // heads
    return jnp.concatenate([stacked[h * rows : (h + 1) * rows] for h in range(heads)], axis=1)


def lane_loop(width, body):
    count = width // LANES

    def step(j, carry):
        body(j // count, pl.ds(pl.multiple_of((j % count) * LANES, LANES), LANES))
        return carry

    lax.fori_loop(0, PAIR * count, step, 0)


def band_loop(tokens, body, carry):
    return lax.fori_loop(0, tokens // BAND, lambda j, c: body(pl.multiple_of(j * BAND, BAND), c), carry)


def row_loop(tokens, body, size=ROWS):
    count = tokens // size

    def step(j, carry):
        body(j // count, pl.multiple_of(j * size, size))
        return carry

    lax.fori_loop(0, PAIR * count, step, 0)


def pair_loop(body):
    def step(j, carry):
        body(j)
        return carry

    lax.fori_loop(0, PAIR, step, 0)


def attn_kernel_body(
    flow, s_ref, xo, xc, xx, xd, mod, kern, wqkv, wout,
    full_out, grouped_out, q_out, k_out, v_out, ctx_out, keep_out, send_out,
    held, padded,
):
    n = s_ref[0]
    core = jnp.bitwise_and(n, 1)
    share, tokens = xo.shape[1], xo.shape[2]
    width = full_out.shape[1]
    tall = tokens + 2 * SIDE
    zero_edges(padded)
    flow.need(xo, xc, xx, xd, mod, kern)
    gather_features(n, (xo, xc, xx, xd), held, full_out)
    flow.sent(full_out)

    def rows(rel, at):
        lat = jnp.bitwise_xor(rel, core)
        normed, _ = norm_stats(full_out[pl.ds(at, ROWS), :].astype(F32))
        here = pl.ds(pl.multiple_of(at + (2 * rel + 1) * SIDE, SIDE), ROWS)
        padded[here, :] = normed * (1.0 + mod[lat, 1:2, :]) + mod[lat, 0:1, :]

    row_loop(tokens, rows)

    def lanes(rel, at):
        taps = taps_of(kern, at)
        for band in range(0, tokens, BAND):
            here = pl.ds(pl.multiple_of(rel * tokens + band, BAND), BAND)
            grouped_out[here, at] = conv_band(padded, pl.multiple_of(rel * tall + band, SIDE), at, taps).astype(BF)

    lane_loop(width, lanes)
    flow.sent(grouped_out)
    flow.need(wqkv, wout)
    grouped = grouped_out[...]
    q_out[...] = dot_nt(grouped, wqkv[0]).astype(BF)
    k_out[...] = dot_nt(grouped, wqkv[1]).astype(BF)
    v_out[...] = dot_nt(grouped, wqkv[2]).astype(BF)
    flow.sent(q_out, k_out, v_out)
    masks = head_masks(share)
    heads = len(masks)

    def attend(rel):
        here = pl.ds(pl.multiple_of(rel * tokens, tokens), tokens)
        query, key, value = q_out[here, :], k_out[here, :], v_out[here, :]
        parts = []
        for parity in range(2):
            q = half_rows(query, parity)
            k = half_rows(key, parity)
            v = half_rows(value, parity)
            probs = softmax_rows(jnp.concatenate([q * m for m in masks], axis=0), k)
            low = beside(probs.astype(BF), heads)
            parts.append(dot(low, jnp.concatenate([v * m for m in masks], axis=0)).astype(BF))
        ctx_out[here, :] = join_rows(*parts)

    pair_loop(attend)
    flow.sent(ctx_out)
    send_out[...] = dot(ctx_out[tokens : 2 * tokens, :], wout[...]).astype(BF)
    flow.sent(send_out)
    keep_out[...] = dot(ctx_out[0:tokens, :], wout[...]).astype(BF)
    flow.sent(keep_out)


def ffn_kernel_body(
    first, flow, s_ref, go, gc, gx, gd, full, att, mod, up, down, kern, kgrad_in,
    g_out, second_out, active_out, gfed_out, ghid_out, keep_out, send_out, mods_out, kgrad_out, fkeep_out, fsend_out,
    held, padded, slope, gpad, mid, fed, low, sums, turned,
):
    n = s_ref[0]
    core = jnp.bitwise_and(n, 1)
    share, tokens = go.shape[1], go.shape[2]
    units = up.shape[1]
    tall = tokens + 2 * SIDE
    zero_edges(padded)
    zero_edges(gpad)
    flow.need(go, gc, gx, gd)
    gather_features(n, (go, gc, gx, gd), held, g_out)
    flow.sent(g_out)
    flow.need(full, att, mod, kgrad_in)
    kgrad_out[...] = jnp.zeros(kgrad_out.shape, F32) if first else kgrad_in[...]

    def rows(rel, at):
        lat = jnp.bitwise_xor(rel, core)
        here = pl.ds(at, ROWS)
        middle = full[here, :].astype(F32) + mod[lat, 2:3, :] * att[here, :].astype(F32)
        mid[here, :] = middle
        normed, _ = norm_stats(middle)
        second_out[here, :] = (normed * (1.0 + mod[lat, 4:5, :]) + mod[lat, 3:4, :]).astype(BF)
        gfed_out[here, :] = (mod[lat, 5:6, :] * g_out[here, :].astype(F32)).astype(BF)

    row_loop(tokens, rows)
    flow.sent(second_out, gfed_out)
    flow.need(up, kern)
    hidden = dot(second_out[...], up[...])
    for rel in range(PAIR):
        padded[inside(padded, rel), :] = hidden[rel * tokens : (rel + 1) * tokens]

    def lanes(rel, at):
        taps = taps_of(kern, at)
        for band in range(0, tokens, BAND):
            here = pl.ds(pl.multiple_of(rel * tokens + band, BAND), BAND)
            mixed = conv_band(padded, pl.multiple_of(rel * tall + band, SIDE), at, taps)
            square = mixed * mixed
            curve = jnp.tanh(GELU_A * mixed * (1.0 + GELU_B * square))
            half = 0.5 * (1.0 + curve)
            active_out[here, at] = (mixed * half).astype(BF)
            slope[here, at] = half + (0.5 * GELU_A) * mixed * (1.0 - curve * curve) * (
                1.0 + (3.0 * GELU_B) * square
            )

    lane_loop(units, lanes)
    flow.sent(active_out)
    flow.need(down)
    fed[...] = dot(active_out[...], down[...])
    sums[...] = jnp.zeros(sums.shape, F32)

    def rows_fed(rel, at):
        lat = jnp.bitwise_xor(rel, core)
        here = pl.ds(at, ROWS)
        term = fed[here, :]
        sums[lat] += fold_rows(term * g_out[here, :].astype(F32))
        low[here, :] = (mod[lat, 5:6, :] * term + 0.25 * mid[here, :]).astype(BF)

    row_loop(tokens, rows_fed)
    for lat in range(PAIR):
        mods_out[lat] = jnp.sum(sums[lat], 0, keepdims=True)
    by_core(core, low, share, fkeep_out, fsend_out, turned)
    flow.sent(fkeep_out, fsend_out, mods_out)
    gact = dot_nt(gfed_out[...], down[...]).astype(BF).astype(F32)
    for rel in range(PAIR):
        here = slice(rel * tokens, (rel + 1) * tokens)
        gpad[inside(gpad, rel), :] = gact[here] * slope[here, :]

    def lanes_back(rel, at):
        taps = taps_of(kern, at)
        sums = [None] * 9
        for band in range(0, tokens, BAND):
            here = pl.ds(pl.multiple_of(rel * tokens + band, BAND), BAND)
            base = pl.multiple_of(rel * tall + band, SIDE)
            total, shifted = conv_back_band(gpad, base, at, taps)
            ghid_out[here, at] = total.astype(BF)
            for r in range(3):
                values = padded[pl.ds(base + SIDE * r, BAND), at]
                for c in range(3):
                    part = fold_rows(values * shifted[c])
                    sums[3 * r + c] = part if sums[3 * r + c] is None else sums[3 * r + c] + part
        for t in range(9):
            kgrad_out[t : t + 1, at] += jnp.sum(sums[t], 0, keepdims=True)

    lane_loop(units, lanes_back)
    flow.sent(ghid_out, kgrad_out)
    send_out[...] = dot_nt(ghid_out[tokens : 2 * tokens, :], up[...]).astype(BF)
    flow.sent(send_out)
    keep_out[...] = dot_nt(ghid_out[0:tokens, :], up[...]).astype(BF)
    flow.sent(keep_out)


def attn_back_body(
    flow, s_ref, full, att, gs, gfull, mod, q_in, k_in, v_in, wout, gates,
    gatt_out, gqkv_out, gmid_out, mods_out,
    sums, gctx,
):
    core = jnp.bitwise_and(s_ref[0], 1)
    tokens = full.shape[0] // PAIR
    width = full.shape[1]
    share = q_in.shape[1]
    mods_out[...] = jnp.zeros(mods_out.shape, F32)
    sums[...] = jnp.zeros(sums.shape, F32)
    flow.need(full, att, gs, gfull, mod)

    def rows(rel, at):
        lat = jnp.bitwise_xor(rel, core)
        here = pl.ds(at, ROWS)
        gate1 = mod[lat, 2:3, :]
        attended = att[here, :].astype(F32)
        normed, inv = norm_stats(full[here, :].astype(F32) + gate1 * attended)
        grad = gs[here, :].astype(F32)
        inner = grad * (1.0 + mod[lat, 4:5, :])
        mean_a = jnp.sum(inner, -1, keepdims=True) * (1.0 / width)
        mean_b = jnp.sum(inner * normed, -1, keepdims=True) * (1.0 / width)
        whole_grad = gfull[here, :].astype(F32) + inv * (inner - mean_a - normed * mean_b)
        gmid_out[here, :] = whole_grad.astype(BF)
        gatt_out[here, :] = (gate1 * whole_grad).astype(BF)
        sums[3 * lat] += fold_rows(attended * whole_grad)
        sums[3 * lat + 1] += fold_rows(grad)
        sums[3 * lat + 2] += fold_rows(grad * normed)

    row_loop(tokens, rows)
    for lat in range(PAIR):
        for k in range(3):
            mods_out[lat, 2 + k : 3 + k, :] = 0.25 * jnp.sum(sums[3 * lat + k], 0, keepdims=True)
    flow.need(wout, q_in, k_in, v_in, gates)
    for lat in range(PAIR):
        mods_out[lat, 5:6, :] = gates[lat]
    flow.sent(gatt_out, gmid_out, mods_out)
    gctx[...] = dot_nt(gatt_out[...], wout[...]).astype(BF)
    masks = head_masks(share)
    heads = len(masks)
    factor = 1.0 / math.sqrt(HEAD_DIM)

    def attend(rel):
        here = pl.ds(pl.multiple_of(rel * tokens, tokens), tokens)
        query, key, value, grads = q_in[here, :], k_in[here, :], v_in[here, :], gctx[here, :]
        parts_q, parts_k, parts_v = [], [], []
        for parity in range(2):
            q = half_rows(query, parity)
            k = half_rows(key, parity)
            v = half_rows(value, parity)
            gc = half_rows(grads, parity)
            q_all = jnp.concatenate([q * m for m in masks], axis=0)
            k_all = jnp.concatenate([k * m for m in masks], axis=0)
            gc_all = jnp.concatenate([gc * m for m in masks], axis=0)
            probs = softmax_rows(q_all, k)
            parts_v.append(dot_tn(probs.astype(BF), gc_all).astype(BF))
            gprobs = dot_nt(gc_all, v).astype(BF).astype(F32)
            gscores = (probs * (gprobs - jnp.sum(probs * gprobs, -1, keepdims=True))).astype(BF)
            parts_q.append((dot(beside(gscores, heads), k_all) * factor).astype(BF))
            parts_k.append((dot_tn(gscores, q_all) * factor).astype(BF))
        for k, parts in enumerate((parts_q, parts_k, parts_v)):
            gqkv_out[here, k * share : (k + 1) * share] = join_rows(*parts)

    pair_loop(attend)
    flow.sent(gqkv_out)


def input_back_body(
    closing, flow, s_ref, full, mod, gqkv, wqkv, kern, kgrad_in, gmid, mods_in, before,
    kgrad_out, mods_out, keep_out, send_out,
    normed1, scale1, first, gpad, gback, low, mods, rows_out, turned,
):
    core = jnp.bitwise_and(s_ref[0], 1)
    tokens = full.shape[0] // PAIR
    width = full.shape[1]
    share = gqkv.shape[1] // 3
    tall = tokens + 2 * SIDE
    zero_edges(first)
    zero_edges(gpad)
    flow.need(full, mod)

    def rows_first(rel, at):
        lat = jnp.bitwise_xor(rel, core)
        here = pl.ds(at, FEW_ROWS)
        normed, inv = norm_stats(full[here, :].astype(F32))
        normed1[here, :] = normed
        scale1[here, :] = jnp.broadcast_to(inv, (FEW_ROWS, LANES))
        inside_rows = pl.ds(pl.multiple_of(at + (2 * rel + 1) * SIDE, SIDE), FEW_ROWS)
        first[inside_rows, :] = normed * (1.0 + mod[lat, 1:2, :]) + mod[lat, 0:1, :]

    row_loop(tokens, rows_first, FEW_ROWS)
    flow.need(gqkv, wqkv, kern, kgrad_in, gmid, mods_in, before)
    kgrad_out[...] = kgrad_in[...] if closing else jnp.zeros(kgrad_out.shape, F32)
    mods[...] = mods_in[...]
    for rel in range(PAIR):
        here = slice(rel * tokens, (rel + 1) * tokens)
        gpad[inside(gpad, rel), :] = dot(gqkv[here, :], wqkv[...])

    def lanes(rel, at):
        taps = taps_of(kern, at)

        def bands(band, sums):
            here = pl.ds(pl.multiple_of(rel * tokens + band, BAND), BAND)
            base = pl.multiple_of(rel * tall + band, SIDE)
            total, shifted = conv_back_band(gpad, base, at, taps)
            gback[here, at] = total
            values = [first[pl.ds(base + SIDE * r, BAND), at] for r in range(3)]
            parts = [fold_rows(values[r] * shifted[c]) for r in range(3) for c in range(3)]
            parts += [fold_rows(total), fold_rows(total * normed1[here, at])]
            return [a + b for a, b in zip(sums, parts)]

        *sums, shift_sum, scale_sum = band_loop(tokens, bands, [jnp.zeros((8, LANES), F32)] * 11)
        for t in range(9):
            kgrad_out[t : t + 1, at] += jnp.sum(sums[t], 0, keepdims=True)
        lat = jnp.bitwise_xor(rel, core)
        mods[lat, 0:1, at] = jnp.sum(shift_sum, 0, keepdims=True)
        mods[lat, 1:2, at] = jnp.sum(scale_sum, 0, keepdims=True)

    lane_loop(width, lanes)
    if closing:
        rows_out[...] = jnp.zeros(rows_out.shape, F32)
        for lat in range(PAIR):
            rows_out[6 * lat : 6 * lat + 6, :] = before[lat, 0:6, :]
            rows_out[6 * (PAIR + lat) : 6 * (PAIR + lat) + 6, :] = mods[lat, 0:6, :]
        rows_out[12 * PAIR : 12 * PAIR + 9, :] = kgrad_out[0:9, :]
        mods_out[...] = rows_out[...].astype(BF)
    else:
        mods_out[...] = mods[...]
    flow.sent(mods_out, kgrad_out)

    def rows_back(rel, at):
        lat = jnp.bitwise_xor(rel, core)
        here = pl.ds(at, FEW_ROWS)
        inner = gback[here, :] * (1.0 + mod[lat, 1:2, :])
        normed = normed1[here, :]
        mean_a = jnp.sum(inner, -1, keepdims=True) * (1.0 / width)
        mean_b = jnp.sum(inner * normed, -1, keepdims=True) * (1.0 / width)
        grad = scale1[here, 0:1] * (inner - mean_a - normed * mean_b)
        low[here, :] = (grad + 0.25 * gmid[here, :].astype(F32)).astype(BF)

    row_loop(tokens, rows_back, FEW_ROWS)
    by_core(core, low, share, keep_out, send_out, turned)
    flow.sent(keep_out, send_out)


class Flow:
    def __init__(self, arrivals, departures):
        self.arrivals, self.departures = arrivals, departures
        self.leaving = []
        for _, copy in arrivals:
            copy.start()

    def need(self, *refs):
        for ref in refs:
            for _, copy in [a for a in self.arrivals if a[0] is ref]:
                copy.wait()
            self.arrivals = [a for a in self.arrivals if a[0] is not ref]

    def sent(self, *refs):
        for ref in refs:
            for held, copy in self.departures:
                if held is ref:
                    copy.start()
                    self.leaving.append(copy)

    def end(self):
        for copy in self.leaving:
            copy.wait()


def call(body, name, scalars, ins, outs, scratch, flops, held=()):
    n_in, n_out = len(ins), len(outs)
    places, buffer_shapes = [], []
    for array, window, into in ins:
        dims = array.shape if window is None else (PAIR,) + array.shape[1:]
        if into is None:
            buffer_shapes.append((dims, array.dtype))
        elif into[0].start == 0:
            buffer_shapes.append(((PAIR * dims[0],) + dims[1:], array.dtype))
        places.append(len(buffer_shapes) - 1)

    def run(s_ref, *refs):
        sources = refs[:n_in]
        targets = refs[n_in + len(held) : n_in + len(held) + n_out]
        buffers = refs[n_in + len(held) + n_out : -1]
        sems = refs[-1]
        n_held = len(buffer_shapes)
        buffers_in, buffers_out = buffers[:n_held], buffers[n_held : n_held + n_out]
        rest = buffers[n_held + n_out :]
        arrivals, departures = [], []
        for k, (source, (_, window, into)) in enumerate(zip(sources, ins)):
            view = source if window is None else source.at[window]
            buffer = buffers_in[places[k]]
            target = buffer if into is None else buffer.at[into]
            arrivals.append((buffer, pltpu.make_async_copy(view, target, sems.at[k])))
        for k, (target, buffer, out) in enumerate(zip(targets, buffers_out, outs)):
            view = target if out[2] is None else target.at[out[2]]
            departures.append((buffer, pltpu.make_async_copy(buffer, view, sems.at[n_in + k])))
        flow = Flow(arrivals, departures)
        body(flow, s_ref, *buffers_in, *buffers_out, *rest)
        flow.end()

    anywhere = pl.BlockSpec(memory_space=pl.ANY)
    return pl.pallas_call(
        run,
        name=name,
        out_shape=[jax.ShapeDtypeStruct(o[0], o[1]) for o in outs],
        grid_spec=pltpu.PrefetchScalarGridSpec(
            num_scalar_prefetch=1,
            grid=(1,),
            in_specs=[anywhere] * (n_in + len(held)),
            out_specs=[anywhere] * n_out,
            scratch_shapes=[pltpu.VMEM(dims, dtype) for dims, dtype in buffer_shapes]
            + [pltpu.VMEM(o[3], o[1]) for o in outs]
            + scratch
            + [pltpu.SemaphoreType.DMA((n_in + n_out,))],
        ),
        input_output_aliases={1 + n_in + k: n_out - len(held) + k for k in range(len(held))},
        compiler_params=pltpu.CompilerParams(vmem_limit_bytes=VMEM_LIMIT),
        cost_estimate=pl.CostEstimate(flops=flops, bytes_accessed=10**6, transcendentals=0),
    )(scalars, *[i[0] for i in ins], *held)


def slices_out(slots, slot, share, tokens):
    return ((2, slots, share, tokens), BF, (slice(None), pl.ds(PAIR * slot, PAIR)), (2, PAIR, share, tokens))


def whole(array):
    return (array, None, None)


def stacked(arrays):
    rows = arrays[0].shape[0]
    return [(v, None, (pl.ds(k * rows, rows),)) for k, v in enumerate(arrays)]


def whole_out(dims, dtype):
    return (dims, dtype, None, dims)


def pair_of(array, pair):
    return (array, (pl.ds(PAIR * pair, PAIR),), None)


def split_low(v):
    high = v.astype(BF)
    return high, (v - high.astype(F32)).astype(BF)


def rows_product(a, b):
    (ah, al), (bh, bl) = split_low(a), split_low(b)
    return dot_tn(jnp.concatenate([ah, al, ah], 0), jnp.concatenate([bh, bh, bl], 0))


def back_product(a, weight):
    (ah, al), (wh, wl) = split_low(a), split_low(weight)
    return dot_nt(ah, wh) + dot_nt(al, wh) + dot_nt(ah, wl)


def product(a, weight):
    (ah, al), (wh, wl) = split_low(a), split_low(weight)
    return dot(ah, wh) + dot(al, wh) + dot(ah, wl)


def silu(v):
    return v / (1.0 + jnp.exp(-v))


def silu_slope(v):
    gate = 1.0 / (1.0 + jnp.exp(-v))
    return gate * (1.0 + v * (1.0 - gate))


def row_blocks(source, target, sems, rows):
    return [
        pltpu.make_async_copy(source.at[pl.ds(at, rows)], target.at[pl.ds(at, rows)], sems.at[at // rows])
        for at in range(0, source.shape[0], rows)
    ]


def condition_body(
    embedded, bias, time_in, time_out, ada, mod_out, inner_pre, inner, outer_pre, outer, held_in, held_out, held, sums, parts, sems,
):
    depth = ada.shape[0]
    per_dev, count, width = mod_out.shape
    first = pltpu.make_async_copy(time_in, held_in, sems.at[0])
    second = pltpu.make_async_copy(time_out, held_out, sems.at[1])
    blocks = row_blocks(ada, held, sems.at[pl.ds(2, depth // WEIGHT_ROWS)], WEIGHT_ROWS)
    for copy in [first, second] + blocks:
        copy.start()
    first.wait()
    inner_pre[...] = product(embedded[...], held_in[...])
    inner[...] = silu(inner_pre[...])
    second.wait()
    outer_pre[...] = product(inner[...], held_out[...])
    outer[...] = silu(outer_pre[...])
    wide_bias = [jnp.concatenate([bias[k + j : k + j + 1, :] for j in range(width // LANES)], 1)
                 for k in range(0, bias.shape[0], width // LANES)]
    total = jnp.concatenate(wide_bias, 1)
    sums[...] = jnp.broadcast_to(total, sums.shape)
    for k in range(depth // WEIGHT_ROWS):
        parts[k] = outer[0:8, k * WEIGHT_ROWS : (k + 1) * WEIGHT_ROWS]

    def add(k, carry):
        rows = pl.ds(pl.multiple_of(k * WEIGHT_ROWS, WEIGHT_ROWS), WEIGHT_ROWS)
        pltpu.make_async_copy(ada.at[rows], held.at[rows], sems.at[2 + k]).wait()
        sums[...] += product(parts[k], held[rows, :])
        return carry

    lax.fori_loop(0, depth // WEIGHT_ROWS, add, 0)
    total = sums[...]
    for lat in range(per_dev):
        for k in range(count):
            mod_out[lat, k : k + 1, :] = total[lat : lat + 1, k * width : (k + 1) * width]


def condition(embedded, time_in, time_out, ada_weight, ada_bias, per_dev, width):
    latent_total = embedded.shape[0]
    depth, columns = ada_weight.shape
    vmem = pl.BlockSpec(memory_space=pltpu.VMEM)
    anywhere = pl.BlockSpec(memory_space=pl.ANY)
    rows = jax.ShapeDtypeStruct((latent_total, depth), F32)
    return pl.pallas_call(
        condition_body,
        name="condition",
        in_specs=[vmem, vmem, anywhere, anywhere, anywhere],
        out_specs=[vmem] * 5,
        out_shape=[jax.ShapeDtypeStruct((per_dev, columns // width, width), F32), rows, rows, rows, rows],
        scratch_shapes=[
            pltpu.VMEM(time_in.shape, F32),
            pltpu.VMEM(time_out.shape, F32),
            pltpu.VMEM(ada_weight.shape, F32),
            pltpu.VMEM((8, columns), F32),
            pltpu.VMEM((depth // WEIGHT_ROWS, 8, WEIGHT_ROWS), F32),
            pltpu.SemaphoreType.DMA((2 + depth // WEIGHT_ROWS,)),
        ],
        compiler_params=pltpu.CompilerParams(vmem_limit_bytes=VMEM_LIMIT),
        cost_estimate=pl.CostEstimate(flops=8 * 10**9, bytes_accessed=10**6, transcendentals=0),
    )(embedded, ada_bias.reshape(columns // LANES, LANES), time_in, time_out, ada_weight)


def condition_back_body(
    factor, gmod, embedded, inner_pre, inner, outer_pre, outer, time_out, ada,
    time_in_grad, time_out_grad, ada_grad, held_out, held, outer_grad, columns, sems, arriving, leaving,
):
    count = ada.shape[0] // BACK_ROWS

    def block_copy(source, target, sem, k):
        rows = pl.ds(k * BACK_ROWS, BACK_ROWS)
        return pltpu.make_async_copy(source.at[rows], target.at[rows], sem.at[k])

    first = pltpu.make_async_copy(time_out, held_out, sems.at[0])
    for k in range(count):
        block_copy(ada, held, arriving, k).start()
    first.start()
    high, low = split_low(outer[...])
    both = jnp.concatenate([high, low], 0)
    for k in range(count):
        columns[k] = both[:, k * BACK_ROWS : (k + 1) * BACK_ROWS]

    def block(k, carry):
        rows = pl.ds(pl.multiple_of(k * BACK_ROWS, BACK_ROWS), BACK_ROWS)
        block_copy(ada, held, arriving, k).wait()
        grads = gmod[...]
        high, low = split_low(held[rows, :])
        outer_grad[rows, :] = dot_nt(high, grads) + dot_nt(low, grads)
        held[rows, :] = dot_tn(columns[k], jnp.concatenate([grads, grads], 0)) * factor
        block_copy(held, ada_grad, leaving, k).start()
        return carry

    lax.fori_loop(0, count, block, 0)
    first.wait()
    back = outer_grad[...].T * factor * silu_slope(outer_pre[...])
    time_out_grad[...] = rows_product(inner[...], back)
    back = back_product(back, held_out[...]) * silu_slope(inner_pre[...])
    time_in_grad[...] = rows_product(embedded[...], back)
    for k in range(count):
        block_copy(held, ada_grad, leaving, k).wait()


def condition_back(gmod, embedded, stages, time_out, ada_weight, factor):
    depth = ada_weight.shape[0]
    latent_total = gmod.shape[0]
    vmem = pl.BlockSpec(memory_space=pltpu.VMEM)
    anywhere = pl.BlockSpec(memory_space=pl.ANY)
    time_in_dims = (embedded.shape[1], time_out.shape[0])
    return pl.pallas_call(
        functools.partial(condition_back_body, factor),
        name="condition_back",
        in_specs=[vmem] * 6 + [anywhere] * 2,
        out_specs=[vmem, vmem, anywhere],
        out_shape=[
            jax.ShapeDtypeStruct(time_in_dims, F32),
            jax.ShapeDtypeStruct(time_out.shape, F32),
            jax.ShapeDtypeStruct(ada_weight.shape, F32),
        ],
        scratch_shapes=[
            pltpu.VMEM(time_out.shape, F32),
            pltpu.VMEM(ada_weight.shape, F32),
            pltpu.VMEM((depth, latent_total), F32),
            pltpu.VMEM((depth // BACK_ROWS, 2 * latent_total, BACK_ROWS), BF),
            pltpu.SemaphoreType.DMA((1,)),
            pltpu.SemaphoreType.DMA((depth // BACK_ROWS,)),
            pltpu.SemaphoreType.DMA((depth // BACK_ROWS,)),
        ],
        compiler_params=pltpu.CompilerParams(vmem_limit_bytes=VMEM_LIMIT),
        cost_estimate=pl.CostEstimate(flops=1, bytes_accessed=1, transcendentals=0),
    )(gmod, embedded, *stages, time_out, ada_weight)


def attn_forward(scalars, pair, x_parts, mod, attn_kernel, qkv_weight, out_weight):
    _, share, tokens = x_parts[0].shape
    width = out_weight.shape[1]
    rows = PAIR * tokens
    thin = whole_out((rows, share), BF)
    half = whole_out((tokens, width), BF)
    return call(
        attn_kernel_body, "attn_fwd", scalars,
        [pair_of(v, pair) for v in x_parts] + [pair_of(mod, pair), whole(attn_kernel), whole(qkv_weight), whole(out_weight)],
        [whole_out((rows, width), BF), whole_out((rows, width), BF), thin, thin, thin, thin, half, half],
        [pltpu.VMEM((4, share, tokens), BF), pltpu.VMEM((PAIR * (tokens + 2 * SIDE), width), F32)],
        6_000_000_000,
    )


def feed_forward(scalars, pair, full, att, g_parts, mod, up_weight, down_weight, ffn_kernel, slots, taps, held):
    _, share, tokens = g_parts[0].shape
    width, units = up_weight.shape
    rows = PAIR * tokens
    tall = PAIR * (tokens + 2 * SIDE)
    broad = whole_out((rows, width), BF)
    hidden = whole_out((rows, units), BF)
    half = whole_out((tokens, width), BF)
    slices = slices_out(slots, pair, share, tokens)
    return call(
        functools.partial(ffn_kernel_body, pair == 0), "ffn", scalars,
        [pair_of(v, pair) for v in g_parts] + [whole(full)] + stacked(att)
        + [pair_of(mod, pair), whole(up_weight), whole(down_weight), whole(ffn_kernel), whole(taps)],
        [broad, broad, hidden, broad, hidden, half, half, whole_out((PAIR, 1, width), F32), whole_out((16, units), F32),
         slices, slices],
        [pltpu.VMEM((4, share, tokens), BF), pltpu.VMEM((tall, units), F32), pltpu.VMEM((rows, units), F32),
         pltpu.VMEM((tall, units), F32), pltpu.VMEM((rows, width), F32), pltpu.VMEM((rows, width), F32),
         pltpu.VMEM((rows, width), BF), pltpu.VMEM((PAIR, 8, width), F32), pltpu.VMEM((width, tokens), BF)],
        10_000_000_000, held,
    )


def attn_backward(scalars, pair, full, att, gsec, gfull, mod, qkv, out_weight, gates):
    tokens, width = att[0].shape
    share = out_weight.shape[0]
    rows = PAIR * tokens
    broad = whole_out((rows, width), BF)
    return call(
        attn_back_body, "attn_bwd", scalars,
        [whole(full)] + stacked(att) + stacked(gsec) + [whole(gfull), pair_of(mod, pair)]
        + [whole(v) for v in qkv] + [whole(out_weight), whole(gates)],
        [broad, whole_out((rows, 3 * share), BF), broad, whole_out((PAIR, 8, width), F32)],
        [pltpu.VMEM((3 * PAIR, 8, width), F32), pltpu.VMEM((rows, share), BF)],
        6_000_000_000,
    )


def input_backward(scalars, pair, full, mod, gqkv, qkv_weight, attn_kernel, taps, gmid, mods_in, before, slots, held):
    rows, width = full.shape
    tokens = rows // PAIR
    share = gqkv.shape[1] // 3
    tall = PAIR * (tokens + 2 * SIDE)
    slices = slices_out(slots, slots // PAIR // 2 + pair, share, tokens)
    closing = pair > 0
    mods = whole_out((PACKED, width), BF) if closing else whole_out((PAIR, 8, width), F32)
    return call(
        functools.partial(input_back_body, closing), "input_bwd", scalars,
        [whole(full), pair_of(mod, pair), whole(gqkv), whole(qkv_weight), whole(attn_kernel), whole(taps), whole(gmid),
         whole(mods_in), whole(before)],
        [whole_out((16, width), F32), mods, slices, slices],
        [pltpu.VMEM((rows, width), F32), pltpu.VMEM((rows, LANES), F32), pltpu.VMEM((tall, width), F32),
         pltpu.VMEM((tall, width), F32), pltpu.VMEM((rows, width), F32), pltpu.VMEM((rows, width), BF),
         pltpu.VMEM((PAIR, 8, width), F32), pltpu.VMEM((PACKED, width), F32), pltpu.VMEM((width, tokens), BF)],
        6_000_000_000, held,
    )


def core_swap(v):
    return lax.ppermute(v, "narrow", [(0, 1), (1, 0), (2, 3), (3, 2)])


def x_swap(v):
    return lax.ppermute(v, "narrow", [(0, 2), (2, 0), (1, 3), (3, 1)])


def sum_pair(a, b):
    return (a.astype(F32) + b.astype(F32)).astype(BF)


def slice_halves(x, keep, arrived):
    both = sum_pair(keep, arrived)
    return (
        lax.dynamic_index_in_dim(both, x, 0, keepdims=False),
        lax.dynamic_index_in_dim(both, 1 - x, 0, keepdims=False),
    )


def wide_swap(v, bit, count):
    return lax.ppermute(v, "wide", [(i, i ^ bit) for i in range(count)])


def pick(v, parts, at):
    rows = v.shape[0] // parts
    return lax.dynamic_slice_in_dim(v, at * rows, rows, 0)


def in_place(bit, own, came, axis):
    dims = own.shape[:axis] + (2,) + own.shape[axis + 1 :]
    return jnp.where(lax.broadcasted_iota(jnp.int32, dims, axis) == bit, own, came)


class WideSum:
    def __init__(self, product, at, count, back=None):
        self.count, self.dims = count, product.shape
        self.levels = count.bit_length() - 1
        self.bits = [at // (1 << k) % 2 for k in range(self.levels)]
        self.ahead = list(range(self.levels))
        self.back = list(reversed(self.ahead)) if back is None else back
        self.opened = False
        self.held = product

    def swap(self, sent, level):
        self.came = wide_swap(sent, 1 << level, self.count)

    def halve(self, held, came):
        level = self.ahead[0]
        if level == 0:
            held = pick(held, 2, self.bits[0])
        if len(self.ahead) == 1:
            return (sum_pair(held, came),)
        bit = self.bits[level + 1]
        return tuple(sum_pair(pick(held, 2, at), pick(came, 2, at)) for at in (1 - bit, bit))

    def pending(self):
        if not self.opened:
            return lambda v: pick(v, 2, 1 - self.bits[0]), (self.held,)
        if self.ahead:
            return self.halve, (self.held, self.came)
        level = self.back[0]
        return lambda a, b: in_place(self.bits[level], a, b, level), (self.held, self.came)

    def accept(self, out):
        if not self.opened:
            self.opened = True
            self.swap(out, 0)
        elif self.ahead:
            self.ahead.pop(0)
            self.held = out[-1]
            if self.ahead:
                self.swap(out[0], self.ahead[0])
            else:
                self.held = self.held.reshape((1,) * self.levels + self.held.shape)
                self.swap(self.held, self.back[0])
        else:
            self.back.pop(0)
            self.held = out
            self.swap(out, self.back[0])

    def done(self):
        return self.opened and not self.ahead and len(self.back) == 1

    def finish(self, order, shape=lambda v: v):
        level = self.back[0]
        return order(
            lambda a, b: shape(in_place(self.bits[level], a, b, level).reshape(self.dims)), self.held, self.came
        )


class Steps:
    def __init__(self, came, steps):
        self.came, self.steps = came, list(steps)

    def pending(self):
        return self.steps[0][0], self.came

    def accept(self, out):
        _, move = self.steps.pop(0)
        self.came = move(out)

    def done(self):
        return not self.steps


class Order:
    def __init__(self):
        self.last = ()

    def __call__(self, step, *inputs):
        inputs, _ = lax.optimization_barrier((inputs, self.last))
        out = step(*inputs)
        self.last = tuple(jax.tree.leaves(out)[:1])
        return out

    def advance(self, *chains):
        chains = [c for c in chains if not c.done()]
        if chains:
            work = [c.pending() for c in chains]
            outs = self(lambda *v: [w[0](*a) for w, a in zip(work, v)], *[w[1] for w in work])
            self.last = tuple(jax.tree.leaves(out)[0] for out in outs)
            for chain, out in zip(chains, outs):
                chain.accept(out)


def after(value, *others):
    return lax.optimization_barrier((value, others))[0]


def embed_times(stamps):
    halved = FREQ // 2
    freqs = jnp.exp(-math.log(10000.0) * jnp.arange(halved, dtype=F32) / halved)
    angles = stamps[:, None] * freqs[None, :]
    return jnp.concatenate([jnp.cos(angles), jnp.sin(angles)], 1)


def body(
    latents, cotangent, timesteps, time_in, time_out, ada_weight, ada_bias,
    attn_kernel, qkv_weight, out_weight, up_weight, ffn_kernel, down_weight,
):
    wide_count = lax.axis_size("wide")
    wide_at = lax.axis_index("wide")
    n = lax.axis_index("narrow")
    per_dev, tokens, share = latents.shape
    width = out_weight.shape[1]
    units = up_weight.shape[1]
    latent_total = timesteps.shape[0]
    scalars = n.astype(jnp.int32).reshape(1)

    steps, bit = [0], wide_count // 2
    while bit:
        steps, bit = steps + [k ^ bit for k in steps], bit // 2
    met = jnp.bitwise_xor(jnp.array(steps, jnp.int32), wide_at)
    stamps = timesteps.reshape(wide_count, per_dev)[met].reshape(latent_total).astype(F32)
    embedded = embed_times(stamps)
    mod, *stages = condition(embedded, time_in, time_out, ada_weight, ada_bias, per_dev, width)
    x = n // 2
    factor = 1.0 / latent_total

    def token_product(lefts, rights):
        total = None
        for a, b in zip(lefts, rights):
            part = dot_tn(a, b)
            total = part if total is None else total + part
        return (total * factor).astype(BF)

    x_own = jnp.swapaxes(latents, 1, 2)
    g_own = jnp.swapaxes(cotangent, 1, 2)
    qkv_rows = jnp.swapaxes(qkv_weight, 1, 2)
    qkv_all = qkv_rows.reshape(3 * share, width)
    order = Order()
    x_across = x_swap(x_own)
    x_across = after(x_across, mod)
    g_across = x_swap(after(g_own, x_across))
    x_parts = (x_own, core_swap(x_own), x_across, core_swap(x_across))
    g_parts = (g_own, core_swap(g_own), g_across, core_swap(g_across))

    def attend(pair):
        return lambda parts: attn_forward(scalars, pair, parts, mod, attn_kernel, qkv_rows, out_weight)

    fwd_a = order(attend(0), x_parts)
    here_a = order(sum_pair, fwd_a[6], core_swap(fwd_a[7]))
    fwd_b = order(attend(1), after(x_parts, g_across))
    att_a = order(sum_pair, here_a, x_swap(here_a))
    here_b = order(sum_pair, fwd_b[6], core_swap(fwd_b[7]))
    att_a = (att_a, core_swap(att_a))

    slots = 2 * per_dev

    def feed(pair, full, taps, held=()):
        return lambda att, parts: feed_forward(
            scalars, pair, full, att, parts, mod, up_weight, down_weight, ffn_kernel, slots, taps, held
        )

    ffn_a = order(feed(0, fwd_a[0], ffn_kernel), att_a, g_parts)
    att_b = order(sum_pair, here_b, x_swap(here_b))
    att_b = (att_b, core_swap(att_b))
    here_a = order(sum_pair, ffn_a[5], core_swap(ffn_a[6]))
    ffn_b = order(feed(1, fwd_b[0], ffn_a[8], ffn_a[9:11]), att_b, g_parts)
    sec_a = order(sum_pair, here_a, x_swap(here_a))
    sec_a = (sec_a, core_swap(sec_a))
    down_product = order(token_product, [ffn_a[2], ffn_b[2]], [ffn_a[3], ffn_b[3]])
    down_sum = WideSum(down_product, wide_at, wide_count)
    order.advance(down_sum)
    here_b = order(sum_pair, ffn_b[5], core_swap(ffn_b[6]))
    up_product = order(token_product, [ffn_a[1], ffn_b[1]], [ffn_a[4], ffn_b[4]])
    up_sum = WideSum(up_product, wide_at, wide_count)
    order.advance(up_sum)

    def attend_back(pair, fwd, ffn):
        return lambda att, sec: attn_backward(
            scalars, pair, fwd[0], att, sec, ffn[0], mod, fwd[2:5], out_weight, ffn[7]
        )

    def input_back(pair, fwd, taps, before, held):
        return lambda gqkv, gmid, mods: input_backward(
            scalars, pair, fwd[0], mod, gqkv, qkv_all, attn_kernel, taps, gmid, mods, before, slots, held
        )

    back_a = order(attend_back(0, fwd_a, ffn_a), att_a, sec_a)
    sec_b = order(sum_pair, here_b, x_swap(here_b))
    sec_b = (sec_b, core_swap(sec_b))
    order.advance(down_sum)
    back_b = order(attend_back(1, fwd_b, ffn_b), att_b, sec_b)
    order.advance(down_sum)
    attn_product = order(
        lambda grads, grouped, contexts, attended: jnp.concatenate(
            [token_product(grads, grouped), token_product(contexts, attended)], 0
        ),
        [back_a[1], back_b[1]], [fwd_a[1], fwd_b[1]], [fwd_a[5], fwd_b[5]], [back_a[0], back_b[0]],
    )
    levels = wide_count.bit_length() - 1
    attn_sum = WideSum(attn_product, wide_at, wide_count, [0] + list(range(levels - 1, 0, -1)))
    order.advance(attn_sum)
    order.advance(up_sum)
    order.advance(down_sum)
    in_a = order(input_back(0, fwd_a, attn_kernel, attn_kernel, ffn_b[9:11]), *back_a[1:4])
    order.advance(down_sum, up_sum)
    order.advance(attn_sum)
    in_b = order(input_back(1, fwd_b, in_a[0], in_a[1], in_a[2:4]), *back_b[1:4])
    order.advance(down_sum)

    rows = 6 * per_dev
    bits = [1 << k for k in reversed(range(levels))]
    moves = [lambda v, bit=bit: (v, wide_swap(v, bit, wide_count)) for bit in bits]
    join = lambda a, b: jnp.concatenate([a, b], 0)
    whole_rows = lambda a, b, c: join(sum_pair(a, b)[: rows + 9], c[:9].astype(BF))[None]
    mods = Steps(
        (in_b[1], core_swap(in_b[1])),
        [(sum_pair, lambda v: (v, x_swap(v), ffn_b[8]))]
        + [(work, move) for work, move in zip([whole_rows] + [join] * len(bits), moves)],
    )
    order.advance(up_sum)
    order.advance(mods)
    order.advance(attn_sum)
    order.advance(mods)
    order.advance(up_sum)
    while not down_sum.done():
        order.advance(down_sum)
    down_grad = down_sum.finish(order, lambda v: v.astype(F32))
    order.advance(attn_sum, mods)
    order.advance(mods)
    order.advance(up_sum)
    order.advance(attn_sum)
    made = order(functools.partial(slice_halves, x), in_b[2], core_swap(in_b[3]))
    while not all(c.done() for c in (mods, up_sum)):
        order.advance(mods)
        order.advance(up_sum)

    def unpack(held):
        gmod = held[:, :rows].reshape(latent_total, 6 * width)
        taps = jnp.sum(held[:, rows:].astype(F32), 0) * factor
        return gmod, jnp.sum(gmod.astype(F32), 0) * factor, taps[:9], taps[9:]

    gmod, ada_bias_grad, attn_taps, ffn_taps = order(lambda a, b: unpack(join(a, b)), *mods.came)
    while not attn_sum.done():
        order.advance(attn_sum)
    time_in_grad, time_out_grad, ada_weight_grad = order(
        lambda g: condition_back(g, embedded, stages, time_out, ada_weight, factor), gmod
    )
    up_grad = up_sum.finish(order, lambda v: v.astype(F32))
    finals = order(sum_pair, made[0], x_swap(made[1]))
    qkv_rows_grad, out_grad = attn_sum.finish(order, lambda v: (v[: 3 * share].astype(F32), v[3 * share :].astype(F32)))
    qkv_grad = jnp.swapaxes(qkv_rows_grad.reshape(3, share, width), 1, 2)
    final_out = jnp.swapaxes(finals[:per_dev], 1, 2)
    final_grad = jnp.swapaxes(finals[per_dev:], 1, 2)
    return (
        final_out, final_grad, time_in_grad, time_out_grad, ada_weight_grad, ada_bias_grad,
        attn_taps, qkv_grad, out_grad, up_grad, ffn_taps, down_grad,
    )


def solution(mesh):
    tokens = P("wide", None, "narrow")
    weights = (P(None, None, "narrow"), P("narrow", None), P(None, "narrow"), P(None, "narrow"), P("narrow", None))
    return jax.shard_map(
        body,
        mesh=mesh,
        in_specs=(tokens, tokens, P(), P(), P(), P(), P(), P()) + weights,
        out_specs=(tokens, tokens, P(), P(), P(), P(), P()) + weights,
        check_vma=False,
    )
```

```python
import functools
import math

import jax
import jax.numpy as jnp
from jax import lax
from jax.experimental import pallas as pl
from jax.experimental.pallas import tpu as pltpu
from jax.sharding import PartitionSpec as P

HEAD_DIM = 64
FREQ = 256
SIDE = 16
PAIR = 2

BF = jnp.bfloat16
F32 = jnp.float32
HIGHEST = lax.Precision.HIGHEST
LANES = 128
ROWS = 128
FEW_ROWS = 128
BAND = 64
GELU_A = math.sqrt(2.0 / math.pi)
GELU_B = 0.044715
EPS = 1e-06
VMEM_LIMIT = 60 * 1024 * 1024
WEIGHT_ROWS = 256
BACK_ROWS = 64
PACKED = 40


def dot(a, b):
    return lax.dot_general(a, b, (((1,), (0,)), ((), ())), preferred_element_type=F32)


def dot_nt(a, b):
    return lax.dot_general(a, b, (((1,), (1,)), ((), ())), preferred_element_type=F32)


def dot_tn(a, b):
    return lax.dot_general(a, b, (((0,), (0,)), ((), ())), preferred_element_type=F32)


def column_of(rows):
    return lax.broadcasted_iota(jnp.int32, (rows, LANES), 0) % SIDE


def from_left(v):
    moved = pltpu.roll(v, 1, 0)
    return jnp.where(column_of(v.shape[0]) == 0, 0.0, moved)


def from_right(v):
    moved = pltpu.roll(v, v.shape[0] - 1, 0)
    return jnp.where(column_of(v.shape[0]) == SIDE - 1, 0.0, moved)


def conv_band(padded, at, lanes, kern):
    rows = [padded[pl.ds(at + SIDE * r, BAND), lanes] for r in range(3)]
    mixed = [
        rows[0] * kern[c] + rows[1] * kern[3 + c] + rows[2] * kern[6 + c] for c in range(3)
    ]
    return from_left(mixed[0]) + mixed[1] + from_right(mixed[2])


def conv_back_band(padded_grad, at, lanes, kern):
    wide = padded_grad[pl.ds(at, BAND + 2 * SIDE), lanes]
    shifted = [from_right(wide), wide, from_left(wide)]
    total = None
    for r in range(3):
        for c in range(3):
            low = SIDE * (2 - r)
            term = shifted[c][low : low + BAND] * kern[3 * r + c]
            total = term if total is None else total + term
    return total, [s[SIDE : SIDE + BAND] for s in shifted]


def fold_rows(v):
    total = v[0:8]
    for at in range(8, v.shape[0], 8):
        total = total + v[at : at + 8]
    return total


def taps_of(kern_ref, lanes):
    block = kern_ref[:, lanes]
    return [block[t : t + 1] for t in range(9)]


def zero_edges(ref):
    edge = jnp.zeros((SIDE, ref.shape[1]), F32)
    tall = ref.shape[0] // PAIR
    for rel in range(PAIR):
        ref[rel * tall : rel * tall + SIDE, :] = edge
        ref[(rel + 1) * tall - SIDE : (rel + 1) * tall, :] = edge


def inside(ref, rel):
    tall = ref.shape[0] // PAIR
    return slice(rel * tall + SIDE, (rel + 1) * tall - SIDE)


def gather_features(n, parts, held, out):
    _, share, tokens = parts[0].shape
    core = jnp.bitwise_and(n, 1)

    def one(rel):
        for step, part in enumerate(parts):
            held[jnp.bitwise_xor(n, step)] = part[jnp.bitwise_xor(rel, core)]
        out[pl.ds(pl.multiple_of(rel * tokens, tokens), tokens), :] = held[...].reshape(len(parts) * share, tokens).T

    pair_loop(one)


def by_core(core, low, share, keep_out, send_out, turned):
    tokens = low.shape[0] // PAIR

    def one(rel):
        lat = jnp.bitwise_xor(rel, core)
        turned[...] = low[pl.ds(pl.multiple_of(rel * tokens, tokens), tokens), :].T
        for x in range(2):
            here = pl.ds(pl.multiple_of((2 * x + core) * share, 16), share)
            there = pl.ds(pl.multiple_of((2 * x + 1 - core) * share, 16), share)
            keep_out[x, lat] = turned[here, :]
            send_out[x, lat] = turned[there, :]

    pair_loop(one)


def norm_stats(v):
    width = v.shape[1]
    mean = jnp.sum(v, -1, keepdims=True) * (1.0 / width)
    center = v - mean
    spread = jnp.sum(center * center, -1, keepdims=True) * (1.0 / width)
    scale = lax.rsqrt(spread + EPS)
    return center * scale, scale


def head_masks(share):
    lane = lax.broadcasted_iota(jnp.int32, (1, share), 1) // HEAD_DIM
    return [(lane == h).astype(F32).astype(BF) for h in range(share // HEAD_DIM)]


def half_rows(v, parity):
    tokens, width = v.shape
    split = v.reshape(tokens // (2 * SIDE), 2, SIDE, width)
    return split[:, parity].reshape(tokens // 2, width)


def join_rows(even, odd):
    half, width = even.shape
    both = jnp.stack([even.reshape(half // SIDE, SIDE, width), odd.reshape(half // SIDE, SIDE, width)], 1)
    return both.reshape(2 * half, width)


def softmax_rows(queries, keys):
    scores = dot_nt(queries, keys) * (1.0 / math.sqrt(HEAD_DIM))
    rows = lax.broadcasted_iota(jnp.int32, scores.shape, 0)
    cols = lax.broadcasted_iota(jnp.int32, scores.shape, 1)
    same = (rows + cols) % 2 == 0
    scores = jnp.where(same, scores, -1e30)
    top = jnp.max(scores, -1, keepdims=True)
    grown = jnp.where(same, jnp.exp(scores - top), 0.0)
    return grown / jnp.sum(grown, -1, keepdims=True)


def beside(stacked, heads):
    rows = stacked.shape[0] // heads
    return jnp.concatenate([stacked[h * rows : (h + 1) * rows] for h in range(heads)], axis=1)


def lane_loop(width, body):
    count = width // LANES

    def step(j, carry):
        body(j // count, pl.ds(pl.multiple_of((j % count) * LANES, LANES), LANES))
        return carry

    lax.fori_loop(0, PAIR * count, step, 0)


def band_loop(tokens, body, carry):
    return lax.fori_loop(0, tokens // BAND, lambda j, c: body(pl.multiple_of(j * BAND, BAND), c), carry)


def row_loop(tokens, body, size=ROWS):
    count = tokens // size

    def step(j, carry):
        body(j // count, pl.multiple_of(j * size, size))
        return carry

    lax.fori_loop(0, PAIR * count, step, 0)


def pair_loop(body):
    def step(j, carry):
        body(j)
        return carry

    lax.fori_loop(0, PAIR, step, 0)


def attn_kernel_body(
    flow, s_ref, xo, xc, xx, xd, mod, kern, wqkv, wout,
    full_out, grouped_out, q_out, k_out, v_out, ctx_out, keep_out, send_out,
    held, padded,
):
    n = s_ref[0]
    core = jnp.bitwise_and(n, 1)
    share, tokens = xo.shape[1], xo.shape[2]
    width = full_out.shape[1]
    tall = tokens + 2 * SIDE
    zero_edges(padded)
    flow.need(xo, xc, xx, xd, mod, kern)
    gather_features(n, (xo, xc, xx, xd), held, full_out)
    flow.sent(full_out)

    def rows(rel, at):
        lat = jnp.bitwise_xor(rel, core)
        normed, _ = norm_stats(full_out[pl.ds(at, ROWS), :].astype(F32))
        here = pl.ds(pl.multiple_of(at + (2 * rel + 1) * SIDE, SIDE), ROWS)
        padded[here, :] = normed * (1.0 + mod[lat, 1:2, :]) + mod[lat, 0:1, :]

    row_loop(tokens, rows)

    def lanes(rel, at):
        taps = taps_of(kern, at)
        for band in range(0, tokens, BAND):
            here = pl.ds(pl.multiple_of(rel * tokens + band, BAND), BAND)
            grouped_out[here, at] = conv_band(padded, pl.multiple_of(rel * tall + band, SIDE), at, taps).astype(BF)

    lane_loop(width, lanes)
    flow.sent(grouped_out)
    flow.need(wqkv, wout)
    grouped = grouped_out[...]
    q_out[...] = dot_nt(grouped, wqkv[0]).astype(BF)
    k_out[...] = dot_nt(grouped, wqkv[1]).astype(BF)
    v_out[...] = dot_nt(grouped, wqkv[2]).astype(BF)
    flow.sent(q_out, k_out, v_out)
    masks = head_masks(share)
    heads = len(masks)

    def attend(rel):
        here = pl.ds(pl.multiple_of(rel * tokens, tokens), tokens)
        query, key, value = q_out[here, :], k_out[here, :], v_out[here, :]
        parts = []
        for parity in range(2):
            q = half_rows(query, parity)
            k = half_rows(key, parity)
            v = half_rows(value, parity)
            probs = softmax_rows(jnp.concatenate([q * m for m in masks], axis=0), k)
            low = beside(probs.astype(BF), heads)
            parts.append(dot(low, jnp.concatenate([v * m for m in masks], axis=0)).astype(BF))
        ctx_out[here, :] = join_rows(*parts)

    pair_loop(attend)
    flow.sent(ctx_out)
    send_out[...] = dot(ctx_out[tokens : 2 * tokens, :], wout[...]).astype(BF)
    flow.sent(send_out)
    keep_out[...] = dot(ctx_out[0:tokens, :], wout[...]).astype(BF)
    flow.sent(keep_out)


def ffn_kernel_body(
    first, flow, s_ref, go, gc, gx, gd, full, att, mod, up, down, kern, kgrad_in,
    g_out, second_out, active_out, gfed_out, ghid_out, keep_out, send_out, mods_out, kgrad_out, fkeep_out, fsend_out,
    held, padded, slope, gpad, mid, fed, low, sums, turned,
):
    n = s_ref[0]
    core = jnp.bitwise_and(n, 1)
    share, tokens = go.shape[1], go.shape[2]
    units = up.shape[1]
    tall = tokens + 2 * SIDE
    zero_edges(padded)
    zero_edges(gpad)
    flow.need(go, gc, gx, gd)
    gather_features(n, (go, gc, gx, gd), held, g_out)
    flow.sent(g_out)
    flow.need(full, att, mod, kgrad_in)
    kgrad_out[...] = jnp.zeros(kgrad_out.shape, F32) if first else kgrad_in[...]

    def rows(rel, at):
        lat = jnp.bitwise_xor(rel, core)
        here = pl.ds(at, ROWS)
        middle = full[here, :].astype(F32) + mod[lat, 2:3, :] * att[here, :].astype(F32)
        mid[here, :] = middle
        normed, _ = norm_stats(middle)
        second_out[here, :] = (normed * (1.0 + mod[lat, 4:5, :]) + mod[lat, 3:4, :]).astype(BF)
        gfed_out[here, :] = (mod[lat, 5:6, :] * g_out[here, :].astype(F32)).astype(BF)

    row_loop(tokens, rows)
    flow.sent(second_out, gfed_out)
    flow.need(up, kern)
    hidden = dot(second_out[...], up[...])
    for rel in range(PAIR):
        padded[inside(padded, rel), :] = hidden[rel * tokens : (rel + 1) * tokens]

    def lanes(rel, at):
        taps = taps_of(kern, at)
        for band in range(0, tokens, BAND):
            here = pl.ds(pl.multiple_of(rel * tokens + band, BAND), BAND)
            mixed = conv_band(padded, pl.multiple_of(rel * tall + band, SIDE), at, taps)
            square = mixed * mixed
            curve = jnp.tanh(GELU_A * mixed * (1.0 + GELU_B * square))
            half = 0.5 * (1.0 + curve)
            active_out[here, at] = (mixed * half).astype(BF)
            slope[here, at] = half + (0.5 * GELU_A) * mixed * (1.0 - curve * curve) * (
                1.0 + (3.0 * GELU_B) * square
            )

    lane_loop(units, lanes)
    flow.sent(active_out)
    flow.need(down)
    fed[...] = dot(active_out[...], down[...])
    sums[...] = jnp.zeros(sums.shape, F32)

    def rows_fed(rel, at):
        lat = jnp.bitwise_xor(rel, core)
        here = pl.ds(at, ROWS)
        term = fed[here, :]
        sums[lat] += fold_rows(term * g_out[here, :].astype(F32))
        low[here, :] = (mod[lat, 5:6, :] * term + 0.25 * mid[here, :]).astype(BF)

    row_loop(tokens, rows_fed)
    for lat in range(PAIR):
        mods_out[lat] = jnp.sum(sums[lat], 0, keepdims=True)
    by_core(core, low, share, fkeep_out, fsend_out, turned)
    flow.sent(fkeep_out, fsend_out, mods_out)
    gact = dot_nt(gfed_out[...], down[...]).astype(BF).astype(F32)
    for rel in range(PAIR):
        here = slice(rel * tokens, (rel + 1) * tokens)
        gpad[inside(gpad, rel), :] = gact[here] * slope[here, :]

    def lanes_back(rel, at):
        taps = taps_of(kern, at)
        sums = [None] * 9
        for band in range(0, tokens, BAND):
            here = pl.ds(pl.multiple_of(rel * tokens + band, BAND), BAND)
            base = pl.multiple_of(rel * tall + band, SIDE)
            total, shifted = conv_back_band(gpad, base, at, taps)
            ghid_out[here, at] = total.astype(BF)
            for r in range(3):
                values = padded[pl.ds(base + SIDE * r, BAND), at]
                for c in range(3):
                    part = fold_rows(values * shifted[c])
                    sums[3 * r + c] = part if sums[3 * r + c] is None else sums[3 * r + c] + part
        for t in range(9):
            kgrad_out[t : t + 1, at] += jnp.sum(sums[t], 0, keepdims=True)

    lane_loop(units, lanes_back)
    flow.sent(ghid_out, kgrad_out)
    send_out[...] = dot_nt(ghid_out[tokens : 2 * tokens, :], up[...]).astype(BF)
    flow.sent(send_out)
    keep_out[...] = dot_nt(ghid_out[0:tokens, :], up[...]).astype(BF)
    flow.sent(keep_out)


def attn_back_body(
    flow, s_ref, full, att, gs, gfull, mod, q_in, k_in, v_in, wout, gates,
    gatt_out, gqkv_out, gmid_out, mods_out,
    sums, gctx,
):
    core = jnp.bitwise_and(s_ref[0], 1)
    tokens = full.shape[0] // PAIR
    width = full.shape[1]
    share = q_in.shape[1]
    mods_out[...] = jnp.zeros(mods_out.shape, F32)
    sums[...] = jnp.zeros(sums.shape, F32)
    flow.need(full, att, gs, gfull, mod)

    def rows(rel, at):
        lat = jnp.bitwise_xor(rel, core)
        here = pl.ds(at, ROWS)
        gate1 = mod[lat, 2:3, :]
        attended = att[here, :].astype(F32)
        normed, inv = norm_stats(full[here, :].astype(F32) + gate1 * attended)
        grad = gs[here, :].astype(F32)
        inner = grad * (1.0 + mod[lat, 4:5, :])
        mean_a = jnp.sum(inner, -1, keepdims=True) * (1.0 / width)
        mean_b = jnp.sum(inner * normed, -1, keepdims=True) * (1.0 / width)
        whole_grad = gfull[here, :].astype(F32) + inv * (inner - mean_a - normed * mean_b)
        gmid_out[here, :] = whole_grad.astype(BF)
        gatt_out[here, :] = (gate1 * whole_grad).astype(BF)
        sums[3 * lat] += fold_rows(attended * whole_grad)
        sums[3 * lat + 1] += fold_rows(grad)
        sums[3 * lat + 2] += fold_rows(grad * normed)

    row_loop(tokens, rows)
    for lat in range(PAIR):
        for k in range(3):
            mods_out[lat, 2 + k : 3 + k, :] = 0.25 * jnp.sum(sums[3 * lat + k], 0, keepdims=True)
    flow.need(wout, q_in, k_in, v_in, gates)
    for lat in range(PAIR):
        mods_out[lat, 5:6, :] = gates[lat]
    flow.sent(gatt_out, gmid_out, mods_out)
    gctx[...] = dot_nt(gatt_out[...], wout[...]).astype(BF)
    masks = head_masks(share)
    heads = len(masks)
    factor = 1.0 / math.sqrt(HEAD_DIM)

    def attend(rel):
        here = pl.ds(pl.multiple_of(rel * tokens, tokens), tokens)
        query, key, value, grads = q_in[here, :], k_in[here, :], v_in[here, :], gctx[here, :]
        parts_q, parts_k, parts_v = [], [], []
        for parity in range(2):
            q = half_rows(query, parity)
            k = half_rows(key, parity)
            v = half_rows(value, parity)
            gc = half_rows(grads, parity)
            q_all = jnp.concatenate([q * m for m in masks], axis=0)
            k_all = jnp.concatenate([k * m for m in masks], axis=0)
            gc_all = jnp.concatenate([gc * m for m in masks], axis=0)
            probs = softmax_rows(q_all, k)
            parts_v.append(dot_tn(probs.astype(BF), gc_all).astype(BF))
            gprobs = dot_nt(gc_all, v).astype(BF).astype(F32)
            gscores = (probs * (gprobs - jnp.sum(probs * gprobs, -1, keepdims=True))).astype(BF)
            parts_q.append((dot(beside(gscores, heads), k_all) * factor).astype(BF))
            parts_k.append((dot_tn(gscores, q_all) * factor).astype(BF))
        for k, parts in enumerate((parts_q, parts_k, parts_v)):
            gqkv_out[here, k * share : (k + 1) * share] = join_rows(*parts)

    pair_loop(attend)
    flow.sent(gqkv_out)


def input_back_body(
    closing, flow, s_ref, full, mod, gqkv, wqkv, kern, kgrad_in, gmid, mods_in, before,
    kgrad_out, mods_out, keep_out, send_out,
    normed1, scale1, first, gpad, gback, low, mods, rows_out, turned,
):
    core = jnp.bitwise_and(s_ref[0], 1)
    tokens = full.shape[0] // PAIR
    width = full.shape[1]
    share = gqkv.shape[1] // 3
    tall = tokens + 2 * SIDE
    zero_edges(first)
    zero_edges(gpad)
    flow.need(full, mod)

    def rows_first(rel, at):
        lat = jnp.bitwise_xor(rel, core)
        here = pl.ds(at, FEW_ROWS)
        normed, inv = norm_stats(full[here, :].astype(F32))
        normed1[here, :] = normed
        scale1[here, :] = jnp.broadcast_to(inv, (FEW_ROWS, LANES))
        inside_rows = pl.ds(pl.multiple_of(at + (2 * rel + 1) * SIDE, SIDE), FEW_ROWS)
        first[inside_rows, :] = normed * (1.0 + mod[lat, 1:2, :]) + mod[lat, 0:1, :]

    row_loop(tokens, rows_first, FEW_ROWS)
    flow.need(gqkv, wqkv, kern, kgrad_in, gmid, mods_in, before)
    kgrad_out[...] = kgrad_in[...] if closing else jnp.zeros(kgrad_out.shape, F32)
    mods[...] = mods_in[...]
    for rel in range(PAIR):
        here = slice(rel * tokens, (rel + 1) * tokens)
        gpad[inside(gpad, rel), :] = dot(gqkv[here, :], wqkv[...])

    def lanes(rel, at):
        taps = taps_of(kern, at)
        sums = [None] * 9
        shift_sum, scale_sum = None, None
        for band in range(0, tokens, BAND):
            here = pl.ds(pl.multiple_of(rel * tokens + band, BAND), BAND)
            base = pl.multiple_of(rel * tall + band, SIDE)
            total, shifted = conv_back_band(gpad, base, at, taps)
            gback[here, at] = total
            part_a, part_b = fold_rows(total), fold_rows(total * normed1[here, at])
            shift_sum = part_a if shift_sum is None else shift_sum + part_a
            scale_sum = part_b if scale_sum is None else scale_sum + part_b
            for r in range(3):
                values = first[pl.ds(base + SIDE * r, BAND), at]
                for c in range(3):
                    part = fold_rows(values * shifted[c])
                    sums[3 * r + c] = part if sums[3 * r + c] is None else sums[3 * r + c] + part
        for t in range(9):
            kgrad_out[t : t + 1, at] += jnp.sum(sums[t], 0, keepdims=True)
        lat = jnp.bitwise_xor(rel, core)
        mods[lat, 0:1, at] = jnp.sum(shift_sum, 0, keepdims=True)
        mods[lat, 1:2, at] = jnp.sum(scale_sum, 0, keepdims=True)

    lane_loop(width, lanes)
    if closing:
        rows_out[...] = jnp.zeros(rows_out.shape, F32)
        for lat in range(PAIR):
            rows_out[6 * lat : 6 * lat + 6, :] = before[lat, 0:6, :]
            rows_out[6 * (PAIR + lat) : 6 * (PAIR + lat) + 6, :] = mods[lat, 0:6, :]
        rows_out[12 * PAIR : 12 * PAIR + 9, :] = kgrad_out[0:9, :]
        mods_out[...] = rows_out[...].astype(BF)
    else:
        mods_out[...] = mods[...]
    flow.sent(mods_out, kgrad_out)

    def rows_back(rel, at):
        lat = jnp.bitwise_xor(rel, core)
        here = pl.ds(at, FEW_ROWS)
        inner = gback[here, :] * (1.0 + mod[lat, 1:2, :])
        normed = normed1[here, :]
        mean_a = jnp.sum(inner, -1, keepdims=True) * (1.0 / width)
        mean_b = jnp.sum(inner * normed, -1, keepdims=True) * (1.0 / width)
        grad = scale1[here, 0:1] * (inner - mean_a - normed * mean_b)
        low[here, :] = (grad + 0.25 * gmid[here, :].astype(F32)).astype(BF)

    row_loop(tokens, rows_back, FEW_ROWS)
    by_core(core, low, share, keep_out, send_out, turned)
    flow.sent(keep_out, send_out)


class Flow:
    def __init__(self, arrivals, departures):
        self.arrivals, self.departures = arrivals, departures
        self.leaving = []
        for _, copy in arrivals:
            copy.start()

    def need(self, *refs):
        for ref in refs:
            for _, copy in [a for a in self.arrivals if a[0] is ref]:
                copy.wait()
            self.arrivals = [a for a in self.arrivals if a[0] is not ref]

    def sent(self, *refs):
        for ref in refs:
            for held, copy in self.departures:
                if held is ref:
                    copy.start()
                    self.leaving.append(copy)

    def end(self):
        for copy in self.leaving:
            copy.wait()


def call(body, name, scalars, ins, outs, scratch, flops, held=()):
    n_in, n_out = len(ins), len(outs)
    places, buffer_shapes = [], []
    for array, window, into in ins:
        dims = array.shape if window is None else (PAIR,) + array.shape[1:]
        if into is None:
            buffer_shapes.append((dims, array.dtype))
        elif into[0].start == 0:
            buffer_shapes.append(((PAIR * dims[0],) + dims[1:], array.dtype))
        places.append(len(buffer_shapes) - 1)

    def run(s_ref, *refs):
        sources = refs[:n_in]
        targets = refs[n_in + len(held) : n_in + len(held) + n_out]
        buffers = refs[n_in + len(held) + n_out : -1]
        sems = refs[-1]
        n_held = len(buffer_shapes)
        buffers_in, buffers_out = buffers[:n_held], buffers[n_held : n_held + n_out]
        rest = buffers[n_held + n_out :]
        arrivals, departures = [], []
        for k, (source, (_, window, into)) in enumerate(zip(sources, ins)):
            view = source if window is None else source.at[window]
            buffer = buffers_in[places[k]]
            target = buffer if into is None else buffer.at[into]
            arrivals.append((buffer, pltpu.make_async_copy(view, target, sems.at[k])))
        for k, (target, buffer, out) in enumerate(zip(targets, buffers_out, outs)):
            view = target if out[2] is None else target.at[out[2]]
            departures.append((buffer, pltpu.make_async_copy(buffer, view, sems.at[n_in + k])))
        flow = Flow(arrivals, departures)
        body(flow, s_ref, *buffers_in, *buffers_out, *rest)
        flow.end()

    anywhere = pl.BlockSpec(memory_space=pl.ANY)
    return pl.pallas_call(
        run,
        name=name,
        out_shape=[jax.ShapeDtypeStruct(o[0], o[1]) for o in outs],
        grid_spec=pltpu.PrefetchScalarGridSpec(
            num_scalar_prefetch=1,
            grid=(1,),
            in_specs=[anywhere] * (n_in + len(held)),
            out_specs=[anywhere] * n_out,
            scratch_shapes=[pltpu.VMEM(dims, dtype) for dims, dtype in buffer_shapes]
            + [pltpu.VMEM(o[3], o[1]) for o in outs]
            + scratch
            + [pltpu.SemaphoreType.DMA((n_in + n_out,))],
        ),
        input_output_aliases={1 + n_in + k: n_out - len(held) + k for k in range(len(held))},
        compiler_params=pltpu.CompilerParams(vmem_limit_bytes=VMEM_LIMIT),
        cost_estimate=pl.CostEstimate(flops=flops, bytes_accessed=10**6, transcendentals=0),
    )(scalars, *[i[0] for i in ins], *held)


def slices_out(slots, slot, share, tokens):
    return ((2, slots, share, tokens), BF, (slice(None), pl.ds(PAIR * slot, PAIR)), (2, PAIR, share, tokens))


def whole(array):
    return (array, None, None)


def stacked(arrays):
    rows = arrays[0].shape[0]
    return [(v, None, (pl.ds(k * rows, rows),)) for k, v in enumerate(arrays)]


def whole_out(dims, dtype):
    return (dims, dtype, None, dims)


def pair_of(array, pair):
    return (array, (pl.ds(PAIR * pair, PAIR),), None)


def split_low(v):
    high = v.astype(BF)
    return high, (v - high.astype(F32)).astype(BF)


def rows_product(a, b):
    (ah, al), (bh, bl) = split_low(a), split_low(b)
    return dot_tn(jnp.concatenate([ah, al, ah], 0), jnp.concatenate([bh, bh, bl], 0))


def back_product(a, weight):
    (ah, al), (wh, wl) = split_low(a), split_low(weight)
    return dot_nt(ah, wh) + dot_nt(al, wh) + dot_nt(ah, wl)


def product(a, weight):
    (ah, al), (wh, wl) = split_low(a), split_low(weight)
    return dot(ah, wh) + dot(al, wh) + dot(ah, wl)


def silu(v):
    return v / (1.0 + jnp.exp(-v))


def silu_slope(v):
    gate = 1.0 / (1.0 + jnp.exp(-v))
    return gate * (1.0 + v * (1.0 - gate))


def row_blocks(source, target, sems, rows):
    return [
        pltpu.make_async_copy(source.at[pl.ds(at, rows)], target.at[pl.ds(at, rows)], sems.at[at // rows])
        for at in range(0, source.shape[0], rows)
    ]


def condition_body(
    embedded, bias, time_in, time_out, ada, mod_out, inner_pre, inner, outer_pre, outer, held_in, held_out, held, sums, parts, sems,
):
    depth = ada.shape[0]
    per_dev, count, width = mod_out.shape
    first = pltpu.make_async_copy(time_in, held_in, sems.at[0])
    second = pltpu.make_async_copy(time_out, held_out, sems.at[1])
    blocks = row_blocks(ada, held, sems.at[pl.ds(2, depth // WEIGHT_ROWS)], WEIGHT_ROWS)
    for copy in [first, second] + blocks:
        copy.start()
    first.wait()
    inner_pre[...] = product(embedded[...], held_in[...])
    inner[...] = silu(inner_pre[...])
    second.wait()
    outer_pre[...] = product(inner[...], held_out[...])
    outer[...] = silu(outer_pre[...])
    wide_bias = [jnp.concatenate([bias[k + j : k + j + 1, :] for j in range(width // LANES)], 1)
                 for k in range(0, bias.shape[0], width // LANES)]
    total = jnp.concatenate(wide_bias, 1)
    sums[...] = jnp.broadcast_to(total, sums.shape)
    for k in range(depth // WEIGHT_ROWS):
        parts[k] = outer[0:8, k * WEIGHT_ROWS : (k + 1) * WEIGHT_ROWS]

    def add(k, carry):
        rows = pl.ds(pl.multiple_of(k * WEIGHT_ROWS, WEIGHT_ROWS), WEIGHT_ROWS)
        pltpu.make_async_copy(ada.at[rows], held.at[rows], sems.at[2 + k]).wait()
        sums[...] += product(parts[k], held[rows, :])
        return carry

    lax.fori_loop(0, depth // WEIGHT_ROWS, add, 0)
    total = sums[...]
    for lat in range(per_dev):
        for k in range(count):
            mod_out[lat, k : k + 1, :] = total[lat : lat + 1, k * width : (k + 1) * width]


def condition(embedded, time_in, time_out, ada_weight, ada_bias, per_dev, width):
    latent_total = embedded.shape[0]
    depth, columns = ada_weight.shape
    vmem = pl.BlockSpec(memory_space=pltpu.VMEM)
    anywhere = pl.BlockSpec(memory_space=pl.ANY)
    rows = jax.ShapeDtypeStruct((latent_total, depth), F32)
    return pl.pallas_call(
        condition_body,
        name="condition",
        in_specs=[vmem, vmem, anywhere, anywhere, anywhere],
        out_specs=[vmem] * 5,
        out_shape=[jax.ShapeDtypeStruct((per_dev, columns // width, width), F32), rows, rows, rows, rows],
        scratch_shapes=[
            pltpu.VMEM(time_in.shape, F32),
            pltpu.VMEM(time_out.shape, F32),
            pltpu.VMEM(ada_weight.shape, F32),
            pltpu.VMEM((8, columns), F32),
            pltpu.VMEM((depth // WEIGHT_ROWS, 8, WEIGHT_ROWS), F32),
            pltpu.SemaphoreType.DMA((2 + depth // WEIGHT_ROWS,)),
        ],
        compiler_params=pltpu.CompilerParams(vmem_limit_bytes=VMEM_LIMIT),
        cost_estimate=pl.CostEstimate(flops=8 * 10**9, bytes_accessed=10**6, transcendentals=0),
    )(embedded, ada_bias.reshape(columns // LANES, LANES), time_in, time_out, ada_weight)


def condition_back_body(
    factor, gmod, embedded, inner_pre, inner, outer_pre, outer, time_out, ada,
    time_in_grad, time_out_grad, ada_grad, held_out, held, outer_grad, columns, sems, arriving, leaving,
):
    count = ada.shape[0] // BACK_ROWS

    def block_copy(source, target, sem, k):
        rows = pl.ds(k * BACK_ROWS, BACK_ROWS)
        return pltpu.make_async_copy(source.at[rows], target.at[rows], sem.at[k])

    first = pltpu.make_async_copy(time_out, held_out, sems.at[0])
    for k in range(count):
        block_copy(ada, held, arriving, k).start()
    first.start()
    high, low = split_low(outer[...])
    both = jnp.concatenate([high, low], 0)
    for k in range(count):
        columns[k] = both[:, k * BACK_ROWS : (k + 1) * BACK_ROWS]

    def block(k, carry):
        rows = pl.ds(pl.multiple_of(k * BACK_ROWS, BACK_ROWS), BACK_ROWS)
        block_copy(ada, held, arriving, k).wait()
        grads = gmod[...]
        high, low = split_low(held[rows, :])
        outer_grad[rows, :] = dot_nt(high, grads) + dot_nt(low, grads)
        held[rows, :] = dot_tn(columns[k], jnp.concatenate([grads, grads], 0)) * factor
        block_copy(held, ada_grad, leaving, k).start()
        return carry

    lax.fori_loop(0, count, block, 0)
    first.wait()
    back = outer_grad[...].T * factor * silu_slope(outer_pre[...])
    time_out_grad[...] = rows_product(inner[...], back)
    back = back_product(back, held_out[...]) * silu_slope(inner_pre[...])
    time_in_grad[...] = rows_product(embedded[...], back)
    for k in range(count):
        block_copy(held, ada_grad, leaving, k).wait()


def condition_back(gmod, embedded, stages, time_out, ada_weight, factor):
    depth = ada_weight.shape[0]
    latent_total = gmod.shape[0]
    vmem = pl.BlockSpec(memory_space=pltpu.VMEM)
    anywhere = pl.BlockSpec(memory_space=pl.ANY)
    time_in_dims = (embedded.shape[1], time_out.shape[0])
    return pl.pallas_call(
        functools.partial(condition_back_body, factor),
        name="condition_back",
        in_specs=[vmem] * 6 + [anywhere] * 2,
        out_specs=[vmem, vmem, anywhere],
        out_shape=[
            jax.ShapeDtypeStruct(time_in_dims, F32),
            jax.ShapeDtypeStruct(time_out.shape, F32),
            jax.ShapeDtypeStruct(ada_weight.shape, F32),
        ],
        scratch_shapes=[
            pltpu.VMEM(time_out.shape, F32),
            pltpu.VMEM(ada_weight.shape, F32),
            pltpu.VMEM((depth, latent_total), F32),
            pltpu.VMEM((depth // BACK_ROWS, 2 * latent_total, BACK_ROWS), BF),
            pltpu.SemaphoreType.DMA((1,)),
            pltpu.SemaphoreType.DMA((depth // BACK_ROWS,)),
            pltpu.SemaphoreType.DMA((depth // BACK_ROWS,)),
        ],
        compiler_params=pltpu.CompilerParams(vmem_limit_bytes=VMEM_LIMIT),
        cost_estimate=pl.CostEstimate(flops=1, bytes_accessed=1, transcendentals=0),
    )(gmod, embedded, *stages, time_out, ada_weight)


def attn_forward(scalars, pair, x_parts, mod, attn_kernel, qkv_weight, out_weight):
    _, share, tokens = x_parts[0].shape
    width = out_weight.shape[1]
    rows = PAIR * tokens
    thin = whole_out((rows, share), BF)
    half = whole_out((tokens, width), BF)
    return call(
        attn_kernel_body, "attn_fwd", scalars,
        [pair_of(v, pair) for v in x_parts] + [pair_of(mod, pair), whole(attn_kernel), whole(qkv_weight), whole(out_weight)],
        [whole_out((rows, width), BF), whole_out((rows, width), BF), thin, thin, thin, thin, half, half],
        [pltpu.VMEM((4, share, tokens), BF), pltpu.VMEM((PAIR * (tokens + 2 * SIDE), width), F32)],
        6_000_000_000,
    )


def feed_forward(scalars, pair, full, att, g_parts, mod, up_weight, down_weight, ffn_kernel, slots, taps, held):
    _, share, tokens = g_parts[0].shape
    width, units = up_weight.shape
    rows = PAIR * tokens
    tall = PAIR * (tokens + 2 * SIDE)
    broad = whole_out((rows, width), BF)
    hidden = whole_out((rows, units), BF)
    half = whole_out((tokens, width), BF)
    slices = slices_out(slots, pair, share, tokens)
    return call(
        functools.partial(ffn_kernel_body, pair == 0), "ffn", scalars,
        [pair_of(v, pair) for v in g_parts] + [whole(full)] + stacked(att)
        + [pair_of(mod, pair), whole(up_weight), whole(down_weight), whole(ffn_kernel), whole(taps)],
        [broad, broad, hidden, broad, hidden, half, half, whole_out((PAIR, 1, width), F32), whole_out((16, units), F32),
         slices, slices],
        [pltpu.VMEM((4, share, tokens), BF), pltpu.VMEM((tall, units), F32), pltpu.VMEM((rows, units), F32),
         pltpu.VMEM((tall, units), F32), pltpu.VMEM((rows, width), F32), pltpu.VMEM((rows, width), F32),
         pltpu.VMEM((rows, width), BF), pltpu.VMEM((PAIR, 8, width), F32), pltpu.VMEM((width, tokens), BF)],
        10_000_000_000, held,
    )


def attn_backward(scalars, pair, full, att, gsec, gfull, mod, qkv, out_weight, gates):
    tokens, width = att[0].shape
    share = out_weight.shape[0]
    rows = PAIR * tokens
    broad = whole_out((rows, width), BF)
    return call(
        attn_back_body, "attn_bwd", scalars,
        [whole(full)] + stacked(att) + stacked(gsec) + [whole(gfull), pair_of(mod, pair)]
        + [whole(v) for v in qkv] + [whole(out_weight), whole(gates)],
        [broad, whole_out((rows, 3 * share), BF), broad, whole_out((PAIR, 8, width), F32)],
        [pltpu.VMEM((3 * PAIR, 8, width), F32), pltpu.VMEM((rows, share), BF)],
        6_000_000_000,
    )


def input_backward(scalars, pair, full, mod, gqkv, qkv_weight, attn_kernel, taps, gmid, mods_in, before, slots, held):
    rows, width = full.shape
    tokens = rows // PAIR
    share = gqkv.shape[1] // 3
    tall = PAIR * (tokens + 2 * SIDE)
    slices = slices_out(slots, slots // PAIR // 2 + pair, share, tokens)
    closing = pair > 0
    mods = whole_out((PACKED, width), BF) if closing else whole_out((PAIR, 8, width), F32)
    return call(
        functools.partial(input_back_body, closing), "input_bwd", scalars,
        [whole(full), pair_of(mod, pair), whole(gqkv), whole(qkv_weight), whole(attn_kernel), whole(taps), whole(gmid),
         whole(mods_in), whole(before)],
        [whole_out((16, width), F32), mods, slices, slices],
        [pltpu.VMEM((rows, width), F32), pltpu.VMEM((rows, LANES), F32), pltpu.VMEM((tall, width), F32),
         pltpu.VMEM((tall, width), F32), pltpu.VMEM((rows, width), F32), pltpu.VMEM((rows, width), BF),
         pltpu.VMEM((PAIR, 8, width), F32), pltpu.VMEM((PACKED, width), F32), pltpu.VMEM((width, tokens), BF)],
        6_000_000_000, held,
    )


def core_swap(v):
    return lax.ppermute(v, "narrow", [(0, 1), (1, 0), (2, 3), (3, 2)])


def x_swap(v):
    return lax.ppermute(v, "narrow", [(0, 2), (2, 0), (1, 3), (3, 1)])


def sum_pair(a, b):
    return (a.astype(F32) + b.astype(F32)).astype(BF)


def slice_halves(x, keep, arrived):
    both = sum_pair(keep, arrived)
    return (
        lax.dynamic_index_in_dim(both, x, 0, keepdims=False),
        lax.dynamic_index_in_dim(both, 1 - x, 0, keepdims=False),
    )


def wide_swap(v, bit, count):
    return lax.ppermute(v, "wide", [(i, i ^ bit) for i in range(count)])


def pick(v, parts, at):
    rows = v.shape[0] // parts
    return lax.dynamic_slice_in_dim(v, at * rows, rows, 0)


def in_place(second, own, came, axis):
    dims = own.shape[:axis] + (2,) + own.shape[axis + 1 :]
    chosen = lax.broadcast_in_dim(second, dims, (axis,))
    return jnp.where(chosen, own, came)


class WideSum:
    def __init__(self, product, bits, masks, count, back=None):
        self.count, self.dims, self.bits, self.masks = count, product.shape, bits, masks
        self.levels = count.bit_length() - 1
        self.ahead = list(range(self.levels))
        self.back = list(reversed(self.ahead)) if back is None else back
        self.opened = False
        self.held = product

    def swap(self, sent, level):
        self.came = wide_swap(sent, 1 << level, self.count)

    def halve(self, held, came):
        level = self.ahead[0]
        if level == 0:
            held = pick(held, 2, self.bits[0])
        if len(self.ahead) == 1:
            return (sum_pair(held, came),)
        bit = self.bits[level + 1]
        return tuple(sum_pair(pick(held, 2, at), pick(came, 2, at)) for at in (1 - bit, bit))

    def pending(self):
        if not self.opened:
            return lambda v: pick(v, 2, 1 - self.bits[0]), (self.held,)
        if self.ahead:
            return self.halve, (self.held, self.came)
        level = self.back[0]
        return lambda a, b: in_place(self.masks[level], a, b, level), (self.held, self.came)

    def accept(self, out):
        if not self.opened:
            self.opened = True
            self.swap(out, 0)
        elif self.ahead:
            self.ahead.pop(0)
            self.held = out[-1]
            if self.ahead:
                self.swap(out[0], self.ahead[0])
            else:
                self.held = self.held.reshape((1,) * self.levels + self.held.shape)
                self.swap(self.held, self.back[0])
        else:
            self.back.pop(0)
            self.held = out
            self.swap(out, self.back[0])

    def done(self):
        return self.opened and not self.ahead and len(self.back) == 1

    def finish(self, order, dtype):
        level = self.back[0]
        whole_sum = order(lambda a, b: in_place(self.masks[level], a, b, level).astype(dtype), self.held, self.came)
        return lax.optimization_barrier(whole_sum).reshape(self.dims)


class Steps:
    def __init__(self, came, steps):
        self.came, self.steps = came, list(steps)

    def pending(self):
        return self.steps[0][0], self.came

    def accept(self, out):
        _, move = self.steps.pop(0)
        self.came = move(out)

    def done(self):
        return not self.steps


class Order:
    def __init__(self):
        self.last = ()

    def __call__(self, step, *inputs):
        inputs, _ = lax.optimization_barrier((inputs, self.last))
        out = step(*inputs)
        self.last = tuple(jax.tree.leaves(out)[:1])
        return out

    def advance(self, *chains):
        chains = [c for c in chains if not c.done()]
        if chains:
            work = [c.pending() for c in chains]
            outs = self(lambda *v: [w[0](*a) for w, a in zip(work, v)], *[w[1] for w in work])
            self.last = tuple(jax.tree.leaves(out)[0] for out in outs)
            for chain, out in zip(chains, outs):
                chain.accept(out)


def after(value, *others):
    return lax.optimization_barrier((value, others))[0]


def embed_times(stamps):
    halved = FREQ // 2
    freqs = jnp.exp(-math.log(10000.0) * jnp.arange(halved, dtype=F32) / halved)
    angles = stamps[:, None] * freqs[None, :]
    return jnp.concatenate([jnp.cos(angles), jnp.sin(angles)], 1)


def body(
    latents, cotangent, timesteps, time_in, time_out, ada_weight, ada_bias,
    attn_kernel, qkv_weight, out_weight, up_weight, ffn_kernel, down_weight,
):
    wide_count = lax.axis_size("wide")
    wide_at = lax.axis_index("wide")
    n = lax.axis_index("narrow")
    per_dev, tokens, share = latents.shape
    width = out_weight.shape[1]
    units = up_weight.shape[1]
    latent_total = timesteps.shape[0]
    scalars = n.astype(jnp.int32).reshape(1)

    steps, bit = [0], wide_count // 2
    while bit:
        steps, bit = steps + [k ^ bit for k in steps], bit // 2
    met = jnp.bitwise_xor(jnp.array(steps, jnp.int32), wide_at)
    stamps = timesteps.reshape(wide_count, per_dev)[met].reshape(latent_total).astype(F32)
    embedded = embed_times(stamps)
    mod, *stages = condition(embedded, time_in, time_out, ada_weight, ada_bias, per_dev, width)
    x = n // 2
    factor = 1.0 / latent_total

    def token_product(lefts, rights):
        total = None
        for a, b in zip(lefts, rights):
            part = dot_tn(a, b)
            total = part if total is None else total + part
        return (total * factor).astype(BF)

    x_own = jnp.swapaxes(latents, 1, 2)
    g_own = jnp.swapaxes(cotangent, 1, 2)
    qkv_rows = jnp.swapaxes(qkv_weight, 1, 2)
    qkv_all = qkv_rows.reshape(3 * share, width)
    order = Order()
    x_across = x_swap(x_own)
    x_across = after(x_across, mod)
    g_across = x_swap(after(g_own, x_across))
    x_parts = (x_own, core_swap(x_own), x_across, core_swap(x_across))
    g_parts = (g_own, core_swap(g_own), g_across, core_swap(g_across))

    def attend(pair):
        return lambda parts: attn_forward(scalars, pair, parts, mod, attn_kernel, qkv_rows, out_weight)

    fwd_a = order(attend(0), x_parts)
    here_a = order(sum_pair, fwd_a[6], core_swap(fwd_a[7]))
    fwd_b = order(attend(1), after(x_parts, g_across))
    levels = wide_count.bit_length() - 1
    places = [jnp.bitwise_and(jnp.right_shift(wide_at, k), 1) for k in range(levels)]
    masks = [jnp.arange(2, dtype=jnp.int32) == place for place in places]
    att_a, masks = order(lambda a, b, m: (sum_pair(a, b), m), here_a, x_swap(here_a), masks)
    here_b = order(sum_pair, fwd_b[6], core_swap(fwd_b[7]))
    att_a = (att_a, core_swap(att_a))

    slots = 2 * per_dev

    def feed(pair, full, taps, held=()):
        return lambda att, parts: feed_forward(
            scalars, pair, full, att, parts, mod, up_weight, down_weight, ffn_kernel, slots, taps, held
        )

    ffn_a = order(feed(0, fwd_a[0], ffn_kernel), att_a, g_parts)
    att_b = order(sum_pair, here_b, x_swap(here_b))
    att_b = (att_b, core_swap(att_b))
    here_a = order(sum_pair, ffn_a[5], core_swap(ffn_a[6]))
    ffn_b = order(feed(1, fwd_b[0], ffn_a[8], ffn_a[9:11]), att_b, g_parts)
    sec_a = order(sum_pair, here_a, x_swap(here_a))
    sec_a = (sec_a, core_swap(sec_a))
    down_product = order(token_product, [ffn_a[2], ffn_b[2]], [ffn_a[3], ffn_b[3]])
    down_sum = WideSum(down_product, places, masks, wide_count)
    order.advance(down_sum)
    here_b = order(sum_pair, ffn_b[5], core_swap(ffn_b[6]))
    up_product = order(token_product, [ffn_a[1], ffn_b[1]], [ffn_a[4], ffn_b[4]])
    up_sum = WideSum(up_product, places, masks, wide_count)
    order.advance(up_sum)

    def attend_back(pair, fwd, ffn):
        return lambda att, sec: attn_backward(
            scalars, pair, fwd[0], att, sec, ffn[0], mod, fwd[2:5], out_weight, ffn[7]
        )

    def input_back(pair, fwd, taps, before, held):
        return lambda gqkv, gmid, mods: input_backward(
            scalars, pair, fwd[0], mod, gqkv, qkv_all, attn_kernel, taps, gmid, mods, before, slots, held
        )

    back_a = order(attend_back(0, fwd_a, ffn_a), att_a, sec_a)
    sec_b = order(sum_pair, here_b, x_swap(here_b))
    sec_b = (sec_b, core_swap(sec_b))
    order.advance(down_sum)
    back_b = order(attend_back(1, fwd_b, ffn_b), att_b, sec_b)
    order.advance(down_sum)
    attn_product = order(
        lambda grads, grouped, contexts, attended: jnp.concatenate(
            [token_product(grads, grouped), token_product(contexts, attended)], 0
        ),
        [back_a[1], back_b[1]], [fwd_a[1], fwd_b[1]], [fwd_a[5], fwd_b[5]], [back_a[0], back_b[0]],
    )
    attn_sum = WideSum(attn_product, places, masks, wide_count, [0] + list(range(levels - 1, 0, -1)))
    order.advance(attn_sum)
    order.advance(up_sum)
    order.advance(down_sum)
    in_a = order(input_back(0, fwd_a, attn_kernel, attn_kernel, ffn_b[9:11]), *back_a[1:4])
    order.advance(down_sum, up_sum)
    order.advance(attn_sum)
    in_b = order(input_back(1, fwd_b, in_a[0], in_a[1], in_a[2:4]), *back_b[1:4])
    order.advance(down_sum)

    rows = 6 * per_dev
    bits = [1 << k for k in reversed(range(levels))]
    moves = [lambda v, bit=bit: (v, wide_swap(v, bit, wide_count)) for bit in bits]
    join = lambda a, b: jnp.concatenate([a, b], 0)
    whole_rows = lambda a, b, c: join(sum_pair(a, b)[: rows + 9], c[:9].astype(BF))[None]
    mods = Steps(
        (in_b[1], core_swap(in_b[1])),
        [(sum_pair, lambda v: (v, x_swap(v), ffn_b[8]))]
        + [(work, move) for work, move in zip([whole_rows] + [join] * len(bits), moves)],
    )
    order.advance(up_sum)
    order.advance(mods)
    order.advance(attn_sum)
    order.advance(mods)
    order.advance(up_sum)
    while not down_sum.done():
        order.advance(down_sum)
    down_grad = down_sum.finish(order, F32)
    made = order(functools.partial(slice_halves, x), in_b[2], core_swap(in_b[3]))
    order.advance(attn_sum, mods)
    order.advance(mods)
    order.advance(up_sum)
    order.advance(attn_sum)
    while not all(c.done() for c in (mods, up_sum)):
        order.advance(mods)
        order.advance(up_sum)

    def unpack(held):
        gmod = held[:, :rows].reshape(latent_total, 6 * width)
        taps = jnp.sum(held[:, rows:].astype(F32), 0) * factor
        return gmod, jnp.sum(gmod.astype(F32), 0) * factor, taps[:9], taps[9:]

    unpacked = order(lambda a, b: unpack(join(a, b)), *mods.came)
    order.last = tuple(unpacked)
    gmod, ada_bias_grad, attn_taps, ffn_taps = unpacked
    finals = order(sum_pair, made[0], x_swap(made[1]))
    while not attn_sum.done():
        order.advance(attn_sum)
    time_in_grad, time_out_grad, ada_weight_grad = order(
        lambda g: condition_back(g, embedded, stages, time_out, ada_weight, factor), gmod
    )
    up_grad = up_sum.finish(order, F32)
    attn_grads = attn_sum.finish(order, BF)
    qkv_rows_grad, out_grad = attn_grads[: 3 * share].astype(F32), attn_grads[3 * share :].astype(F32)
    qkv_grad = jnp.swapaxes(qkv_rows_grad.reshape(3, share, width), 1, 2)
    final_out = jnp.swapaxes(finals[:per_dev], 1, 2)
    final_grad = jnp.swapaxes(finals[per_dev:], 1, 2)
    return (
        final_out, final_grad, time_in_grad, time_out_grad, ada_weight_grad, ada_bias_grad,
        attn_taps, qkv_grad, out_grad, up_grad, ffn_taps, down_grad,
    )


def solution(mesh):
    tokens = P("wide", None, "narrow")
    weights = (P(None, None, "narrow"), P("narrow", None), P(None, "narrow"), P(None, "narrow"), P("narrow", None))
    return jax.shard_map(
        body,
        mesh=mesh,
        in_specs=(tokens, tokens, P(), P(), P(), P(), P(), P()) + weights,
        out_specs=(tokens, tokens, P(), P(), P(), P(), P()) + weights,
        check_vma=False,
    )
```

```python
import functools
import math

import jax
import jax.numpy as jnp
from jax import lax
from jax.experimental import pallas as pl
from jax.experimental.pallas import tpu as pltpu
from jax.sharding import PartitionSpec as P

HEAD_DIM = 64
SIDE = 16
PAIR = 2
PAIRS = 2

BF = jnp.bfloat16
F32 = jnp.float32
HIGHEST = lax.Precision.HIGHEST
LANES = 128
ROWS = 128
FEW_ROWS = 128
BAND = 64
GELU_A = math.sqrt(2.0 / math.pi)
GELU_B = 0.044715
EPS = 1e-06
VMEM_LIMIT = 60 * 1024 * 1024
WEIGHT_ROWS = 256
BACK_ROWS = 64
PACKED = 40


def dot(a, b):
    return lax.dot_general(a, b, (((1,), (0,)), ((), ())), preferred_element_type=F32)


def dot_nt(a, b):
    return lax.dot_general(a, b, (((1,), (1,)), ((), ())), preferred_element_type=F32)


def dot_tn(a, b):
    return lax.dot_general(a, b, (((0,), (0,)), ((), ())), preferred_element_type=F32)


def column_of(rows):
    return lax.broadcasted_iota(jnp.int32, (rows, LANES), 0) % SIDE


def from_left(v):
    moved = pltpu.roll(v, 1, 0)
    return jnp.where(column_of(v.shape[0]) == 0, 0.0, moved)


def from_right(v):
    moved = pltpu.roll(v, v.shape[0] - 1, 0)
    return jnp.where(column_of(v.shape[0]) == SIDE - 1, 0.0, moved)


def conv_band(padded, at, lanes, kern):
    rows = [padded[pl.ds(at + SIDE * r, BAND), lanes] for r in range(3)]
    mixed = [
        rows[0] * kern[c] + rows[1] * kern[3 + c] + rows[2] * kern[6 + c] for c in range(3)
    ]
    return from_left(mixed[0]) + mixed[1] + from_right(mixed[2])


def conv_back_band(padded_grad, at, lanes, kern):
    wide = padded_grad[pl.ds(at, BAND + 2 * SIDE), lanes]
    shifted = [from_right(wide), wide, from_left(wide)]
    total = None
    for r in range(3):
        for c in range(3):
            low = SIDE * (2 - r)
            term = shifted[c][low : low + BAND] * kern[3 * r + c]
            total = term if total is None else total + term
    return total, [s[SIDE : SIDE + BAND] for s in shifted]


def fold_rows(v):
    total = v[0:8]
    for at in range(8, v.shape[0], 8):
        total = total + v[at : at + 8]
    return total


def taps_of(kern_ref, lanes):
    block = kern_ref[:, lanes]
    return [block[t : t + 1] for t in range(9)]


def zero_edges(ref):
    edge = jnp.zeros((SIDE, ref.shape[1]), F32)
    tall = ref.shape[0] // PAIR
    for rel in range(PAIR):
        ref[rel * tall : rel * tall + SIDE, :] = edge
        ref[(rel + 1) * tall - SIDE : (rel + 1) * tall, :] = edge


def inside(ref, rel):
    tall = ref.shape[0] // PAIR
    return slice(rel * tall + SIDE, (rel + 1) * tall - SIDE)


def gather_features(n, parts, held, out):
    _, share, tokens = parts[0].shape
    core = jnp.bitwise_and(n, 1)

    def one(rel):
        for step, part in enumerate(parts):
            held[jnp.bitwise_xor(n, step)] = part[jnp.bitwise_xor(rel, core)]
        out[pl.ds(pl.multiple_of(rel * tokens, tokens), tokens), :] = held[...].reshape(len(parts) * share, tokens).T

    pair_loop(one)


def by_core(core, low, share, keep_out, send_out, turned):
    tokens = low.shape[0] // PAIR

    def one(rel):
        lat = jnp.bitwise_xor(rel, core)
        turned[...] = low[pl.ds(pl.multiple_of(rel * tokens, tokens), tokens), :].T
        for x in range(2):
            here = pl.ds(pl.multiple_of((2 * x + core) * share, 16), share)
            there = pl.ds(pl.multiple_of((2 * x + 1 - core) * share, 16), share)
            keep_out[x, lat] = turned[here, :]
            send_out[x, lat] = turned[there, :]

    pair_loop(one)


def norm_stats(v):
    width = v.shape[1]
    mean = jnp.sum(v, -1, keepdims=True) * (1.0 / width)
    center = v - mean
    spread = jnp.sum(center * center, -1, keepdims=True) * (1.0 / width)
    scale = lax.rsqrt(spread + EPS)
    return center * scale, scale


def head_masks(share):
    lane = lax.broadcasted_iota(jnp.int32, (1, share), 1) // HEAD_DIM
    return [(lane == h).astype(F32).astype(BF) for h in range(share // HEAD_DIM)]


def half_rows(v, parity):
    tokens, width = v.shape
    split = v.reshape(tokens // (2 * SIDE), 2, SIDE, width)
    return split[:, parity].reshape(tokens // 2, width)


def join_rows(even, odd):
    half, width = even.shape
    both = jnp.stack([even.reshape(half // SIDE, SIDE, width), odd.reshape(half // SIDE, SIDE, width)], 1)
    return both.reshape(2 * half, width)


def softmax_rows(queries, keys):
    scores = dot_nt(queries, keys) * (1.0 / math.sqrt(HEAD_DIM))
    rows = lax.broadcasted_iota(jnp.int32, scores.shape, 0)
    cols = lax.broadcasted_iota(jnp.int32, scores.shape, 1)
    same = (rows + cols) % 2 == 0
    scores = jnp.where(same, scores, -1e30)
    top = jnp.max(scores, -1, keepdims=True)
    grown = jnp.where(same, jnp.exp(scores - top), 0.0)
    return grown / jnp.sum(grown, -1, keepdims=True)


def beside(stacked, heads):
    rows = stacked.shape[0] // heads
    return jnp.concatenate([stacked[h * rows : (h + 1) * rows] for h in range(heads)], axis=1)


def lane_loop(width, body):
    count = width // LANES

    def step(j, carry):
        body(j // count, pl.ds(pl.multiple_of((j % count) * LANES, LANES), LANES))
        return carry

    lax.fori_loop(0, PAIR * count, step, 0)


def band_loop(tokens, body, carry):
    return lax.fori_loop(0, tokens // BAND, lambda j, c: body(pl.multiple_of(j * BAND, BAND), c), carry)


def row_loop(tokens, body, size=ROWS):
    count = tokens // size

    def step(j, carry):
        body(j // count, pl.multiple_of(j * size, size))
        return carry

    lax.fori_loop(0, PAIR * count, step, 0)


def pair_loop(body):
    def step(j, carry):
        body(j)
        return carry

    lax.fori_loop(0, PAIR, step, 0)


def attn_kernel_body(
    flow, s_ref, xo, xc, xx, xd, mod, kern, wqkv, wout,
    full_out, q_out, k_out, v_out, keep_out, send_out, grouped_out, ctx_out,
    held, padded,
):
    n = s_ref[0]
    core = jnp.bitwise_and(n, 1)
    share, tokens = xo.shape[1], xo.shape[2]
    width = full_out.shape[1]
    tall = tokens + 2 * SIDE
    zero_edges(padded)
    flow.need(xo, xc, xx, xd, mod, kern)
    gather_features(n, (xo, xc, xx, xd), held, full_out)
    flow.sent(full_out)

    def rows(rel, at):
        lat = jnp.bitwise_xor(rel, core)
        normed, _ = norm_stats(full_out[pl.ds(at, ROWS), :].astype(F32))
        here = pl.ds(pl.multiple_of(at + (2 * rel + 1) * SIDE, SIDE), ROWS)
        padded[here, :] = normed * (1.0 + mod[lat, 1:2, :]) + mod[lat, 0:1, :]

    row_loop(tokens, rows)

    def lanes(rel, at):
        taps = taps_of(kern, at)
        for band in range(0, tokens, BAND):
            here = pl.ds(pl.multiple_of(rel * tokens + band, BAND), BAND)
            grouped_out[here, at] = conv_band(padded, pl.multiple_of(rel * tall + band, SIDE), at, taps).astype(BF)

    lane_loop(width, lanes)
    flow.sent(grouped_out)
    flow.need(wqkv, wout)
    grouped = grouped_out[...]
    q_out[...] = dot_nt(grouped, wqkv[0]).astype(BF)
    k_out[...] = dot_nt(grouped, wqkv[1]).astype(BF)
    v_out[...] = dot_nt(grouped, wqkv[2]).astype(BF)
    flow.sent(q_out, k_out, v_out)
    masks = head_masks(share)
    heads = len(masks)

    def attend(rel):
        here = pl.ds(pl.multiple_of(rel * tokens, tokens), tokens)
        query, key, value = q_out[here, :], k_out[here, :], v_out[here, :]
        parts = []
        for parity in range(2):
            q = half_rows(query, parity)
            k = half_rows(key, parity)
            v = half_rows(value, parity)
            probs = softmax_rows(jnp.concatenate([q * m for m in masks], axis=0), k)
            low = beside(probs.astype(BF), heads)
            parts.append(dot(low, jnp.concatenate([v * m for m in masks], axis=0)).astype(BF))
        ctx_out[here, :] = join_rows(*parts)

    pair_loop(attend)
    flow.sent(ctx_out)
    send_out[...] = dot(ctx_out[tokens : 2 * tokens, :], wout[...]).astype(BF)
    flow.sent(send_out)
    keep_out[...] = dot(ctx_out[0:tokens, :], wout[...]).astype(BF)
    flow.sent(keep_out)


def ffn_kernel_body(
    first, flow, s_ref, go, gc, gx, gd, full, att, mod, up, down, kern, kgrad_in,
    g_out, keep_out, send_out, mods_out, kgrad_out, active_out, gfed_out, second_out, ghid_out, fkeep_out, fsend_out,
    held, padded, slope, gpad, mid, fed, low, sums, turned,
):
    n = s_ref[0]
    core = jnp.bitwise_and(n, 1)
    share, tokens = go.shape[1], go.shape[2]
    units = up.shape[1]
    tall = tokens + 2 * SIDE
    zero_edges(padded)
    zero_edges(gpad)
    flow.need(go, gc, gx, gd)
    gather_features(n, (go, gc, gx, gd), held, g_out)
    flow.sent(g_out)
    flow.need(full, att, mod, kgrad_in)
    kgrad_out[...] = jnp.zeros(kgrad_out.shape, F32) if first else kgrad_in[...]

    def rows(rel, at):
        lat = jnp.bitwise_xor(rel, core)
        here = pl.ds(at, ROWS)
        middle = full[here, :].astype(F32) + mod[lat, 2:3, :] * att[here, :].astype(F32)
        mid[here, :] = middle
        normed, _ = norm_stats(middle)
        second_out[here, :] = (normed * (1.0 + mod[lat, 4:5, :]) + mod[lat, 3:4, :]).astype(BF)
        gfed_out[here, :] = (mod[lat, 5:6, :] * g_out[here, :].astype(F32)).astype(BF)

    row_loop(tokens, rows)
    flow.sent(second_out, gfed_out)
    flow.need(up, kern)
    hidden = dot(second_out[...], up[...])
    for rel in range(PAIR):
        padded[inside(padded, rel), :] = hidden[rel * tokens : (rel + 1) * tokens]

    def lanes(rel, at):
        taps = taps_of(kern, at)
        for band in range(0, tokens, BAND):
            here = pl.ds(pl.multiple_of(rel * tokens + band, BAND), BAND)
            mixed = conv_band(padded, pl.multiple_of(rel * tall + band, SIDE), at, taps)
            square = mixed * mixed
            curve = jnp.tanh(GELU_A * mixed * (1.0 + GELU_B * square))
            half = 0.5 * (1.0 + curve)
            active_out[here, at] = (mixed * half).astype(BF)
            slope[here, at] = half + (0.5 * GELU_A) * mixed * (1.0 - curve * curve) * (
                1.0 + (3.0 * GELU_B) * square
            )

    lane_loop(units, lanes)
    flow.sent(active_out)
    flow.need(down)
    fed[...] = dot(active_out[...], down[...])
    sums[...] = jnp.zeros(sums.shape, F32)

    def rows_fed(rel, at):
        lat = jnp.bitwise_xor(rel, core)
        here = pl.ds(at, ROWS)
        term = fed[here, :]
        sums[lat] += fold_rows(term * g_out[here, :].astype(F32))
        low[here, :] = (mod[lat, 5:6, :] * term + 0.25 * mid[here, :]).astype(BF)

    row_loop(tokens, rows_fed)
    for lat in range(PAIR):
        mods_out[lat] = jnp.sum(sums[lat], 0, keepdims=True)
    by_core(core, low, share, fkeep_out, fsend_out, turned)
    flow.sent(fkeep_out, fsend_out, mods_out)
    gact = dot_nt(gfed_out[...], down[...]).astype(BF).astype(F32)
    for rel in range(PAIR):
        here = slice(rel * tokens, (rel + 1) * tokens)
        gpad[inside(gpad, rel), :] = gact[here] * slope[here, :]

    def lanes_back(rel, at):
        taps = taps_of(kern, at)
        sums = [None] * 9
        for band in range(0, tokens, BAND):
            here = pl.ds(pl.multiple_of(rel * tokens + band, BAND), BAND)
            base = pl.multiple_of(rel * tall + band, SIDE)
            total, shifted = conv_back_band(gpad, base, at, taps)
            ghid_out[here, at] = total.astype(BF)
            for r in range(3):
                values = padded[pl.ds(base + SIDE * r, BAND), at]
                for c in range(3):
                    part = fold_rows(values * shifted[c])
                    sums[3 * r + c] = part if sums[3 * r + c] is None else sums[3 * r + c] + part
        for t in range(9):
            kgrad_out[t : t + 1, at] += jnp.sum(sums[t], 0, keepdims=True)

    lane_loop(units, lanes_back)
    flow.sent(ghid_out, kgrad_out)
    send_out[...] = dot_nt(ghid_out[tokens : 2 * tokens, :], up[...]).astype(BF)
    flow.sent(send_out)
    keep_out[...] = dot_nt(ghid_out[0:tokens, :], up[...]).astype(BF)
    flow.sent(keep_out)


def attn_back_body(
    flow, s_ref, full, att, gs, gfull, mod, q_in, k_in, v_in, wout, gates,
    gmid_out, mods_out, gatt_out, gqkv_out,
    sums, gctx,
):
    core = jnp.bitwise_and(s_ref[0], 1)
    tokens = full.shape[0] // PAIR
    width = full.shape[1]
    share = q_in.shape[1]
    mods_out[...] = jnp.zeros(mods_out.shape, F32)
    sums[...] = jnp.zeros(sums.shape, F32)
    flow.need(full, att, gs, gfull, mod)

    def rows(rel, at):
        lat = jnp.bitwise_xor(rel, core)
        here = pl.ds(at, ROWS)
        gate1 = mod[lat, 2:3, :]
        attended = att[here, :].astype(F32)
        normed, inv = norm_stats(full[here, :].astype(F32) + gate1 * attended)
        grad = gs[here, :].astype(F32)
        inner = grad * (1.0 + mod[lat, 4:5, :])
        mean_a = jnp.sum(inner, -1, keepdims=True) * (1.0 / width)
        mean_b = jnp.sum(inner * normed, -1, keepdims=True) * (1.0 / width)
        whole_grad = gfull[here, :].astype(F32) + inv * (inner - mean_a - normed * mean_b)
        gmid_out[here, :] = whole_grad.astype(BF)
        gatt_out[here, :] = (gate1 * whole_grad).astype(BF)
        sums[3 * lat] += fold_rows(attended * whole_grad)
        sums[3 * lat + 1] += fold_rows(grad)
        sums[3 * lat + 2] += fold_rows(grad * normed)

    row_loop(tokens, rows)
    for lat in range(PAIR):
        for k in range(3):
            mods_out[lat, 2 + k : 3 + k, :] = 0.25 * jnp.sum(sums[3 * lat + k], 0, keepdims=True)
    flow.need(wout, q_in, k_in, v_in, gates)
    for lat in range(PAIR):
        mods_out[lat, 5:6, :] = gates[lat]
    flow.sent(gatt_out, gmid_out, mods_out)
    gctx[...] = dot_nt(gatt_out[...], wout[...]).astype(BF)
    masks = head_masks(share)
    heads = len(masks)
    factor = 1.0 / math.sqrt(HEAD_DIM)

    def attend(rel):
        here = pl.ds(pl.multiple_of(rel * tokens, tokens), tokens)
        query, key, value, grads = q_in[here, :], k_in[here, :], v_in[here, :], gctx[here, :]
        parts_q, parts_k, parts_v = [], [], []
        for parity in range(2):
            q = half_rows(query, parity)
            k = half_rows(key, parity)
            v = half_rows(value, parity)
            gc = half_rows(grads, parity)
            q_all = jnp.concatenate([q * m for m in masks], axis=0)
            k_all = jnp.concatenate([k * m for m in masks], axis=0)
            gc_all = jnp.concatenate([gc * m for m in masks], axis=0)
            probs = softmax_rows(q_all, k)
            parts_v.append(dot_tn(probs.astype(BF), gc_all).astype(BF))
            gprobs = dot_nt(gc_all, v).astype(BF).astype(F32)
            gscores = (probs * (gprobs - jnp.sum(probs * gprobs, -1, keepdims=True))).astype(BF)
            parts_q.append((dot(beside(gscores, heads), k_all) * factor).astype(BF))
            parts_k.append((dot_tn(gscores, q_all) * factor).astype(BF))
        for k, parts in enumerate((parts_q, parts_k, parts_v)):
            gqkv_out[here, k * share : (k + 1) * share] = join_rows(*parts)

    pair_loop(attend)
    flow.sent(gqkv_out)


def input_back_body(
    closing, flow, s_ref, full, mod, gqkv, wqkv, kern, kgrad_in, gmid, mods_in, before,
    kgrad_out, mods_out, keep_out, send_out,
    normed1, scale1, first, gpad, gback, low, mods, rows_out, turned,
):
    core = jnp.bitwise_and(s_ref[0], 1)
    tokens = full.shape[0] // PAIR
    width = full.shape[1]
    share = gqkv.shape[1] // 3
    tall = tokens + 2 * SIDE
    zero_edges(first)
    zero_edges(gpad)
    flow.need(full, mod)

    def rows_first(rel, at):
        lat = jnp.bitwise_xor(rel, core)
        here = pl.ds(at, FEW_ROWS)
        normed, inv = norm_stats(full[here, :].astype(F32))
        normed1[here, :] = normed
        scale1[here, :] = jnp.broadcast_to(inv, (FEW_ROWS, LANES))
        inside_rows = pl.ds(pl.multiple_of(at + (2 * rel + 1) * SIDE, SIDE), FEW_ROWS)
        first[inside_rows, :] = normed * (1.0 + mod[lat, 1:2, :]) + mod[lat, 0:1, :]

    row_loop(tokens, rows_first, FEW_ROWS)
    flow.need(gqkv, wqkv, kern, kgrad_in, gmid, mods_in, before)
    kgrad_out[...] = kgrad_in[...] if closing else jnp.zeros(kgrad_out.shape, F32)
    mods[...] = mods_in[...]
    for rel in range(PAIR):
        here = slice(rel * tokens, (rel + 1) * tokens)
        gpad[inside(gpad, rel), :] = dot(gqkv[here, :], wqkv[...])

    def lanes(rel, at):
        taps = taps_of(kern, at)
        sums = [None] * 9
        shift_sum, scale_sum = None, None
        for band in range(0, tokens, BAND):
            here = pl.ds(pl.multiple_of(rel * tokens + band, BAND), BAND)
            base = pl.multiple_of(rel * tall + band, SIDE)
            total, shifted = conv_back_band(gpad, base, at, taps)
            gback[here, at] = total
            part_a, part_b = fold_rows(total), fold_rows(total * normed1[here, at])
            shift_sum = part_a if shift_sum is None else shift_sum + part_a
            scale_sum = part_b if scale_sum is None else scale_sum + part_b
            for r in range(3):
                values = first[pl.ds(base + SIDE * r, BAND), at]
                for c in range(3):
                    part = fold_rows(values * shifted[c])
                    sums[3 * r + c] = part if sums[3 * r + c] is None else sums[3 * r + c] + part
        for t in range(9):
            kgrad_out[t : t + 1, at] += jnp.sum(sums[t], 0, keepdims=True)
        lat = jnp.bitwise_xor(rel, core)
        mods[lat, 0:1, at] = jnp.sum(shift_sum, 0, keepdims=True)
        mods[lat, 1:2, at] = jnp.sum(scale_sum, 0, keepdims=True)

    lane_loop(width, lanes)
    if closing:
        rows_out[...] = jnp.zeros(rows_out.shape, F32)
        for lat in range(PAIR):
            rows_out[6 * lat : 6 * lat + 6, :] = before[lat, 0:6, :]
            rows_out[6 * (PAIR + lat) : 6 * (PAIR + lat) + 6, :] = mods[lat, 0:6, :]
        rows_out[12 * PAIR : 12 * PAIR + 9, :] = kgrad_out[0:9, :]
        mods_out[...] = rows_out[...].astype(BF)
    else:
        mods_out[...] = mods[...]
    flow.sent(mods_out, kgrad_out)

    def rows_back(rel, at):
        lat = jnp.bitwise_xor(rel, core)
        here = pl.ds(at, FEW_ROWS)
        inner = gback[here, :] * (1.0 + mod[lat, 1:2, :])
        normed = normed1[here, :]
        mean_a = jnp.sum(inner, -1, keepdims=True) * (1.0 / width)
        mean_b = jnp.sum(inner * normed, -1, keepdims=True) * (1.0 / width)
        grad = scale1[here, 0:1] * (inner - mean_a - normed * mean_b)
        low[here, :] = (grad + 0.25 * gmid[here, :].astype(F32)).astype(BF)

    row_loop(tokens, rows_back, FEW_ROWS)
    by_core(core, low, share, keep_out, send_out, turned)
    flow.sent(keep_out, send_out)


class Flow:
    def __init__(self, arrivals, departures):
        self.arrivals, self.departures = arrivals, departures
        self.leaving = []
        for _, copy in arrivals:
            copy.start()

    def need(self, *refs):
        for ref in refs:
            for _, copy in [a for a in self.arrivals if a[0] is ref]:
                copy.wait()
            self.arrivals = [a for a in self.arrivals if a[0] is not ref]

    def sent(self, *refs):
        for ref in refs:
            for held, copy in self.departures:
                if held is ref:
                    copy.start()
                    self.leaving.append(copy)

    def end(self):
        for copy in self.leaving:
            copy.wait()


def call(body, name, scalars, ins, outs, scratch, flops, held=()):
    n_in, n_out = len(ins), len(outs)
    places, buffer_shapes = [], []
    for array, window, into in ins:
        dims = array.shape if window is None else (window[0].size,) + array.shape[1:]
        if into is None:
            buffer_shapes.append((dims, array.dtype))
        elif into[0].start == 0:
            buffer_shapes.append(((PAIR * dims[0],) + dims[1:], array.dtype))
        places.append(len(buffer_shapes) - 1)

    def run(s_ref, *refs):
        sources = refs[:n_in]
        targets = refs[n_in + len(held) : n_in + len(held) + n_out]
        buffers = refs[n_in + len(held) + n_out : -1]
        sems = refs[-1]
        n_held = len(buffer_shapes)
        buffers_in, buffers_out = buffers[:n_held], buffers[n_held : n_held + n_out]
        rest = buffers[n_held + n_out :]
        arrivals, departures = [], []
        for k, (source, (_, window, into)) in enumerate(zip(sources, ins)):
            view = source if window is None else source.at[window]
            buffer = buffers_in[places[k]]
            target = buffer if into is None else buffer.at[into]
            arrivals.append((buffer, pltpu.make_async_copy(view, target, sems.at[k])))
        for k, (target, buffer, out) in enumerate(zip(targets, buffers_out, outs)):
            view = target if out[2] is None else target.at[out[2]]
            departures.append((buffer, pltpu.make_async_copy(buffer, view, sems.at[n_in + k])))
        flow = Flow(arrivals, departures)
        body(flow, s_ref, *buffers_in, *buffers_out, *rest)
        flow.end()

    anywhere = pl.BlockSpec(memory_space=pl.ANY)
    return pl.pallas_call(
        run,
        name=name,
        out_shape=[jax.ShapeDtypeStruct(o[0], o[1]) for o in outs],
        grid_spec=pltpu.PrefetchScalarGridSpec(
            num_scalar_prefetch=1,
            grid=(1,),
            in_specs=[anywhere] * (n_in + len(held)),
            out_specs=[anywhere] * n_out,
            scratch_shapes=[pltpu.VMEM(dims, dtype) for dims, dtype in buffer_shapes]
            + [pltpu.VMEM(o[3], o[1]) for o in outs]
            + scratch
            + [pltpu.SemaphoreType.DMA((n_in + n_out,))],
        ),
        input_output_aliases={1 + n_in + k: n_out - len(held) + k for k in range(len(held))},
        compiler_params=pltpu.CompilerParams(vmem_limit_bytes=VMEM_LIMIT),
        cost_estimate=pl.CostEstimate(flops=flops, bytes_accessed=10**6, transcendentals=0),
    )(scalars, *[i[0] for i in ins], *held)


def slices_out(slots, slot, share, tokens):
    return ((2, slots, share, tokens), BF, (slice(None), pl.ds(PAIR * slot, PAIR)), (2, PAIR, share, tokens))


def whole(array):
    return (array, None, None)


def stacked(arrays):
    rows = arrays[0].shape[0]
    return [(v, None, (pl.ds(k * rows, rows),)) for k, v in enumerate(arrays)]


def whole_out(dims, dtype):
    return (dims, dtype, None, dims)


def pair_rows(array, pair):
    rows = array.shape[0] // PAIRS
    return (array, (pl.ds(rows * pair, rows),), None)


def pair_rows_out(rows, width, pair):
    return ((PAIRS * rows, width), BF, (pl.ds(rows * pair, rows),), (rows, width))


def pair_of(array, pair):
    return (array, (pl.ds(PAIR * pair, PAIR),), None)


def split_low(v):
    high = v.astype(BF)
    return high, (v - high.astype(F32)).astype(BF)


def rows_product(a, b):
    (ah, al), (bh, bl) = split_low(a), split_low(b)
    return dot_tn(jnp.concatenate([ah, al, ah], 0), jnp.concatenate([bh, bh, bl], 0))


def back_product(a, weight):
    (ah, al), (wh, wl) = split_low(a), split_low(weight)
    return dot_nt(ah, wh) + dot_nt(al, wh) + dot_nt(ah, wl)


def product(a, weight):
    (ah, al), (wh, wl) = split_low(a), split_low(weight)
    return dot(ah, wh) + dot(al, wh) + dot(ah, wl)


def silu(v):
    return v / (1.0 + jnp.exp(-v))


def silu_slope(v):
    gate = 1.0 / (1.0 + jnp.exp(-v))
    return gate * (1.0 + v * (1.0 - gate))


def row_blocks(source, target, sems, rows):
    return [
        pltpu.make_async_copy(source.at[pl.ds(at, rows)], target.at[pl.ds(at, rows)], sems.at[at // rows])
        for at in range(0, source.shape[0], rows)
    ]


def condition_body(
    steps, stamps, wide, bias, time_in, time_out, ada,
    mod_out, embedded, inner_pre, inner, outer_pre, outer, held_in, held_out, held, sums, parts, rows_of, sems,
):
    depth = ada.shape[0]
    per_dev, count, width = mod_out.shape
    first = pltpu.make_async_copy(time_in, held_in, sems.at[0])
    second = pltpu.make_async_copy(time_out, held_out, sems.at[1])
    blocks = row_blocks(ada, held, sems.at[pl.ds(2, depth // WEIGHT_ROWS)], WEIGHT_ROWS)
    for copy in [first, second] + blocks:
        copy.start()
    halved = embedded.shape[1] // 2
    for r in range(embedded.shape[0]):
        at = jnp.bitwise_xor(wide[0], steps[r // per_dev]) * per_dev + r % per_dev
        rows_of[r : r + 1, :] = jnp.broadcast_to(stamps[at].astype(F32), (1, halved))
    order = lax.broadcasted_iota(jnp.int32, (1, halved), 1).astype(F32)
    angles = rows_of[...] * jnp.exp(-math.log(10000.0) * order / halved)
    embedded[:, 0:halved] = jnp.cos(angles)
    embedded[:, halved:] = jnp.sin(angles)
    first.wait()
    inner_pre[...] = product(embedded[...], held_in[...])
    inner[...] = silu(inner_pre[...])
    second.wait()
    outer_pre[...] = product(inner[...], held_out[...])
    outer[...] = silu(outer_pre[...])
    wide_bias = [jnp.concatenate([bias[k + j : k + j + 1, :] for j in range(width // LANES)], 1)
                 for k in range(0, bias.shape[0], width // LANES)]
    total = jnp.concatenate(wide_bias, 1)
    sums[...] = jnp.broadcast_to(total, sums.shape)
    for k in range(depth // WEIGHT_ROWS):
        parts[k] = outer[0:8, k * WEIGHT_ROWS : (k + 1) * WEIGHT_ROWS]

    def add(k, carry):
        rows = pl.ds(pl.multiple_of(k * WEIGHT_ROWS, WEIGHT_ROWS), WEIGHT_ROWS)
        pltpu.make_async_copy(ada.at[rows], held.at[rows], sems.at[2 + k]).wait()
        sums[...] += product(parts[k], held[rows, :])
        return carry

    lax.fori_loop(0, depth // WEIGHT_ROWS, add, 0)
    total = sums[...]
    for lat in range(per_dev):
        for k in range(count):
            mod_out[lat, k : k + 1, :] = total[lat : lat + 1, k * width : (k + 1) * width]


def condition(steps, stamps, wide, time_in, time_out, ada_weight, ada_bias, per_dev, width):
    latent_total = stamps.shape[0]
    depth, columns = ada_weight.shape
    vmem = pl.BlockSpec(memory_space=pltpu.VMEM)
    anywhere = pl.BlockSpec(memory_space=pl.ANY)
    rows = jax.ShapeDtypeStruct((latent_total, depth), F32)
    return pl.pallas_call(
        functools.partial(condition_body, steps),
        name="condition",
        in_specs=[pl.BlockSpec(memory_space=pltpu.SMEM)] * 2 + [vmem, anywhere, anywhere, anywhere],
        out_specs=[vmem] * 6,
        out_shape=[
            jax.ShapeDtypeStruct((per_dev, columns // width, width), F32),
            jax.ShapeDtypeStruct((latent_total, time_in.shape[0]), F32),
            rows, rows, rows, rows,
        ],
        scratch_shapes=[
            pltpu.VMEM(time_in.shape, F32),
            pltpu.VMEM(time_out.shape, F32),
            pltpu.VMEM(ada_weight.shape, F32),
            pltpu.VMEM((8, columns), F32),
            pltpu.VMEM((depth // WEIGHT_ROWS, 8, WEIGHT_ROWS), F32),
            pltpu.VMEM((latent_total, time_in.shape[0] // 2), F32),
            pltpu.SemaphoreType.DMA((2 + depth // WEIGHT_ROWS,)),
        ],
        compiler_params=pltpu.CompilerParams(vmem_limit_bytes=VMEM_LIMIT),
        cost_estimate=pl.CostEstimate(flops=8 * 10**9, bytes_accessed=10**6, transcendentals=0),
    )(stamps, wide, ada_bias.reshape(columns // LANES, LANES), time_in, time_out, ada_weight)


def condition_back_body(
    factor, gmod, embedded, inner_pre, inner, outer_pre, outer, time_out, ada,
    time_in_grad, time_out_grad, ada_grad, held_out, held, outer_grad, columns, sems, arriving, leaving,
):
    count = ada.shape[0] // BACK_ROWS

    def block_copy(source, target, sem, k):
        rows = pl.ds(k * BACK_ROWS, BACK_ROWS)
        return pltpu.make_async_copy(source.at[rows], target.at[rows], sem.at[k])

    first = pltpu.make_async_copy(time_out, held_out, sems.at[0])
    for k in range(count):
        block_copy(ada, held, arriving, k).start()
    first.start()
    high, low = split_low(outer[...])
    both = jnp.concatenate([high, low], 0)
    for k in range(count):
        columns[k] = both[:, k * BACK_ROWS : (k + 1) * BACK_ROWS]

    def block(k, carry):
        rows = pl.ds(pl.multiple_of(k * BACK_ROWS, BACK_ROWS), BACK_ROWS)
        block_copy(ada, held, arriving, k).wait()
        grads = gmod[...]
        high, low = split_low(held[rows, :])
        outer_grad[rows, :] = dot_nt(high, grads) + dot_nt(low, grads)
        held[rows, :] = dot_tn(columns[k], jnp.concatenate([grads, grads], 0)) * factor
        block_copy(held, ada_grad, leaving, k).start()
        return carry

    lax.fori_loop(0, count, block, 0)
    first.wait()
    back = outer_grad[...].T * factor * silu_slope(outer_pre[...])
    time_out_grad[...] = rows_product(inner[...], back)
    back = back_product(back, held_out[...]) * silu_slope(inner_pre[...])
    time_in_grad[...] = rows_product(embedded[...], back)
    for k in range(count):
        block_copy(held, ada_grad, leaving, k).wait()


def condition_back(gmod, embedded, stages, time_out, ada_weight, factor):
    depth = ada_weight.shape[0]
    latent_total = gmod.shape[0]
    vmem = pl.BlockSpec(memory_space=pltpu.VMEM)
    anywhere = pl.BlockSpec(memory_space=pl.ANY)
    time_in_dims = (embedded.shape[1], time_out.shape[0])
    return pl.pallas_call(
        functools.partial(condition_back_body, factor),
        name="condition_back",
        in_specs=[vmem] * 6 + [anywhere] * 2,
        out_specs=[vmem, vmem, anywhere],
        out_shape=[
            jax.ShapeDtypeStruct(time_in_dims, F32),
            jax.ShapeDtypeStruct(time_out.shape, F32),
            jax.ShapeDtypeStruct(ada_weight.shape, F32),
        ],
        scratch_shapes=[
            pltpu.VMEM(time_out.shape, F32),
            pltpu.VMEM(ada_weight.shape, F32),
            pltpu.VMEM((depth, latent_total), F32),
            pltpu.VMEM((depth // BACK_ROWS, 2 * latent_total, BACK_ROWS), BF),
            pltpu.SemaphoreType.DMA((1,)),
            pltpu.SemaphoreType.DMA((depth // BACK_ROWS,)),
            pltpu.SemaphoreType.DMA((depth // BACK_ROWS,)),
        ],
        compiler_params=pltpu.CompilerParams(vmem_limit_bytes=VMEM_LIMIT),
        cost_estimate=pl.CostEstimate(flops=1, bytes_accessed=1, transcendentals=0),
    )(gmod, embedded, *stages, time_out, ada_weight)


def attn_forward(scalars, pair, x_parts, mod, attn_kernel, qkv_weight, out_weight, held):
    _, share, tokens = x_parts[0].shape
    width = out_weight.shape[1]
    rows = PAIR * tokens
    thin = whole_out((rows, share), BF)
    half = whole_out((tokens, width), BF)
    return call(
        attn_kernel_body, "attn_fwd", scalars,
        [pair_of(v, pair) for v in x_parts] + [pair_of(mod, pair), whole(attn_kernel), whole(qkv_weight), whole(out_weight)],
        [whole_out((rows, width), BF), thin, thin, thin, half, half, pair_rows_out(rows, width, pair),
         pair_rows_out(rows, share, pair)],
        [pltpu.VMEM((4, share, tokens), BF), pltpu.VMEM((PAIR * (tokens + 2 * SIDE), width), F32)],
        6_000_000_000, held,
    )


def feed_forward(scalars, pair, full, att, g_parts, mod, up_weight, down_weight, ffn_kernel, slots, taps, held):
    _, share, tokens = g_parts[0].shape
    width, units = up_weight.shape
    rows = PAIR * tokens
    tall = PAIR * (tokens + 2 * SIDE)
    half = whole_out((tokens, width), BF)
    slices = slices_out(slots, pair, share, tokens)
    return call(
        functools.partial(ffn_kernel_body, pair == 0), "ffn", scalars,
        [pair_of(v, pair) for v in g_parts] + [whole(full)] + stacked(att)
        + [pair_of(mod, pair), whole(up_weight), whole(down_weight), whole(ffn_kernel), whole(taps)],
        [whole_out((rows, width), BF), half, half, whole_out((PAIR, 1, width), F32), whole_out((16, units), F32),
         whole_out((rows, units), BF), whole_out((rows, width), BF), pair_rows_out(rows, width, pair),
         pair_rows_out(rows, units, pair), slices, slices],
        [pltpu.VMEM((4, share, tokens), BF), pltpu.VMEM((tall, units), F32), pltpu.VMEM((rows, units), F32),
         pltpu.VMEM((tall, units), F32), pltpu.VMEM((rows, width), F32), pltpu.VMEM((rows, width), F32),
         pltpu.VMEM((rows, width), BF), pltpu.VMEM((PAIR, 8, width), F32), pltpu.VMEM((width, tokens), BF)],
        10_000_000_000, held,
    )


def attn_backward(scalars, pair, full, att, gsec, gfull, mod, qkv, out_weight, gates, held):
    tokens, width = att[0].shape
    share = out_weight.shape[0]
    rows = PAIR * tokens
    broad = whole_out((rows, width), BF)
    return call(
        attn_back_body, "attn_bwd", scalars,
        [whole(full)] + stacked(att) + stacked(gsec) + [whole(gfull), pair_of(mod, pair)]
        + [whole(v) for v in qkv] + [whole(out_weight), whole(gates)],
        [broad, whole_out((PAIR, 8, width), F32), pair_rows_out(rows, width, pair), pair_rows_out(rows, 3 * share, pair)],
        [pltpu.VMEM((3 * PAIR, 8, width), F32), pltpu.VMEM((rows, share), BF)],
        6_000_000_000, held,
    )


def input_backward(scalars, pair, full, mod, gqkv, qkv_weight, attn_kernel, taps, gmid, mods_in, before, slots, held):
    rows, width = full.shape
    tokens = rows // PAIR
    share = gqkv.shape[1] // 3
    tall = PAIR * (tokens + 2 * SIDE)
    slices = slices_out(slots, slots // PAIR // 2 + pair, share, tokens)
    closing = pair > 0
    mods = whole_out((PACKED, width), BF) if closing else whole_out((PAIR, 8, width), F32)
    return call(
        functools.partial(input_back_body, closing), "input_bwd", scalars,
        [whole(full), pair_of(mod, pair), pair_rows(gqkv, pair), whole(qkv_weight), whole(attn_kernel), whole(taps), whole(gmid),
         whole(mods_in), whole(before)],
        [whole_out((16, width), F32), mods, slices, slices],
        [pltpu.VMEM((rows, width), F32), pltpu.VMEM((rows, LANES), F32), pltpu.VMEM((tall, width), F32),
         pltpu.VMEM((tall, width), F32), pltpu.VMEM((rows, width), F32), pltpu.VMEM((rows, width), BF),
         pltpu.VMEM((PAIR, 8, width), F32), pltpu.VMEM((PACKED, width), F32), pltpu.VMEM((width, tokens), BF)],
        6_000_000_000, held,
    )


def core_swap(v):
    return lax.ppermute(v, "narrow", [(0, 1), (1, 0), (2, 3), (3, 2)])


def x_swap(v):
    return lax.ppermute(v, "narrow", [(0, 2), (2, 0), (1, 3), (3, 1)])


def sum_pair(a, b):
    return (a.astype(F32) + b.astype(F32)).astype(BF)


def slice_halves(x, keep, arrived):
    both = sum_pair(keep, arrived)
    return (
        lax.dynamic_index_in_dim(both, x, 0, keepdims=False),
        lax.dynamic_index_in_dim(both, 1 - x, 0, keepdims=False),
    )


def wide_swap(v, bit, count):
    return lax.ppermute(v, "wide", [(i, i ^ bit) for i in range(count)])


def pick(v, parts, at):
    rows = v.shape[0] // parts
    return lax.dynamic_slice_in_dim(v, at * rows, rows, 0)


def in_place(second, own, came, axis):
    dims = own.shape[:axis] + (2,) + own.shape[axis + 1 :]
    chosen = lax.broadcast_in_dim(second, dims, (axis,))
    return jnp.where(chosen, own, came)


class WideSum:
    def __init__(self, product, bits, masks, count, back=None):
        self.count, self.dims, self.bits, self.masks = count, product.shape, bits, masks
        self.levels = count.bit_length() - 1
        self.ahead = list(range(self.levels))
        self.back = list(reversed(self.ahead)) if back is None else back
        self.opened = False
        self.held = product

    def swap(self, sent, level):
        self.came = wide_swap(sent, 1 << level, self.count)

    def halve(self, held, came):
        level = self.ahead[0]
        if level == 0:
            held = pick(held, 2, self.bits[0])
        if len(self.ahead) == 1:
            return (sum_pair(held, came),)
        bit = self.bits[level + 1]
        return tuple(sum_pair(pick(held, 2, at), pick(came, 2, at)) for at in (1 - bit, bit))

    def pending(self):
        if not self.opened:
            return lambda v: pick(v, 2, 1 - self.bits[0]), (self.held,)
        if self.ahead:
            return self.halve, (self.held, self.came)
        level = self.back[0]
        return lambda a, b: in_place(self.masks[level], a, b, level), (self.held, self.came)

    def accept(self, out):
        if not self.opened:
            self.opened = True
            self.swap(out, 0)
        elif self.ahead:
            self.ahead.pop(0)
            self.held = out[-1]
            if self.ahead:
                self.swap(out[0], self.ahead[0])
            else:
                self.held = self.held.reshape((1,) * self.levels + self.held.shape)
                self.swap(self.held, self.back[0])
        else:
            self.back.pop(0)
            self.held = out
            self.swap(out, self.back[0])

    def done(self):
        return self.opened and not self.ahead and len(self.back) == 1

    def finish(self, order, dtype):
        level = self.back[0]
        whole_sum = order(lambda a, b: in_place(self.masks[level], a, b, level).astype(dtype), self.held, self.came)
        return lax.optimization_barrier(whole_sum).reshape(self.dims)


class Steps:
    def __init__(self, came, steps):
        self.came, self.steps = came, list(steps)

    def pending(self):
        return self.steps[0][0], self.came

    def accept(self, out):
        _, move = self.steps.pop(0)
        self.came = move(out)

    def done(self):
        return not self.steps


class Order:
    def __init__(self):
        self.last = ()

    def __call__(self, step, *inputs):
        inputs, _ = lax.optimization_barrier((inputs, self.last))
        out = step(*inputs)
        self.last = tuple(jax.tree.leaves(out)[:1])
        return out

    def advance(self, *chains):
        chains = [c for c in chains if not c.done()]
        if chains:
            work = [c.pending() for c in chains]
            outs = self(lambda *v: [w[0](*a) for w, a in zip(work, v)], *[w[1] for w in work])
            self.last = tuple(jax.tree.leaves(out)[0] for out in outs)
            for chain, out in zip(chains, outs):
                chain.accept(out)


def after(value, *others):
    return lax.optimization_barrier((value, others))[0]


def body(
    latents, cotangent, timesteps, time_in, time_out, ada_weight, ada_bias,
    attn_kernel, qkv_weight, out_weight, up_weight, ffn_kernel, down_weight,
):
    wide_count = lax.axis_size("wide")
    wide_at = lax.axis_index("wide")
    n = lax.axis_index("narrow")
    per_dev, tokens, share = latents.shape
    width = out_weight.shape[1]
    units = up_weight.shape[1]
    latent_total = timesteps.shape[0]
    scalars = n.astype(jnp.int32).reshape(1)

    steps, bit = [0], wide_count // 2
    while bit:
        steps, bit = steps + [k ^ bit for k in steps], bit // 2
    mod, embedded, *stages = condition(
        steps, timesteps, wide_at.astype(jnp.int32).reshape(1), time_in, time_out, ada_weight, ada_bias, per_dev, width
    )
    x = n // 2
    factor = 1.0 / latent_total

    def token_products(lefts, rights):
        return (sum(dot_tn(a, b) for a, b in zip(lefts, rights)) * factor).astype(BF)

    x_own = jnp.swapaxes(latents, 1, 2)
    g_own = jnp.swapaxes(cotangent, 1, 2)
    qkv_rows = jnp.swapaxes(qkv_weight, 1, 2)
    qkv_all = qkv_rows.reshape(3 * share, width)
    order = Order()
    x_across = x_swap(x_own)
    x_across = after(x_across, mod)
    g_across = x_swap(after(g_own, x_across))
    x_parts = (x_own, core_swap(x_own), x_across, core_swap(x_across))
    g_parts = (g_own, core_swap(g_own), g_across, core_swap(g_across))

    def attend(pair, held=()):
        return lambda parts: attn_forward(scalars, pair, parts, mod, attn_kernel, qkv_rows, out_weight, held)

    fwd_a = order(attend(0), x_parts)
    here_a = order(sum_pair, fwd_a[4], core_swap(fwd_a[5]))
    fwd_b = order(attend(1, fwd_a[6:8]), after(x_parts, g_across))
    levels = wide_count.bit_length() - 1
    places = [jnp.bitwise_and(jnp.right_shift(wide_at, k), 1) for k in range(levels)]
    masks = [jnp.arange(2, dtype=jnp.int32) == place for place in places]
    att_a, masks = order(lambda a, b, m: (sum_pair(a, b), m), here_a, x_swap(here_a), masks)
    here_b = order(sum_pair, fwd_b[4], core_swap(fwd_b[5]))
    att_a = (att_a, core_swap(att_a))

    slots = 2 * per_dev

    def feed(pair, full, taps, held=()):
        return lambda att, parts: feed_forward(
            scalars, pair, full, att, parts, mod, up_weight, down_weight, ffn_kernel, slots, taps, held
        )

    ffn_a = order(feed(0, fwd_a[0], ffn_kernel), att_a, g_parts)
    att_b = order(sum_pair, here_b, x_swap(here_b))
    att_b = (att_b, core_swap(att_b))
    here_a = order(sum_pair, ffn_a[1], core_swap(ffn_a[2]))
    ffn_b = order(feed(1, fwd_b[0], ffn_a[4], ffn_a[7:11]), att_b, g_parts)
    sec_a = order(sum_pair, here_a, x_swap(here_a))
    sec_a = (sec_a, core_swap(sec_a))
    down_product = order(token_products, [ffn_a[5], ffn_b[5]], [ffn_a[6], ffn_b[6]])
    down_sum = WideSum(down_product, places, masks, wide_count)
    order.advance(down_sum)
    here_b = order(sum_pair, ffn_b[1], core_swap(ffn_b[2]))
    up_product = order(token_products, [ffn_b[7]], [ffn_b[8]])
    up_sum = WideSum(up_product, places, masks, wide_count)
    order.advance(up_sum)

    def attend_back(pair, fwd, ffn, held=()):
        return lambda att, sec: attn_backward(
            scalars, pair, fwd[0], att, sec, ffn[0], mod, fwd[1:4], out_weight, ffn[3], held
        )

    def input_back(pair, fwd, taps, before, held):
        return lambda gqkv, gmid, mods: input_backward(
            scalars, pair, fwd[0], mod, gqkv, qkv_all, attn_kernel, taps, gmid, mods, before, slots, held
        )

    back_a = order(attend_back(0, fwd_a, ffn_a), att_a, sec_a)
    sec_b = order(sum_pair, here_b, x_swap(here_b))
    sec_b = (sec_b, core_swap(sec_b))
    order.advance(down_sum)
    back_b = order(attend_back(1, fwd_b, ffn_b, back_a[2:4]), att_b, sec_b)
    order.advance(down_sum)
    attn_product = order(
        lambda grads, grouped, contexts, attended: jnp.concatenate(
            [token_products([grads], [grouped]), token_products([contexts], [attended])], 0
        ),
        back_b[3], fwd_b[6], fwd_b[7], back_b[2],
    )
    attn_sum = WideSum(attn_product, places, masks, wide_count, [0] + list(range(levels - 1, 0, -1)))
    order.advance(attn_sum)
    order.advance(up_sum)
    order.advance(down_sum)
    in_a = order(input_back(0, fwd_a, attn_kernel, attn_kernel, ffn_b[9:11]), back_b[3], *back_a[:2])
    order.advance(down_sum, up_sum)
    order.advance(attn_sum)
    in_b = order(input_back(1, fwd_b, in_a[0], in_a[1], in_a[2:4]), back_b[3], *back_b[:2])
    order.advance(down_sum)

    rows = 6 * per_dev
    bits = [1 << k for k in reversed(range(levels))]
    moves = [lambda v, bit=bit: (v, wide_swap(v, bit, wide_count)) for bit in bits]
    join = lambda a, b: jnp.concatenate([a, b], 0)
    whole_rows = lambda a, b, c: join(sum_pair(a, b)[: rows + 9], c[:9].astype(BF))[None]
    mods = Steps(
        (in_b[1], core_swap(in_b[1])),
        [(sum_pair, lambda v: (v, x_swap(v), ffn_b[4]))]
        + [(work, move) for work, move in zip([whole_rows] + [join] * len(bits), moves)],
    )
    order.advance(up_sum)
    order.advance(mods)
    order.advance(attn_sum)
    order.advance(mods)
    order.advance(up_sum)
    while not down_sum.done():
        order.advance(down_sum)
    down_grad = down_sum.finish(order, F32)
    made = order(functools.partial(slice_halves, x), in_b[2], core_swap(in_b[3]))
    order.advance(attn_sum, mods)
    order.advance(mods)
    order.advance(up_sum)
    order.advance(attn_sum)
    while not all(c.done() for c in (mods, up_sum)):
        order.advance(mods)
        order.advance(up_sum)

    def unpack(held):
        gmod = held[:, :rows].reshape(latent_total, 6 * width)
        taps = jnp.sum(held[:, rows:].astype(F32), 0) * factor
        return gmod, jnp.sum(gmod.astype(F32), 0) * factor, taps[:9], taps[9:]

    unpacked = order(lambda a, b: unpack(join(a, b)), *mods.came)
    order.last = tuple(unpacked)
    gmod, ada_bias_grad, attn_taps, ffn_taps = unpacked
    finals = order(sum_pair, made[0], x_swap(made[1]))
    while not attn_sum.done():
        order.advance(attn_sum)
    time_in_grad, time_out_grad, ada_weight_grad = order(
        lambda g: condition_back(g, embedded, stages, time_out, ada_weight, factor), gmod
    )
    up_grad = up_sum.finish(order, F32)
    attn_grads = attn_sum.finish(order, BF)
    qkv_rows_grad, out_grad = attn_grads[: 3 * share].astype(F32), attn_grads[3 * share :].astype(F32)
    qkv_grad = jnp.swapaxes(qkv_rows_grad.reshape(3, share, width), 1, 2)
    final_out = jnp.swapaxes(finals[:per_dev], 1, 2)
    final_grad = jnp.swapaxes(finals[per_dev:], 1, 2)
    return (
        final_out, final_grad, time_in_grad, time_out_grad, ada_weight_grad, ada_bias_grad,
        attn_taps, qkv_grad, out_grad, up_grad, ffn_taps, down_grad,
    )


def solution(mesh):
    tokens = P("wide", None, "narrow")
    weights = (P(None, None, "narrow"), P("narrow", None), P(None, "narrow"), P(None, "narrow"), P("narrow", None))
    return jax.shard_map(
        body,
        mesh=mesh,
        in_specs=(tokens, tokens, P(), P(), P(), P(), P(), P()) + weights,
        out_specs=(tokens, tokens, P(), P(), P(), P(), P()) + weights,
        check_vma=False,
    )
```

```python
import functools
import math

import jax
import jax.numpy as jnp
from jax import lax
from jax.experimental import pallas as pl
from jax.experimental.pallas import tpu as pltpu
from jax.sharding import PartitionSpec as P

HEAD_DIM = 64
SIDE = 16
PAIR = 2
PAIRS = 2

BF = jnp.bfloat16
F32 = jnp.float32
HIGHEST = lax.Precision.HIGHEST
LANES = 128
ROWS = 128
FEW_ROWS = 128
BAND = 64
GELU_A = math.sqrt(2.0 / math.pi)
GELU_B = 0.044715
EPS = 1e-06
VMEM_LIMIT = 60 * 1024 * 1024
WEIGHT_ROWS = 256
BACK_ROWS = 64
PACKED = 40


def dot(a, b):
    return lax.dot_general(a, b, (((1,), (0,)), ((), ())), preferred_element_type=F32)


def dot_nt(a, b):
    return lax.dot_general(a, b, (((1,), (1,)), ((), ())), preferred_element_type=F32)


def dot_tn(a, b):
    return lax.dot_general(a, b, (((0,), (0,)), ((), ())), preferred_element_type=F32)


def column_of(rows):
    return lax.broadcasted_iota(jnp.int32, (rows, LANES), 0) % SIDE


def from_left(v):
    moved = pltpu.roll(v, 1, 0)
    return jnp.where(column_of(v.shape[0]) == 0, 0.0, moved)


def from_right(v):
    moved = pltpu.roll(v, v.shape[0] - 1, 0)
    return jnp.where(column_of(v.shape[0]) == SIDE - 1, 0.0, moved)


def conv_band(padded, at, lanes, kern):
    rows = [padded[pl.ds(at + SIDE * r, BAND), lanes] for r in range(3)]
    mixed = [
        rows[0] * kern[c] + rows[1] * kern[3 + c] + rows[2] * kern[6 + c] for c in range(3)
    ]
    return from_left(mixed[0]) + mixed[1] + from_right(mixed[2])


def conv_back_band(padded_grad, at, lanes, kern):
    wide = padded_grad[pl.ds(at, BAND + 2 * SIDE), lanes]
    shifted = [from_right(wide), wide, from_left(wide)]
    total = None
    for r in range(3):
        for c in range(3):
            low = SIDE * (2 - r)
            term = shifted[c][low : low + BAND] * kern[3 * r + c]
            total = term if total is None else total + term
    return total, [s[SIDE : SIDE + BAND] for s in shifted]


def fold_rows(v):
    total = v[0:8]
    for at in range(8, v.shape[0], 8):
        total = total + v[at : at + 8]
    return total


def taps_of(kern_ref, lanes):
    block = kern_ref[:, lanes]
    return [block[t : t + 1] for t in range(9)]


def zero_edges(ref):
    edge = jnp.zeros((SIDE, ref.shape[1]), F32)
    tall = ref.shape[0] // PAIR
    for rel in range(PAIR):
        ref[rel * tall : rel * tall + SIDE, :] = edge
        ref[(rel + 1) * tall - SIDE : (rel + 1) * tall, :] = edge


def inside(ref, rel):
    tall = ref.shape[0] // PAIR
    return slice(rel * tall + SIDE, (rel + 1) * tall - SIDE)


def gather_features(n, parts, held, out):
    _, share, tokens = parts[0].shape
    core = jnp.bitwise_and(n, 1)

    def one(rel):
        for step, part in enumerate(parts):
            held[jnp.bitwise_xor(n, step)] = part[jnp.bitwise_xor(rel, core)]
        out[pl.ds(pl.multiple_of(rel * tokens, tokens), tokens), :] = held[...].reshape(len(parts) * share, tokens).T

    pair_loop(one)


def by_core(core, low, share, keep_out, send_out, turned):
    tokens = low.shape[0] // PAIR

    def one(rel):
        lat = jnp.bitwise_xor(rel, core)
        turned[...] = low[pl.ds(pl.multiple_of(rel * tokens, tokens), tokens), :].T
        for x in range(2):
            here = pl.ds(pl.multiple_of((2 * x + core) * share, 16), share)
            there = pl.ds(pl.multiple_of((2 * x + 1 - core) * share, 16), share)
            keep_out[x, lat] = turned[here, :]
            send_out[x, lat] = turned[there, :]

    pair_loop(one)


def norm_stats(v):
    width = v.shape[1]
    mean = jnp.sum(v, -1, keepdims=True) * (1.0 / width)
    center = v - mean
    spread = jnp.sum(center * center, -1, keepdims=True) * (1.0 / width)
    scale = lax.rsqrt(spread + EPS)
    return center * scale, scale


def head_masks(share):
    lane = lax.broadcasted_iota(jnp.int32, (1, share), 1) // HEAD_DIM
    return [(lane == h).astype(F32).astype(BF) for h in range(share // HEAD_DIM)]


def half_rows(v, parity):
    tokens, width = v.shape
    split = v.reshape(tokens // (2 * SIDE), 2, SIDE, width)
    return split[:, parity].reshape(tokens // 2, width)


def join_rows(even, odd):
    half, width = even.shape
    both = jnp.stack([even.reshape(half // SIDE, SIDE, width), odd.reshape(half // SIDE, SIDE, width)], 1)
    return both.reshape(2 * half, width)


def softmax_rows(queries, keys):
    scores = dot_nt(queries, keys) * (1.0 / math.sqrt(HEAD_DIM))
    rows = lax.broadcasted_iota(jnp.int32, scores.shape, 0)
    cols = lax.broadcasted_iota(jnp.int32, scores.shape, 1)
    same = (rows + cols) % 2 == 0
    scores = jnp.where(same, scores, -1e30)
    top = jnp.max(scores, -1, keepdims=True)
    grown = jnp.where(same, jnp.exp(scores - top), 0.0)
    return grown / jnp.sum(grown, -1, keepdims=True)


def beside(stacked, heads):
    rows = stacked.shape[0] // heads
    return jnp.concatenate([stacked[h * rows : (h + 1) * rows] for h in range(heads)], axis=1)


def lane_loop(width, body):
    count = width // LANES

    def step(j, carry):
        body(j // count, pl.ds(pl.multiple_of((j % count) * LANES, LANES), LANES))
        return carry

    lax.fori_loop(0, PAIR * count, step, 0)


def band_loop(tokens, body, carry):
    return lax.fori_loop(0, tokens // BAND, lambda j, c: body(pl.multiple_of(j * BAND, BAND), c), carry)


def row_loop(tokens, body, size=ROWS):
    count = tokens // size

    def step(j, carry):
        body(j // count, pl.multiple_of(j * size, size))
        return carry

    lax.fori_loop(0, PAIR * count, step, 0)


def pair_loop(body):
    def step(j, carry):
        body(j)
        return carry

    lax.fori_loop(0, PAIR, step, 0)


def attn_kernel_body(
    flow, s_ref, xo, xc, xx, xd, mod, kern, wqkv, wout,
    full_out, q_out, k_out, v_out, keep_out, send_out, grouped_out, ctx_out,
    held, padded,
):
    n = s_ref[0]
    core = jnp.bitwise_and(n, 1)
    share, tokens = xo.shape[1], xo.shape[2]
    width = full_out.shape[1]
    tall = tokens + 2 * SIDE
    zero_edges(padded)
    flow.need(xo, xc, xx, xd, mod, kern)
    gather_features(n, (xo, xc, xx, xd), held, full_out)
    flow.sent(full_out)

    def rows(rel, at):
        lat = jnp.bitwise_xor(rel, core)
        normed, _ = norm_stats(full_out[pl.ds(at, ROWS), :].astype(F32))
        here = pl.ds(pl.multiple_of(at + (2 * rel + 1) * SIDE, SIDE), ROWS)
        padded[here, :] = normed * (1.0 + mod[lat, 1:2, :]) + mod[lat, 0:1, :]

    row_loop(tokens, rows)

    def lanes(rel, at):
        taps = taps_of(kern, at)
        for band in range(0, tokens, BAND):
            here = pl.ds(pl.multiple_of(rel * tokens + band, BAND), BAND)
            grouped_out[here, at] = conv_band(padded, pl.multiple_of(rel * tall + band, SIDE), at, taps).astype(BF)

    lane_loop(width, lanes)
    flow.sent(grouped_out)
    flow.need(wqkv, wout)
    grouped = grouped_out[...]
    q_out[...] = dot_nt(grouped, wqkv[0]).astype(BF)
    k_out[...] = dot_nt(grouped, wqkv[1]).astype(BF)
    v_out[...] = dot_nt(grouped, wqkv[2]).astype(BF)
    flow.sent(q_out, k_out, v_out)
    masks = head_masks(share)
    heads = len(masks)

    def attend(rel):
        here = pl.ds(pl.multiple_of(rel * tokens, tokens), tokens)
        query, key, value = q_out[here, :], k_out[here, :], v_out[here, :]
        parts = []
        for parity in range(2):
            q = half_rows(query, parity)
            k = half_rows(key, parity)
            v = half_rows(value, parity)
            probs = softmax_rows(jnp.concatenate([q * m for m in masks], axis=0), k)
            low = beside(probs.astype(BF), heads)
            parts.append(dot(low, jnp.concatenate([v * m for m in masks], axis=0)).astype(BF))
        ctx_out[here, :] = join_rows(*parts)

    pair_loop(attend)
    flow.sent(ctx_out)
    send_out[...] = dot(ctx_out[tokens : 2 * tokens, :], wout[...]).astype(BF)
    flow.sent(send_out)
    keep_out[...] = dot(ctx_out[0:tokens, :], wout[...]).astype(BF)
    flow.sent(keep_out)


def ffn_kernel_body(
    first, flow, s_ref, go, gc, gx, gd, full, att, mod, up, down, kern, kgrad_in,
    g_out, keep_out, send_out, mods_out, kgrad_out, active_out, gfed_out, second_out, ghid_out, fkeep_out, fsend_out,
    held, padded, slope, gpad, mid, fed, low, sums, turned,
):
    n = s_ref[0]
    core = jnp.bitwise_and(n, 1)
    share, tokens = go.shape[1], go.shape[2]
    units = up.shape[1]
    tall = tokens + 2 * SIDE
    zero_edges(padded)
    zero_edges(gpad)
    flow.need(go, gc, gx, gd)
    gather_features(n, (go, gc, gx, gd), held, g_out)
    flow.sent(g_out)
    flow.need(full, att, mod, kgrad_in)
    kgrad_out[...] = jnp.zeros(kgrad_out.shape, F32) if first else kgrad_in[...]

    def rows(rel, at):
        lat = jnp.bitwise_xor(rel, core)
        here = pl.ds(at, ROWS)
        middle = full[here, :].astype(F32) + mod[lat, 2:3, :] * att[here, :].astype(F32)
        mid[here, :] = middle
        normed, _ = norm_stats(middle)
        second_out[here, :] = (normed * (1.0 + mod[lat, 4:5, :]) + mod[lat, 3:4, :]).astype(BF)
        gfed_out[here, :] = (mod[lat, 5:6, :] * g_out[here, :].astype(F32)).astype(BF)

    row_loop(tokens, rows)
    flow.sent(second_out, gfed_out)
    flow.need(up, kern)
    hidden = dot(second_out[...], up[...])
    for rel in range(PAIR):
        padded[inside(padded, rel), :] = hidden[rel * tokens : (rel + 1) * tokens]

    def lanes(rel, at):
        taps = taps_of(kern, at)
        for band in range(0, tokens, BAND):
            here = pl.ds(pl.multiple_of(rel * tokens + band, BAND), BAND)
            mixed = conv_band(padded, pl.multiple_of(rel * tall + band, SIDE), at, taps)
            square = mixed * mixed
            curve = jnp.tanh(GELU_A * mixed * (1.0 + GELU_B * square))
            half = 0.5 * (1.0 + curve)
            active_out[here, at] = (mixed * half).astype(BF)
            slope[here, at] = half + (0.5 * GELU_A) * mixed * (1.0 - curve * curve) * (
                1.0 + (3.0 * GELU_B) * square
            )

    lane_loop(units, lanes)
    flow.sent(active_out)
    flow.need(down)
    fed[...] = dot(active_out[...], down[...])
    sums[...] = jnp.zeros(sums.shape, F32)

    def rows_fed(rel, at):
        lat = jnp.bitwise_xor(rel, core)
        here = pl.ds(at, ROWS)
        term = fed[here, :]
        sums[lat] += fold_rows(term * g_out[here, :].astype(F32))
        low[here, :] = (mod[lat, 5:6, :] * term + 0.25 * mid[here, :]).astype(BF)

    row_loop(tokens, rows_fed)
    for lat in range(PAIR):
        mods_out[lat] = jnp.sum(sums[lat], 0, keepdims=True)
    by_core(core, low, share, fkeep_out, fsend_out, turned)
    flow.sent(fkeep_out, fsend_out, mods_out)
    gact = dot_nt(gfed_out[...], down[...]).astype(BF).astype(F32)
    for rel in range(PAIR):
        here = slice(rel * tokens, (rel + 1) * tokens)
        gpad[inside(gpad, rel), :] = gact[here] * slope[here, :]

    def lanes_back(rel, at):
        taps = taps_of(kern, at)
        sums = [None] * 9
        for band in range(0, tokens, BAND):
            here = pl.ds(pl.multiple_of(rel * tokens + band, BAND), BAND)
            base = pl.multiple_of(rel * tall + band, SIDE)
            total, shifted = conv_back_band(gpad, base, at, taps)
            ghid_out[here, at] = total.astype(BF)
            for r in range(3):
                values = padded[pl.ds(base + SIDE * r, BAND), at]
                for c in range(3):
                    part = fold_rows(values * shifted[c])
                    sums[3 * r + c] = part if sums[3 * r + c] is None else sums[3 * r + c] + part
        for t in range(9):
            kgrad_out[t : t + 1, at] += jnp.sum(sums[t], 0, keepdims=True)

    lane_loop(units, lanes_back)
    flow.sent(ghid_out, kgrad_out)
    send_out[...] = dot_nt(ghid_out[tokens : 2 * tokens, :], up[...]).astype(BF)
    flow.sent(send_out)
    keep_out[...] = dot_nt(ghid_out[0:tokens, :], up[...]).astype(BF)
    flow.sent(keep_out)


def attn_back_body(
    flow, s_ref, full, att, gs, gfull, mod, q_in, k_in, v_in, wout, gates,
    gmid_out, mods_out, gatt_out, gqkv_out,
    sums, gctx,
):
    core = jnp.bitwise_and(s_ref[0], 1)
    tokens = full.shape[0] // PAIR
    width = full.shape[1]
    share = q_in.shape[1]
    mods_out[...] = jnp.zeros(mods_out.shape, F32)
    sums[...] = jnp.zeros(sums.shape, F32)
    flow.need(full, att, gs, gfull, mod)

    def rows(rel, at):
        lat = jnp.bitwise_xor(rel, core)
        here = pl.ds(at, ROWS)
        gate1 = mod[lat, 2:3, :]
        attended = att[here, :].astype(F32)
        normed, inv = norm_stats(full[here, :].astype(F32) + gate1 * attended)
        grad = gs[here, :].astype(F32)
        inner = grad * (1.0 + mod[lat, 4:5, :])
        mean_a = jnp.sum(inner, -1, keepdims=True) * (1.0 / width)
        mean_b = jnp.sum(inner * normed, -1, keepdims=True) * (1.0 / width)
        whole_grad = gfull[here, :].astype(F32) + inv * (inner - mean_a - normed * mean_b)
        gmid_out[here, :] = whole_grad.astype(BF)
        gatt_out[here, :] = (gate1 * whole_grad).astype(BF)
        sums[3 * lat] += fold_rows(attended * whole_grad)
        sums[3 * lat + 1] += fold_rows(grad)
        sums[3 * lat + 2] += fold_rows(grad * normed)

    row_loop(tokens, rows)
    for lat in range(PAIR):
        for k in range(3):
            mods_out[lat, 2 + k : 3 + k, :] = 0.25 * jnp.sum(sums[3 * lat + k], 0, keepdims=True)
    flow.need(wout, q_in, k_in, v_in, gates)
    for lat in range(PAIR):
        mods_out[lat, 5:6, :] = gates[lat]
    flow.sent(gatt_out, gmid_out, mods_out)
    gctx[...] = dot_nt(gatt_out[...], wout[...]).astype(BF)
    masks = head_masks(share)
    heads = len(masks)
    factor = 1.0 / math.sqrt(HEAD_DIM)

    def attend(rel):
        here = pl.ds(pl.multiple_of(rel * tokens, tokens), tokens)
        query, key, value, grads = q_in[here, :], k_in[here, :], v_in[here, :], gctx[here, :]
        parts_q, parts_k, parts_v = [], [], []
        for parity in range(2):
            q = half_rows(query, parity)
            k = half_rows(key, parity)
            v = half_rows(value, parity)
            gc = half_rows(grads, parity)
            q_all = jnp.concatenate([q * m for m in masks], axis=0)
            k_all = jnp.concatenate([k * m for m in masks], axis=0)
            gc_all = jnp.concatenate([gc * m for m in masks], axis=0)
            probs = softmax_rows(q_all, k)
            parts_v.append(dot_tn(probs.astype(BF), gc_all).astype(BF))
            gprobs = dot_nt(gc_all, v).astype(BF).astype(F32)
            gscores = (probs * (gprobs - jnp.sum(probs * gprobs, -1, keepdims=True))).astype(BF)
            parts_q.append((dot(beside(gscores, heads), k_all) * factor).astype(BF))
            parts_k.append((dot_tn(gscores, q_all) * factor).astype(BF))
        for k, parts in enumerate((parts_q, parts_k, parts_v)):
            gqkv_out[here, k * share : (k + 1) * share] = join_rows(*parts)

    pair_loop(attend)
    flow.sent(gqkv_out)


def input_back_body(
    closing, flow, s_ref, full, mod, gqkv, wqkv, kern, kgrad_in, gmid, mods_in, before,
    kgrad_out, mods_out, keep_out, send_out,
    normed1, scale1, first, gpad, gback, low, mods, rows_out, turned,
):
    core = jnp.bitwise_and(s_ref[0], 1)
    tokens = full.shape[0] // PAIR
    width = full.shape[1]
    share = gqkv.shape[1] // 3
    tall = tokens + 2 * SIDE
    zero_edges(first)
    zero_edges(gpad)
    flow.need(full, mod)

    def rows_first(rel, at):
        lat = jnp.bitwise_xor(rel, core)
        here = pl.ds(at, FEW_ROWS)
        normed, inv = norm_stats(full[here, :].astype(F32))
        normed1[here, :] = normed
        scale1[here, :] = jnp.broadcast_to(inv, (FEW_ROWS, LANES))
        inside_rows = pl.ds(pl.multiple_of(at + (2 * rel + 1) * SIDE, SIDE), FEW_ROWS)
        first[inside_rows, :] = normed * (1.0 + mod[lat, 1:2, :]) + mod[lat, 0:1, :]

    row_loop(tokens, rows_first, FEW_ROWS)
    flow.need(gqkv, wqkv, kern, kgrad_in, gmid, mods_in, before)
    kgrad_out[...] = kgrad_in[...] if closing else jnp.zeros(kgrad_out.shape, F32)
    mods[...] = mods_in[...]
    for rel in range(PAIR):
        here = slice(rel * tokens, (rel + 1) * tokens)
        gpad[inside(gpad, rel), :] = dot(gqkv[here, :], wqkv[...])

    def lanes(rel, at):
        taps = taps_of(kern, at)
        sums = [None] * 9
        shift_sum, scale_sum = None, None
        for band in range(0, tokens, BAND):
            here = pl.ds(pl.multiple_of(rel * tokens + band, BAND), BAND)
            base = pl.multiple_of(rel * tall + band, SIDE)
            total, shifted = conv_back_band(gpad, base, at, taps)
            gback[here, at] = total
            part_a, part_b = fold_rows(total), fold_rows(total * normed1[here, at])
            shift_sum = part_a if shift_sum is None else shift_sum + part_a
            scale_sum = part_b if scale_sum is None else scale_sum + part_b
            for r in range(3):
                values = first[pl.ds(base + SIDE * r, BAND), at]
                for c in range(3):
                    part = fold_rows(values * shifted[c])
                    sums[3 * r + c] = part if sums[3 * r + c] is None else sums[3 * r + c] + part
        for t in range(9):
            kgrad_out[t : t + 1, at] += jnp.sum(sums[t], 0, keepdims=True)
        lat = jnp.bitwise_xor(rel, core)
        mods[lat, 0:1, at] = jnp.sum(shift_sum, 0, keepdims=True)
        mods[lat, 1:2, at] = jnp.sum(scale_sum, 0, keepdims=True)

    lane_loop(width, lanes)
    if closing:
        rows_out[...] = jnp.zeros(rows_out.shape, F32)
        for lat in range(PAIR):
            rows_out[6 * lat : 6 * lat + 6, :] = before[lat, 0:6, :]
            rows_out[6 * (PAIR + lat) : 6 * (PAIR + lat) + 6, :] = mods[lat, 0:6, :]
        rows_out[12 * PAIR : 12 * PAIR + 9, :] = kgrad_out[0:9, :]
        mods_out[...] = rows_out[...].astype(BF)
    else:
        mods_out[...] = mods[...]
    flow.sent(mods_out, kgrad_out)

    def rows_back(rel, at):
        lat = jnp.bitwise_xor(rel, core)
        here = pl.ds(at, FEW_ROWS)
        inner = gback[here, :] * (1.0 + mod[lat, 1:2, :])
        normed = normed1[here, :]
        mean_a = jnp.sum(inner, -1, keepdims=True) * (1.0 / width)
        mean_b = jnp.sum(inner * normed, -1, keepdims=True) * (1.0 / width)
        grad = scale1[here, 0:1] * (inner - mean_a - normed * mean_b)
        low[here, :] = (grad + 0.25 * gmid[here, :].astype(F32)).astype(BF)

    row_loop(tokens, rows_back, FEW_ROWS)
    by_core(core, low, share, keep_out, send_out, turned)
    flow.sent(keep_out, send_out)


class Flow:
    def __init__(self, arrivals, departures):
        self.arrivals, self.departures = arrivals, departures
        self.leaving = []
        for _, copy in arrivals:
            copy.start()

    def need(self, *refs):
        for ref in refs:
            for _, copy in [a for a in self.arrivals if a[0] is ref]:
                copy.wait()
            self.arrivals = [a for a in self.arrivals if a[0] is not ref]

    def sent(self, *refs):
        for ref in refs:
            for held, copy in self.departures:
                if held is ref:
                    copy.start()
                    self.leaving.append(copy)

    def end(self):
        for copy in self.leaving:
            copy.wait()


def call(body, name, scalars, ins, outs, scratch, flops, held=()):
    n_in, n_out = len(ins), len(outs)
    places, buffer_shapes = [], []
    for array, window, into in ins:
        dims = array.shape if window is None else (window[0].size,) + array.shape[1:]
        if into is None:
            buffer_shapes.append((dims, array.dtype))
        elif into[0].start == 0:
            buffer_shapes.append(((PAIR * dims[0],) + dims[1:], array.dtype))
        places.append(len(buffer_shapes) - 1)

    def run(s_ref, *refs):
        sources = refs[:n_in]
        targets = refs[n_in + len(held) : n_in + len(held) + n_out]
        buffers = refs[n_in + len(held) + n_out : -1]
        sems = refs[-1]
        n_held = len(buffer_shapes)
        buffers_in, buffers_out = buffers[:n_held], buffers[n_held : n_held + n_out]
        rest = buffers[n_held + n_out :]
        arrivals, departures = [], []
        for k, (source, (_, window, into)) in enumerate(zip(sources, ins)):
            view = source if window is None else source.at[window]
            buffer = buffers_in[places[k]]
            target = buffer if into is None else buffer.at[into]
            arrivals.append((buffer, pltpu.make_async_copy(view, target, sems.at[k])))
        for k, (target, buffer, out) in enumerate(zip(targets, buffers_out, outs)):
            view = target if out[2] is None else target.at[out[2]]
            departures.append((buffer, pltpu.make_async_copy(buffer, view, sems.at[n_in + k])))
        flow = Flow(arrivals, departures)
        body(flow, s_ref, *buffers_in, *buffers_out, *rest)
        flow.end()

    anywhere = pl.BlockSpec(memory_space=pl.ANY)
    return pl.pallas_call(
        run,
        name=name,
        out_shape=[jax.ShapeDtypeStruct(o[0], o[1]) for o in outs],
        grid_spec=pltpu.PrefetchScalarGridSpec(
            num_scalar_prefetch=1,
            grid=(1,),
            in_specs=[anywhere] * (n_in + len(held)),
            out_specs=[anywhere] * n_out,
            scratch_shapes=[pltpu.VMEM(dims, dtype) for dims, dtype in buffer_shapes]
            + [pltpu.VMEM(o[3], o[1]) for o in outs]
            + scratch
            + [pltpu.SemaphoreType.DMA((n_in + n_out,))],
        ),
        input_output_aliases={1 + n_in + k: n_out - len(held) + k for k in range(len(held))},
        compiler_params=pltpu.CompilerParams(vmem_limit_bytes=VMEM_LIMIT),
        cost_estimate=pl.CostEstimate(flops=flops, bytes_accessed=10**6, transcendentals=0),
    )(scalars, *[i[0] for i in ins], *held)


def slices_out(slots, slot, share, tokens):
    return ((2, slots, share, tokens), BF, (slice(None), pl.ds(PAIR * slot, PAIR)), (2, PAIR, share, tokens))


def whole(array):
    return (array, None, None)


def stacked(arrays):
    rows = arrays[0].shape[0]
    return [(v, None, (pl.ds(k * rows, rows),)) for k, v in enumerate(arrays)]


def whole_out(dims, dtype):
    return (dims, dtype, None, dims)


def pair_rows(array, pair):
    rows = array.shape[0] // PAIRS
    return (array, (pl.ds(rows * pair, rows),), None)


def pair_rows_out(rows, width, pair):
    return ((PAIRS * rows, width), BF, (pl.ds(rows * pair, rows),), (rows, width))


def pair_of(array, pair):
    return (array, (pl.ds(PAIR * pair, PAIR),), None)


def split_low(v):
    high = v.astype(BF)
    return high, (v - high.astype(F32)).astype(BF)


def rows_product(a, b):
    (ah, al), (bh, bl) = split_low(a), split_low(b)
    return dot_tn(jnp.concatenate([ah, al, ah], 0), jnp.concatenate([bh, bh, bl], 0))


def back_product(a, weight):
    (ah, al), (wh, wl) = split_low(a), split_low(weight)
    return dot_nt(ah, wh) + dot_nt(al, wh) + dot_nt(ah, wl)


def product(a, weight):
    (ah, al), (wh, wl) = split_low(a), split_low(weight)
    return dot(ah, wh) + dot(al, wh) + dot(ah, wl)


def silu(v):
    return v / (1.0 + jnp.exp(-v))


def silu_slope(v):
    gate = 1.0 / (1.0 + jnp.exp(-v))
    return gate * (1.0 + v * (1.0 - gate))


def row_blocks(source, target, sems, rows):
    return [
        pltpu.make_async_copy(source.at[pl.ds(at, rows)], target.at[pl.ds(at, rows)], sems.at[at // rows])
        for at in range(0, source.shape[0], rows)
    ]


def condition_body(
    steps, stamps, wide, bias, time_in, time_out, ada,
    mod_out, embedded, inner_pre, inner, outer_pre, outer, held_in, held_out, held, sums, parts, rows_of, sems,
):
    depth = ada.shape[0]
    per_dev, count, width = mod_out.shape
    first = pltpu.make_async_copy(time_in, held_in, sems.at[0])
    second = pltpu.make_async_copy(time_out, held_out, sems.at[1])
    blocks = row_blocks(ada, held, sems.at[pl.ds(2, depth // WEIGHT_ROWS)], WEIGHT_ROWS)
    for copy in [first, second] + blocks:
        copy.start()
    halved = embedded.shape[1] // 2
    for r in range(embedded.shape[0]):
        at = jnp.bitwise_xor(wide[0], steps[r // per_dev]) * per_dev + r % per_dev
        rows_of[r : r + 1, :] = jnp.broadcast_to(stamps[at].astype(F32), (1, halved))
    order = lax.broadcasted_iota(jnp.int32, (1, halved), 1).astype(F32)
    angles = rows_of[...] * jnp.exp(-math.log(10000.0) * order / halved)
    embedded[:, 0:halved] = jnp.cos(angles)
    embedded[:, halved:] = jnp.sin(angles)
    first.wait()
    inner_pre[...] = product(embedded[...], held_in[...])
    inner[...] = silu(inner_pre[...])
    second.wait()
    outer_pre[...] = product(inner[...], held_out[...])
    outer[...] = silu(outer_pre[...])
    wide_bias = [jnp.concatenate([bias[k + j : k + j + 1, :] for j in range(width // LANES)], 1)
                 for k in range(0, bias.shape[0], width // LANES)]
    total = jnp.concatenate(wide_bias, 1)
    sums[...] = jnp.broadcast_to(total, sums.shape)
    for k in range(depth // WEIGHT_ROWS):
        parts[k] = outer[0:8, k * WEIGHT_ROWS : (k + 1) * WEIGHT_ROWS]

    def add(k, carry):
        rows = pl.ds(pl.multiple_of(k * WEIGHT_ROWS, WEIGHT_ROWS), WEIGHT_ROWS)
        pltpu.make_async_copy(ada.at[rows], held.at[rows], sems.at[2 + k]).wait()
        sums[...] += product(parts[k], held[rows, :])
        return carry

    lax.fori_loop(0, depth // WEIGHT_ROWS, add, 0)
    total = sums[...]
    for lat in range(per_dev):
        for k in range(count):
            mod_out[lat, k : k + 1, :] = total[lat : lat + 1, k * width : (k + 1) * width]


def condition(steps, stamps, wide, time_in, time_out, ada_weight, ada_bias, per_dev, width):
    latent_total = stamps.shape[0]
    depth, columns = ada_weight.shape
    vmem = pl.BlockSpec(memory_space=pltpu.VMEM)
    anywhere = pl.BlockSpec(memory_space=pl.ANY)
    rows = jax.ShapeDtypeStruct((latent_total, depth), F32)
    return pl.pallas_call(
        functools.partial(condition_body, steps),
        name="condition",
        in_specs=[pl.BlockSpec(memory_space=pltpu.SMEM)] * 2 + [vmem, anywhere, anywhere, anywhere],
        out_specs=[vmem] * 6,
        out_shape=[
            jax.ShapeDtypeStruct((per_dev, columns // width, width), F32),
            jax.ShapeDtypeStruct((latent_total, time_in.shape[0]), F32),
            rows, rows, rows, rows,
        ],
        scratch_shapes=[
            pltpu.VMEM(time_in.shape, F32),
            pltpu.VMEM(time_out.shape, F32),
            pltpu.VMEM(ada_weight.shape, F32),
            pltpu.VMEM((8, columns), F32),
            pltpu.VMEM((depth // WEIGHT_ROWS, 8, WEIGHT_ROWS), F32),
            pltpu.VMEM((latent_total, time_in.shape[0] // 2), F32),
            pltpu.SemaphoreType.DMA((2 + depth // WEIGHT_ROWS,)),
        ],
        compiler_params=pltpu.CompilerParams(vmem_limit_bytes=VMEM_LIMIT),
        cost_estimate=pl.CostEstimate(flops=8 * 10**9, bytes_accessed=10**6, transcendentals=0),
    )(stamps, wide, ada_bias.reshape(columns // LANES, LANES), time_in, time_out, ada_weight)


def condition_back_body(
    factor, gmod, embedded, inner_pre, inner, outer_pre, outer, time_out, ada,
    time_in_grad, time_out_grad, ada_grad, held_out, held, outer_grad, columns, sems, arriving, leaving,
):
    count = ada.shape[0] // BACK_ROWS

    def block_copy(source, target, sem, k):
        rows = pl.ds(k * BACK_ROWS, BACK_ROWS)
        return pltpu.make_async_copy(source.at[rows], target.at[rows], sem.at[k])

    first = pltpu.make_async_copy(time_out, held_out, sems.at[0])
    for k in range(count):
        block_copy(ada, held, arriving, k).start()
    first.start()
    high, low = split_low(outer[...])
    both = jnp.concatenate([high, low], 0)
    for k in range(count):
        columns[k] = both[:, k * BACK_ROWS : (k + 1) * BACK_ROWS]

    def block(k, carry):
        rows = pl.ds(pl.multiple_of(k * BACK_ROWS, BACK_ROWS), BACK_ROWS)
        block_copy(ada, held, arriving, k).wait()
        grads = gmod[...]
        high, low = split_low(held[rows, :])
        outer_grad[rows, :] = dot_nt(high, grads) + dot_nt(low, grads)
        held[rows, :] = dot_tn(columns[k], jnp.concatenate([grads, grads], 0)) * factor
        block_copy(held, ada_grad, leaving, k).start()
        return carry

    lax.fori_loop(0, count, block, 0)
    first.wait()
    back = outer_grad[...].T * factor * silu_slope(outer_pre[...])
    time_out_grad[...] = rows_product(inner[...], back)
    back = back_product(back, held_out[...]) * silu_slope(inner_pre[...])
    time_in_grad[...] = rows_product(embedded[...], back)
    for k in range(count):
        block_copy(held, ada_grad, leaving, k).wait()


def condition_back(gmod, embedded, stages, time_out, ada_weight, factor):
    depth = ada_weight.shape[0]
    latent_total = gmod.shape[0]
    vmem = pl.BlockSpec(memory_space=pltpu.VMEM)
    anywhere = pl.BlockSpec(memory_space=pl.ANY)
    time_in_dims = (embedded.shape[1], time_out.shape[0])
    return pl.pallas_call(
        functools.partial(condition_back_body, factor),
        name="condition_back",
        in_specs=[vmem] * 6 + [anywhere] * 2,
        out_specs=[vmem, vmem, anywhere],
        out_shape=[
            jax.ShapeDtypeStruct(time_in_dims, F32),
            jax.ShapeDtypeStruct(time_out.shape, F32),
            jax.ShapeDtypeStruct(ada_weight.shape, F32),
        ],
        scratch_shapes=[
            pltpu.VMEM(time_out.shape, F32),
            pltpu.VMEM(ada_weight.shape, F32),
            pltpu.VMEM((depth, latent_total), F32),
            pltpu.VMEM((depth // BACK_ROWS, 2 * latent_total, BACK_ROWS), BF),
            pltpu.SemaphoreType.DMA((1,)),
            pltpu.SemaphoreType.DMA((depth // BACK_ROWS,)),
            pltpu.SemaphoreType.DMA((depth // BACK_ROWS,)),
        ],
        compiler_params=pltpu.CompilerParams(vmem_limit_bytes=VMEM_LIMIT),
        cost_estimate=pl.CostEstimate(flops=1, bytes_accessed=1, transcendentals=0),
    )(gmod, embedded, *stages, time_out, ada_weight)


def attn_forward(scalars, pair, x_parts, mod, attn_kernel, qkv_weight, out_weight, held):
    _, share, tokens = x_parts[0].shape
    width = out_weight.shape[1]
    rows = PAIR * tokens
    thin = whole_out((rows, share), BF)
    half = whole_out((tokens, width), BF)
    return call(
        attn_kernel_body, "attn_fwd", scalars,
        [pair_of(v, pair) for v in x_parts] + [pair_of(mod, pair), whole(attn_kernel), whole(qkv_weight), whole(out_weight)],
        [whole_out((rows, width), BF), thin, thin, thin, half, half, pair_rows_out(rows, width, pair),
         pair_rows_out(rows, share, pair)],
        [pltpu.VMEM((4, share, tokens), BF), pltpu.VMEM((PAIR * (tokens + 2 * SIDE), width), F32)],
        6_000_000_000, held,
    )


def feed_forward(scalars, pair, full, att, g_parts, mod, up_weight, down_weight, ffn_kernel, slots, taps, held):
    _, share, tokens = g_parts[0].shape
    width, units = up_weight.shape
    rows = PAIR * tokens
    tall = PAIR * (tokens + 2 * SIDE)
    half = whole_out((tokens, width), BF)
    slices = slices_out(slots, pair, share, tokens)
    return call(
        functools.partial(ffn_kernel_body, pair == 0), "ffn", scalars,
        [pair_of(v, pair) for v in g_parts] + [whole(full)] + stacked(att)
        + [pair_of(mod, pair), whole(up_weight), whole(down_weight), whole(ffn_kernel), whole(taps)],
        [whole_out((rows, width), BF), half, half, whole_out((PAIR, 1, width), F32), whole_out((16, units), F32),
         whole_out((rows, units), BF), whole_out((rows, width), BF), pair_rows_out(rows, width, pair),
         pair_rows_out(rows, units, pair), slices, slices],
        [pltpu.VMEM((4, share, tokens), BF), pltpu.VMEM((tall, units), F32), pltpu.VMEM((rows, units), F32),
         pltpu.VMEM((tall, units), F32), pltpu.VMEM((rows, width), F32), pltpu.VMEM((rows, width), F32),
         pltpu.VMEM((rows, width), BF), pltpu.VMEM((PAIR, 8, width), F32), pltpu.VMEM((width, tokens), BF)],
        10_000_000_000, held,
    )


def attn_backward(scalars, pair, full, att, gsec, gfull, mod, qkv, out_weight, gates, held):
    tokens, width = att[0].shape
    share = out_weight.shape[0]
    rows = PAIR * tokens
    broad = whole_out((rows, width), BF)
    return call(
        attn_back_body, "attn_bwd", scalars,
        [whole(full)] + stacked(att) + stacked(gsec) + [whole(gfull), pair_of(mod, pair)]
        + [whole(v) for v in qkv] + [whole(out_weight), whole(gates)],
        [broad, whole_out((PAIR, 8, width), F32), pair_rows_out(rows, width, pair), pair_rows_out(rows, 3 * share, pair)],
        [pltpu.VMEM((3 * PAIR, 8, width), F32), pltpu.VMEM((rows, share), BF)],
        6_000_000_000, held,
    )


def input_backward(scalars, pair, full, mod, gqkv, qkv_weight, attn_kernel, taps, gmid, mods_in, before, slots, held):
    rows, width = full.shape
    tokens = rows // PAIR
    share = gqkv.shape[1] // 3
    tall = PAIR * (tokens + 2 * SIDE)
    slices = slices_out(slots, slots // PAIR // 2 + pair, share, tokens)
    closing = pair > 0
    mods = whole_out((PACKED, width), BF) if closing else whole_out((PAIR, 8, width), F32)
    return call(
        functools.partial(input_back_body, closing), "input_bwd", scalars,
        [whole(full), pair_of(mod, pair), pair_rows(gqkv, pair), whole(qkv_weight), whole(attn_kernel), whole(taps), whole(gmid),
         whole(mods_in), whole(before)],
        [whole_out((16, width), F32), mods, slices, slices],
        [pltpu.VMEM((rows, width), F32), pltpu.VMEM((rows, LANES), F32), pltpu.VMEM((tall, width), F32),
         pltpu.VMEM((tall, width), F32), pltpu.VMEM((rows, width), F32), pltpu.VMEM((rows, width), BF),
         pltpu.VMEM((PAIR, 8, width), F32), pltpu.VMEM((PACKED, width), F32), pltpu.VMEM((width, tokens), BF)],
        6_000_000_000, held,
    )


def core_swap(v):
    return lax.ppermute(v, "narrow", [(0, 1), (1, 0), (2, 3), (3, 2)])


def x_swap(v):
    return lax.ppermute(v, "narrow", [(0, 2), (2, 0), (1, 3), (3, 1)])


def sum_pair(a, b):
    return (a.astype(F32) + b.astype(F32)).astype(BF)


def slice_halves(x, keep, arrived):
    both = sum_pair(keep, arrived)
    return (
        lax.dynamic_index_in_dim(both, x, 0, keepdims=False),
        lax.dynamic_index_in_dim(both, 1 - x, 0, keepdims=False),
    )


def wide_swap(v, bit, count):
    return lax.ppermute(v, "wide", [(i, i ^ bit) for i in range(count)])


def pick(v, parts, at):
    rows = v.shape[0] // parts
    return lax.dynamic_slice_in_dim(v, at * rows, rows, 0)


def in_place(second, own, came, axis):
    dims = own.shape[:axis] + (2,) + own.shape[axis + 1 :]
    chosen = lax.broadcast_in_dim(second, dims, (axis,))
    return jnp.where(chosen, own, came)


class WideSum:
    def __init__(self, product, bits, masks, count, back=None):
        self.count, self.dims, self.bits, self.masks = count, product.shape, bits, masks
        self.levels = count.bit_length() - 1
        self.ahead = list(range(self.levels))
        self.back = list(reversed(self.ahead)) if back is None else back
        self.opened = False
        self.held = product

    def swap(self, sent, level):
        self.came = wide_swap(sent, 1 << level, self.count)

    def halve(self, held, came):
        level = self.ahead[0]
        if level == 0:
            held = pick(held, 2, self.bits[0])
        if len(self.ahead) == 1:
            return (sum_pair(held, came),)
        bit = self.bits[level + 1]
        return tuple(sum_pair(pick(held, 2, at), pick(came, 2, at)) for at in (1 - bit, bit))

    def pending(self):
        if not self.opened:
            return lambda v: pick(v, 2, 1 - self.bits[0]), (self.held,)
        if self.ahead:
            return self.halve, (self.held, self.came)
        level = self.back[0]
        return lambda a, b: in_place(self.masks[level], a, b, level), (self.held, self.came)

    def accept(self, out):
        if not self.opened:
            self.opened = True
            self.swap(out, 0)
        elif self.ahead:
            self.ahead.pop(0)
            self.held = out[-1]
            if self.ahead:
                self.swap(out[0], self.ahead[0])
            else:
                self.held = self.held.reshape((1,) * self.levels + self.held.shape)
                self.swap(self.held, self.back[0])
        else:
            self.back.pop(0)
            self.held = out
            self.swap(out, self.back[0])

    def done(self):
        return self.opened and not self.ahead and len(self.back) == 1

    def finish(self, order, dtype):
        level = self.back[0]
        whole_sum = order(lambda a, b: in_place(self.masks[level], a, b, level).astype(dtype), self.held, self.came)
        return lax.optimization_barrier(whole_sum).reshape(self.dims)


class Steps:
    def __init__(self, came, steps):
        self.came, self.steps = came, list(steps)

    def pending(self):
        return self.steps[0][0], self.came

    def accept(self, out):
        _, move = self.steps.pop(0)
        self.came = move(out)

    def done(self):
        return not self.steps


class Order:
    def __init__(self):
        self.last = ()

    def __call__(self, step, *inputs):
        inputs, _ = lax.optimization_barrier((inputs, self.last))
        out = step(*inputs)
        self.last = tuple(jax.tree.leaves(out)[:1])
        return out

    def advance(self, *chains):
        chains = [c for c in chains if not c.done()]
        if chains:
            work = [c.pending() for c in chains]
            outs = self(lambda *v: [w[0](*a) for w, a in zip(work, v)], *[w[1] for w in work])
            self.last = tuple(jax.tree.leaves(out)[0] for out in outs)
            for chain, out in zip(chains, outs):
                chain.accept(out)


def after(value, *others):
    return lax.optimization_barrier((value, others))[0]


def body(
    latents, cotangent, timesteps, time_in, time_out, ada_weight, ada_bias,
    attn_kernel, qkv_weight, out_weight, up_weight, ffn_kernel, down_weight,
):
    wide_count = lax.axis_size("wide")
    wide_at = lax.axis_index("wide")
    n = lax.axis_index("narrow")
    per_dev, tokens, share = latents.shape
    width = out_weight.shape[1]
    units = up_weight.shape[1]
    latent_total = timesteps.shape[0]
    scalars = n.astype(jnp.int32).reshape(1)

    steps, bit = [0], wide_count // 2
    while bit:
        steps, bit = steps + [k ^ bit for k in steps], bit // 2
    mod, embedded, *stages = condition(
        steps, timesteps, wide_at.astype(jnp.int32).reshape(1), time_in, time_out, ada_weight, ada_bias, per_dev, width
    )
    x = n // 2
    factor = 1.0 / latent_total

    def token_products(lefts, rights):
        return (sum(dot_tn(a, b) for a, b in zip(lefts, rights)) * factor).astype(BF)

    x_own = jnp.swapaxes(latents, 1, 2)
    g_own = jnp.swapaxes(cotangent, 1, 2)
    qkv_rows = jnp.swapaxes(qkv_weight, 1, 2)
    qkv_all = qkv_rows.reshape(3 * share, width)
    order = Order()
    x_across = x_swap(x_own)
    x_across = after(x_across, mod)
    g_across = x_swap(after(g_own, x_across))
    x_parts = (x_own, core_swap(x_own), x_across, core_swap(x_across))
    g_parts = (g_own, core_swap(g_own), g_across, core_swap(g_across))

    def attend(pair, held=()):
        return lambda parts: attn_forward(scalars, pair, parts, mod, attn_kernel, qkv_rows, out_weight, held)

    fwd_a = order(attend(0), x_parts)
    here_a = order(sum_pair, fwd_a[4], core_swap(fwd_a[5]))
    fwd_b = order(attend(1, fwd_a[6:8]), after(x_parts, g_across))
    levels = wide_count.bit_length() - 1
    places = [jnp.bitwise_and(jnp.right_shift(wide_at, k), 1) for k in range(levels)]
    masks = [jnp.arange(2, dtype=jnp.int32) == place for place in places]
    att_a, masks = order(lambda a, b, m: (sum_pair(a, b), m), here_a, x_swap(here_a), masks)
    here_b = order(sum_pair, fwd_b[4], core_swap(fwd_b[5]))
    att_a = (att_a, core_swap(att_a))

    slots = 2 * per_dev

    def feed(pair, full, taps, held=()):
        return lambda att, parts: feed_forward(
            scalars, pair, full, att, parts, mod, up_weight, down_weight, ffn_kernel, slots, taps, held
        )

    ffn_a = order(feed(0, fwd_a[0], ffn_kernel), att_a, g_parts)
    att_b = order(sum_pair, here_b, x_swap(here_b))
    att_b = (att_b, core_swap(att_b))
    here_a = order(sum_pair, ffn_a[1], core_swap(ffn_a[2]))
    ffn_b = order(feed(1, fwd_b[0], ffn_a[4], ffn_a[7:11]), att_b, g_parts)
    sec_a = order(sum_pair, here_a, x_swap(here_a))
    sec_a = (sec_a, core_swap(sec_a))
    down_product = order(token_products, [ffn_a[5], ffn_b[5]], [ffn_a[6], ffn_b[6]])
    down_sum = WideSum(down_product, places, masks, wide_count)
    order.advance(down_sum)
    here_b = order(sum_pair, ffn_b[1], core_swap(ffn_b[2]))
    up_product = order(token_products, [ffn_b[7]], [ffn_b[8]])
    up_sum = WideSum(up_product, places, masks, wide_count)
    order.advance(up_sum)

    def attend_back(pair, fwd, ffn, held=()):
        return lambda att, sec: attn_backward(
            scalars, pair, fwd[0], att, sec, ffn[0], mod, fwd[1:4], out_weight, ffn[3], held
        )

    def input_back(pair, fwd, taps, before, held):
        return lambda gqkv, gmid, mods: input_backward(
            scalars, pair, fwd[0], mod, gqkv, qkv_all, attn_kernel, taps, gmid, mods, before, slots, held
        )

    back_a = order(attend_back(0, fwd_a, ffn_a), att_a, sec_a)
    sec_b = order(sum_pair, here_b, x_swap(here_b))
    sec_b = (sec_b, core_swap(sec_b))
    order.advance(down_sum)
    back_b = order(attend_back(1, fwd_b, ffn_b, back_a[2:4]), att_b, sec_b)
    order.advance(down_sum)
    attn_product = order(
        lambda grads, grouped, contexts, attended: jnp.concatenate(
            [token_products([grads], [grouped]), token_products([contexts], [attended])], 0
        ),
        back_b[3], fwd_b[6], fwd_b[7], back_b[2],
    )
    attn_sum = WideSum(attn_product, places, masks, wide_count, [0] + list(range(levels - 1, 0, -1)))
    order.advance(attn_sum)
    order.advance(up_sum)
    order.advance(down_sum)
    in_a = order(input_back(0, fwd_a, attn_kernel, attn_kernel, ffn_b[9:11]), back_b[3], *back_a[:2])
    order.advance(down_sum, up_sum)
    order.advance(attn_sum)
    in_b = order(input_back(1, fwd_b, in_a[0], in_a[1], in_a[2:4]), back_b[3], *back_b[:2])
    order.advance(down_sum)

    rows = 6 * per_dev
    bits = [1 << k for k in reversed(range(levels))]
    moves = [lambda v, bit=bit: (v, wide_swap(v, bit, wide_count)) for bit in bits]
    join = lambda a, b: jnp.concatenate([a, b], 0)
    whole_rows = lambda a, b, c: join(sum_pair(a, b)[: rows + 9], c[:9].astype(BF))[None]
    mods = Steps(
        (in_b[1], core_swap(in_b[1])),
        [(sum_pair, lambda v: (v, x_swap(v), ffn_b[4]))]
        + [(work, move) for work, move in zip([whole_rows] + [join] * len(bits), moves)],
    )
    order.advance(up_sum)
    order.advance(mods)
    order.advance(attn_sum)
    order.advance(mods)
    order.advance(up_sum)
    while not down_sum.done():
        order.advance(down_sum)
    down_grad = down_sum.finish(order, F32)
    made = order(functools.partial(slice_halves, x), in_b[2], core_swap(in_b[3]))
    order.advance(attn_sum, mods)
    order.advance(mods)
    order.advance(up_sum)
    order.advance(attn_sum)
    while not all(c.done() for c in (mods, up_sum)):
        order.advance(mods)
        order.advance(up_sum)

    def unpack(held):
        gmod = held[:, :rows].reshape(latent_total, 6 * width)
        taps = jnp.sum(held[:, rows:].astype(F32), 0) * factor
        return gmod, jnp.sum(gmod.astype(F32), 0) * factor, taps[:9], taps[9:]

    unpacked = order(lambda a, b: unpack(join(a, b)), *mods.came)
    order.last = tuple(unpacked)
    gmod, ada_bias_grad, attn_taps, ffn_taps = unpacked
    final_out, final_grad = order(
        lambda a, b: (sum_pair(a[:per_dev], b[:per_dev]), sum_pair(a[per_dev:], b[per_dev:])), made[0], x_swap(made[1])
    )
    order.last = (final_out, final_grad)
    up_grad = up_sum.finish(order, F32)
    while not attn_sum.done():
        order.advance(attn_sum)
    time_in_grad, time_out_grad, ada_weight_grad = order(
        lambda g: condition_back(g, embedded, stages, time_out, ada_weight, factor), gmod
    )
    attn_grads = attn_sum.finish(order, BF)
    qkv_rows_grad, out_grad = attn_grads[: 3 * share].astype(F32), attn_grads[3 * share :].astype(F32)
    qkv_grad = jnp.swapaxes(qkv_rows_grad.reshape(3, share, width), 1, 2)
    final_out = jnp.swapaxes(final_out, 1, 2)
    final_grad = jnp.swapaxes(final_grad, 1, 2)
    return (
        final_out, final_grad, time_in_grad, time_out_grad, ada_weight_grad, ada_bias_grad,
        attn_taps, qkv_grad, out_grad, up_grad, ffn_taps, down_grad,
    )


def solution(mesh):
    tokens = P("wide", None, "narrow")
    weights = (P(None, None, "narrow"), P("narrow", None), P(None, "narrow"), P(None, "narrow"), P("narrow", None))
    return jax.shard_map(
        body,
        mesh=mesh,
        in_specs=(tokens, tokens, P(), P(), P(), P(), P(), P()) + weights,
        out_specs=(tokens, tokens, P(), P(), P(), P(), P()) + weights,
        check_vma=False,
    )
```

```python
import functools
import math

import jax
import jax.numpy as jnp
from jax import lax
from jax.experimental import pallas as pl
from jax.experimental.pallas import tpu as pltpu
from jax.sharding import PartitionSpec as P

HEAD_DIM = 64
SIDE = 16
PAIR = 2
PAIRS = 2

BF = jnp.bfloat16
F32 = jnp.float32
HIGHEST = lax.Precision.HIGHEST
LANES = 128
ROWS = 128
FEW_ROWS = 128
MANY_ROWS = 256
BAND = 64
GELU_A = math.sqrt(2.0 / math.pi)
GELU_B = 0.044715
EPS = 1e-06
VMEM_LIMIT = 60 * 1024 * 1024
WEIGHT_ROWS = 256
BACK_ROWS = 128
PACKED = 40


def dot(a, b):
    return lax.dot_general(a, b, (((1,), (0,)), ((), ())), preferred_element_type=F32)


def dot_nt(a, b):
    return lax.dot_general(a, b, (((1,), (1,)), ((), ())), preferred_element_type=F32)


def dot_tn(a, b):
    return lax.dot_general(a, b, (((0,), (0,)), ((), ())), preferred_element_type=F32)


def column_of(rows):
    return lax.broadcasted_iota(jnp.int32, (rows, LANES), 0) % SIDE


def from_left(v):
    moved = pltpu.roll(v, 1, 0)
    return jnp.where(column_of(v.shape[0]) == 0, 0.0, moved)


def from_right(v):
    moved = pltpu.roll(v, v.shape[0] - 1, 0)
    return jnp.where(column_of(v.shape[0]) == SIDE - 1, 0.0, moved)


def conv_band(padded, at, lanes, kern):
    rows = [padded[pl.ds(at + SIDE * r, BAND), lanes] for r in range(3)]
    mixed = [
        rows[0] * kern[c] + rows[1] * kern[3 + c] + rows[2] * kern[6 + c] for c in range(3)
    ]
    return from_left(mixed[0]) + mixed[1] + from_right(mixed[2])


def conv_back_band(padded_grad, at, lanes, kern):
    wide = padded_grad[pl.ds(at, BAND + 2 * SIDE), lanes]
    shifted = [from_right(wide), wide, from_left(wide)]
    total = None
    for r in range(3):
        for c in range(3):
            low = SIDE * (2 - r)
            term = shifted[c][low : low + BAND] * kern[3 * r + c]
            total = term if total is None else total + term
    return total, [s[SIDE : SIDE + BAND] for s in shifted]


def fold_rows(v):
    total = v[0:8]
    for at in range(8, v.shape[0], 8):
        total = total + v[at : at + 8]
    return total


def taps_of(kern_ref, lanes):
    block = kern_ref[:, lanes]
    return [block[t : t + 1] for t in range(9)]


def zero_edges(ref):
    edge = jnp.zeros((SIDE, ref.shape[1]), F32)
    tall = ref.shape[0] // PAIR
    for rel in range(PAIR):
        ref[rel * tall : rel * tall + SIDE, :] = edge
        ref[(rel + 1) * tall - SIDE : (rel + 1) * tall, :] = edge


def inside(ref, rel):
    tall = ref.shape[0] // PAIR
    return slice(rel * tall + SIDE, (rel + 1) * tall - SIDE)


def gather_features(n, parts, held, out):
    _, share, tokens = parts[0].shape
    core = jnp.bitwise_and(n, 1)

    def one(rel):
        for step, part in enumerate(parts):
            held[jnp.bitwise_xor(n, step)] = part[jnp.bitwise_xor(rel, core)]
        out[pl.ds(pl.multiple_of(rel * tokens, tokens), tokens), :] = held[...].reshape(len(parts) * share, tokens).T

    pair_loop(one)


def by_core(core, low, share, keep_out, send_out, turned):
    tokens = low.shape[0] // PAIR

    def one(rel):
        lat = jnp.bitwise_xor(rel, core)
        turned[...] = low[pl.ds(pl.multiple_of(rel * tokens, tokens), tokens), :].T
        for x in range(2):
            here = pl.ds(pl.multiple_of((2 * x + core) * share, 16), share)
            there = pl.ds(pl.multiple_of((2 * x + 1 - core) * share, 16), share)
            keep_out[x, lat] = turned[here, :]
            send_out[x, lat] = turned[there, :]

    pair_loop(one)


def norm_stats(v):
    width = v.shape[1]
    mean = jnp.sum(v, -1, keepdims=True) * (1.0 / width)
    center = v - mean
    spread = jnp.sum(center * center, -1, keepdims=True) * (1.0 / width)
    scale = lax.rsqrt(spread + EPS)
    return center * scale, scale


def head_masks(share):
    lane = lax.broadcasted_iota(jnp.int32, (1, share), 1) // HEAD_DIM
    return [(lane == h).astype(F32).astype(BF) for h in range(share // HEAD_DIM)]


def half_rows(v, parity):
    tokens, width = v.shape
    split = v.reshape(tokens // (2 * SIDE), 2, SIDE, width)
    return split[:, parity].reshape(tokens // 2, width)


def join_rows(even, odd):
    half, width = even.shape
    both = jnp.stack([even.reshape(half // SIDE, SIDE, width), odd.reshape(half // SIDE, SIDE, width)], 1)
    return both.reshape(2 * half, width)


def softmax_rows(queries, keys):
    scores = dot_nt(queries, keys) * (1.0 / math.sqrt(HEAD_DIM))
    rows = lax.broadcasted_iota(jnp.int32, scores.shape, 0)
    cols = lax.broadcasted_iota(jnp.int32, scores.shape, 1)
    same = (rows + cols) % 2 == 0
    scores = jnp.where(same, scores, -1e30)
    top = jnp.max(scores, -1, keepdims=True)
    grown = jnp.where(same, jnp.exp(scores - top), 0.0)
    return grown / jnp.sum(grown, -1, keepdims=True)


def beside(stacked, heads):
    rows = stacked.shape[0] // heads
    return jnp.concatenate([stacked[h * rows : (h + 1) * rows] for h in range(heads)], axis=1)


def lane_loop(width, body):
    count = width // LANES

    def step(j, carry):
        body(j // count, pl.ds(pl.multiple_of((j % count) * LANES, LANES), LANES))
        return carry

    lax.fori_loop(0, PAIR * count, step, 0)


def band_loop(tokens, body, carry):
    return lax.fori_loop(0, tokens // BAND, lambda j, c: body(pl.multiple_of(j * BAND, BAND), c), carry)


def row_loop(tokens, body, size=ROWS):
    count = tokens // size

    def step(j, carry):
        body(j // count, pl.multiple_of(j * size, size))
        return carry

    lax.fori_loop(0, PAIR * count, step, 0)


def pair_loop(body):
    def step(j, carry):
        body(j)
        return carry

    lax.fori_loop(0, PAIR, step, 0)


def attn_kernel_body(
    flow, s_ref, xo, xc, xx, xd, mod, kern, wqkv, wout,
    full_out, q_out, k_out, v_out, keep_out, send_out, grouped_out, ctx_out,
    held, padded,
):
    n = s_ref[0]
    core = jnp.bitwise_and(n, 1)
    share, tokens = xo.shape[1], xo.shape[2]
    width = full_out.shape[1]
    tall = tokens + 2 * SIDE
    zero_edges(padded)
    flow.need(xo, xc, xx, xd, mod, kern)
    gather_features(n, (xo, xc, xx, xd), held, full_out)
    flow.sent(full_out)

    def rows(rel, at):
        lat = jnp.bitwise_xor(rel, core)
        normed, _ = norm_stats(full_out[pl.ds(at, MANY_ROWS), :].astype(F32))
        here = pl.ds(pl.multiple_of(at + (2 * rel + 1) * SIDE, SIDE), MANY_ROWS)
        padded[here, :] = normed * (1.0 + mod[lat, 1:2, :]) + mod[lat, 0:1, :]

    row_loop(tokens, rows, MANY_ROWS)

    def lanes(rel, at):
        taps = taps_of(kern, at)
        for band in range(0, tokens, BAND):
            here = pl.ds(pl.multiple_of(rel * tokens + band, BAND), BAND)
            grouped_out[here, at] = conv_band(padded, pl.multiple_of(rel * tall + band, SIDE), at, taps).astype(BF)

    lane_loop(width, lanes)
    flow.sent(grouped_out)
    flow.need(wqkv, wout)
    grouped = grouped_out[...]
    q_out[...] = dot_nt(grouped, wqkv[0]).astype(BF)
    k_out[...] = dot_nt(grouped, wqkv[1]).astype(BF)
    v_out[...] = dot_nt(grouped, wqkv[2]).astype(BF)
    flow.sent(q_out, k_out, v_out)
    masks = head_masks(share)
    heads = len(masks)

    def attend(rel):
        here = pl.ds(pl.multiple_of(rel * tokens, tokens), tokens)
        query, key, value = q_out[here, :], k_out[here, :], v_out[here, :]
        parts = []
        for parity in range(2):
            q = half_rows(query, parity)
            k = half_rows(key, parity)
            v = half_rows(value, parity)
            probs = softmax_rows(jnp.concatenate([q * m for m in masks], axis=0), k)
            low = beside(probs.astype(BF), heads)
            parts.append(dot(low, jnp.concatenate([v * m for m in masks], axis=0)).astype(BF))
        ctx_out[here, :] = join_rows(*parts)

    pair_loop(attend)
    flow.sent(ctx_out)
    send_out[...] = dot(ctx_out[tokens : 2 * tokens, :], wout[...]).astype(BF)
    flow.sent(send_out)
    keep_out[...] = dot(ctx_out[0:tokens, :], wout[...]).astype(BF)
    flow.sent(keep_out)


def ffn_kernel_body(
    first, flow, s_ref, go, gc, gx, gd, full, att, mod, up, down, kern, kgrad_in,
    g_out, keep_out, send_out, mods_out, kgrad_out, active_out, gfed_out, second_out, ghid_out, fkeep_out, fsend_out,
    held, padded, slope, gpad, mid, fed, low, sums, turned,
):
    n = s_ref[0]
    core = jnp.bitwise_and(n, 1)
    share, tokens = go.shape[1], go.shape[2]
    units = up.shape[1]
    tall = tokens + 2 * SIDE
    zero_edges(padded)
    zero_edges(gpad)
    flow.need(go, gc, gx, gd)
    gather_features(n, (go, gc, gx, gd), held, g_out)
    flow.sent(g_out)
    flow.need(full, att, mod, kgrad_in)
    kgrad_out[...] = jnp.zeros(kgrad_out.shape, F32) if first else kgrad_in[...]

    def rows(rel, at):
        lat = jnp.bitwise_xor(rel, core)
        here = pl.ds(at, ROWS)
        middle = full[here, :].astype(F32) + mod[lat, 2:3, :] * att[here, :].astype(F32)
        mid[here, :] = middle
        normed, _ = norm_stats(middle)
        second_out[here, :] = (normed * (1.0 + mod[lat, 4:5, :]) + mod[lat, 3:4, :]).astype(BF)
        gfed_out[here, :] = (mod[lat, 5:6, :] * g_out[here, :].astype(F32)).astype(BF)

    row_loop(tokens, rows)
    flow.sent(second_out, gfed_out)
    flow.need(up, kern)
    hidden = dot(second_out[...], up[...])
    for rel in range(PAIR):
        padded[inside(padded, rel), :] = hidden[rel * tokens : (rel + 1) * tokens]

    def lanes(rel, at):
        taps = taps_of(kern, at)
        for band in range(0, tokens, BAND):
            here = pl.ds(pl.multiple_of(rel * tokens + band, BAND), BAND)
            mixed = conv_band(padded, pl.multiple_of(rel * tall + band, SIDE), at, taps)
            square = mixed * mixed
            curve = jnp.tanh(GELU_A * mixed * (1.0 + GELU_B * square))
            half = 0.5 * (1.0 + curve)
            active_out[here, at] = (mixed * half).astype(BF)
            slope[here, at] = half + (0.5 * GELU_A) * mixed * (1.0 - curve * curve) * (
                1.0 + (3.0 * GELU_B) * square
            )

    lane_loop(units, lanes)
    flow.sent(active_out)
    flow.need(down)
    fed[...] = dot(active_out[...], down[...])
    sums[...] = jnp.zeros(sums.shape, F32)

    def rows_fed(rel, at):
        lat = jnp.bitwise_xor(rel, core)
        here = pl.ds(at, ROWS)
        term = fed[here, :]
        sums[lat] += fold_rows(term * g_out[here, :].astype(F32))
        low[here, :] = (mod[lat, 5:6, :] * term + 0.25 * mid[here, :]).astype(BF)

    row_loop(tokens, rows_fed)
    for lat in range(PAIR):
        mods_out[lat] = jnp.sum(sums[lat], 0, keepdims=True)
    by_core(core, low, share, fkeep_out, fsend_out, turned)
    flow.sent(fkeep_out, fsend_out, mods_out)
    gact = dot_nt(gfed_out[...], down[...]).astype(BF).astype(F32)
    for rel in range(PAIR):
        here = slice(rel * tokens, (rel + 1) * tokens)
        gpad[inside(gpad, rel), :] = gact[here] * slope[here, :]

    def lanes_back(rel, at):
        taps = taps_of(kern, at)
        sums = [None] * 9
        for band in range(0, tokens, BAND):
            here = pl.ds(pl.multiple_of(rel * tokens + band, BAND), BAND)
            base = pl.multiple_of(rel * tall + band, SIDE)
            total, shifted = conv_back_band(gpad, base, at, taps)
            ghid_out[here, at] = total.astype(BF)
            for r in range(3):
                values = padded[pl.ds(base + SIDE * r, BAND), at]
                for c in range(3):
                    part = fold_rows(values * shifted[c])
                    sums[3 * r + c] = part if sums[3 * r + c] is None else sums[3 * r + c] + part
        for t in range(9):
            kgrad_out[t : t + 1, at] += jnp.sum(sums[t], 0, keepdims=True)

    lane_loop(units, lanes_back)
    flow.sent(ghid_out, kgrad_out)
    send_out[...] = dot_nt(ghid_out[tokens : 2 * tokens, :], up[...]).astype(BF)
    flow.sent(send_out)
    keep_out[...] = dot_nt(ghid_out[0:tokens, :], up[...]).astype(BF)
    flow.sent(keep_out)


def attn_back_body(
    flow, s_ref, full, att, gs, gfull, mod, q_in, k_in, v_in, wout, gates,
    gmid_out, mods_out, gatt_out, gqkv_out,
    sums, gctx,
):
    core = jnp.bitwise_and(s_ref[0], 1)
    tokens = full.shape[0] // PAIR
    width = full.shape[1]
    share = q_in.shape[1]
    mods_out[...] = jnp.zeros(mods_out.shape, F32)
    sums[...] = jnp.zeros(sums.shape, F32)
    flow.need(full, att, gs, gfull, mod)

    def rows(rel, at):
        lat = jnp.bitwise_xor(rel, core)
        here = pl.ds(at, ROWS)
        gate1 = mod[lat, 2:3, :]
        attended = att[here, :].astype(F32)
        normed, inv = norm_stats(full[here, :].astype(F32) + gate1 * attended)
        grad = gs[here, :].astype(F32)
        inner = grad * (1.0 + mod[lat, 4:5, :])
        mean_a = jnp.sum(inner, -1, keepdims=True) * (1.0 / width)
        mean_b = jnp.sum(inner * normed, -1, keepdims=True) * (1.0 / width)
        whole_grad = gfull[here, :].astype(F32) + inv * (inner - mean_a - normed * mean_b)
        gmid_out[here, :] = whole_grad.astype(BF)
        gatt_out[here, :] = (gate1 * whole_grad).astype(BF)
        sums[3 * lat] += fold_rows(attended * whole_grad)
        sums[3 * lat + 1] += fold_rows(grad)
        sums[3 * lat + 2] += fold_rows(grad * normed)

    row_loop(tokens, rows)
    for lat in range(PAIR):
        for k in range(3):
            mods_out[lat, 2 + k : 3 + k, :] = 0.25 * jnp.sum(sums[3 * lat + k], 0, keepdims=True)
    flow.need(wout, q_in, k_in, v_in, gates)
    for lat in range(PAIR):
        mods_out[lat, 5:6, :] = gates[lat]
    flow.sent(gatt_out, gmid_out, mods_out)
    gctx[...] = dot_nt(gatt_out[...], wout[...]).astype(BF)
    masks = head_masks(share)
    heads = len(masks)
    factor = 1.0 / math.sqrt(HEAD_DIM)

    def attend(rel):
        here = pl.ds(pl.multiple_of(rel * tokens, tokens), tokens)
        query, key, value, grads = q_in[here, :], k_in[here, :], v_in[here, :], gctx[here, :]
        parts_q, parts_k, parts_v = [], [], []
        for parity in range(2):
            q = half_rows(query, parity)
            k = half_rows(key, parity)
            v = half_rows(value, parity)
            gc = half_rows(grads, parity)
            q_all = jnp.concatenate([q * m for m in masks], axis=0)
            k_all = jnp.concatenate([k * m for m in masks], axis=0)
            gc_all = jnp.concatenate([gc * m for m in masks], axis=0)
            probs = softmax_rows(q_all, k)
            parts_v.append(dot_tn(probs.astype(BF), gc_all).astype(BF))
            gprobs = dot_nt(gc_all, v).astype(BF).astype(F32)
            gscores = (probs * (gprobs - jnp.sum(probs * gprobs, -1, keepdims=True))).astype(BF)
            parts_q.append((dot(beside(gscores, heads), k_all) * factor).astype(BF))
            parts_k.append((dot_tn(gscores, q_all) * factor).astype(BF))
        for k, parts in enumerate((parts_q, parts_k, parts_v)):
            gqkv_out[here, k * share : (k + 1) * share] = join_rows(*parts)

    pair_loop(attend)
    flow.sent(gqkv_out)


def input_back_body(
    closing, flow, s_ref, full, mod, gqkv, wqkv, kern, kgrad_in, gmid, mods_in, before,
    kgrad_out, mods_out, keep_out, send_out,
    normed1, scale1, first, gpad, gback, low, mods, rows_out, turned,
):
    core = jnp.bitwise_and(s_ref[0], 1)
    tokens = full.shape[0] // PAIR
    width = full.shape[1]
    share = gqkv.shape[1] // 3
    tall = tokens + 2 * SIDE
    zero_edges(first)
    zero_edges(gpad)
    flow.need(full, mod)

    def rows_first(rel, at):
        lat = jnp.bitwise_xor(rel, core)
        here = pl.ds(at, FEW_ROWS)
        normed, inv = norm_stats(full[here, :].astype(F32))
        normed1[here, :] = normed
        scale1[here, :] = jnp.broadcast_to(inv, (FEW_ROWS, LANES))
        inside_rows = pl.ds(pl.multiple_of(at + (2 * rel + 1) * SIDE, SIDE), FEW_ROWS)
        first[inside_rows, :] = normed * (1.0 + mod[lat, 1:2, :]) + mod[lat, 0:1, :]

    row_loop(tokens, rows_first, FEW_ROWS)
    flow.need(gqkv, wqkv, kern, kgrad_in, gmid, mods_in, before)
    kgrad_out[...] = kgrad_in[...] if closing else jnp.zeros(kgrad_out.shape, F32)
    mods[...] = mods_in[...]
    for rel in range(PAIR):
        here = slice(rel * tokens, (rel + 1) * tokens)
        gpad[inside(gpad, rel), :] = dot(gqkv[here, :], wqkv[...])

    def lanes(rel, at):
        taps = taps_of(kern, at)
        sums = [None] * 9
        shift_sum, scale_sum = None, None
        for band in range(0, tokens, BAND):
            here = pl.ds(pl.multiple_of(rel * tokens + band, BAND), BAND)
            base = pl.multiple_of(rel * tall + band, SIDE)
            total, shifted = conv_back_band(gpad, base, at, taps)
            gback[here, at] = total
            part_a, part_b = fold_rows(total), fold_rows(total * normed1[here, at])
            shift_sum = part_a if shift_sum is None else shift_sum + part_a
            scale_sum = part_b if scale_sum is None else scale_sum + part_b
            for r in range(3):
                values = first[pl.ds(base + SIDE * r, BAND), at]
                for c in range(3):
                    part = fold_rows(values * shifted[c])
                    sums[3 * r + c] = part if sums[3 * r + c] is None else sums[3 * r + c] + part
        for t in range(9):
            kgrad_out[t : t + 1, at] += jnp.sum(sums[t], 0, keepdims=True)
        lat = jnp.bitwise_xor(rel, core)
        mods[lat, 0:1, at] = jnp.sum(shift_sum, 0, keepdims=True)
        mods[lat, 1:2, at] = jnp.sum(scale_sum, 0, keepdims=True)

    lane_loop(width, lanes)
    if closing:
        rows_out[...] = jnp.zeros(rows_out.shape, F32)
        for lat in range(PAIR):
            rows_out[6 * lat : 6 * lat + 6, :] = before[lat, 0:6, :]
            rows_out[6 * (PAIR + lat) : 6 * (PAIR + lat) + 6, :] = mods[lat, 0:6, :]
        rows_out[12 * PAIR : 12 * PAIR + 9, :] = kgrad_out[0:9, :]
        mods_out[...] = rows_out[...].astype(BF)
    else:
        mods_out[...] = mods[...]
    flow.sent(mods_out, kgrad_out)

    def rows_back(rel, at):
        lat = jnp.bitwise_xor(rel, core)
        here = pl.ds(at, FEW_ROWS)
        inner = gback[here, :] * (1.0 + mod[lat, 1:2, :])
        normed = normed1[here, :]
        mean_a = jnp.sum(inner, -1, keepdims=True) * (1.0 / width)
        mean_b = jnp.sum(inner * normed, -1, keepdims=True) * (1.0 / width)
        grad = scale1[here, 0:1] * (inner - mean_a - normed * mean_b)
        low[here, :] = (grad + 0.25 * gmid[here, :].astype(F32)).astype(BF)

    row_loop(tokens, rows_back, FEW_ROWS)
    by_core(core, low, share, keep_out, send_out, turned)
    flow.sent(keep_out, send_out)


class Flow:
    def __init__(self, arrivals, departures):
        self.arrivals, self.departures = arrivals, departures
        self.leaving = []
        for _, copy in arrivals:
            copy.start()

    def need(self, *refs):
        for ref in refs:
            for _, copy in [a for a in self.arrivals if a[0] is ref]:
                copy.wait()
            self.arrivals = [a for a in self.arrivals if a[0] is not ref]

    def sent(self, *refs):
        for ref in refs:
            for held, copy in self.departures:
                if held is ref:
                    copy.start()
                    self.leaving.append(copy)

    def end(self):
        for copy in self.leaving:
            copy.wait()


def call(body, name, scalars, ins, outs, scratch, flops, held=()):
    n_in, n_out = len(ins), len(outs)
    places, buffer_shapes = [], []
    for array, window, into in ins:
        dims = array.shape if window is None else (window[0].size,) + array.shape[1:]
        if into is None:
            buffer_shapes.append((dims, array.dtype))
        elif into[0].start == 0:
            buffer_shapes.append(((PAIR * dims[0],) + dims[1:], array.dtype))
        places.append(len(buffer_shapes) - 1)

    def run(s_ref, *refs):
        sources = refs[:n_in]
        targets = refs[n_in + len(held) : n_in + len(held) + n_out]
        buffers = refs[n_in + len(held) + n_out : -1]
        sems = refs[-1]
        n_held = len(buffer_shapes)
        buffers_in, buffers_out = buffers[:n_held], buffers[n_held : n_held + n_out]
        rest = buffers[n_held + n_out :]
        arrivals, departures = [], []
        for k, (source, (_, window, into)) in enumerate(zip(sources, ins)):
            view = source if window is None else source.at[window]
            buffer = buffers_in[places[k]]
            target = buffer if into is None else buffer.at[into]
            arrivals.append((buffer, pltpu.make_async_copy(view, target, sems.at[k])))
        for k, (target, buffer, out) in enumerate(zip(targets, buffers_out, outs)):
            view = target if out[2] is None else target.at[out[2]]
            departures.append((buffer, pltpu.make_async_copy(buffer, view, sems.at[n_in + k])))
        flow = Flow(arrivals, departures)
        body(flow, s_ref, *buffers_in, *buffers_out, *rest)
        flow.end()

    anywhere = pl.BlockSpec(memory_space=pl.ANY)
    return pl.pallas_call(
        run,
        name=name,
        out_shape=[jax.ShapeDtypeStruct(o[0], o[1]) for o in outs],
        grid_spec=pltpu.PrefetchScalarGridSpec(
            num_scalar_prefetch=1,
            grid=(1,),
            in_specs=[anywhere] * (n_in + len(held)),
            out_specs=[anywhere] * n_out,
            scratch_shapes=[pltpu.VMEM(dims, dtype) for dims, dtype in buffer_shapes]
            + [pltpu.VMEM(o[3], o[1]) for o in outs]
            + scratch
            + [pltpu.SemaphoreType.DMA((n_in + n_out,))],
        ),
        input_output_aliases={1 + n_in + k: n_out - len(held) + k for k in range(len(held))},
        compiler_params=pltpu.CompilerParams(vmem_limit_bytes=VMEM_LIMIT),
        cost_estimate=pl.CostEstimate(flops=flops, bytes_accessed=10**6, transcendentals=0),
    )(scalars, *[i[0] for i in ins], *held)


def slices_out(slots, slot, share, tokens):
    return ((2, slots, share, tokens), BF, (slice(None), pl.ds(PAIR * slot, PAIR)), (2, PAIR, share, tokens))


def whole(array):
    return (array, None, None)


def stacked(arrays):
    rows = arrays[0].shape[0]
    return [(v, None, (pl.ds(k * rows, rows),)) for k, v in enumerate(arrays)]


def whole_out(dims, dtype):
    return (dims, dtype, None, dims)


def pair_rows(array, pair):
    rows = array.shape[0] // PAIRS
    return (array, (pl.ds(rows * pair, rows),), None)


def pair_rows_out(rows, width, pair):
    return ((PAIRS * rows, width), BF, (pl.ds(rows * pair, rows),), (rows, width))


def pair_of(array, pair):
    return (array, (pl.ds(PAIR * pair, PAIR),), None)


def split_low(v):
    high = v.astype(BF)
    return high, (v - high.astype(F32)).astype(BF)


def rows_product(a, b):
    (ah, al), (bh, bl) = split_low(a), split_low(b)
    return dot_tn(jnp.concatenate([ah, al, ah], 0), jnp.concatenate([bh, bh, bl], 0))


def back_product(a, weight):
    (ah, al), (wh, wl) = split_low(a), split_low(weight)
    return dot_nt(ah, wh) + dot_nt(al, wh) + dot_nt(ah, wl)


def product(a, weight):
    (ah, al), (wh, wl) = split_low(a), split_low(weight)
    return dot(ah, wh) + dot(al, wh) + dot(ah, wl)


def silu(v):
    return v / (1.0 + jnp.exp(-v))


def silu_slope(v):
    gate = 1.0 / (1.0 + jnp.exp(-v))
    return gate * (1.0 + v * (1.0 - gate))


def row_blocks(source, target, sems, rows):
    return [
        pltpu.make_async_copy(source.at[pl.ds(at, rows)], target.at[pl.ds(at, rows)], sems.at[at // rows])
        for at in range(0, source.shape[0], rows)
    ]


def condition_body(
    steps, stamps, wide, bias, time_in, time_out, ada,
    mod_out, embedded, inner_pre, inner, outer_pre, outer, held_in, held_out, held, sums, parts, rows_of, sems,
):
    depth = ada.shape[0]
    per_dev, count, width = mod_out.shape
    first = pltpu.make_async_copy(time_in, held_in, sems.at[0])
    second = pltpu.make_async_copy(time_out, held_out, sems.at[1])
    blocks = row_blocks(ada, held, sems.at[pl.ds(2, depth // WEIGHT_ROWS)], WEIGHT_ROWS)
    for copy in [first, second] + blocks:
        copy.start()
    halved = embedded.shape[1] // 2
    for r in range(embedded.shape[0]):
        at = jnp.bitwise_xor(wide[0], steps[r // per_dev]) * per_dev + r % per_dev
        rows_of[r : r + 1, :] = jnp.broadcast_to(stamps[at].astype(F32), (1, halved))
    order = lax.broadcasted_iota(jnp.int32, (1, halved), 1).astype(F32)
    angles = rows_of[...] * jnp.exp(-math.log(10000.0) * order / halved)
    embedded[:, 0:halved] = jnp.cos(angles)
    embedded[:, halved:] = jnp.sin(angles)
    first.wait()
    inner_pre[...] = product(embedded[...], held_in[...])
    inner[...] = silu(inner_pre[...])
    second.wait()
    outer_pre[...] = product(inner[...], held_out[...])
    outer[...] = silu(outer_pre[...])
    wide_bias = [jnp.concatenate([bias[k + j : k + j + 1, :] for j in range(width // LANES)], 1)
                 for k in range(0, bias.shape[0], width // LANES)]
    total = jnp.concatenate(wide_bias, 1)
    sums[...] = jnp.broadcast_to(total, sums.shape)
    for k in range(depth // WEIGHT_ROWS):
        parts[k] = outer[0:8, k * WEIGHT_ROWS : (k + 1) * WEIGHT_ROWS]

    def add(k, carry):
        rows = pl.ds(pl.multiple_of(k * WEIGHT_ROWS, WEIGHT_ROWS), WEIGHT_ROWS)
        pltpu.make_async_copy(ada.at[rows], held.at[rows], sems.at[2 + k]).wait()
        sums[...] += product(parts[k], held[rows, :])
        return carry

    lax.fori_loop(0, depth // WEIGHT_ROWS, add, 0)
    total = sums[...]
    for lat in range(per_dev):
        for k in range(count):
            mod_out[lat, k : k + 1, :] = total[lat : lat + 1, k * width : (k + 1) * width]


def condition(steps, stamps, wide, time_in, time_out, ada_weight, ada_bias, per_dev, width):
    latent_total = stamps.shape[0]
    depth, columns = ada_weight.shape
    vmem = pl.BlockSpec(memory_space=pltpu.VMEM)
    anywhere = pl.BlockSpec(memory_space=pl.ANY)
    rows = jax.ShapeDtypeStruct((latent_total, depth), F32)
    return pl.pallas_call(
        functools.partial(condition_body, steps),
        name="condition",
        in_specs=[pl.BlockSpec(memory_space=pltpu.SMEM)] * 2 + [vmem, anywhere, anywhere, anywhere],
        out_specs=[vmem] * 6,
        out_shape=[
            jax.ShapeDtypeStruct((per_dev, columns // width, width), F32),
            jax.ShapeDtypeStruct((latent_total, time_in.shape[0]), F32),
            rows, rows, rows, rows,
        ],
        scratch_shapes=[
            pltpu.VMEM(time_in.shape, F32),
            pltpu.VMEM(time_out.shape, F32),
            pltpu.VMEM(ada_weight.shape, F32),
            pltpu.VMEM((8, columns), F32),
            pltpu.VMEM((depth // WEIGHT_ROWS, 8, WEIGHT_ROWS), F32),
            pltpu.VMEM((latent_total, time_in.shape[0] // 2), F32),
            pltpu.SemaphoreType.DMA((2 + depth // WEIGHT_ROWS,)),
        ],
        compiler_params=pltpu.CompilerParams(vmem_limit_bytes=VMEM_LIMIT),
        cost_estimate=pl.CostEstimate(flops=8 * 10**9, bytes_accessed=10**6, transcendentals=0),
    )(stamps, wide, ada_bias.reshape(columns // LANES, LANES), time_in, time_out, ada_weight)


def condition_back_body(
    factor, gmod, embedded, inner_pre, inner, outer_pre, outer, time_out, ada,
    time_in_grad, time_out_grad, ada_grad, held_out, held, outer_grad, columns, sems, arriving, leaving,
):
    count = ada.shape[0] // BACK_ROWS

    def block_copy(source, target, sem, k):
        rows = pl.ds(k * BACK_ROWS, BACK_ROWS)
        return pltpu.make_async_copy(source.at[rows], target.at[rows], sem.at[k])

    first = pltpu.make_async_copy(time_out, held_out, sems.at[0])
    for k in range(count):
        block_copy(ada, held, arriving, k).start()
    first.start()
    high, low = split_low(outer[...])
    both = jnp.concatenate([high, low], 0)
    for k in range(count):
        columns[k] = both[:, k * BACK_ROWS : (k + 1) * BACK_ROWS]

    def block(k, carry):
        rows = pl.ds(pl.multiple_of(k * BACK_ROWS, BACK_ROWS), BACK_ROWS)
        block_copy(ada, held, arriving, k).wait()
        grads = gmod[...]
        high, low = split_low(held[rows, :])
        outer_grad[rows, :] = dot_nt(high, grads) + dot_nt(low, grads)
        held[rows, :] = dot_tn(columns[k], jnp.concatenate([grads, grads], 0)) * factor
        block_copy(held, ada_grad, leaving, k).start()
        return carry

    lax.fori_loop(0, count, block, 0)
    first.wait()
    back = outer_grad[...].T * factor * silu_slope(outer_pre[...])
    time_out_grad[...] = rows_product(inner[...], back)
    back = back_product(back, held_out[...]) * silu_slope(inner_pre[...])
    time_in_grad[...] = rows_product(embedded[...], back)
    for k in range(count):
        block_copy(held, ada_grad, leaving, k).wait()


def condition_back(gmod, embedded, stages, time_out, ada_weight, factor):
    depth = ada_weight.shape[0]
    latent_total = gmod.shape[0]
    vmem = pl.BlockSpec(memory_space=pltpu.VMEM)
    anywhere = pl.BlockSpec(memory_space=pl.ANY)
    time_in_dims = (embedded.shape[1], time_out.shape[0])
    return pl.pallas_call(
        functools.partial(condition_back_body, factor),
        name="condition_back",
        in_specs=[vmem] * 6 + [anywhere] * 2,
        out_specs=[vmem, vmem, anywhere],
        out_shape=[
            jax.ShapeDtypeStruct(time_in_dims, F32),
            jax.ShapeDtypeStruct(time_out.shape, F32),
            jax.ShapeDtypeStruct(ada_weight.shape, F32),
        ],
        scratch_shapes=[
            pltpu.VMEM(time_out.shape, F32),
            pltpu.VMEM(ada_weight.shape, F32),
            pltpu.VMEM((depth, latent_total), F32),
            pltpu.VMEM((depth // BACK_ROWS, 2 * latent_total, BACK_ROWS), BF),
            pltpu.SemaphoreType.DMA((1,)),
            pltpu.SemaphoreType.DMA((depth // BACK_ROWS,)),
            pltpu.SemaphoreType.DMA((depth // BACK_ROWS,)),
        ],
        compiler_params=pltpu.CompilerParams(vmem_limit_bytes=VMEM_LIMIT),
        cost_estimate=pl.CostEstimate(flops=1, bytes_accessed=1, transcendentals=0),
    )(gmod, embedded, *stages, time_out, ada_weight)


def attn_forward(scalars, pair, x_parts, mod, attn_kernel, qkv_weight, out_weight, held):
    _, share, tokens = x_parts[0].shape
    width = out_weight.shape[1]
    rows = PAIR * tokens
    thin = whole_out((rows, share), BF)
    half = whole_out((tokens, width), BF)
    return call(
        attn_kernel_body, "attn_fwd", scalars,
        [pair_of(v, pair) for v in x_parts] + [pair_of(mod, pair), whole(attn_kernel), whole(qkv_weight), whole(out_weight)],
        [whole_out((rows, width), BF), thin, thin, thin, half, half, pair_rows_out(rows, width, pair),
         pair_rows_out(rows, share, pair)],
        [pltpu.VMEM((4, share, tokens), BF), pltpu.VMEM((PAIR * (tokens + 2 * SIDE), width), F32)],
        6_000_000_000, held,
    )


def feed_forward(scalars, pair, full, att, g_parts, mod, up_weight, down_weight, ffn_kernel, slots, taps, held):
    _, share, tokens = g_parts[0].shape
    width, units = up_weight.shape
    rows = PAIR * tokens
    tall = PAIR * (tokens + 2 * SIDE)
    half = whole_out((tokens, width), BF)
    slices = slices_out(slots, pair, share, tokens)
    return call(
        functools.partial(ffn_kernel_body, pair == 0), "ffn", scalars,
        [pair_of(v, pair) for v in g_parts] + [whole(full)] + stacked(att)
        + [pair_of(mod, pair), whole(up_weight), whole(down_weight), whole(ffn_kernel), whole(taps)],
        [whole_out((rows, width), BF), half, half, whole_out((PAIR, 1, width), F32), whole_out((16, units), F32),
         whole_out((rows, units), BF), whole_out((rows, width), BF), pair_rows_out(rows, width, pair),
         pair_rows_out(rows, units, pair), slices, slices],
        [pltpu.VMEM((4, share, tokens), BF), pltpu.VMEM((tall, units), F32), pltpu.VMEM((rows, units), F32),
         pltpu.VMEM((tall, units), F32), pltpu.VMEM((rows, width), F32), pltpu.VMEM((rows, width), F32),
         pltpu.VMEM((rows, width), BF), pltpu.VMEM((PAIR, 8, width), F32), pltpu.VMEM((width, tokens), BF)],
        10_000_000_000, held,
    )


def attn_backward(scalars, pair, full, att, gsec, gfull, mod, qkv, out_weight, gates, held):
    tokens, width = att[0].shape
    share = out_weight.shape[0]
    rows = PAIR * tokens
    broad = whole_out((rows, width), BF)
    return call(
        attn_back_body, "attn_bwd", scalars,
        [whole(full)] + stacked(att) + stacked(gsec) + [whole(gfull), pair_of(mod, pair)]
        + [whole(v) for v in qkv] + [whole(out_weight), whole(gates)],
        [broad, whole_out((PAIR, 8, width), F32), pair_rows_out(rows, width, pair), pair_rows_out(rows, 3 * share, pair)],
        [pltpu.VMEM((3 * PAIR, 8, width), F32), pltpu.VMEM((rows, share), BF)],
        6_000_000_000, held,
    )


def input_backward(scalars, pair, full, mod, gqkv, qkv_weight, attn_kernel, taps, gmid, mods_in, before, slots, held):
    rows, width = full.shape
    tokens = rows // PAIR
    share = gqkv.shape[1] // 3
    tall = PAIR * (tokens + 2 * SIDE)
    slices = slices_out(slots, slots // PAIR // 2 + pair, share, tokens)
    closing = pair > 0
    mods = whole_out((PACKED, width), BF) if closing else whole_out((PAIR, 8, width), F32)
    return call(
        functools.partial(input_back_body, closing), "input_bwd", scalars,
        [whole(full), pair_of(mod, pair), pair_rows(gqkv, pair), whole(qkv_weight), whole(attn_kernel), whole(taps), whole(gmid),
         whole(mods_in), whole(before)],
        [whole_out((16, width), F32), mods, slices, slices],
        [pltpu.VMEM((rows, width), F32), pltpu.VMEM((rows, LANES), F32), pltpu.VMEM((tall, width), F32),
         pltpu.VMEM((tall, width), F32), pltpu.VMEM((rows, width), F32), pltpu.VMEM((rows, width), BF),
         pltpu.VMEM((PAIR, 8, width), F32), pltpu.VMEM((PACKED, width), F32), pltpu.VMEM((width, tokens), BF)],
        6_000_000_000, held,
    )


def core_swap(v):
    return lax.ppermute(v, "narrow", [(0, 1), (1, 0), (2, 3), (3, 2)])


def x_swap(v):
    return lax.ppermute(v, "narrow", [(0, 2), (2, 0), (1, 3), (3, 1)])


def sum_pair(a, b):
    return (a.astype(F32) + b.astype(F32)).astype(BF)


def slice_halves(x, keep, arrived):
    both = sum_pair(keep, arrived)
    return (
        lax.dynamic_index_in_dim(both, x, 0, keepdims=False),
        lax.dynamic_index_in_dim(both, 1 - x, 0, keepdims=False),
    )


def wide_swap(v, bit, count):
    return lax.ppermute(v, "wide", [(i, i ^ bit) for i in range(count)])


def pick(v, parts, at):
    rows = v.shape[0] // parts
    return lax.dynamic_slice_in_dim(v, at * rows, rows, 0)


def in_place(second, own, came, axis):
    dims = own.shape[:axis] + (2,) + own.shape[axis + 1 :]
    chosen = lax.broadcast_in_dim(second, dims, (axis,))
    return jnp.where(chosen, own, came)


class WideSum:
    def __init__(self, product, bits, masks, count, back=None):
        self.count, self.dims, self.bits, self.masks = count, product.shape, bits, masks
        self.levels = count.bit_length() - 1
        self.ahead = list(range(self.levels))
        self.back = list(reversed(self.ahead)) if back is None else back
        self.opened = False
        self.held = product

    def swap(self, sent, level):
        self.came = wide_swap(sent, 1 << level, self.count)

    def halve(self, held, came):
        level = self.ahead[0]
        if level == 0:
            held = pick(held, 2, self.bits[0])
        if len(self.ahead) == 1:
            return (sum_pair(held, came),)
        bit = self.bits[level + 1]
        return tuple(sum_pair(pick(held, 2, at), pick(came, 2, at)) for at in (1 - bit, bit))

    def pending(self):
        if not self.opened:
            return lambda v: pick(v, 2, 1 - self.bits[0]), (self.held,)
        if self.ahead:
            return self.halve, (self.held, self.came)
        level = self.back[0]
        return lambda a, b: in_place(self.masks[level], a, b, level), (self.held, self.came)

    def accept(self, out):
        if not self.opened:
            self.opened = True
            self.swap(out, 0)
        elif self.ahead:
            self.ahead.pop(0)
            self.held = out[-1]
            if self.ahead:
                self.swap(out[0], self.ahead[0])
            else:
                self.held = self.held.reshape((1,) * self.levels + self.held.shape)
                self.swap(self.held, self.back[0])
        else:
            self.back.pop(0)
            self.held = out
            self.swap(out, self.back[0])

    def done(self):
        return self.opened and not self.ahead and len(self.back) == 1

    def finish(self, order, dtype):
        level = self.back[0]
        whole_sum = order(lambda a, b: in_place(self.masks[level], a, b, level).astype(dtype), self.held, self.came)
        return lax.optimization_barrier(whole_sum).reshape(self.dims)


class Steps:
    def __init__(self, came, steps):
        self.came, self.steps = came, list(steps)

    def pending(self):
        return self.steps[0][0], self.came

    def accept(self, out):
        _, move = self.steps.pop(0)
        self.came = move(out)

    def done(self):
        return not self.steps


class Order:
    def __init__(self):
        self.last = ()

    def __call__(self, step, *inputs):
        inputs, _ = lax.optimization_barrier((inputs, self.last))
        out = step(*inputs)
        self.last = tuple(jax.tree.leaves(out)[:1])
        return out

    def advance(self, *chains):
        chains = [c for c in chains if not c.done()]
        if chains:
            work = [c.pending() for c in chains]
            outs = self(lambda *v: [w[0](*a) for w, a in zip(work, v)], *[w[1] for w in work])
            self.last = tuple(jax.tree.leaves(out)[0] for out in outs)
            for chain, out in zip(chains, outs):
                chain.accept(out)


def after(value, *others):
    return lax.optimization_barrier((value, others))[0]


def body(
    latents, cotangent, timesteps, time_in, time_out, ada_weight, ada_bias,
    attn_kernel, qkv_weight, out_weight, up_weight, ffn_kernel, down_weight,
):
    wide_count = lax.axis_size("wide")
    wide_at = lax.axis_index("wide")
    n = lax.axis_index("narrow")
    per_dev, tokens, share = latents.shape
    width = out_weight.shape[1]
    units = up_weight.shape[1]
    latent_total = timesteps.shape[0]
    scalars = n.astype(jnp.int32).reshape(1)

    steps, bit = [0], wide_count // 2
    while bit:
        steps, bit = steps + [k ^ bit for k in steps], bit // 2
    mod, embedded, *stages = condition(
        steps, timesteps, wide_at.astype(jnp.int32).reshape(1), time_in, time_out, ada_weight, ada_bias, per_dev, width
    )
    x = n // 2
    factor = 1.0 / latent_total

    def token_products(lefts, rights):
        return (sum(dot_tn(a, b) for a, b in zip(lefts, rights)) * factor).astype(BF)

    x_own = jnp.swapaxes(latents, 1, 2)
    g_own = jnp.swapaxes(cotangent, 1, 2)
    qkv_rows = jnp.swapaxes(qkv_weight, 1, 2)
    qkv_all = qkv_rows.reshape(3 * share, width)
    order = Order()
    x_across = x_swap(x_own)
    x_across = after(x_across, mod)
    g_across = x_swap(after(g_own, x_across))
    x_parts = (x_own, core_swap(x_own), x_across, core_swap(x_across))
    g_parts = (g_own, core_swap(g_own), g_across, core_swap(g_across))

    def attend(pair, held=()):
        return lambda parts: attn_forward(scalars, pair, parts, mod, attn_kernel, qkv_rows, out_weight, held)

    fwd_a = order(attend(0), x_parts)
    here_a = order(sum_pair, fwd_a[4], core_swap(fwd_a[5]))
    fwd_b = order(attend(1, fwd_a[6:8]), after(x_parts, g_across))
    levels = wide_count.bit_length() - 1
    places = [jnp.bitwise_and(jnp.right_shift(wide_at, k), 1) for k in range(levels)]
    masks = [jnp.arange(2, dtype=jnp.int32) == place for place in places]
    att_a, masks = order(lambda a, b, m: (sum_pair(a, b), m), here_a, x_swap(here_a), masks)
    here_b = order(sum_pair, fwd_b[4], core_swap(fwd_b[5]))
    att_a = (att_a, core_swap(att_a))

    slots = 2 * per_dev

    def feed(pair, full, taps, held=()):
        return lambda att, parts: feed_forward(
            scalars, pair, full, att, parts, mod, up_weight, down_weight, ffn_kernel, slots, taps, held
        )

    ffn_a = order(feed(0, fwd_a[0], ffn_kernel), att_a, g_parts)
    att_b = order(sum_pair, here_b, x_swap(here_b))
    att_b = (att_b, core_swap(att_b))
    here_a = order(sum_pair, ffn_a[1], core_swap(ffn_a[2]))
    ffn_b = order(feed(1, fwd_b[0], ffn_a[4], ffn_a[7:11]), att_b, g_parts)
    sec_a = order(sum_pair, here_a, x_swap(here_a))
    sec_a = (sec_a, core_swap(sec_a))
    down_product = order(token_products, [ffn_a[5], ffn_b[5]], [ffn_a[6], ffn_b[6]])
    down_sum = WideSum(down_product, places, masks, wide_count)
    order.advance(down_sum)
    here_b = order(sum_pair, ffn_b[1], core_swap(ffn_b[2]))
    up_product = order(token_products, [ffn_b[7]], [ffn_b[8]])
    up_sum = WideSum(up_product, places, masks, wide_count)
    order.advance(up_sum)

    def attend_back(pair, fwd, ffn, held=()):
        return lambda att, sec: attn_backward(
            scalars, pair, fwd[0], att, sec, ffn[0], mod, fwd[1:4], out_weight, ffn[3], held
        )

    def input_back(pair, fwd, taps, before, held):
        return lambda gqkv, gmid, mods: input_backward(
            scalars, pair, fwd[0], mod, gqkv, qkv_all, attn_kernel, taps, gmid, mods, before, slots, held
        )

    back_a = order(attend_back(0, fwd_a, ffn_a), att_a, sec_a)
    sec_b = order(sum_pair, here_b, x_swap(here_b))
    sec_b = (sec_b, core_swap(sec_b))
    order.advance(down_sum)
    back_b = order(attend_back(1, fwd_b, ffn_b, back_a[2:4]), att_b, sec_b)
    order.advance(down_sum)
    attn_product = order(
        lambda grads, grouped, contexts, attended: jnp.concatenate(
            [token_products([grads], [grouped]), token_products([contexts], [attended])], 0
        ),
        back_b[3], fwd_b[6], fwd_b[7], back_b[2],
    )
    attn_sum = WideSum(attn_product, places, masks, wide_count, [0] + list(range(levels - 1, 0, -1)))
    order.advance(attn_sum)
    order.advance(up_sum)
    order.advance(down_sum)
    in_a = order(input_back(0, fwd_a, attn_kernel, attn_kernel, ffn_b[9:11]), back_b[3], *back_a[:2])
    order.advance(down_sum, up_sum)
    order.advance(attn_sum)
    in_b = order(input_back(1, fwd_b, in_a[0], in_a[1], in_a[2:4]), back_b[3], *back_b[:2])
    order.advance(down_sum)

    rows = 6 * per_dev
    bits = [1 << k for k in reversed(range(levels))]
    moves = [lambda v, bit=bit: (v, wide_swap(v, bit, wide_count)) for bit in bits]
    join = lambda a, b: jnp.concatenate([a, b], 0)
    whole_rows = lambda a, b, c: join(sum_pair(a, b)[: rows + 9], c[:9].astype(BF))[None]
    mods = Steps(
        (in_b[1], core_swap(in_b[1])),
        [(sum_pair, lambda v: (v, x_swap(v), ffn_b[4]))]
        + [(work, move) for work, move in zip([whole_rows] + [join] * len(bits), moves)],
    )
    order.advance(up_sum)
    order.advance(mods)
    order.advance(attn_sum)
    order.advance(mods)
    order.advance(up_sum)
    while not down_sum.done():
        order.advance(down_sum)
    down_grad = down_sum.finish(order, F32)
    made = order(functools.partial(slice_halves, x), in_b[2], core_swap(in_b[3]))
    order.advance(attn_sum, mods)
    order.advance(mods)
    order.advance(up_sum)
    order.advance(attn_sum)
    while not all(c.done() for c in (mods, up_sum)):
        order.advance(mods)
        order.advance(up_sum)

    def unpack(held):
        gmod = held[:, :rows].reshape(latent_total, 6 * width)
        taps = jnp.sum(held[:, rows:].astype(F32), 0) * factor
        return gmod, jnp.sum(gmod.astype(F32), 0) * factor, taps[:9], taps[9:]

    unpacked = order(lambda a, b: unpack(join(a, b)), *mods.came)
    order.last = tuple(unpacked)
    gmod, ada_bias_grad, attn_taps, ffn_taps = unpacked
    final_out, final_grad = order(
        lambda a, b: (sum_pair(a[:per_dev], b[:per_dev]), sum_pair(a[per_dev:], b[per_dev:])), made[0], x_swap(made[1])
    )
    order.last = (final_out, final_grad)
    while not attn_sum.done():
        order.advance(attn_sum)
    time_in_grad, time_out_grad, ada_weight_grad = order(
        lambda g: condition_back(g, embedded, stages, time_out, ada_weight, factor), gmod
    )
    up_grad = up_sum.finish(order, F32)
    attn_grads = attn_sum.finish(order, BF)
    qkv_rows_grad, out_grad = attn_grads[: 3 * share].astype(F32), attn_grads[3 * share :].astype(F32)
    qkv_grad = jnp.swapaxes(qkv_rows_grad.reshape(3, share, width), 1, 2)
    final_out = jnp.swapaxes(final_out, 1, 2)
    final_grad = jnp.swapaxes(final_grad, 1, 2)
    return (
        final_out, final_grad, time_in_grad, time_out_grad, ada_weight_grad, ada_bias_grad,
        attn_taps, qkv_grad, out_grad, up_grad, ffn_taps, down_grad,
    )


def solution(mesh):
    tokens = P("wide", None, "narrow")
    weights = (P(None, None, "narrow"), P("narrow", None), P(None, "narrow"), P(None, "narrow"), P("narrow", None))
    return jax.shard_map(
        body,
        mesh=mesh,
        in_specs=(tokens, tokens, P(), P(), P(), P(), P(), P()) + weights,
        out_specs=(tokens, tokens, P(), P(), P(), P(), P()) + weights,
        check_vma=False,
    )
```

```python
import functools
import math

import jax
import jax.numpy as jnp
from jax import lax
from jax.experimental import pallas as pl
from jax.experimental.pallas import tpu as pltpu
from jax.sharding import PartitionSpec as P

HEAD_DIM = 64
SIDE = 16
PAIR = 2
PAIRS = 2

BF = jnp.bfloat16
F32 = jnp.float32
HIGHEST = lax.Precision.HIGHEST
LANES = 128
ROWS = 128
FEW_ROWS = 128
MANY_ROWS = 256
BAND = 64
GELU_A = math.sqrt(2.0 / math.pi)
GELU_B = 0.044715
EPS = 1e-06
VMEM_LIMIT = 60 * 1024 * 1024
WEIGHT_ROWS = 256
BACK_ROWS = 128
PACKED = 40


def dot(a, b):
    return lax.dot_general(a, b, (((1,), (0,)), ((), ())), preferred_element_type=F32)


def dot_nt(a, b):
    return lax.dot_general(a, b, (((1,), (1,)), ((), ())), preferred_element_type=F32)


def dot_tn(a, b):
    return lax.dot_general(a, b, (((0,), (0,)), ((), ())), preferred_element_type=F32)


def column_of(rows):
    return lax.broadcasted_iota(jnp.int32, (rows, LANES), 0) % SIDE


def from_left(v):
    moved = pltpu.roll(v, 1, 0)
    return jnp.where(column_of(v.shape[0]) == 0, 0.0, moved)


def from_right(v):
    moved = pltpu.roll(v, v.shape[0] - 1, 0)
    return jnp.where(column_of(v.shape[0]) == SIDE - 1, 0.0, moved)


def conv_band(padded, at, lanes, kern):
    rows = [padded[pl.ds(at + SIDE * r, BAND), lanes] for r in range(3)]
    mixed = [
        rows[0] * kern[c] + rows[1] * kern[3 + c] + rows[2] * kern[6 + c] for c in range(3)
    ]
    return from_left(mixed[0]) + mixed[1] + from_right(mixed[2])


def conv_back_band(padded_grad, at, lanes, kern):
    wide = padded_grad[pl.ds(at, BAND + 2 * SIDE), lanes]
    shifted = [from_right(wide), wide, from_left(wide)]
    total = None
    for r in range(3):
        for c in range(3):
            low = SIDE * (2 - r)
            term = shifted[c][low : low + BAND] * kern[3 * r + c]
            total = term if total is None else total + term
    return total, [s[SIDE : SIDE + BAND] for s in shifted]


def fold_rows(v):
    total = v[0:8]
    for at in range(8, v.shape[0], 8):
        total = total + v[at : at + 8]
    return total


def taps_of(kern_ref, lanes):
    block = kern_ref[:, lanes]
    return [block[t : t + 1] for t in range(9)]


def zero_edges(ref):
    edge = jnp.zeros((SIDE, ref.shape[1]), F32)
    tall = ref.shape[0] // PAIR
    for rel in range(PAIR):
        ref[rel * tall : rel * tall + SIDE, :] = edge
        ref[(rel + 1) * tall - SIDE : (rel + 1) * tall, :] = edge


def inside(ref, rel):
    tall = ref.shape[0] // PAIR
    return slice(rel * tall + SIDE, (rel + 1) * tall - SIDE)


def gather_features(n, parts, held, out):
    _, share, tokens = parts[0].shape
    core = jnp.bitwise_and(n, 1)

    def one(rel):
        for step, part in enumerate(parts):
            held[jnp.bitwise_xor(n, step)] = part[jnp.bitwise_xor(rel, core)]
        out[pl.ds(pl.multiple_of(rel * tokens, tokens), tokens), :] = held[...].reshape(len(parts) * share, tokens).T

    pair_loop(one)


def by_core(core, low, share, keep_out, send_out, turned):
    tokens = low.shape[0] // PAIR

    def one(rel):
        lat = jnp.bitwise_xor(rel, core)
        turned[...] = low[pl.ds(pl.multiple_of(rel * tokens, tokens), tokens), :].T
        for x in range(2):
            here = pl.ds(pl.multiple_of((2 * x + core) * share, 16), share)
            there = pl.ds(pl.multiple_of((2 * x + 1 - core) * share, 16), share)
            keep_out[x, lat] = turned[here, :]
            send_out[x, lat] = turned[there, :]

    pair_loop(one)


def norm_stats(v):
    width = v.shape[1]
    mean = jnp.sum(v, -1, keepdims=True) * (1.0 / width)
    center = v - mean
    spread = jnp.sum(center * center, -1, keepdims=True) * (1.0 / width)
    scale = lax.rsqrt(spread + EPS)
    return center * scale, scale


def head_masks(share):
    lane = lax.broadcasted_iota(jnp.int32, (1, share), 1) // HEAD_DIM
    return [(lane == h).astype(F32).astype(BF) for h in range(share // HEAD_DIM)]


def half_rows(v, parity):
    tokens, width = v.shape
    split = v.reshape(tokens // (2 * SIDE), 2, SIDE, width)
    return split[:, parity].reshape(tokens // 2, width)


def join_rows(even, odd):
    half, width = even.shape
    both = jnp.stack([even.reshape(half // SIDE, SIDE, width), odd.reshape(half // SIDE, SIDE, width)], 1)
    return both.reshape(2 * half, width)


def softmax_rows(queries, keys):
    scores = dot_nt(queries, keys) * (1.0 / math.sqrt(HEAD_DIM))
    rows = lax.broadcasted_iota(jnp.int32, scores.shape, 0)
    cols = lax.broadcasted_iota(jnp.int32, scores.shape, 1)
    same = (rows + cols) % 2 == 0
    scores = jnp.where(same, scores, -1e30)
    top = jnp.max(scores, -1, keepdims=True)
    grown = jnp.where(same, jnp.exp(scores - top), 0.0)
    return grown / jnp.sum(grown, -1, keepdims=True)


def beside(stacked, heads):
    rows = stacked.shape[0] // heads
    return jnp.concatenate([stacked[h * rows : (h + 1) * rows] for h in range(heads)], axis=1)


def lane_loop(width, body):
    count = width // LANES

    def step(j, carry):
        body(j // count, pl.ds(pl.multiple_of((j % count) * LANES, LANES), LANES))
        return carry

    lax.fori_loop(0, PAIR * count, step, 0)


def band_loop(tokens, body, carry):
    return lax.fori_loop(0, tokens // BAND, lambda j, c: body(pl.multiple_of(j * BAND, BAND), c), carry)


def row_loop(tokens, body, size=ROWS):
    count = tokens // size

    def step(j, carry):
        body(j // count, pl.multiple_of(j * size, size))
        return carry

    lax.fori_loop(0, PAIR * count, step, 0)


def pair_loop(body):
    def step(j, carry):
        body(j)
        return carry

    lax.fori_loop(0, PAIR, step, 0)


def attn_kernel_body(
    flow, s_ref, xo, xc, xx, xd, mod, kern, wqkv, wout,
    full_out, q_out, k_out, v_out, keep_out, send_out, grouped_out, ctx_out,
    held, padded,
):
    n = s_ref[0]
    core = jnp.bitwise_and(n, 1)
    share, tokens = xo.shape[1], xo.shape[2]
    width = full_out.shape[1]
    tall = tokens + 2 * SIDE
    zero_edges(padded)
    flow.need(xo, xc, xx, xd, mod, kern)
    gather_features(n, (xo, xc, xx, xd), held, full_out)
    flow.sent(full_out)

    def rows(rel, at):
        lat = jnp.bitwise_xor(rel, core)
        normed, _ = norm_stats(full_out[pl.ds(at, MANY_ROWS), :].astype(F32))
        here = pl.ds(pl.multiple_of(at + (2 * rel + 1) * SIDE, SIDE), MANY_ROWS)
        padded[here, :] = normed * (1.0 + mod[lat, 1:2, :]) + mod[lat, 0:1, :]

    row_loop(tokens, rows, MANY_ROWS)

    def lanes(rel, at):
        taps = taps_of(kern, at)
        for band in range(0, tokens, BAND):
            here = pl.ds(pl.multiple_of(rel * tokens + band, BAND), BAND)
            grouped_out[here, at] = conv_band(padded, pl.multiple_of(rel * tall + band, SIDE), at, taps).astype(BF)

    lane_loop(width, lanes)
    flow.sent(grouped_out)
    flow.need(wqkv, wout)
    grouped = grouped_out[...]
    q_out[...] = dot_nt(grouped, wqkv[0]).astype(BF)
    k_out[...] = dot_nt(grouped, wqkv[1]).astype(BF)
    v_out[...] = dot_nt(grouped, wqkv[2]).astype(BF)
    flow.sent(q_out, k_out, v_out)
    masks = head_masks(share)
    heads = len(masks)

    def attend(rel):
        here = pl.ds(pl.multiple_of(rel * tokens, tokens), tokens)
        query, key, value = q_out[here, :], k_out[here, :], v_out[here, :]
        parts = []
        for parity in range(2):
            q = half_rows(query, parity)
            k = half_rows(key, parity)
            v = half_rows(value, parity)
            probs = softmax_rows(jnp.concatenate([q * m for m in masks], axis=0), k)
            low = beside(probs.astype(BF), heads)
            parts.append(dot(low, jnp.concatenate([v * m for m in masks], axis=0)).astype(BF))
        ctx_out[here, :] = join_rows(*parts)

    pair_loop(attend)
    flow.sent(ctx_out)
    send_out[...] = dot(ctx_out[tokens : 2 * tokens, :], wout[...]).astype(BF)
    flow.sent(send_out)
    keep_out[...] = dot(ctx_out[0:tokens, :], wout[...]).astype(BF)
    flow.sent(keep_out)


def ffn_kernel_body(
    first, flow, s_ref, go, gc, gx, gd, full, att, mod, up, down, kern, kgrad_in,
    g_out, keep_out, send_out, mods_out, kgrad_out, active_out, gfed_out, second_out, ghid_out, fkeep_out, fsend_out,
    held, padded, slope, gpad, mid, fed, low, sums, turned,
):
    n = s_ref[0]
    core = jnp.bitwise_and(n, 1)
    share, tokens = go.shape[1], go.shape[2]
    units = up.shape[1]
    tall = tokens + 2 * SIDE
    zero_edges(padded)
    zero_edges(gpad)
    flow.need(go, gc, gx, gd)
    gather_features(n, (go, gc, gx, gd), held, g_out)
    flow.sent(g_out)
    flow.need(full, att, mod, kgrad_in)
    kgrad_out[...] = jnp.zeros(kgrad_out.shape, F32) if first else kgrad_in[...]

    def rows(rel, at):
        lat = jnp.bitwise_xor(rel, core)
        here = pl.ds(at, ROWS)
        middle = full[here, :].astype(F32) + mod[lat, 2:3, :] * att[here, :].astype(F32)
        mid[here, :] = middle
        normed, _ = norm_stats(middle)
        second_out[here, :] = (normed * (1.0 + mod[lat, 4:5, :]) + mod[lat, 3:4, :]).astype(BF)
        gfed_out[here, :] = (mod[lat, 5:6, :] * g_out[here, :].astype(F32)).astype(BF)

    row_loop(tokens, rows)
    flow.sent(second_out, gfed_out)
    flow.need(up, kern)
    hidden = dot(second_out[...], up[...])
    for rel in range(PAIR):
        padded[inside(padded, rel), :] = hidden[rel * tokens : (rel + 1) * tokens]

    def lanes(rel, at):
        taps = taps_of(kern, at)
        for band in range(0, tokens, BAND):
            here = pl.ds(pl.multiple_of(rel * tokens + band, BAND), BAND)
            mixed = conv_band(padded, pl.multiple_of(rel * tall + band, SIDE), at, taps)
            square = mixed * mixed
            curve = jnp.tanh(GELU_A * mixed * (1.0 + GELU_B * square))
            half = 0.5 * (1.0 + curve)
            active_out[here, at] = (mixed * half).astype(BF)
            slope[here, at] = half + (0.5 * GELU_A) * mixed * (1.0 - curve * curve) * (
                1.0 + (3.0 * GELU_B) * square
            )

    lane_loop(units, lanes)
    flow.sent(active_out)
    flow.need(down)
    fed[...] = dot(active_out[...], down[...])
    sums[...] = jnp.zeros(sums.shape, F32)

    def rows_fed(rel, at):
        lat = jnp.bitwise_xor(rel, core)
        here = pl.ds(at, ROWS)
        term = fed[here, :]
        sums[lat] += fold_rows(term * g_out[here, :].astype(F32))
        low[here, :] = (mod[lat, 5:6, :] * term + 0.25 * mid[here, :]).astype(BF)

    row_loop(tokens, rows_fed)
    for lat in range(PAIR):
        mods_out[lat] = jnp.sum(sums[lat], 0, keepdims=True)
    by_core(core, low, share, fkeep_out, fsend_out, turned)
    flow.sent(fkeep_out, fsend_out, mods_out)
    gact = dot_nt(gfed_out[...], down[...]).astype(BF).astype(F32)
    for rel in range(PAIR):
        here = slice(rel * tokens, (rel + 1) * tokens)
        gpad[inside(gpad, rel), :] = gact[here] * slope[here, :]

    def lanes_back(rel, at):
        taps = taps_of(kern, at)
        sums = [None] * 9
        for band in range(0, tokens, BAND):
            here = pl.ds(pl.multiple_of(rel * tokens + band, BAND), BAND)
            base = pl.multiple_of(rel * tall + band, SIDE)
            total, shifted = conv_back_band(gpad, base, at, taps)
            ghid_out[here, at] = total.astype(BF)
            for r in range(3):
                values = padded[pl.ds(base + SIDE * r, BAND), at]
                for c in range(3):
                    part = fold_rows(values * shifted[c])
                    sums[3 * r + c] = part if sums[3 * r + c] is None else sums[3 * r + c] + part
        for t in range(9):
            kgrad_out[t : t + 1, at] += jnp.sum(sums[t], 0, keepdims=True)

    lane_loop(units, lanes_back)
    flow.sent(ghid_out, kgrad_out)
    send_out[...] = dot_nt(ghid_out[tokens : 2 * tokens, :], up[...]).astype(BF)
    flow.sent(send_out)
    keep_out[...] = dot_nt(ghid_out[0:tokens, :], up[...]).astype(BF)
    flow.sent(keep_out)


def attn_back_body(
    flow, s_ref, full, att, gs, gfull, mod, q_in, k_in, v_in, wout, gates,
    gmid_out, mods_out, gatt_out, gqkv_out,
    sums, gctx,
):
    core = jnp.bitwise_and(s_ref[0], 1)
    tokens = full.shape[0] // PAIR
    width = full.shape[1]
    share = q_in.shape[1]
    mods_out[...] = jnp.zeros(mods_out.shape, F32)
    sums[...] = jnp.zeros(sums.shape, F32)
    flow.need(full, att, gs, gfull, mod)

    def rows(rel, at):
        lat = jnp.bitwise_xor(rel, core)
        here = pl.ds(at, ROWS)
        gate1 = mod[lat, 2:3, :]
        attended = att[here, :].astype(F32)
        normed, inv = norm_stats(full[here, :].astype(F32) + gate1 * attended)
        grad = gs[here, :].astype(F32)
        inner = grad * (1.0 + mod[lat, 4:5, :])
        mean_a = jnp.sum(inner, -1, keepdims=True) * (1.0 / width)
        mean_b = jnp.sum(inner * normed, -1, keepdims=True) * (1.0 / width)
        whole_grad = gfull[here, :].astype(F32) + inv * (inner - mean_a - normed * mean_b)
        gmid_out[here, :] = whole_grad.astype(BF)
        gatt_out[here, :] = (gate1 * whole_grad).astype(BF)
        sums[3 * lat] += fold_rows(attended * whole_grad)
        sums[3 * lat + 1] += fold_rows(grad)
        sums[3 * lat + 2] += fold_rows(grad * normed)

    row_loop(tokens, rows)
    for lat in range(PAIR):
        for k in range(3):
            mods_out[lat, 2 + k : 3 + k, :] = 0.25 * jnp.sum(sums[3 * lat + k], 0, keepdims=True)
    flow.need(wout, q_in, k_in, v_in, gates)
    for lat in range(PAIR):
        mods_out[lat, 5:6, :] = gates[lat]
    flow.sent(gatt_out, gmid_out, mods_out)
    gctx[...] = dot_nt(gatt_out[...], wout[...]).astype(BF)
    masks = head_masks(share)
    heads = len(masks)
    factor = 1.0 / math.sqrt(HEAD_DIM)

    def attend(rel):
        here = pl.ds(pl.multiple_of(rel * tokens, tokens), tokens)
        query, key, value, grads = q_in[here, :], k_in[here, :], v_in[here, :], gctx[here, :]
        parts_q, parts_k, parts_v = [], [], []
        for parity in range(2):
            q = half_rows(query, parity)
            k = half_rows(key, parity)
            v = half_rows(value, parity)
            gc = half_rows(grads, parity)
            q_all = jnp.concatenate([q * m for m in masks], axis=0)
            k_all = jnp.concatenate([k * m for m in masks], axis=0)
            gc_all = jnp.concatenate([gc * m for m in masks], axis=0)
            probs = softmax_rows(q_all, k)
            parts_v.append(dot_tn(probs.astype(BF), gc_all).astype(BF))
            gprobs = dot_nt(gc_all, v).astype(BF).astype(F32)
            gscores = (probs * (gprobs - jnp.sum(probs * gprobs, -1, keepdims=True))).astype(BF)
            parts_q.append((dot(beside(gscores, heads), k_all) * factor).astype(BF))
            parts_k.append((dot_tn(gscores, q_all) * factor).astype(BF))
        for k, parts in enumerate((parts_q, parts_k, parts_v)):
            gqkv_out[here, k * share : (k + 1) * share] = join_rows(*parts)

    pair_loop(attend)
    flow.sent(gqkv_out)


def input_back_body(
    closing, flow, s_ref, full, mod, gqkv, wqkv, kern, kgrad_in, gmid, mods_in, before,
    kgrad_out, mods_out, keep_out, send_out,
    normed1, scale1, first, gpad, gback, low, mods, rows_out, turned,
):
    core = jnp.bitwise_and(s_ref[0], 1)
    tokens = full.shape[0] // PAIR
    width = full.shape[1]
    share = gqkv.shape[1] // 3
    tall = tokens + 2 * SIDE
    zero_edges(first)
    zero_edges(gpad)
    flow.need(full, mod)

    def rows_first(rel, at):
        lat = jnp.bitwise_xor(rel, core)
        here = pl.ds(at, FEW_ROWS)
        normed, inv = norm_stats(full[here, :].astype(F32))
        normed1[here, :] = normed
        scale1[here, :] = jnp.broadcast_to(inv, (FEW_ROWS, LANES))
        inside_rows = pl.ds(pl.multiple_of(at + (2 * rel + 1) * SIDE, SIDE), FEW_ROWS)
        first[inside_rows, :] = normed * (1.0 + mod[lat, 1:2, :]) + mod[lat, 0:1, :]

    row_loop(tokens, rows_first, FEW_ROWS)
    flow.need(gqkv, wqkv, kern, kgrad_in, gmid, mods_in, before)
    kgrad_out[...] = kgrad_in[...] if closing else jnp.zeros(kgrad_out.shape, F32)
    mods[...] = mods_in[...]
    for rel in range(PAIR):
        here = slice(rel * tokens, (rel + 1) * tokens)
        gpad[inside(gpad, rel), :] = dot(gqkv[here, :], wqkv[...])

    def lanes(rel, at):
        taps = taps_of(kern, at)
        sums = [None] * 9
        shift_sum, scale_sum = None, None
        for band in range(0, tokens, BAND):
            here = pl.ds(pl.multiple_of(rel * tokens + band, BAND), BAND)
            base = pl.multiple_of(rel * tall + band, SIDE)
            total, shifted = conv_back_band(gpad, base, at, taps)
            gback[here, at] = total
            part_a, part_b = fold_rows(total), fold_rows(total * normed1[here, at])
            shift_sum = part_a if shift_sum is None else shift_sum + part_a
            scale_sum = part_b if scale_sum is None else scale_sum + part_b
            for r in range(3):
                values = first[pl.ds(base + SIDE * r, BAND), at]
                for c in range(3):
                    part = fold_rows(values * shifted[c])
                    sums[3 * r + c] = part if sums[3 * r + c] is None else sums[3 * r + c] + part
        for t in range(9):
            kgrad_out[t : t + 1, at] += jnp.sum(sums[t], 0, keepdims=True)
        lat = jnp.bitwise_xor(rel, core)
        mods[lat, 0:1, at] = jnp.sum(shift_sum, 0, keepdims=True)
        mods[lat, 1:2, at] = jnp.sum(scale_sum, 0, keepdims=True)

    lane_loop(width, lanes)
    if closing:
        rows_out[...] = jnp.zeros(rows_out.shape, F32)
        for lat in range(PAIR):
            rows_out[6 * lat : 6 * lat + 6, :] = before[lat, 0:6, :]
            rows_out[6 * (PAIR + lat) : 6 * (PAIR + lat) + 6, :] = mods[lat, 0:6, :]
        rows_out[12 * PAIR : 12 * PAIR + 9, :] = kgrad_out[0:9, :]
        mods_out[...] = rows_out[...].astype(BF)
    else:
        mods_out[...] = mods[...]
    flow.sent(mods_out, kgrad_out)

    def rows_back(rel, at):
        lat = jnp.bitwise_xor(rel, core)
        here = pl.ds(at, FEW_ROWS)
        inner = gback[here, :] * (1.0 + mod[lat, 1:2, :])
        normed = normed1[here, :]
        mean_a = jnp.sum(inner, -1, keepdims=True) * (1.0 / width)
        mean_b = jnp.sum(inner * normed, -1, keepdims=True) * (1.0 / width)
        grad = scale1[here, 0:1] * (inner - mean_a - normed * mean_b)
        low[here, :] = (grad + 0.25 * gmid[here, :].astype(F32)).astype(BF)

    row_loop(tokens, rows_back, FEW_ROWS)
    by_core(core, low, share, keep_out, send_out, turned)
    flow.sent(keep_out, send_out)


class Flow:
    def __init__(self, arrivals, departures):
        self.arrivals, self.departures = arrivals, departures
        self.leaving = []
        for _, copy in arrivals:
            copy.start()

    def need(self, *refs):
        for ref in refs:
            for _, copy in [a for a in self.arrivals if a[0] is ref]:
                copy.wait()
            self.arrivals = [a for a in self.arrivals if a[0] is not ref]

    def sent(self, *refs):
        for ref in refs:
            for held, copy in self.departures:
                if held is ref:
                    copy.start()
                    self.leaving.append(copy)

    def end(self):
        for copy in self.leaving:
            copy.wait()


def call(body, name, scalars, ins, outs, scratch, flops, held=()):
    n_in, n_out = len(ins), len(outs)
    places, buffer_shapes = [], []
    for array, window, into in ins:
        dims = array.shape if window is None else (window[0].size,) + array.shape[1:]
        if into is None:
            buffer_shapes.append((dims, array.dtype))
        elif into[0].start == 0:
            buffer_shapes.append(((PAIR * dims[0],) + dims[1:], array.dtype))
        places.append(len(buffer_shapes) - 1)

    def run(s_ref, *refs):
        sources = refs[:n_in]
        targets = refs[n_in + len(held) : n_in + len(held) + n_out]
        buffers = refs[n_in + len(held) + n_out : -1]
        sems = refs[-1]
        n_held = len(buffer_shapes)
        buffers_in, buffers_out = buffers[:n_held], buffers[n_held : n_held + n_out]
        rest = buffers[n_held + n_out :]
        arrivals, departures = [], []
        for k, (source, (_, window, into)) in enumerate(zip(sources, ins)):
            view = source if window is None else source.at[window]
            buffer = buffers_in[places[k]]
            target = buffer if into is None else buffer.at[into]
            arrivals.append((buffer, pltpu.make_async_copy(view, target, sems.at[k])))
        for k, (target, buffer, out) in enumerate(zip(targets, buffers_out, outs)):
            view = target if out[2] is None else target.at[out[2]]
            departures.append((buffer, pltpu.make_async_copy(buffer, view, sems.at[n_in + k])))
        flow = Flow(arrivals, departures)
        body(flow, s_ref, *buffers_in, *buffers_out, *rest)
        flow.end()

    anywhere = pl.BlockSpec(memory_space=pl.ANY)
    return pl.pallas_call(
        run,
        name=name,
        out_shape=[jax.ShapeDtypeStruct(o[0], o[1]) for o in outs],
        grid_spec=pltpu.PrefetchScalarGridSpec(
            num_scalar_prefetch=1,
            grid=(1,),
            in_specs=[anywhere] * (n_in + len(held)),
            out_specs=[anywhere] * n_out,
            scratch_shapes=[pltpu.VMEM(dims, dtype) for dims, dtype in buffer_shapes]
            + [pltpu.VMEM(o[3], o[1]) for o in outs]
            + scratch
            + [pltpu.SemaphoreType.DMA((n_in + n_out,))],
        ),
        input_output_aliases={1 + n_in + k: n_out - len(held) + k for k in range(len(held))},
        compiler_params=pltpu.CompilerParams(vmem_limit_bytes=VMEM_LIMIT),
        cost_estimate=pl.CostEstimate(flops=flops, bytes_accessed=10**6, transcendentals=0),
    )(scalars, *[i[0] for i in ins], *held)


def slices_out(slots, slot, share, tokens):
    return ((2, slots, share, tokens), BF, (slice(None), pl.ds(PAIR * slot, PAIR)), (2, PAIR, share, tokens))


def whole(array):
    return (array, None, None)


def stacked(arrays):
    rows = arrays[0].shape[0]
    return [(v, None, (pl.ds(k * rows, rows),)) for k, v in enumerate(arrays)]


def whole_out(dims, dtype):
    return (dims, dtype, None, dims)


def pair_rows(array, pair):
    rows = array.shape[0] // PAIRS
    return (array, (pl.ds(rows * pair, rows),), None)


def pair_rows_out(rows, width, pair):
    return ((PAIRS * rows, width), BF, (pl.ds(rows * pair, rows),), (rows, width))


def pair_of(array, pair):
    return (array, (pl.ds(PAIR * pair, PAIR),), None)


def split_low(v):
    high = v.astype(BF)
    return high, (v - high.astype(F32)).astype(BF)


def rows_product(a, b):
    (ah, al), (bh, bl) = split_low(a), split_low(b)
    return dot_tn(jnp.concatenate([ah, al, ah], 0), jnp.concatenate([bh, bh, bl], 0))


def back_product(a, weight):
    (ah, al), (wh, wl) = split_low(a), split_low(weight)
    return dot_nt(ah, wh) + dot_nt(al, wh) + dot_nt(ah, wl)


def product(a, weight):
    (ah, al), (wh, wl) = split_low(a), split_low(weight)
    return dot(ah, wh) + dot(al, wh) + dot(ah, wl)


def silu(v):
    return v / (1.0 + jnp.exp(-v))


def silu_slope(v):
    gate = 1.0 / (1.0 + jnp.exp(-v))
    return gate * (1.0 + v * (1.0 - gate))


def row_blocks(source, target, sems, rows):
    return [
        pltpu.make_async_copy(source.at[pl.ds(at, rows)], target.at[pl.ds(at, rows)], sems.at[at // rows])
        for at in range(0, source.shape[0], rows)
    ]


def condition_body(
    steps, stamps, wide, bias, time_in, time_out, ada,
    mod_out, embedded, inner_pre, inner, outer_pre, outer, held_in, held_out, held, sums, parts, rows_of, sems,
):
    depth = ada.shape[0]
    per_dev, count, width = mod_out.shape
    first = pltpu.make_async_copy(time_in, held_in, sems.at[0])
    second = pltpu.make_async_copy(time_out, held_out, sems.at[1])
    blocks = row_blocks(ada, held, sems.at[pl.ds(2, depth // WEIGHT_ROWS)], WEIGHT_ROWS)
    for copy in [first, second] + blocks:
        copy.start()
    halved = embedded.shape[1] // 2
    for r in range(embedded.shape[0]):
        at = jnp.bitwise_xor(wide[0], steps[r // per_dev]) * per_dev + r % per_dev
        rows_of[r : r + 1, :] = jnp.broadcast_to(stamps[at].astype(F32), (1, halved))
    order = lax.broadcasted_iota(jnp.int32, (1, halved), 1).astype(F32)
    angles = rows_of[...] * jnp.exp(-math.log(10000.0) * order / halved)
    embedded[:, 0:halved] = jnp.cos(angles)
    embedded[:, halved:] = jnp.sin(angles)
    first.wait()
    inner_pre[...] = product(embedded[...], held_in[...])
    inner[...] = silu(inner_pre[...])
    second.wait()
    outer_pre[...] = product(inner[...], held_out[...])
    outer[...] = silu(outer_pre[...])
    wide_bias = [jnp.concatenate([bias[k + j : k + j + 1, :] for j in range(width // LANES)], 1)
                 for k in range(0, bias.shape[0], width // LANES)]
    total = jnp.concatenate(wide_bias, 1)
    sums[...] = jnp.broadcast_to(total, sums.shape)
    for k in range(depth // WEIGHT_ROWS):
        parts[k] = outer[0:8, k * WEIGHT_ROWS : (k + 1) * WEIGHT_ROWS]

    def add(k, carry):
        rows = pl.ds(pl.multiple_of(k * WEIGHT_ROWS, WEIGHT_ROWS), WEIGHT_ROWS)
        pltpu.make_async_copy(ada.at[rows], held.at[rows], sems.at[2 + k]).wait()
        sums[...] += product(parts[k], held[rows, :])
        return carry

    lax.fori_loop(0, depth // WEIGHT_ROWS, add, 0)
    total = sums[...]
    for lat in range(per_dev):
        for k in range(count):
            mod_out[lat, k : k + 1, :] = total[lat : lat + 1, k * width : (k + 1) * width]


def condition(steps, stamps, wide, time_in, time_out, ada_weight, ada_bias, per_dev, width):
    latent_total = stamps.shape[0]
    depth, columns = ada_weight.shape
    vmem = pl.BlockSpec(memory_space=pltpu.VMEM)
    anywhere = pl.BlockSpec(memory_space=pl.ANY)
    rows = jax.ShapeDtypeStruct((latent_total, depth), F32)
    return pl.pallas_call(
        functools.partial(condition_body, steps),
        name="condition",
        in_specs=[pl.BlockSpec(memory_space=pltpu.SMEM)] * 2 + [vmem, anywhere, anywhere, anywhere],
        out_specs=[vmem] * 6,
        out_shape=[
            jax.ShapeDtypeStruct((per_dev, columns // width, width), F32),
            jax.ShapeDtypeStruct((latent_total, time_in.shape[0]), F32),
            rows, rows, rows, rows,
        ],
        scratch_shapes=[
            pltpu.VMEM(time_in.shape, F32),
            pltpu.VMEM(time_out.shape, F32),
            pltpu.VMEM(ada_weight.shape, F32),
            pltpu.VMEM((8, columns), F32),
            pltpu.VMEM((depth // WEIGHT_ROWS, 8, WEIGHT_ROWS), F32),
            pltpu.VMEM((latent_total, time_in.shape[0] // 2), F32),
            pltpu.SemaphoreType.DMA((2 + depth // WEIGHT_ROWS,)),
        ],
        compiler_params=pltpu.CompilerParams(vmem_limit_bytes=VMEM_LIMIT),
        cost_estimate=pl.CostEstimate(flops=8 * 10**9, bytes_accessed=10**6, transcendentals=0),
    )(stamps, wide, ada_bias.reshape(columns // LANES, LANES), time_in, time_out, ada_weight)


def condition_back_body(
    factor, gmod, embedded, inner_pre, inner, outer_pre, outer, time_out, ada,
    time_in_grad, time_out_grad, ada_grad, held_out, held, outer_grad, columns, sems, arriving, leaving,
):
    count = ada.shape[0] // BACK_ROWS

    def block_copy(source, target, sem, k):
        rows = pl.ds(k * BACK_ROWS, BACK_ROWS)
        return pltpu.make_async_copy(source.at[rows], target.at[rows], sem.at[k])

    first = pltpu.make_async_copy(time_out, held_out, sems.at[0])
    for k in range(count):
        block_copy(ada, held, arriving, k).start()
    first.start()
    high, low = split_low(outer[...])
    both = jnp.concatenate([high, low], 0)
    for k in range(count):
        columns[k] = both[:, k * BACK_ROWS : (k + 1) * BACK_ROWS]

    def block(k, carry):
        rows = pl.ds(pl.multiple_of(k * BACK_ROWS, BACK_ROWS), BACK_ROWS)
        block_copy(ada, held, arriving, k).wait()
        grads = gmod[...]
        high, low = split_low(held[rows, :])
        outer_grad[rows, :] = dot_nt(high, grads) + dot_nt(low, grads)
        held[rows, :] = dot_tn(columns[k], jnp.concatenate([grads, grads], 0)) * factor
        block_copy(held, ada_grad, leaving, k).start()
        return carry

    lax.fori_loop(0, count, block, 0)
    first.wait()
    back = outer_grad[...].T * factor * silu_slope(outer_pre[...])
    time_out_grad[...] = rows_product(inner[...], back)
    back = back_product(back, held_out[...]) * silu_slope(inner_pre[...])
    time_in_grad[...] = rows_product(embedded[...], back)
    for k in range(count):
        block_copy(held, ada_grad, leaving, k).wait()


def condition_back(gmod, embedded, stages, time_out, ada_weight, factor):
    depth = ada_weight.shape[0]
    latent_total = gmod.shape[0]
    vmem = pl.BlockSpec(memory_space=pltpu.VMEM)
    anywhere = pl.BlockSpec(memory_space=pl.ANY)
    time_in_dims = (embedded.shape[1], time_out.shape[0])
    return pl.pallas_call(
        functools.partial(condition_back_body, factor),
        name="condition_back",
        in_specs=[vmem] * 6 + [anywhere] * 2,
        out_specs=[vmem, vmem, anywhere],
        out_shape=[
            jax.ShapeDtypeStruct(time_in_dims, F32),
            jax.ShapeDtypeStruct(time_out.shape, F32),
            jax.ShapeDtypeStruct(ada_weight.shape, F32),
        ],
        scratch_shapes=[
            pltpu.VMEM(time_out.shape, F32),
            pltpu.VMEM(ada_weight.shape, F32),
            pltpu.VMEM((depth, latent_total), F32),
            pltpu.VMEM((depth // BACK_ROWS, 2 * latent_total, BACK_ROWS), BF),
            pltpu.SemaphoreType.DMA((1,)),
            pltpu.SemaphoreType.DMA((depth // BACK_ROWS,)),
            pltpu.SemaphoreType.DMA((depth // BACK_ROWS,)),
        ],
        compiler_params=pltpu.CompilerParams(vmem_limit_bytes=VMEM_LIMIT),
        cost_estimate=pl.CostEstimate(flops=1, bytes_accessed=1, transcendentals=0),
    )(gmod, embedded, *stages, time_out, ada_weight)


def attn_forward(scalars, pair, x_parts, mod, attn_kernel, qkv_weight, out_weight, held):
    _, share, tokens = x_parts[0].shape
    width = out_weight.shape[1]
    rows = PAIR * tokens
    thin = whole_out((rows, share), BF)
    half = whole_out((tokens, width), BF)
    return call(
        attn_kernel_body, "attn_fwd", scalars,
        [pair_of(v, pair) for v in x_parts] + [pair_of(mod, pair), whole(attn_kernel), whole(qkv_weight), whole(out_weight)],
        [whole_out((rows, width), BF), thin, thin, thin, half, half, pair_rows_out(rows, width, pair),
         pair_rows_out(rows, share, pair)],
        [pltpu.VMEM((4, share, tokens), BF), pltpu.VMEM((PAIR * (tokens + 2 * SIDE), width), F32)],
        6_000_000_000, held,
    )


def feed_forward(scalars, pair, full, att, g_parts, mod, up_weight, down_weight, ffn_kernel, slots, taps, held):
    _, share, tokens = g_parts[0].shape
    width, units = up_weight.shape
    rows = PAIR * tokens
    tall = PAIR * (tokens + 2 * SIDE)
    half = whole_out((tokens, width), BF)
    slices = slices_out(slots, pair, share, tokens)
    return call(
        functools.partial(ffn_kernel_body, pair == 0), "ffn", scalars,
        [pair_of(v, pair) for v in g_parts] + [whole(full)] + stacked(att)
        + [pair_of(mod, pair), whole(up_weight), whole(down_weight), whole(ffn_kernel), whole(taps)],
        [whole_out((rows, width), BF), half, half, whole_out((PAIR, 1, width), F32), whole_out((16, units), F32),
         whole_out((rows, units), BF), whole_out((rows, width), BF), pair_rows_out(rows, width, pair),
         pair_rows_out(rows, units, pair), slices, slices],
        [pltpu.VMEM((4, share, tokens), BF), pltpu.VMEM((tall, units), F32), pltpu.VMEM((rows, units), F32),
         pltpu.VMEM((tall, units), F32), pltpu.VMEM((rows, width), F32), pltpu.VMEM((rows, width), F32),
         pltpu.VMEM((rows, width), BF), pltpu.VMEM((PAIR, 8, width), F32), pltpu.VMEM((width, tokens), BF)],
        10_000_000_000, held,
    )


def attn_backward(scalars, pair, full, att, gsec, gfull, mod, qkv, out_weight, gates, held):
    tokens, width = att[0].shape
    share = out_weight.shape[0]
    rows = PAIR * tokens
    broad = whole_out((rows, width), BF)
    return call(
        attn_back_body, "attn_bwd", scalars,
        [whole(full)] + stacked(att) + stacked(gsec) + [whole(gfull), pair_of(mod, pair)]
        + [whole(v) for v in qkv] + [whole(out_weight), whole(gates)],
        [broad, whole_out((PAIR, 8, width), F32), pair_rows_out(rows, width, pair), pair_rows_out(rows, 3 * share, pair)],
        [pltpu.VMEM((3 * PAIR, 8, width), F32), pltpu.VMEM((rows, share), BF)],
        6_000_000_000, held,
    )


def input_backward(scalars, pair, full, mod, gqkv, qkv_weight, attn_kernel, taps, gmid, mods_in, before, slots, held):
    rows, width = full.shape
    tokens = rows // PAIR
    share = gqkv.shape[1] // 3
    tall = PAIR * (tokens + 2 * SIDE)
    slices = slices_out(slots, slots // PAIR // 2 + pair, share, tokens)
    closing = pair > 0
    mods = whole_out((PACKED, width), BF) if closing else whole_out((PAIR, 8, width), F32)
    return call(
        functools.partial(input_back_body, closing), "input_bwd", scalars,
        [whole(full), pair_of(mod, pair), pair_rows(gqkv, pair), whole(qkv_weight), whole(attn_kernel), whole(taps), whole(gmid),
         whole(mods_in), whole(before)],
        [whole_out((16, width), F32), mods, slices, slices],
        [pltpu.VMEM((rows, width), F32), pltpu.VMEM((rows, LANES), F32), pltpu.VMEM((tall, width), F32),
         pltpu.VMEM((tall, width), F32), pltpu.VMEM((rows, width), F32), pltpu.VMEM((rows, width), BF),
         pltpu.VMEM((PAIR, 8, width), F32), pltpu.VMEM((PACKED, width), F32), pltpu.VMEM((width, tokens), BF)],
        6_000_000_000, held,
    )


def core_swap(v):
    return lax.ppermute(v, "narrow", [(0, 1), (1, 0), (2, 3), (3, 2)])


def x_swap(v):
    return lax.ppermute(v, "narrow", [(0, 2), (2, 0), (1, 3), (3, 1)])


def sum_pair(a, b):
    return (a.astype(F32) + b.astype(F32)).astype(BF)


def slice_halves(x, keep, arrived):
    both = sum_pair(keep, arrived)
    return (
        lax.dynamic_index_in_dim(both, x, 0, keepdims=False),
        lax.dynamic_index_in_dim(both, 1 - x, 0, keepdims=False),
    )


def wide_swap(v, bit, count):
    return lax.ppermute(v, "wide", [(i, i ^ bit) for i in range(count)])


def pick(v, parts, at):
    rows = v.shape[0] // parts
    return lax.dynamic_slice_in_dim(v, at * rows, rows, 0)


def in_place(second, own, came, axis):
    dims = own.shape[:axis] + (2,) + own.shape[axis + 1 :]
    chosen = lax.broadcast_in_dim(second, dims, (axis,))
    return jnp.where(chosen, own, came)


class WideSum:
    def __init__(self, product, bits, masks, count, back=None):
        self.count, self.dims, self.bits, self.masks = count, product.shape, bits, masks
        self.levels = count.bit_length() - 1
        self.ahead = list(range(self.levels))
        self.back = list(reversed(self.ahead)) if back is None else back
        self.opened = False
        self.held = product

    def swap(self, sent, level):
        self.came = wide_swap(sent, 1 << level, self.count)

    def halve(self, held, came):
        level = self.ahead[0]
        if level == 0:
            held = pick(held, 2, self.bits[0])
        if len(self.ahead) == 1:
            return (sum_pair(held, came),)
        bit = self.bits[level + 1]
        return tuple(sum_pair(pick(held, 2, at), pick(came, 2, at)) for at in (1 - bit, bit))

    def pending(self):
        if not self.opened:
            return lambda v: pick(v, 2, 1 - self.bits[0]), (self.held,)
        if self.ahead:
            return self.halve, (self.held, self.came)
        level = self.back[0]
        return lambda a, b: in_place(self.masks[level], a, b, level), (self.held, self.came)

    def accept(self, out):
        if not self.opened:
            self.opened = True
            self.swap(out, 0)
        elif self.ahead:
            self.ahead.pop(0)
            self.held = out[-1]
            if self.ahead:
                self.swap(out[0], self.ahead[0])
            else:
                self.held = self.held.reshape((1,) * self.levels + self.held.shape)
                self.swap(self.held, self.back[0])
        else:
            self.back.pop(0)
            self.held = out
            self.swap(out, self.back[0])

    def done(self):
        return self.opened and not self.ahead and len(self.back) == 1

    def finish(self, order, dtype):
        level = self.back[0]
        whole_sum = order(lambda a, b: in_place(self.masks[level], a, b, level).astype(dtype), self.held, self.came)
        return lax.optimization_barrier(whole_sum).reshape(self.dims)


class Steps:
    def __init__(self, came, steps):
        self.came, self.steps = came, list(steps)

    def pending(self):
        return self.steps[0][0], self.came

    def accept(self, out):
        _, move = self.steps.pop(0)
        self.came = move(out)

    def done(self):
        return not self.steps


class Order:
    def __init__(self):
        self.last = ()

    def __call__(self, step, *inputs):
        inputs, _ = lax.optimization_barrier((inputs, self.last))
        out = step(*inputs)
        self.last = tuple(jax.tree.leaves(out)[:1])
        return out

    def advance(self, *chains):
        chains = [c for c in chains if not c.done()]
        if chains:
            work = [c.pending() for c in chains]
            outs = self(lambda *v: [w[0](*a) for w, a in zip(work, v)], *[w[1] for w in work])
            self.last = tuple(jax.tree.leaves(out)[0] for out in outs)
            for chain, out in zip(chains, outs):
                chain.accept(out)


def after(value, *others):
    return lax.optimization_barrier((value, others))[0]


def body(
    latents, cotangent, timesteps, time_in, time_out, ada_weight, ada_bias,
    attn_kernel, qkv_weight, out_weight, up_weight, ffn_kernel, down_weight,
):
    wide_count = lax.axis_size("wide")
    wide_at = lax.axis_index("wide")
    n = lax.axis_index("narrow")
    per_dev, tokens, share = latents.shape
    width = out_weight.shape[1]
    units = up_weight.shape[1]
    latent_total = timesteps.shape[0]
    scalars = n.astype(jnp.int32).reshape(1)

    steps, bit = [0], wide_count // 2
    while bit:
        steps, bit = steps + [k ^ bit for k in steps], bit // 2
    mod, embedded, *stages = condition(
        steps, timesteps, wide_at.astype(jnp.int32).reshape(1), time_in, time_out, ada_weight, ada_bias, per_dev, width
    )
    x = n // 2
    factor = 1.0 / latent_total

    def token_products(lefts, rights):
        return (sum(dot_tn(a, b) for a, b in zip(lefts, rights)) * factor).astype(BF)

    x_own = jnp.swapaxes(latents, 1, 2)
    g_own = jnp.swapaxes(cotangent, 1, 2)
    qkv_rows = jnp.swapaxes(qkv_weight, 1, 2)
    qkv_all = qkv_rows.reshape(3 * share, width)
    order = Order()
    x_across = x_swap(x_own)
    x_across = after(x_across, mod)
    g_across = x_swap(after(g_own, x_across))
    x_parts = (x_own, core_swap(x_own), x_across, core_swap(x_across))
    g_parts = (g_own, core_swap(g_own), g_across, core_swap(g_across))

    def attend(pair, held=()):
        return lambda parts: attn_forward(scalars, pair, parts, mod, attn_kernel, qkv_rows, out_weight, held)

    fwd_a = order(attend(0), x_parts)
    here_a = order(sum_pair, fwd_a[4], core_swap(fwd_a[5]))
    fwd_b = order(attend(1, fwd_a[6:8]), after(x_parts, g_across))
    levels = wide_count.bit_length() - 1
    places = [jnp.bitwise_and(jnp.right_shift(wide_at, k), 1) for k in range(levels)]
    masks = [jnp.arange(2, dtype=jnp.int32) == place for place in places]
    att_a, masks = order(lambda a, b, m: (sum_pair(a, b), m), here_a, x_swap(here_a), masks)
    here_b = order(sum_pair, fwd_b[4], core_swap(fwd_b[5]))
    att_a = (att_a, core_swap(att_a))

    slots = 2 * per_dev

    def feed(pair, full, taps, held=()):
        return lambda att, parts: feed_forward(
            scalars, pair, full, att, parts, mod, up_weight, down_weight, ffn_kernel, slots, taps, held
        )

    ffn_a = order(feed(0, fwd_a[0], ffn_kernel), att_a, g_parts)
    att_b = order(sum_pair, here_b, x_swap(here_b))
    att_b = (att_b, core_swap(att_b))
    here_a = order(sum_pair, ffn_a[1], core_swap(ffn_a[2]))
    ffn_b = order(feed(1, fwd_b[0], ffn_a[4], ffn_a[7:11]), att_b, g_parts)
    sec_a = order(sum_pair, here_a, x_swap(here_a))
    sec_a = (sec_a, core_swap(sec_a))
    down_product = order(token_products, [ffn_a[5], ffn_b[5]], [ffn_a[6], ffn_b[6]])
    down_sum = WideSum(down_product, places, masks, wide_count)
    order.advance(down_sum)
    here_b = order(sum_pair, ffn_b[1], core_swap(ffn_b[2]))
    up_product = order(token_products, [ffn_b[7]], [ffn_b[8]])
    up_sum = WideSum(up_product, places, masks, wide_count)
    order.advance(up_sum)

    def attend_back(pair, fwd, ffn, held=()):
        return lambda att, sec: attn_backward(
            scalars, pair, fwd[0], att, sec, ffn[0], mod, fwd[1:4], out_weight, ffn[3], held
        )

    def input_back(pair, fwd, taps, before, held):
        return lambda gqkv, gmid, mods: input_backward(
            scalars, pair, fwd[0], mod, gqkv, qkv_all, attn_kernel, taps, gmid, mods, before, slots, held
        )

    back_a = order(attend_back(0, fwd_a, ffn_a), att_a, sec_a)
    sec_b = order(sum_pair, here_b, x_swap(here_b))
    sec_b = (sec_b, core_swap(sec_b))
    order.advance(down_sum)
    back_b = order(attend_back(1, fwd_b, ffn_b, back_a[2:4]), att_b, sec_b)
    order.advance(down_sum)
    attn_product = order(
        lambda grads, grouped, contexts, attended: jnp.concatenate(
            [token_products([grads], [grouped]), token_products([contexts], [attended])], 0
        ),
        back_b[3], fwd_b[6], fwd_b[7], back_b[2],
    )
    attn_sum = WideSum(attn_product, places, masks, wide_count, [0] + list(range(levels - 1, 0, -1)))
    order.advance(attn_sum)
    order.advance(up_sum)
    order.advance(down_sum)
    in_a = order(input_back(0, fwd_a, attn_kernel, attn_kernel, ffn_b[9:11]), back_b[3], *back_a[:2])
    order.advance(down_sum, up_sum)
    order.advance(attn_sum)
    in_b = order(input_back(1, fwd_b, in_a[0], in_a[1], in_a[2:4]), back_b[3], *back_b[:2])
    order.advance(down_sum)

    rows = 6 * per_dev
    bits = [1 << k for k in reversed(range(levels))]
    moves = [lambda v, bit=bit: (v, wide_swap(v, bit, wide_count)) for bit in bits]
    join = lambda a, b: jnp.concatenate([a, b], 0)
    whole_rows = lambda a, b, c: join(sum_pair(a, b)[: rows + 9], c[:9].astype(BF))[None]
    mods = Steps(
        (in_b[1], core_swap(in_b[1])),
        [(sum_pair, lambda v: (v, x_swap(v), ffn_b[4]))]
        + [(work, move) for work, move in zip([whole_rows] + [join] * len(bits), moves)],
    )
    order.advance(up_sum)
    order.advance(mods)
    order.advance(attn_sum)
    order.advance(mods)
    order.advance(up_sum)
    while not down_sum.done():
        order.advance(down_sum)
    down_grad = down_sum.finish(order, F32)
    made = order(functools.partial(slice_halves, x), in_b[2], core_swap(in_b[3]))
    order.advance(attn_sum, mods)
    order.advance(attn_sum)
    while not all(c.done() for c in (mods, up_sum)):
        order.advance(mods, up_sum)

    def unpack(held):
        gmod = held[:, :rows].reshape(latent_total, 6 * width)
        taps = jnp.sum(held[:, rows:].astype(F32), 0) * factor
        return gmod, jnp.sum(gmod.astype(F32), 0) * factor, taps[:9], taps[9:]

    final_out, final_grad = order(
        lambda a, b: (sum_pair(a[:per_dev], b[:per_dev]), sum_pair(a[per_dev:], b[per_dev:])), made[0], x_swap(made[1])
    )
    order.last = (final_out, final_grad)
    while not attn_sum.done():
        order.advance(attn_sum)
    unpacked = order(lambda a, b: unpack(join(a, b)), *mods.came)
    order.last = tuple(unpacked)
    gmod, ada_bias_grad, attn_taps, ffn_taps = unpacked
    time_in_grad, time_out_grad, ada_weight_grad = order(
        lambda g: condition_back(g, embedded, stages, time_out, ada_weight, factor), gmod
    )
    up_grad = up_sum.finish(order, F32)
    attn_grads = attn_sum.finish(order, BF)
    qkv_rows_grad, out_grad = attn_grads[: 3 * share].astype(F32), attn_grads[3 * share :].astype(F32)
    qkv_grad = jnp.swapaxes(qkv_rows_grad.reshape(3, share, width), 1, 2)
    final_out = jnp.swapaxes(final_out, 1, 2)
    final_grad = jnp.swapaxes(final_grad, 1, 2)
    return (
        final_out, final_grad, time_in_grad, time_out_grad, ada_weight_grad, ada_bias_grad,
        attn_taps, qkv_grad, out_grad, up_grad, ffn_taps, down_grad,
    )


def solution(mesh):
    tokens = P("wide", None, "narrow")
    weights = (P(None, None, "narrow"), P("narrow", None), P(None, "narrow"), P(None, "narrow"), P("narrow", None))
    return jax.shard_map(
        body,
        mesh=mesh,
        in_specs=(tokens, tokens, P(), P(), P(), P(), P(), P()) + weights,
        out_specs=(tokens, tokens, P(), P(), P(), P(), P()) + weights,
        check_vma=False,
    )
```

```python
import functools
import math

import jax
import jax.numpy as jnp
from jax import lax
from jax.experimental import pallas as pl
from jax.experimental.pallas import tpu as pltpu
from jax.sharding import PartitionSpec as P

HEAD_DIM = 64
SIDE = 16
PAIR = 2
PAIRS = 2

BF = jnp.bfloat16
F32 = jnp.float32
HIGHEST = lax.Precision.HIGHEST
LANES = 128
ROWS = 128
FEW_ROWS = 128
MANY_ROWS = 256
BAND = 64
GELU_A = math.sqrt(2.0 / math.pi)
GELU_B = 0.044715
EPS = 1e-06
VMEM_LIMIT = 60 * 1024 * 1024
WEIGHT_ROWS = 256
BACK_ROWS = 128
PACKED = 40


def dot(a, b):
    return lax.dot_general(a, b, (((1,), (0,)), ((), ())), preferred_element_type=F32)


def dot_nt(a, b):
    return lax.dot_general(a, b, (((1,), (1,)), ((), ())), preferred_element_type=F32)


def dot_tn(a, b):
    return lax.dot_general(a, b, (((0,), (0,)), ((), ())), preferred_element_type=F32)


def column_of(rows):
    return lax.broadcasted_iota(jnp.int32, (rows, LANES), 0) % SIDE


def from_left(v):
    moved = pltpu.roll(v, 1, 0)
    return jnp.where(column_of(v.shape[0]) == 0, 0.0, moved)


def from_right(v):
    moved = pltpu.roll(v, v.shape[0] - 1, 0)
    return jnp.where(column_of(v.shape[0]) == SIDE - 1, 0.0, moved)


def conv_band(padded, at, lanes, kern):
    rows = [padded[pl.ds(at + SIDE * r, BAND), lanes] for r in range(3)]
    mixed = [
        rows[0] * kern[c] + rows[1] * kern[3 + c] + rows[2] * kern[6 + c] for c in range(3)
    ]
    return from_left(mixed[0]) + mixed[1] + from_right(mixed[2])


def conv_back_band(padded_grad, at, lanes, kern):
    wide = padded_grad[pl.ds(at, BAND + 2 * SIDE), lanes]
    shifted = [from_right(wide), wide, from_left(wide)]
    total = None
    for r in range(3):
        for c in range(3):
            low = SIDE * (2 - r)
            term = shifted[c][low : low + BAND] * kern[3 * r + c]
            total = term if total is None else total + term
    return total, [s[SIDE : SIDE + BAND] for s in shifted]


def fold_rows(v):
    total = v[0:8]
    for at in range(8, v.shape[0], 8):
        total = total + v[at : at + 8]
    return total


def taps_of(kern_ref, lanes):
    block = kern_ref[:, lanes]
    return [block[t : t + 1] for t in range(9)]


def zero_edges(ref):
    edge = jnp.zeros((SIDE, ref.shape[1]), F32)
    tall = ref.shape[0] // PAIR
    for rel in range(PAIR):
        ref[rel * tall : rel * tall + SIDE, :] = edge
        ref[(rel + 1) * tall - SIDE : (rel + 1) * tall, :] = edge


def inside(ref, rel):
    tall = ref.shape[0] // PAIR
    return slice(rel * tall + SIDE, (rel + 1) * tall - SIDE)


def gather_features(n, parts, held, out):
    _, share, tokens = parts[0].shape
    core = jnp.bitwise_and(n, 1)

    def one(rel):
        for step, part in enumerate(parts):
            held[jnp.bitwise_xor(n, step)] = part[jnp.bitwise_xor(rel, core)]
        out[pl.ds(pl.multiple_of(rel * tokens, tokens), tokens), :] = held[...].reshape(len(parts) * share, tokens).T

    pair_loop(one)


def by_core(core, low, share, keep_out, send_out, turned):
    tokens = low.shape[0] // PAIR

    def one(rel):
        lat = jnp.bitwise_xor(rel, core)
        turned[...] = low[pl.ds(pl.multiple_of(rel * tokens, tokens), tokens), :].T
        for x in range(2):
            here = pl.ds(pl.multiple_of((2 * x + core) * share, 16), share)
            there = pl.ds(pl.multiple_of((2 * x + 1 - core) * share, 16), share)
            keep_out[x, lat] = turned[here, :]
            send_out[x, lat] = turned[there, :]

    pair_loop(one)


def norm_stats(v):
    width = v.shape[1]
    mean = jnp.sum(v, -1, keepdims=True) * (1.0 / width)
    center = v - mean
    spread = jnp.sum(center * center, -1, keepdims=True) * (1.0 / width)
    scale = lax.rsqrt(spread + EPS)
    return center * scale, scale


def head_masks(share):
    lane = lax.broadcasted_iota(jnp.int32, (1, share), 1) // HEAD_DIM
    return [(lane == h).astype(F32).astype(BF) for h in range(share // HEAD_DIM)]


def half_rows(v, parity):
    tokens, width = v.shape
    split = v.reshape(tokens // (2 * SIDE), 2, SIDE, width)
    return split[:, parity].reshape(tokens // 2, width)


def join_rows(even, odd):
    half, width = even.shape
    both = jnp.stack([even.reshape(half // SIDE, SIDE, width), odd.reshape(half // SIDE, SIDE, width)], 1)
    return both.reshape(2 * half, width)


def softmax_rows(queries, keys):
    scores = dot_nt(queries, keys) * (1.0 / math.sqrt(HEAD_DIM))
    rows = lax.broadcasted_iota(jnp.int32, scores.shape, 0)
    cols = lax.broadcasted_iota(jnp.int32, scores.shape, 1)
    same = (rows + cols) % 2 == 0
    scores = jnp.where(same, scores, -1e30)
    top = jnp.max(scores, -1, keepdims=True)
    grown = jnp.where(same, jnp.exp(scores - top), 0.0)
    return grown / jnp.sum(grown, -1, keepdims=True)


def beside(stacked, heads):
    rows = stacked.shape[0] // heads
    return jnp.concatenate([stacked[h * rows : (h + 1) * rows] for h in range(heads)], axis=1)


def lane_loop(width, body):
    count = width // LANES

    def step(j, carry):
        body(j // count, pl.ds(pl.multiple_of((j % count) * LANES, LANES), LANES))
        return carry

    lax.fori_loop(0, PAIR * count, step, 0)


def band_loop(tokens, body, carry):
    return lax.fori_loop(0, tokens // BAND, lambda j, c: body(pl.multiple_of(j * BAND, BAND), c), carry)


def row_loop(tokens, body, size=ROWS):
    count = tokens // size

    def step(j, carry):
        body(j // count, pl.multiple_of(j * size, size))
        return carry

    lax.fori_loop(0, PAIR * count, step, 0)


def pair_loop(body):
    def step(j, carry):
        body(j)
        return carry

    lax.fori_loop(0, PAIR, step, 0)


def attn_kernel_body(
    flow, s_ref, xo, xc, xx, xd, mod, kern, wqkv, wout,
    full_out, q_out, k_out, v_out, keep_out, send_out, grouped_out, ctx_out,
    held, padded,
):
    n = s_ref[0]
    core = jnp.bitwise_and(n, 1)
    share, tokens = xo.shape[1], xo.shape[2]
    width = full_out.shape[1]
    tall = tokens + 2 * SIDE
    zero_edges(padded)
    flow.need(xo, xc, xx, xd, mod, kern)
    gather_features(n, (xo, xc, xx, xd), held, full_out)
    flow.sent(full_out)

    def rows(rel, at):
        lat = jnp.bitwise_xor(rel, core)
        normed, _ = norm_stats(full_out[pl.ds(at, MANY_ROWS), :].astype(F32))
        here = pl.ds(pl.multiple_of(at + (2 * rel + 1) * SIDE, SIDE), MANY_ROWS)
        padded[here, :] = normed * (1.0 + mod[lat, 1:2, :]) + mod[lat, 0:1, :]

    row_loop(tokens, rows, MANY_ROWS)

    def lanes(rel, at):
        taps = taps_of(kern, at)
        for band in range(0, tokens, BAND):
            here = pl.ds(pl.multiple_of(rel * tokens + band, BAND), BAND)
            grouped_out[here, at] = conv_band(padded, pl.multiple_of(rel * tall + band, SIDE), at, taps).astype(BF)

    lane_loop(width, lanes)
    flow.sent(grouped_out)
    flow.need(wqkv, wout)
    grouped = grouped_out[...]
    q_out[...] = dot_nt(grouped, wqkv[0]).astype(BF)
    k_out[...] = dot_nt(grouped, wqkv[1]).astype(BF)
    v_out[...] = dot_nt(grouped, wqkv[2]).astype(BF)
    flow.sent(q_out, k_out, v_out)
    masks = head_masks(share)
    heads = len(masks)

    def attend(rel):
        here = pl.ds(pl.multiple_of(rel * tokens, tokens), tokens)
        query, key, value = q_out[here, :], k_out[here, :], v_out[here, :]
        parts = []
        for parity in range(2):
            q = half_rows(query, parity)
            k = half_rows(key, parity)
            v = half_rows(value, parity)
            probs = softmax_rows(jnp.concatenate([q * m for m in masks], axis=0), k)
            low = beside(probs.astype(BF), heads)
            parts.append(dot(low, jnp.concatenate([v * m for m in masks], axis=0)).astype(BF))
        ctx_out[here, :] = join_rows(*parts)

    pair_loop(attend)
    flow.sent(ctx_out)
    send_out[...] = dot(ctx_out[tokens : 2 * tokens, :], wout[...]).astype(BF)
    flow.sent(send_out)
    keep_out[...] = dot(ctx_out[0:tokens, :], wout[...]).astype(BF)
    flow.sent(keep_out)


def ffn_kernel_body(
    first, flow, s_ref, go, gc, gx, gd, full, att, mod, up, down, kern, kgrad_in,
    g_out, keep_out, send_out, mods_out, kgrad_out, active_out, gfed_out, second_out, ghid_out, fkeep_out, fsend_out,
    held, padded, slope, gpad, mid, fed, low, sums, turned,
):
    n = s_ref[0]
    core = jnp.bitwise_and(n, 1)
    share, tokens = go.shape[1], go.shape[2]
    units = up.shape[1]
    tall = tokens + 2 * SIDE
    zero_edges(padded)
    zero_edges(gpad)
    flow.need(go, gc, gx, gd)
    gather_features(n, (go, gc, gx, gd), held, g_out)
    flow.sent(g_out)
    flow.need(full, att, mod, kgrad_in)
    kgrad_out[...] = jnp.zeros(kgrad_out.shape, F32) if first else kgrad_in[...]

    def rows(rel, at):
        lat = jnp.bitwise_xor(rel, core)
        here = pl.ds(at, ROWS)
        middle = full[here, :].astype(F32) + mod[lat, 2:3, :] * att[here, :].astype(F32)
        mid[here, :] = middle
        normed, _ = norm_stats(middle)
        second_out[here, :] = (normed * (1.0 + mod[lat, 4:5, :]) + mod[lat, 3:4, :]).astype(BF)
        gfed_out[here, :] = (mod[lat, 5:6, :] * g_out[here, :].astype(F32)).astype(BF)

    row_loop(tokens, rows)
    flow.sent(second_out, gfed_out)
    flow.need(up, kern)
    hidden = dot(second_out[...], up[...])
    for rel in range(PAIR):
        padded[inside(padded, rel), :] = hidden[rel * tokens : (rel + 1) * tokens]

    def lanes(rel, at):
        taps = taps_of(kern, at)
        for band in range(0, tokens, BAND):
            here = pl.ds(pl.multiple_of(rel * tokens + band, BAND), BAND)
            mixed = conv_band(padded, pl.multiple_of(rel * tall + band, SIDE), at, taps)
            square = mixed * mixed
            curve = jnp.tanh(GELU_A * mixed * (1.0 + GELU_B * square))
            half = 0.5 * (1.0 + curve)
            active_out[here, at] = (mixed * half).astype(BF)
            slope[here, at] = half + (0.5 * GELU_A) * mixed * (1.0 - curve * curve) * (
                1.0 + (3.0 * GELU_B) * square
            )

    lane_loop(units, lanes)
    flow.sent(active_out)
    flow.need(down)
    fed[...] = dot(active_out[...], down[...])
    sums[...] = jnp.zeros(sums.shape, F32)

    def rows_fed(rel, at):
        lat = jnp.bitwise_xor(rel, core)
        here = pl.ds(at, ROWS)
        term = fed[here, :]
        sums[lat] += fold_rows(term * g_out[here, :].astype(F32))
        low[here, :] = (mod[lat, 5:6, :] * term + 0.25 * mid[here, :]).astype(BF)

    row_loop(tokens, rows_fed)
    for lat in range(PAIR):
        mods_out[lat] = jnp.sum(sums[lat], 0, keepdims=True)
    by_core(core, low, share, fkeep_out, fsend_out, turned)
    flow.sent(fkeep_out, fsend_out, mods_out)
    gact = dot_nt(gfed_out[...], down[...]).astype(BF).astype(F32)
    for rel in range(PAIR):
        here = slice(rel * tokens, (rel + 1) * tokens)
        gpad[inside(gpad, rel), :] = gact[here] * slope[here, :]

    def lanes_back(rel, at):
        taps = taps_of(kern, at)
        sums = [None] * 9
        for band in range(0, tokens, BAND):
            here = pl.ds(pl.multiple_of(rel * tokens + band, BAND), BAND)
            base = pl.multiple_of(rel * tall + band, SIDE)
            total, shifted = conv_back_band(gpad, base, at, taps)
            ghid_out[here, at] = total.astype(BF)
            for r in range(3):
                values = padded[pl.ds(base + SIDE * r, BAND), at]
                for c in range(3):
                    part = fold_rows(values * shifted[c])
                    sums[3 * r + c] = part if sums[3 * r + c] is None else sums[3 * r + c] + part
        for t in range(9):
            kgrad_out[t : t + 1, at] += jnp.sum(sums[t], 0, keepdims=True)

    lane_loop(units, lanes_back)
    flow.sent(ghid_out, kgrad_out)
    send_out[...] = dot_nt(ghid_out[tokens : 2 * tokens, :], up[...]).astype(BF)
    flow.sent(send_out)
    keep_out[...] = dot_nt(ghid_out[0:tokens, :], up[...]).astype(BF)
    flow.sent(keep_out)


def attn_back_body(
    flow, s_ref, full, att, gs, gfull, mod, q_in, k_in, v_in, wout, gates,
    gmid_out, mods_out, gatt_out, gqkv_out,
    sums, gctx,
):
    core = jnp.bitwise_and(s_ref[0], 1)
    tokens = full.shape[0] // PAIR
    width = full.shape[1]
    share = q_in.shape[1]
    mods_out[...] = jnp.zeros(mods_out.shape, F32)
    sums[...] = jnp.zeros(sums.shape, F32)
    flow.need(full, att, gs, gfull, mod)

    def rows(rel, at):
        lat = jnp.bitwise_xor(rel, core)
        here = pl.ds(at, ROWS)
        gate1 = mod[lat, 2:3, :]
        attended = att[here, :].astype(F32)
        normed, inv = norm_stats(full[here, :].astype(F32) + gate1 * attended)
        grad = gs[here, :].astype(F32)
        inner = grad * (1.0 + mod[lat, 4:5, :])
        mean_a = jnp.sum(inner, -1, keepdims=True) * (1.0 / width)
        mean_b = jnp.sum(inner * normed, -1, keepdims=True) * (1.0 / width)
        whole_grad = gfull[here, :].astype(F32) + inv * (inner - mean_a - normed * mean_b)
        gmid_out[here, :] = whole_grad.astype(BF)
        gatt_out[here, :] = (gate1 * whole_grad).astype(BF)
        sums[3 * lat] += fold_rows(attended * whole_grad)
        sums[3 * lat + 1] += fold_rows(grad)
        sums[3 * lat + 2] += fold_rows(grad * normed)

    row_loop(tokens, rows)
    for lat in range(PAIR):
        for k in range(3):
            mods_out[lat, 2 + k : 3 + k, :] = 0.25 * jnp.sum(sums[3 * lat + k], 0, keepdims=True)
    flow.need(wout, q_in, k_in, v_in, gates)
    for lat in range(PAIR):
        mods_out[lat, 5:6, :] = gates[lat]
    flow.sent(gatt_out, gmid_out, mods_out)
    gctx[...] = dot_nt(gatt_out[...], wout[...]).astype(BF)
    masks = head_masks(share)
    heads = len(masks)
    factor = 1.0 / math.sqrt(HEAD_DIM)

    def attend(rel):
        here = pl.ds(pl.multiple_of(rel * tokens, tokens), tokens)
        query, key, value, grads = q_in[here, :], k_in[here, :], v_in[here, :], gctx[here, :]
        parts_q, parts_k, parts_v = [], [], []
        for parity in range(2):
            q = half_rows(query, parity)
            k = half_rows(key, parity)
            v = half_rows(value, parity)
            gc = half_rows(grads, parity)
            q_all = jnp.concatenate([q * m for m in masks], axis=0)
            k_all = jnp.concatenate([k * m for m in masks], axis=0)
            gc_all = jnp.concatenate([gc * m for m in masks], axis=0)
            probs = softmax_rows(q_all, k)
            parts_v.append(dot_tn(probs.astype(BF), gc_all).astype(BF))
            gprobs = dot_nt(gc_all, v).astype(BF).astype(F32)
            gscores = (probs * (gprobs - jnp.sum(probs * gprobs, -1, keepdims=True))).astype(BF)
            parts_q.append((dot(beside(gscores, heads), k_all) * factor).astype(BF))
            parts_k.append((dot_tn(gscores, q_all) * factor).astype(BF))
        for k, parts in enumerate((parts_q, parts_k, parts_v)):
            gqkv_out[here, k * share : (k + 1) * share] = join_rows(*parts)

    pair_loop(attend)
    flow.sent(gqkv_out)


def input_back_body(
    closing, flow, s_ref, full, mod, gqkv, wqkv, kern, kgrad_in, gmid, mods_in, before,
    kgrad_out, mods_out, keep_out, send_out,
    normed1, scale1, first, gpad, gback, low, mods, rows_out, turned,
):
    core = jnp.bitwise_and(s_ref[0], 1)
    tokens = full.shape[0] // PAIR
    width = full.shape[1]
    share = gqkv.shape[1] // 3
    tall = tokens + 2 * SIDE
    zero_edges(first)
    zero_edges(gpad)
    flow.need(full, mod)

    def rows_first(rel, at):
        lat = jnp.bitwise_xor(rel, core)
        here = pl.ds(at, FEW_ROWS)
        normed, inv = norm_stats(full[here, :].astype(F32))
        normed1[here, :] = normed
        scale1[here, :] = jnp.broadcast_to(inv, (FEW_ROWS, LANES))
        inside_rows = pl.ds(pl.multiple_of(at + (2 * rel + 1) * SIDE, SIDE), FEW_ROWS)
        first[inside_rows, :] = normed * (1.0 + mod[lat, 1:2, :]) + mod[lat, 0:1, :]

    row_loop(tokens, rows_first, FEW_ROWS)
    flow.need(gqkv, wqkv, kern, kgrad_in, gmid, mods_in, before)
    kgrad_out[...] = kgrad_in[...] if closing else jnp.zeros(kgrad_out.shape, F32)
    mods[...] = mods_in[...]
    for rel in range(PAIR):
        here = slice(rel * tokens, (rel + 1) * tokens)
        gpad[inside(gpad, rel), :] = dot(gqkv[here, :], wqkv[...])

    def lanes(rel, at):
        taps = taps_of(kern, at)
        sums = [None] * 9
        shift_sum, scale_sum = None, None
        for band in range(0, tokens, BAND):
            here = pl.ds(pl.multiple_of(rel * tokens + band, BAND), BAND)
            base = pl.multiple_of(rel * tall + band, SIDE)
            total, shifted = conv_back_band(gpad, base, at, taps)
            gback[here, at] = total
            part_a, part_b = fold_rows(total), fold_rows(total * normed1[here, at])
            shift_sum = part_a if shift_sum is None else shift_sum + part_a
            scale_sum = part_b if scale_sum is None else scale_sum + part_b
            for r in range(3):
                values = first[pl.ds(base + SIDE * r, BAND), at]
                for c in range(3):
                    part = fold_rows(values * shifted[c])
                    sums[3 * r + c] = part if sums[3 * r + c] is None else sums[3 * r + c] + part
        for t in range(9):
            kgrad_out[t : t + 1, at] += jnp.sum(sums[t], 0, keepdims=True)
        lat = jnp.bitwise_xor(rel, core)
        mods[lat, 0:1, at] = jnp.sum(shift_sum, 0, keepdims=True)
        mods[lat, 1:2, at] = jnp.sum(scale_sum, 0, keepdims=True)

    lane_loop(width, lanes)
    if closing:
        rows_out[...] = jnp.zeros(rows_out.shape, F32)
        for lat in range(PAIR):
            rows_out[6 * lat : 6 * lat + 6, :] = before[lat, 0:6, :]
            rows_out[6 * (PAIR + lat) : 6 * (PAIR + lat) + 6, :] = mods[lat, 0:6, :]
        rows_out[12 * PAIR : 12 * PAIR + 9, :] = kgrad_out[0:9, :]
        mods_out[...] = rows_out[...].astype(BF)
    else:
        mods_out[...] = mods[...]
    flow.sent(mods_out, kgrad_out)

    def rows_back(rel, at):
        lat = jnp.bitwise_xor(rel, core)
        here = pl.ds(at, FEW_ROWS)
        inner = gback[here, :] * (1.0 + mod[lat, 1:2, :])
        normed = normed1[here, :]
        mean_a = jnp.sum(inner, -1, keepdims=True) * (1.0 / width)
        mean_b = jnp.sum(inner * normed, -1, keepdims=True) * (1.0 / width)
        grad = scale1[here, 0:1] * (inner - mean_a - normed * mean_b)
        low[here, :] = (grad + 0.25 * gmid[here, :].astype(F32)).astype(BF)

    row_loop(tokens, rows_back, FEW_ROWS)
    by_core(core, low, share, keep_out, send_out, turned)
    flow.sent(keep_out, send_out)


class Flow:
    def __init__(self, arrivals, departures):
        self.arrivals, self.departures = arrivals, departures
        self.leaving = []
        for _, copy in arrivals:
            copy.start()

    def need(self, *refs):
        for ref in refs:
            for _, copy in [a for a in self.arrivals if a[0] is ref]:
                copy.wait()
            self.arrivals = [a for a in self.arrivals if a[0] is not ref]

    def sent(self, *refs):
        for ref in refs:
            for held, copy in self.departures:
                if held is ref:
                    copy.start()
                    self.leaving.append(copy)

    def end(self):
        for copy in self.leaving:
            copy.wait()


def call(body, name, scalars, ins, outs, scratch, flops, held=()):
    n_in, n_out = len(ins), len(outs)
    places, buffer_shapes = [], []
    for array, window, into in ins:
        dims = array.shape if window is None else (window[0].size,) + array.shape[1:]
        if into is None:
            buffer_shapes.append((dims, array.dtype))
        elif into[0].start == 0:
            buffer_shapes.append(((PAIR * dims[0],) + dims[1:], array.dtype))
        places.append(len(buffer_shapes) - 1)

    def run(s_ref, *refs):
        sources = refs[:n_in]
        targets = refs[n_in + len(held) : n_in + len(held) + n_out]
        buffers = refs[n_in + len(held) + n_out : -1]
        sems = refs[-1]
        n_held = len(buffer_shapes)
        buffers_in, buffers_out = buffers[:n_held], buffers[n_held : n_held + n_out]
        rest = buffers[n_held + n_out :]
        arrivals, departures = [], []
        for k, (source, (_, window, into)) in enumerate(zip(sources, ins)):
            view = source if window is None else source.at[window]
            buffer = buffers_in[places[k]]
            target = buffer if into is None else buffer.at[into]
            arrivals.append((buffer, pltpu.make_async_copy(view, target, sems.at[k])))
        for k, (target, buffer, out) in enumerate(zip(targets, buffers_out, outs)):
            view = target if out[2] is None else target.at[out[2]]
            departures.append((buffer, pltpu.make_async_copy(buffer, view, sems.at[n_in + k])))
        flow = Flow(arrivals, departures)
        body(flow, s_ref, *buffers_in, *buffers_out, *rest)
        flow.end()

    anywhere = pl.BlockSpec(memory_space=pl.ANY)
    return pl.pallas_call(
        run,
        name=name,
        out_shape=[jax.ShapeDtypeStruct(o[0], o[1]) for o in outs],
        grid_spec=pltpu.PrefetchScalarGridSpec(
            num_scalar_prefetch=1,
            grid=(1,),
            in_specs=[anywhere] * (n_in + len(held)),
            out_specs=[anywhere] * n_out,
            scratch_shapes=[pltpu.VMEM(dims, dtype) for dims, dtype in buffer_shapes]
            + [pltpu.VMEM(o[3], o[1]) for o in outs]
            + scratch
            + [pltpu.SemaphoreType.DMA((n_in + n_out,))],
        ),
        input_output_aliases={1 + n_in + k: n_out - len(held) + k for k in range(len(held))},
        compiler_params=pltpu.CompilerParams(vmem_limit_bytes=VMEM_LIMIT),
        cost_estimate=pl.CostEstimate(flops=flops, bytes_accessed=10**6, transcendentals=0),
    )(scalars, *[i[0] for i in ins], *held)


def slices_out(slots, slot, share, tokens):
    return ((2, slots, share, tokens), BF, (slice(None), pl.ds(PAIR * slot, PAIR)), (2, PAIR, share, tokens))


def whole(array):
    return (array, None, None)


def stacked(arrays):
    rows = arrays[0].shape[0]
    return [(v, None, (pl.ds(k * rows, rows),)) for k, v in enumerate(arrays)]


def whole_out(dims, dtype):
    return (dims, dtype, None, dims)


def pair_rows(array, pair):
    rows = array.shape[0] // PAIRS
    return (array, (pl.ds(rows * pair, rows),), None)


def pair_rows_out(rows, width, pair):
    return ((PAIRS * rows, width), BF, (pl.ds(rows * pair, rows),), (rows, width))


def pair_of(array, pair):
    return (array, (pl.ds(PAIR * pair, PAIR),), None)


def split_low(v):
    high = v.astype(BF)
    return high, (v - high.astype(F32)).astype(BF)


def rows_product(a, b):
    (ah, al), (bh, bl) = split_low(a), split_low(b)
    return dot_tn(jnp.concatenate([ah, al, ah], 0), jnp.concatenate([bh, bh, bl], 0))


def back_product(a, weight):
    (ah, al), (wh, wl) = split_low(a), split_low(weight)
    return dot_nt(ah, wh) + dot_nt(al, wh) + dot_nt(ah, wl)


def product(a, weight):
    (ah, al), (wh, wl) = split_low(a), split_low(weight)
    return dot(ah, wh) + dot(al, wh) + dot(ah, wl)


def silu(v):
    return v / (1.0 + jnp.exp(-v))


def silu_slope(v):
    gate = 1.0 / (1.0 + jnp.exp(-v))
    return gate * (1.0 + v * (1.0 - gate))


def row_blocks(source, target, sems, rows):
    return [
        pltpu.make_async_copy(source.at[pl.ds(at, rows)], target.at[pl.ds(at, rows)], sems.at[at // rows])
        for at in range(0, source.shape[0], rows)
    ]


def condition_body(
    steps, stamps, wide, bias, time_in, time_out, ada,
    mod_out, embedded, inner_pre, inner, outer_pre, outer, held_in, held_out, held, sums, parts, rows_of, sems,
):
    depth = ada.shape[0]
    per_dev, count, width = mod_out.shape
    first = pltpu.make_async_copy(time_in, held_in, sems.at[0])
    second = pltpu.make_async_copy(time_out, held_out, sems.at[1])
    blocks = row_blocks(ada, held, sems.at[pl.ds(2, depth // WEIGHT_ROWS)], WEIGHT_ROWS)
    for copy in [first, second] + blocks:
        copy.start()
    halved = embedded.shape[1] // 2
    for r in range(embedded.shape[0]):
        at = jnp.bitwise_xor(wide[0], steps[r // per_dev]) * per_dev + r % per_dev
        rows_of[r : r + 1, :] = jnp.broadcast_to(stamps[at].astype(F32), (1, halved))
    order = lax.broadcasted_iota(jnp.int32, (1, halved), 1).astype(F32)
    angles = rows_of[...] * jnp.exp(-math.log(10000.0) * order / halved)
    embedded[:, 0:halved] = jnp.cos(angles)
    embedded[:, halved:] = jnp.sin(angles)
    first.wait()
    inner_pre[...] = product(embedded[...], held_in[...])
    inner[...] = silu(inner_pre[...])
    second.wait()
    outer_pre[...] = product(inner[...], held_out[...])
    outer[...] = silu(outer_pre[...])
    wide_bias = [jnp.concatenate([bias[k + j : k + j + 1, :] for j in range(width // LANES)], 1)
                 for k in range(0, bias.shape[0], width // LANES)]
    total = jnp.concatenate(wide_bias, 1)
    sums[...] = jnp.broadcast_to(total, sums.shape)
    for k in range(depth // WEIGHT_ROWS):
        parts[k] = outer[0:8, k * WEIGHT_ROWS : (k + 1) * WEIGHT_ROWS]

    def add(k, carry):
        rows = pl.ds(pl.multiple_of(k * WEIGHT_ROWS, WEIGHT_ROWS), WEIGHT_ROWS)
        pltpu.make_async_copy(ada.at[rows], held.at[rows], sems.at[2 + k]).wait()
        sums[...] += product(parts[k], held[rows, :])
        return carry

    lax.fori_loop(0, depth // WEIGHT_ROWS, add, 0)
    total = sums[...]
    for lat in range(per_dev):
        for k in range(count):
            mod_out[lat, k : k + 1, :] = total[lat : lat + 1, k * width : (k + 1) * width]


def condition(steps, stamps, wide, time_in, time_out, ada_weight, ada_bias, per_dev, width):
    latent_total = stamps.shape[0]
    depth, columns = ada_weight.shape
    vmem = pl.BlockSpec(memory_space=pltpu.VMEM)
    anywhere = pl.BlockSpec(memory_space=pl.ANY)
    rows = jax.ShapeDtypeStruct((latent_total, depth), F32)
    return pl.pallas_call(
        functools.partial(condition_body, steps),
        name="condition",
        in_specs=[pl.BlockSpec(memory_space=pltpu.SMEM)] * 2 + [vmem, anywhere, anywhere, anywhere],
        out_specs=[vmem] * 6,
        out_shape=[
            jax.ShapeDtypeStruct((per_dev, columns // width, width), F32),
            jax.ShapeDtypeStruct((latent_total, time_in.shape[0]), F32),
            rows, rows, rows, rows,
        ],
        scratch_shapes=[
            pltpu.VMEM(time_in.shape, F32),
            pltpu.VMEM(time_out.shape, F32),
            pltpu.VMEM(ada_weight.shape, F32),
            pltpu.VMEM((8, columns), F32),
            pltpu.VMEM((depth // WEIGHT_ROWS, 8, WEIGHT_ROWS), F32),
            pltpu.VMEM((latent_total, time_in.shape[0] // 2), F32),
            pltpu.SemaphoreType.DMA((2 + depth // WEIGHT_ROWS,)),
        ],
        compiler_params=pltpu.CompilerParams(vmem_limit_bytes=VMEM_LIMIT),
        cost_estimate=pl.CostEstimate(flops=8 * 10**9, bytes_accessed=10**6, transcendentals=0),
    )(stamps, wide, ada_bias.reshape(columns // LANES, LANES), time_in, time_out, ada_weight)


def condition_back_body(
    factor, gmod, embedded, inner_pre, inner, outer_pre, outer, time_out, ada,
    time_in_grad, time_out_grad, ada_grad, held_out, held, outer_grad, columns, sems, arriving, leaving,
):
    count = ada.shape[0] // BACK_ROWS

    def block_copy(source, target, sem, k):
        rows = pl.ds(k * BACK_ROWS, BACK_ROWS)
        return pltpu.make_async_copy(source.at[rows], target.at[rows], sem.at[k])

    first = pltpu.make_async_copy(time_out, held_out, sems.at[0])
    for k in range(count):
        block_copy(ada, held, arriving, k).start()
    first.start()
    high, low = split_low(outer[...])
    both = jnp.concatenate([high, low], 0)
    for k in range(count):
        columns[k] = both[:, k * BACK_ROWS : (k + 1) * BACK_ROWS]

    def block(k, carry):
        rows = pl.ds(pl.multiple_of(k * BACK_ROWS, BACK_ROWS), BACK_ROWS)
        block_copy(ada, held, arriving, k).wait()
        grads = gmod[...]
        high, low = split_low(held[rows, :])
        outer_grad[rows, :] = dot_nt(high, grads) + dot_nt(low, grads)
        held[rows, :] = dot_tn(columns[k], jnp.concatenate([grads, grads], 0)) * factor
        block_copy(held, ada_grad, leaving, k).start()
        return carry

    lax.fori_loop(0, count, block, 0)
    first.wait()
    back = outer_grad[...].T * factor * silu_slope(outer_pre[...])
    time_out_grad[...] = rows_product(inner[...], back)
    back = back_product(back, held_out[...]) * silu_slope(inner_pre[...])
    time_in_grad[...] = rows_product(embedded[...], back)
    for k in range(count):
        block_copy(held, ada_grad, leaving, k).wait()


def condition_back(gmod, embedded, stages, time_out, ada_weight, factor):
    depth = ada_weight.shape[0]
    latent_total = gmod.shape[0]
    vmem = pl.BlockSpec(memory_space=pltpu.VMEM)
    anywhere = pl.BlockSpec(memory_space=pl.ANY)
    time_in_dims = (embedded.shape[1], time_out.shape[0])
    return pl.pallas_call(
        functools.partial(condition_back_body, factor),
        name="condition_back",
        in_specs=[vmem] * 6 + [anywhere] * 2,
        out_specs=[vmem, vmem, anywhere],
        out_shape=[
            jax.ShapeDtypeStruct(time_in_dims, F32),
            jax.ShapeDtypeStruct(time_out.shape, F32),
            jax.ShapeDtypeStruct(ada_weight.shape, F32),
        ],
        scratch_shapes=[
            pltpu.VMEM(time_out.shape, F32),
            pltpu.VMEM(ada_weight.shape, F32),
            pltpu.VMEM((depth, latent_total), F32),
            pltpu.VMEM((depth // BACK_ROWS, 2 * latent_total, BACK_ROWS), BF),
            pltpu.SemaphoreType.DMA((1,)),
            pltpu.SemaphoreType.DMA((depth // BACK_ROWS,)),
            pltpu.SemaphoreType.DMA((depth // BACK_ROWS,)),
        ],
        compiler_params=pltpu.CompilerParams(vmem_limit_bytes=VMEM_LIMIT),
        cost_estimate=pl.CostEstimate(flops=1, bytes_accessed=1, transcendentals=0),
    )(gmod, embedded, *stages, time_out, ada_weight)


def attn_forward(scalars, pair, x_parts, mod, attn_kernel, qkv_weight, out_weight, held):
    _, share, tokens = x_parts[0].shape
    width = out_weight.shape[1]
    rows = PAIR * tokens
    thin = whole_out((rows, share), BF)
    half = whole_out((tokens, width), BF)
    return call(
        attn_kernel_body, "attn_fwd", scalars,
        [pair_of(v, pair) for v in x_parts] + [pair_of(mod, pair), whole(attn_kernel), whole(qkv_weight), whole(out_weight)],
        [whole_out((rows, width), BF), thin, thin, thin, half, half, pair_rows_out(rows, width, pair),
         pair_rows_out(rows, share, pair)],
        [pltpu.VMEM((4, share, tokens), BF), pltpu.VMEM((PAIR * (tokens + 2 * SIDE), width), F32)],
        6_000_000_000, held,
    )


def feed_forward(scalars, pair, full, att, g_parts, mod, up_weight, down_weight, ffn_kernel, slots, taps, held):
    _, share, tokens = g_parts[0].shape
    width, units = up_weight.shape
    rows = PAIR * tokens
    tall = PAIR * (tokens + 2 * SIDE)
    half = whole_out((tokens, width), BF)
    slices = slices_out(slots, pair, share, tokens)
    return call(
        functools.partial(ffn_kernel_body, pair == 0), "ffn", scalars,
        [pair_of(v, pair) for v in g_parts] + [whole(full)] + stacked(att)
        + [pair_of(mod, pair), whole(up_weight), whole(down_weight), whole(ffn_kernel), whole(taps)],
        [whole_out((rows, width), BF), half, half, whole_out((PAIR, 1, width), F32), whole_out((16, units), F32),
         whole_out((rows, units), BF), whole_out((rows, width), BF), pair_rows_out(rows, width, pair),
         pair_rows_out(rows, units, pair), slices, slices],
        [pltpu.VMEM((4, share, tokens), BF), pltpu.VMEM((tall, units), F32), pltpu.VMEM((rows, units), F32),
         pltpu.VMEM((tall, units), F32), pltpu.VMEM((rows, width), F32), pltpu.VMEM((rows, width), F32),
         pltpu.VMEM((rows, width), BF), pltpu.VMEM((PAIR, 8, width), F32), pltpu.VMEM((width, tokens), BF)],
        10_000_000_000, held,
    )


def attn_backward(scalars, pair, full, att, gsec, gfull, mod, qkv, out_weight, gates, held):
    tokens, width = att[0].shape
    share = out_weight.shape[0]
    rows = PAIR * tokens
    broad = whole_out((rows, width), BF)
    return call(
        attn_back_body, "attn_bwd", scalars,
        [whole(full)] + stacked(att) + stacked(gsec) + [whole(gfull), pair_of(mod, pair)]
        + [whole(v) for v in qkv] + [whole(out_weight), whole(gates)],
        [broad, whole_out((PAIR, 8, width), F32), pair_rows_out(rows, width, pair), pair_rows_out(rows, 3 * share, pair)],
        [pltpu.VMEM((3 * PAIR, 8, width), F32), pltpu.VMEM((rows, share), BF)],
        6_000_000_000, held,
    )


def input_backward(scalars, pair, full, mod, gqkv, qkv_weight, attn_kernel, taps, gmid, mods_in, before, slots, held):
    rows, width = full.shape
    tokens = rows // PAIR
    share = gqkv.shape[1] // 3
    tall = PAIR * (tokens + 2 * SIDE)
    slices = slices_out(slots, slots // PAIR // 2 + pair, share, tokens)
    closing = pair > 0
    mods = whole_out((PACKED, width), BF) if closing else whole_out((PAIR, 8, width), F32)
    return call(
        functools.partial(input_back_body, closing), "input_bwd", scalars,
        [whole(full), pair_of(mod, pair), pair_rows(gqkv, pair), whole(qkv_weight), whole(attn_kernel), whole(taps), whole(gmid),
         whole(mods_in), whole(before)],
        [whole_out((16, width), F32), mods, slices, slices],
        [pltpu.VMEM((rows, width), F32), pltpu.VMEM((rows, LANES), F32), pltpu.VMEM((tall, width), F32),
         pltpu.VMEM((tall, width), F32), pltpu.VMEM((rows, width), F32), pltpu.VMEM((rows, width), BF),
         pltpu.VMEM((PAIR, 8, width), F32), pltpu.VMEM((PACKED, width), F32), pltpu.VMEM((width, tokens), BF)],
        6_000_000_000, held,
    )


def core_swap(v):
    return lax.ppermute(v, "narrow", [(0, 1), (1, 0), (2, 3), (3, 2)])


def x_swap(v):
    return lax.ppermute(v, "narrow", [(0, 2), (2, 0), (1, 3), (3, 1)])


def sum_pair(a, b):
    return (a.astype(F32) + b.astype(F32)).astype(BF)


def slice_halves(x, keep, arrived):
    both = sum_pair(keep, arrived)
    return (
        lax.dynamic_index_in_dim(both, x, 0, keepdims=False),
        lax.dynamic_index_in_dim(both, 1 - x, 0, keepdims=False),
    )


def wide_swap(v, bit, count):
    return lax.ppermute(v, "wide", [(i, i ^ bit) for i in range(count)])


def pick(v, parts, at):
    rows = v.shape[0] // parts
    return lax.dynamic_slice_in_dim(v, at * rows, rows, 0)


def in_place(second, own, came, axis):
    dims = own.shape[:axis] + (2,) + own.shape[axis + 1 :]
    chosen = lax.broadcast_in_dim(second, dims, (axis,))
    return jnp.where(chosen, own, came)


class WideSum:
    def __init__(self, product, bits, masks, count, back=None):
        self.count, self.dims, self.bits, self.masks = count, product.shape, bits, masks
        self.levels = count.bit_length() - 1
        self.ahead = list(range(self.levels))
        self.back = list(reversed(self.ahead)) if back is None else back
        self.opened = False
        self.held = product

    def swap(self, sent, level):
        self.came = wide_swap(sent, 1 << level, self.count)

    def halve(self, held, came):
        level = self.ahead[0]
        if level == 0:
            held = pick(held, 2, self.bits[0])
        if len(self.ahead) == 1:
            return (sum_pair(held, came),)
        bit = self.bits[level + 1]
        return tuple(sum_pair(pick(held, 2, at), pick(came, 2, at)) for at in (1 - bit, bit))

    def pending(self):
        if not self.opened:
            return lambda v: pick(v, 2, 1 - self.bits[0]), (self.held,)
        if self.ahead:
            return self.halve, (self.held, self.came)
        level = self.back[0]
        return lambda a, b: in_place(self.masks[level], a, b, level), (self.held, self.came)

    def accept(self, out):
        if not self.opened:
            self.opened = True
            self.swap(out, 0)
        elif self.ahead:
            self.ahead.pop(0)
            self.held = out[-1]
            if self.ahead:
                self.swap(out[0], self.ahead[0])
            else:
                self.held = self.held.reshape((1,) * self.levels + self.held.shape)
                self.swap(self.held, self.back[0])
        else:
            self.back.pop(0)
            self.held = out
            self.swap(out, self.back[0])

    def done(self):
        return self.opened and not self.ahead and len(self.back) == 1

    def finish(self, order, dtype):
        level = self.back[0]
        whole_sum = order(lambda a, b: in_place(self.masks[level], a, b, level).astype(dtype), self.held, self.came)
        return lax.optimization_barrier(whole_sum).reshape(self.dims)


class Steps:
    def __init__(self, came, steps):
        self.came, self.steps = came, list(steps)

    def pending(self):
        return self.steps[0][0], self.came

    def accept(self, out):
        _, move = self.steps.pop(0)
        self.came = move(out)

    def done(self):
        return not self.steps


class Order:
    def __init__(self):
        self.last = ()

    def __call__(self, step, *inputs):
        inputs, _ = lax.optimization_barrier((inputs, self.last))
        out = step(*inputs)
        self.last = tuple(jax.tree.leaves(out)[:1])
        return out

    def advance(self, *chains):
        chains = [c for c in chains if not c.done()]
        if chains:
            work = [c.pending() for c in chains]
            outs = self(lambda *v: [w[0](*a) for w, a in zip(work, v)], *[w[1] for w in work])
            self.last = tuple(jax.tree.leaves(out)[0] for out in outs)
            for chain, out in zip(chains, outs):
                chain.accept(out)


def after(value, *others):
    return lax.optimization_barrier((value, others))[0]


def body(
    latents, cotangent, timesteps, time_in, time_out, ada_weight, ada_bias,
    attn_kernel, qkv_weight, out_weight, up_weight, ffn_kernel, down_weight,
):
    wide_count = lax.axis_size("wide")
    wide_at = lax.axis_index("wide")
    n = lax.axis_index("narrow")
    per_dev, tokens, share = latents.shape
    width = out_weight.shape[1]
    units = up_weight.shape[1]
    latent_total = timesteps.shape[0]
    scalars = n.astype(jnp.int32).reshape(1)

    steps, bit = [0], wide_count // 2
    while bit:
        steps, bit = steps + [k ^ bit for k in steps], bit // 2
    mod, embedded, *stages = condition(
        steps, timesteps, wide_at.astype(jnp.int32).reshape(1), time_in, time_out, ada_weight, ada_bias, per_dev, width
    )
    x = n // 2
    factor = 1.0 / latent_total

    def token_products(lefts, rights):
        return (sum(dot_tn(a, b) for a, b in zip(lefts, rights)) * factor).astype(BF)

    x_own = jnp.swapaxes(latents, 1, 2)
    g_own = jnp.swapaxes(cotangent, 1, 2)
    qkv_rows = jnp.swapaxes(qkv_weight, 1, 2)
    qkv_all = qkv_rows.reshape(3 * share, width)
    order = Order()
    x_across = x_swap(x_own)
    x_across = after(x_across, mod)
    g_across = x_swap(after(g_own, x_across))
    x_parts = (x_own, core_swap(x_own), x_across, core_swap(x_across))
    g_parts = (g_own, core_swap(g_own), g_across, core_swap(g_across))

    def attend(pair, held=()):
        return lambda parts: attn_forward(scalars, pair, parts, mod, attn_kernel, qkv_rows, out_weight, held)

    fwd_a = order(attend(0), x_parts)
    here_a = order(sum_pair, fwd_a[4], core_swap(fwd_a[5]))
    fwd_b = order(attend(1, fwd_a[6:8]), after(x_parts, g_across))
    levels = wide_count.bit_length() - 1
    places = [jnp.bitwise_and(jnp.right_shift(wide_at, k), 1) for k in range(levels)]
    masks = [jnp.arange(2, dtype=jnp.int32) == place for place in places]
    att_a, masks = order(lambda a, b, m: (sum_pair(a, b), m), here_a, x_swap(here_a), masks)
    here_b = order(sum_pair, fwd_b[4], core_swap(fwd_b[5]))
    att_a = (att_a, core_swap(att_a))

    slots = 2 * per_dev

    def feed(pair, full, taps, held=()):
        return lambda att, parts: feed_forward(
            scalars, pair, full, att, parts, mod, up_weight, down_weight, ffn_kernel, slots, taps, held
        )

    ffn_a = order(feed(0, fwd_a[0], ffn_kernel), att_a, g_parts)
    att_b = order(sum_pair, here_b, x_swap(here_b))
    att_b = (att_b, core_swap(att_b))
    here_a = order(sum_pair, ffn_a[1], core_swap(ffn_a[2]))
    ffn_b = order(feed(1, fwd_b[0], ffn_a[4], ffn_a[7:11]), att_b, g_parts)
    sec_a = order(sum_pair, here_a, x_swap(here_a))
    sec_a = (sec_a, core_swap(sec_a))
    down_product = order(token_products, [ffn_a[5], ffn_b[5]], [ffn_a[6], ffn_b[6]])
    down_sum = WideSum(down_product, places, masks, wide_count)
    order.advance(down_sum)
    here_b = order(sum_pair, ffn_b[1], core_swap(ffn_b[2]))
    up_product = order(token_products, [ffn_b[7]], [ffn_b[8]])
    up_sum = WideSum(up_product, places, masks, wide_count)
    order.advance(up_sum)

    def attend_back(pair, fwd, ffn, held=()):
        return lambda att, sec: attn_backward(
            scalars, pair, fwd[0], att, sec, ffn[0], mod, fwd[1:4], out_weight, ffn[3], held
        )

    def input_back(pair, fwd, taps, before, held):
        return lambda gqkv, gmid, mods: input_backward(
            scalars, pair, fwd[0], mod, gqkv, qkv_all, attn_kernel, taps, gmid, mods, before, slots, held
        )

    back_a = order(attend_back(0, fwd_a, ffn_a), att_a, sec_a)
    sec_b = order(sum_pair, here_b, x_swap(here_b))
    sec_b = (sec_b, core_swap(sec_b))
    order.advance(down_sum)
    back_b = order(attend_back(1, fwd_b, ffn_b, back_a[2:4]), att_b, sec_b)
    order.advance(down_sum)
    attn_product = order(
        lambda grads, grouped, contexts, attended: jnp.concatenate(
            [token_products([grads], [grouped]), token_products([contexts], [attended])], 0
        ),
        back_b[3], fwd_b[6], fwd_b[7], back_b[2],
    )
    attn_sum = WideSum(attn_product, places, masks, wide_count, [0] + list(range(levels - 1, 0, -1)))
    order.advance(attn_sum)
    order.advance(up_sum)
    order.advance(down_sum)
    in_a = order(input_back(0, fwd_a, attn_kernel, attn_kernel, ffn_b[9:11]), back_b[3], *back_a[:2])
    order.advance(down_sum, up_sum)
    order.advance(attn_sum)
    in_b = order(input_back(1, fwd_b, in_a[0], in_a[1], in_a[2:4]), back_b[3], *back_b[:2])
    order.advance(down_sum)

    rows = 6 * per_dev
    bits = [1 << k for k in reversed(range(levels))]
    moves = [lambda v, bit=bit: (v, wide_swap(v, bit, wide_count)) for bit in bits]
    join = lambda a, b: jnp.concatenate([a, b], 0)
    whole_rows = lambda a, b, c: join(sum_pair(a, b)[: rows + 9], c[:9].astype(BF))[None]
    mods = Steps(
        (in_b[1], core_swap(in_b[1])),
        [(sum_pair, lambda v: (v, x_swap(v), ffn_b[4]))]
        + [(work, move) for work, move in zip([whole_rows] + [join] * len(bits), moves)],
    )
    order.advance(up_sum)
    order.advance(mods)
    order.advance(attn_sum)
    order.advance(mods)
    order.advance(up_sum)
    while not down_sum.done():
        order.advance(down_sum)
    down_grad = down_sum.finish(order, F32)
    made = order(functools.partial(slice_halves, x), in_b[2], core_swap(in_b[3]))
    order.advance(attn_sum, mods)
    order.advance(attn_sum)
    while not all(c.done() for c in (mods, up_sum)):
        order.advance(mods, up_sum)

    def unpack(held):
        gmod = held[:, :rows].reshape(latent_total, 6 * width)
        taps = jnp.sum(held[:, rows:].astype(F32), 0) * factor
        return gmod, jnp.sum(gmod.astype(F32), 0) * factor, taps[:9], taps[9:]

    final_out, final_grad = order(
        lambda a, b: (sum_pair(a[:per_dev], b[:per_dev]), sum_pair(a[per_dev:], b[per_dev:])), made[0], x_swap(made[1])
    )
    order.last = (final_out, final_grad)
    unpacked = order(lambda a, b: unpack(join(a, b)), *mods.came)
    gmod, ada_bias_grad, attn_taps, ffn_taps = unpacked
    while not attn_sum.done():
        order.advance(attn_sum)
    time_in_grad, time_out_grad, ada_weight_grad = order(
        lambda g: condition_back(g, embedded, stages, time_out, ada_weight, factor), gmod
    )
    up_grad = up_sum.finish(order, F32)
    attn_grads = attn_sum.finish(order, BF)
    qkv_rows_grad, out_grad = attn_grads[: 3 * share].astype(F32), attn_grads[3 * share :].astype(F32)
    qkv_grad = jnp.swapaxes(qkv_rows_grad.reshape(3, share, width), 1, 2)
    final_out = jnp.swapaxes(final_out, 1, 2)
    final_grad = jnp.swapaxes(final_grad, 1, 2)
    return (
        final_out, final_grad, time_in_grad, time_out_grad, ada_weight_grad, ada_bias_grad,
        attn_taps, qkv_grad, out_grad, up_grad, ffn_taps, down_grad,
    )


def solution(mesh):
    tokens = P("wide", None, "narrow")
    weights = (P(None, None, "narrow"), P("narrow", None), P(None, "narrow"), P(None, "narrow"), P("narrow", None))
    return jax.shard_map(
        body,
        mesh=mesh,
        in_specs=(tokens, tokens, P(), P(), P(), P(), P(), P()) + weights,
        out_specs=(tokens, tokens, P(), P(), P(), P(), P()) + weights,
        check_vma=False,
    )
```
